32 devices in a mesh: img: 16 (over z, x, core), seq: 2 (over y).
Axes of the slice: x: 2, y: 2, z: 4, core: 2. Of those that a mesh axis runs over, the one named last changes fastest.
Arguments:
- small_in: bfloat16 [32, 1024, 768], P('img', 'seq'), may hold values from -6 to 6
- large_in: bfloat16 [32, 640, 768], P('img', 'seq'), may hold values from -6 to 6
- small_cot: bfloat16 [32, 1024, 768], P('img', 'seq'), may hold values from -6 to 6
- large_cot: bfloat16 [32, 640, 768], P('img', 'seq'), may hold values from -6 to 6
- first_gain: float32 [768], replicated, may hold values from 0.5 to 1.5
- first_bias: float32 [768], replicated, may hold values from -1.75 to 1.75
- query_weight: bfloat16 [768, 768], P('img'), may hold values from -0.21875 to 0.21875
- query_bias: float32 [768], replicated, may hold values from -1.75 to 1.75
- key_weight: bfloat16 [768, 768], P('img'), may hold values from -0.21875 to 0.21875
- value_weight: bfloat16 [768, 768], P('img'), may hold values from -0.21875 to 0.21875
- value_bias: float32 [768], replicated, may hold values from -1.75 to 1.75
- out_weight: bfloat16 [768, 768], P('img'), may hold values from -1.75 to 1.75
- out_bias: float32 [768], replicated, may hold values from -1.75 to 1.75
- attend_scale: float32 [768], replicated, may hold values from 0.5 to 1.5
- second_gain: float32 [768], replicated, may hold values from 0.5 to 1.5
- second_bias: float32 [768], replicated, may hold values from -1.75 to 1.75
- up_weight: bfloat16 [768, 3072], P('img'), may hold values from -0.21875 to 0.21875
- up_bias: float32 [3072], replicated, may hold values from -1.75 to 1.75
- down_weight: bfloat16 [3072, 768], P('img'), may hold values from -0.109375 to 0.109375
- down_bias: float32 [768], replicated, may hold values from -1.75 to 1.75
- feed_scale: float32 [768], replicated, may hold values from 0.5 to 1.5
- rel_table: float32 [12, 2212], replicated, may hold values from -6 to 6
Outputs:
- small_out: bfloat16 [32, 1024, 768], P('img', 'seq')
- large_out: bfloat16 [32, 640, 768], P('img', 'seq')
- small_grad: bfloat16 [32, 1024, 768], P('img', 'seq')
- large_grad: bfloat16 [32, 640, 768], P('img', 'seq')
- grad_first_gain: float32 [768], replicated
- grad_first_bias: float32 [768], replicated
- grad_query: float32 [768, 768], P('img')
- grad_query_bias: float32 [768], replicated
- grad_key: float32 [768, 768], P('img')
- grad_value: float32 [768, 768], P('img')
- grad_value_bias: float32 [768], replicated
- grad_out: float32 [768, 768], P('img')
- grad_out_bias: float32 [768], replicated
- grad_attend_scale: float32 [768], replicated
- grad_second_gain: float32 [768], replicated
- grad_second_bias: float32 [768], replicated
- grad_up: float32 [768, 3072], P('img')
- grad_up_bias: float32 [3072], replicated
- grad_down: float32 [3072, 768], P('img')
- grad_down_bias: float32 [768], replicated
- grad_feed_scale: float32 [768], replicated
- grad_rel_table: float32 [12, 2212], replicated
The draws below stay inside these ranges and needn't reach their ends.
All inputs are finite; a program needn't handle non-finite values.
Results may differ from the reference program's by a relative error of at most 0.015.
Values may be sent and summed in bfloat16 or wider, within the bound.
A program may use at most 448 MiB of HBM per device.

```python
import jax
import jax.numpy as jnp
from jax import lax

D = 768
HEADS = 12
FF = 3072
SGRID = 14
LGRID = 24
SLEN = 256
LLEN = 640
PACK = 4
GROUPS_ALL = 32
NREL = 2212


def shard_levels(stream_key, extent, shards, smallest, largest):
    level = 1.0
    for axis_at, blocks in shards:
        steps = jax.random.uniform(jax.random.fold_in(jax.random.fold_in(stream_key, 6), axis_at), (blocks,), jnp.float32, smallest / len(shards), largest / len(shards))
        level = level * jnp.repeat(jnp.exp(steps), extent[axis_at] // blocks).reshape((-1,) + (1,) * (len(extent) - 1 - axis_at))
    return level


def bell_draw(own_key, extent, width, reach, split=(), held_as=jnp.bfloat16):
    values = jax.random.normal(own_key, extent, jnp.float32) * width
    if len(split) > 0:
        values = shard_levels(own_key, extent, split, -0.22, 0.18) * values
    return jnp.clip(values, min=-reach, max=reach).astype(held_as)


def setup_inputs(seed: int = 0) -> dict:
    keys = jax.random.split(jax.random.key(seed), 23)
    small_in = bell_draw(keys[0], (GROUPS_ALL, PACK * SLEN, D), 1.0, 6.0, ((0, 16), (1, 2)))
    large_in = bell_draw(keys[1], (GROUPS_ALL, LLEN, D), 1.0, 6.0, ((0, 16), (1, 2)))
    small_cot = bell_draw(keys[2], (GROUPS_ALL, PACK * SLEN, D), 1.0, 6.0, ((0, 16), (1, 2)))
    large_cot = bell_draw(keys[3], (GROUPS_ALL, LLEN, D), 1.0, 6.0, ((0, 16), (1, 2)))
    first_gain = jnp.clip(1.0 + 0.1 * jax.random.normal(keys[4], (D,), jnp.float32), 0.5, 1.5)
    first_bias = bell_draw(keys[5], (D,), 0.3, 1.75, (), jnp.float32)
    query_weight = bell_draw(keys[6], (D, D), D ** -0.5, 0.21875, ((0, 16),))
    query_bias = bell_draw(keys[7], (D,), 0.3, 1.75, (), jnp.float32)
    key_weight = bell_draw(keys[8], (D, D), D ** -0.5, 0.21875, ((0, 16),))
    value_weight = bell_draw(keys[9], (D, D), D ** -0.5, 0.21875, ((0, 16),))
    value_bias = bell_draw(keys[10], (D,), 0.3, 1.75, (), jnp.float32)
    out_weight = bell_draw(keys[11], (D, D), (D // 64) ** -0.5, 1.75, ((0, 16),))
    out_bias = bell_draw(keys[12], (D,), 0.3, 1.75, (), jnp.float32)
    attend_scale = jnp.clip(jax.random.uniform(keys[13], (D,), jnp.float32, 0.5, 1.5), 0.5, 1.5)
    second_gain = jnp.clip(1.0 + 0.1 * jax.random.normal(keys[14], (D,), jnp.float32), 0.5, 1.5)
    second_bias = bell_draw(keys[15], (D,), 0.3, 1.75, (), jnp.float32)
    up_weight = bell_draw(keys[16], (D, FF), D ** -0.5, 0.21875, ((0, 16),))
    up_bias = bell_draw(keys[17], (FF,), 0.3, 1.75, (), jnp.float32)
    down_weight = bell_draw(keys[18], (FF, D), FF ** -0.5, 0.109375, ((0, 16),))
    down_bias = bell_draw(keys[19], (D,), 0.3, 1.75, (), jnp.float32)
    feed_scale = jnp.clip(jax.random.uniform(keys[20], (D,), jnp.float32, 0.5, 1.5), 0.5, 1.5)
    rel_table = bell_draw(keys[21], (HEADS, NREL), 1.0, 6.0, (), jnp.float32)
    return {"small_in": small_in, "large_in": large_in, "small_cot": small_cot, "large_cot": large_cot, "first_gain": first_gain, "first_bias": first_bias, "query_weight": query_weight, "query_bias": query_bias, "key_weight": key_weight, "value_weight": value_weight, "value_bias": value_bias, "out_weight": out_weight, "out_bias": out_bias, "attend_scale": attend_scale, "second_gain": second_gain, "second_bias": second_bias, "up_weight": up_weight, "up_bias": up_bias, "down_weight": down_weight, "down_bias": down_bias, "feed_scale": feed_scale, "rel_table": rel_table}


@jax.custom_vjp
def low(v):
    return lax.optimization_barrier(v.astype(jnp.bfloat16)).astype(jnp.float32)

@jax.custom_vjp
def low_back(v):
    return v

def low_keep(v):
    return (low(v), None)

def low_pass(kept, grad):
    return (grad,)

def back_keep(v):
    return (v, None)

def back_low(kept, grad):
    return (low(grad),)
low.defvjp(low_keep, low_pass)
low_back.defvjp(back_keep, back_low)
NEGATIVE = -1e+30
EPSILON = 1e-06

def layer_norm(values, gain, bias):
    center = values - lax.optimization_barrier(jnp.mean(values, axis=-1, keepdims=True))
    spread = lax.optimization_barrier(jnp.mean(center * center, axis=-1, keepdims=True))
    return center * lax.rsqrt(spread + EPSILON) * gain + bias

def matmul(left, right):
    return jnp.dot(left, right, precision=lax.Precision.HIGHEST, preferred_element_type=jnp.float32)

def relative_index(query_place, key_place, grid):
    span = 2 * LGRID - 1
    total_rel = span * span + 3
    query_patch = query_place[:, None] - 1
    key_patch = key_place[None, :] - 1
    rows_apart = query_patch // grid - key_patch // grid
    cols_apart = query_patch % grid - key_patch % grid
    result = (rows_apart + LGRID - 1) * span + cols_apart + LGRID - 1
    query_head = (query_place == 0)[:, None]
    key_head = (key_place == 0)[None, :]
    result = jnp.where(query_head & ~key_head, total_rel - 3, result)
    result = jnp.where(~query_head & key_head, total_rel - 2, result)
    result = jnp.where(query_head & key_head, total_rel - 1, result)
    return jnp.clip(result, 0, total_rel - 1).astype(jnp.int32)

def attend(query, key, value, images, length, grid, table):
    heads = table.shape[0]
    size = query.shape[-1] // heads
    query_heads = query.reshape(images, length, heads, size)
    key_heads = key.reshape(images, length, heads, size)
    value_heads = value.reshape(images, length, heads, size)
    places = jnp.arange(length, dtype=jnp.int32)
    index = relative_index(places, places, grid)
    scores = jnp.einsum('bqhd,bkhd->bhqk', query_heads, key_heads, precision=lax.Precision.HIGHEST) * float(size) ** (-0.5)
    scores = low_back(scores + jnp.take(table, index, axis=1)[None])
    keep = (places < grid * grid + 1)[None, None, None, :]
    probs = jax.nn.softmax(jnp.where(keep, scores, NEGATIVE), axis=-1)
    result = jnp.einsum('bhqk,bkhd->bqhd', low(probs), value_heads, precision=lax.Precision.HIGHEST)
    return result.reshape(images * length, heads * size)

def layer(params, small, large):
    first_gain, first_bias, query_weight, query_bias, key_weight, value_weight, value_bias, out_weight, out_bias, attend_scale, second_gain, second_bias, up_weight, up_bias, down_weight, down_bias, feed_scale, rel_table = params
    small_rows = PACK * SLEN
    inputs = jnp.concatenate([small, large], axis=0)
    hidden = low(layer_norm(inputs, first_gain, first_bias))
    query = low_back(low(matmul(hidden, query_weight) + query_bias))
    key = low_back(low(matmul(hidden, key_weight)))
    value = low_back(low(matmul(hidden, value_weight) + value_bias))
    small_att = attend(query[:small_rows], key[:small_rows], value[:small_rows], PACK, SLEN, SGRID, rel_table)
    large_att = attend(query[small_rows:], key[small_rows:], value[small_rows:], 1, LLEN, LGRID, rel_table)
    mixed = low_back(low(jnp.concatenate([small_att, large_att], axis=0)))
    branch = low_back(matmul(mixed, out_weight) + out_bias)
    residual = inputs + attend_scale * branch
    hidden2 = low(layer_norm(residual, second_gain, second_bias))
    upper = low_back(matmul(hidden2, up_weight) + up_bias)
    active = low(jax.nn.gelu(upper, approximate=False))
    lower = low_back(matmul(active, down_weight) + down_bias)
    small_valid = jnp.arange(small_rows, dtype=jnp.int32) % SLEN < SGRID * SGRID + 1
    large_valid = jnp.arange(LLEN, dtype=jnp.int32) < LGRID * LGRID + 1
    valid = jnp.concatenate([small_valid, large_valid])
    output = jnp.where(valid[:, None], residual + feed_scale * lower, 0.0)
    return (output[:small_rows], output[small_rows:])

def forward(params, small, large):

    def group(pair):
        return layer(params, pair[0], pair[1])
    return lax.map(jax.checkpoint(group), (small, large))

def reference(small_in, large_in, small_cot, large_cot, first_gain, first_bias, query_weight, query_bias, key_weight, value_weight, value_bias, out_weight, out_bias, attend_scale, second_gain, second_bias, up_weight, up_bias, down_weight, down_bias, feed_scale, rel_table):
    params = tuple((item.astype(jnp.float32) for item in (first_gain, first_bias, query_weight, query_bias, key_weight, value_weight, value_bias, out_weight, out_bias, attend_scale, second_gain, second_bias, up_weight, up_bias, down_weight, down_bias, feed_scale, rel_table)))
    small = small_in.astype(jnp.float32)
    large = large_in.astype(jnp.float32)
    outputs, pullback = jax.vjp(forward, params, small, large)
    grads, small_grad, large_grad = pullback((small_cot.astype(jnp.float32), large_cot.astype(jnp.float32)))
    return (outputs[0].astype(jnp.bfloat16), outputs[1].astype(jnp.bfloat16), small_grad.astype(jnp.bfloat16), large_grad.astype(jnp.bfloat16), grads[0], grads[1], grads[2], grads[3], grads[4], grads[5], grads[6], grads[7], grads[8], grads[9], grads[10], grads[11], grads[12], grads[13], grads[14], grads[15], grads[16], grads[17])
```

```python
import functools

import jax
import jax.numpy as jnp
from jax import lax
from jax.experimental import pallas as pl
from jax.experimental.pallas import tpu as pltpu
from jax.sharding import PartitionSpec as P

HEADS = 12
SGRID = 14
LGRID = 24
SLEN = 256
LLEN = 640
SPAD = 208
LPAD = 608
LANES = 128

NEGATIVE = -1e30
EPSILON = 1e-06
F32 = jnp.float32
BF16 = jnp.bfloat16
VMEM_BYTES = 62 << 20


def dot_nn(left, right):
    return lax.dot_general(left, right, (((1,), (0,)), ((), ())), preferred_element_type=F32)


def dot_nt(left, right):
    return lax.dot_general(left, right, (((1,), (1,)), ((), ())), preferred_element_type=F32)


def normalized(values):
    center = values - jnp.mean(values, axis=-1, keepdims=True)
    spread = jnp.mean(center * center, axis=-1, keepdims=True)
    scale = lax.rsqrt(spread + EPSILON)
    return center * scale, scale


def norm_back(grad, normal, scale):
    return scale * (
        grad
        - jnp.mean(grad, axis=-1, keepdims=True)
        - normal * jnp.mean(grad * normal, axis=-1, keepdims=True)
    )


def row_sum(values):
    return jnp.sum(values, axis=0, keepdims=True)


def iota(shape, axis):
    return lax.broadcasted_iota(jnp.int32, shape, axis)


L_WIDTH = 1280
S_WIDTH = 512


def table_sequences(table):
    heads = table.shape[0]
    span = 2 * LGRID - 1
    cells = table[:, : span * span].reshape(heads, span, span)

    def sequences(part, grid, width):
        rows = part.shape[1]
        low = part[:, :, :grid].reshape(heads, rows * grid)
        high = jnp.pad(part[:, :, grid:], ((0, 0), (0, 0), (0, 1))).reshape(heads, rows * grid)
        low = jnp.pad(low, ((0, 0), (0, width - rows * grid)))
        high = jnp.pad(high, ((0, 0), (grid, width - rows * grid - grid)))
        return jnp.stack([low, high], axis=1)

    off = LGRID - SGRID
    large = sequences(cells, LGRID, L_WIDTH)
    small = sequences(cells[:, off : span - off, off : span - off], SGRID, S_WIDTH)
    edge = jnp.broadcast_to(
        jnp.pad(table[:, span * span :], ((0, 0), (0, 5)))[:, :, None], (heads, 8, LANES)
    )
    return large, small, edge


def table_from_sequences(large, small, edge):
    heads = large.shape[0]
    span = 2 * LGRID - 1

    def cells(part, grid):
        rows = 2 * grid - 1
        low = part[:, 0, : rows * grid].reshape(heads, rows, grid)
        high = part[:, 1, grid : grid + rows * grid].reshape(heads, rows, grid)
        return jnp.concatenate([low, high[:, :, : grid - 1]], axis=2)

    off = LGRID - SGRID
    total = cells(large, LGRID) + jnp.pad(
        cells(small, SGRID), ((0, 0), (off, off), (off, off))
    )
    return jnp.concatenate([total.reshape(heads, span * span), edge], axis=1)


def takes_low(rows, width, grid, first):
    step = iota((rows, width), 1) % grid
    row = iota((rows, width), 0)
    low = step >= grid - 1 + first - row
    if first == 1:
        low = low | (row == 0)
    return low


def spread_sequences(seq, rows, width, grid, first):
    low = jnp.broadcast_to(seq[0:1, :], (rows, width))
    high = jnp.broadcast_to(seq[1:2, :], (rows, width))
    chosen = jnp.where(takes_low(rows, width, grid, first), low, high)
    return pltpu.roll(chosen, 1, 1, stride=1, stride_axis=0)


def gather_sequences(spread, rows, width, grid, first):
    row = iota((rows, width), 0) + 1
    for bit in (1, 2, 4, 8, 16):
        spread = jnp.where((row & bit) != 0, pltpu.roll(spread, width - bit, 1), spread)
    low = takes_low(rows, width, grid, first)
    return (
        row_sum(jnp.where(low, spread, 0.0)),
        row_sum(jnp.where(low, 0.0, spread)),
    )


def large_window(block):
    start = (LGRID - block) * LGRID
    return start // LANES, start % LANES


def small_window(block):
    start = (SGRID - 1 - block) * SGRID + SGRID - 1
    return start // LANES, start % LANES


def head_masks():
    lane = iota((1, LANES), 1)
    return (
        jnp.where(lane < LANES // 2, 1.0, 0.0).astype(BF16),
        jnp.where(lane < LANES // 2, 0.0, 1.0).astype(BF16),
    )


def transposed_biases(large_seq, small_seq, edge, wide, narrow, bias_large, bias_small):
    patch_q = edge[0:1, 0:1]
    patch_k = edge[1:2, 0:1]
    both = edge[2:3, 0:1]
    wide[...] = spread_sequences(large_seq, 24, L_WIDTH, LGRID, 1)
    lane = iota((24, LANES), 1)
    row = iota((24, LANES), 0)
    for block in range(LGRID + 1):
        at, turn = large_window(block)
        piece = wide[:, at * LANES : at * LANES + 768]
        if turn:
            piece = pltpu.roll(piece, 768 - turn, 1)
        piece = piece[:, :640]
        if block == 0:
            rest = jnp.where(iota((24, 640), 0) == 0, patch_k, piece)
        elif block == LGRID:
            rest = jnp.where(iota((24, 640), 0) == 0, piece, NEGATIVE)
        else:
            rest = piece
        first = jnp.where(lane == 0, patch_q, rest[:, :LANES])
        if block == 0:
            first = jnp.where((lane == 0) & (row == 0), both, first)
        if block == LGRID:
            first = jnp.where(row == 0, first, NEGATIVE)
        bias_large[pl.ds(block * 24, 24), 0:LANES] = first
        bias_large[pl.ds(block * 24, 24), LANES:640] = rest[:, LANES:]
    bias_large[pl.ds(600, 8), :] = jnp.full((8, 640), NEGATIVE, F32)
    narrow[...] = spread_sequences(small_seq, 16, S_WIDTH, SGRID, 0)
    for block in range(SGRID):
        at, turn = small_window(block)
        piece = narrow[:, at * LANES : at * LANES + 384]
        if turn:
            piece = pltpu.roll(piece, 384 - turn, 1)
        bias_small[pl.ds(1 + SGRID * block, SGRID), :] = piece[:SGRID, :256]
    whole = bias_small[...]
    lane = iota((SPAD, 256), 1)
    row = iota((SPAD, 256), 0)
    whole = jnp.where(lane == 0, patch_q, whole)
    whole = jnp.where(row == 0, patch_k, whole)
    whole = jnp.where((lane == 0) & (row == 0), both, whole)
    bias_small[...] = jnp.where(row > SGRID * SGRID, NEGATIVE, whole)


def attend_kernel(
    n_small,
    n_large,
    large_seq,
    small_seq,
    edge,
    query,
    key,
    value,
    out,
    out_wide,
    probs_small,
    probs_large,
    wide,
    narrow,
    bias_large,
    bias_small,
):
    masks = head_masks()

    @pl.when(pl.program_id(0) == 0)
    def _():
        bias_small[...] = jnp.zeros_like(bias_small)

    members = [(i * SPAD, SPAD, bias_small, probs_small, i) for i in range(n_small)]
    members += [
        (n_small * SPAD + i * LPAD, LPAD, bias_large, probs_large, i) for i in range(n_large)
    ]
    halves = [[] for _ in members]
    for head in range(2):
        transposed_biases(
            large_seq[head], small_seq[head], edge[head], wide, narrow, bias_large, bias_small
        )
        for at, (start, count, bias, probs, which) in enumerate(members):
            rows = pl.ds(start, count)
            scores = dot_nt(key[rows, :], query[rows, :] * masks[head]) + bias[:, :count]
            top = jnp.max(scores, axis=0, keepdims=True)
            weights = jnp.exp(scores - top)
            total = jnp.sum(weights, axis=0, keepdims=True)
            prob = (weights * (1.0 / total)).astype(BF16)
            probs[head, which] = prob
            turned = value[rows, :].T
            halves[at].append(dot_nn(turned[head * 64 : head * 64 + 64, :], prob))
    for at, (start, count, bias, probs, which) in enumerate(members):
        both = jnp.concatenate(halves[at], axis=0).T
        out[pl.ds(start, count), :] = both.astype(BF16)
        out_wide[pl.ds(start, count), :] = both


def attend_back_kernel(
    n_small,
    n_large,
    query,
    key,
    value,
    dout,
    out_wide,
    probs_small,
    probs_large,
    dquery,
    dkey,
    dvalue,
    large_seq,
    small_seq,
    edge,
    wide,
    narrow,
    dsum_small,
    dscore_large,
):
    masks = head_masks()
    lane = iota((1, LANES), 1)
    scale = float(64) ** (-0.5)
    members = [(i * SPAD, SPAD, probs_small, i) for i in range(n_small)]
    members += [(n_small * SPAD + i * LPAD, LPAD, probs_large, i) for i in range(n_large)]
    keep = []
    for head in range(2):
        spot = 64 * (1 - head)
        minus = jnp.where((lane == spot) | (lane == spot + 1), -1.0, 0.0).astype(BF16)
        mask32 = masks[head].astype(F32)
        for at, (start, count, probs, which) in enumerate(members):
            rows = pl.ds(start, count)
            grad = dout[rows, :]
            grad32 = grad.astype(F32) * mask32
            delta = jnp.sum(grad32 * out_wide[rows, :], axis=1, keepdims=True)
            coarse = delta.astype(BF16).astype(F32)
            fine = delta - coarse
            side = jnp.where(lane == spot, coarse, jnp.where(lane == spot + 1, fine, grad32))
            values = value[rows, :] * masks[head] + minus
            prob = probs[head, which]
            dscore = prob.astype(F32) * dot_nt(values, side.astype(BF16))
            if count == SPAD:
                if which == 0:
                    dsum_small[:, :SPAD] = dscore
                else:
                    dsum_small[:, :SPAD] += dscore
            elif which == 0:
                dscore_large[:, :LPAD] = dscore
            else:
                dscore_large[:, :LPAD] += dscore
            low = dscore.astype(BF16)
            turned = key[rows, :].T
            dq = dot_nn(turned[head * 64 : head * 64 + 64, :], low)
            dk = dot_nn(low, query[rows, :])
            dv = dot_nn(prob, grad)
            if head == 0:
                keep.append((dq, dk, dv))
            else:
                first = iota((count, LANES), 1) < 64
                dq0, dk0, dv0 = keep[at]
                dquery[rows, :] = (jnp.concatenate([dq0, dq], axis=0).T * scale).astype(BF16)
                dkey[rows, :] = jnp.where(first, dk0, dk).astype(BF16)
                dvalue[rows, :] = jnp.where(first, dv0, dv).astype(BF16)
        wide[...] = jnp.zeros_like(wide)
        dscore_large[:, LPAD:] = jnp.zeros((LPAD, 768 - LPAD), F32)
        edge_lane = iota((24, 768), 1)
        edge_row = iota((24, 768), 0)
        class_column = jnp.zeros((24, 768), F32)
        class_row = None
        for block in range(LGRID + 1):
            at, turn = large_window(block)
            piece = dscore_large[pl.ds(block * 24, 24), :]
            if block == 0:
                class_row = piece[0:1, :]
                piece = jnp.where(edge_row == 0, 0.0, piece)
            class_column = class_column + piece
            piece = jnp.where(edge_lane == 0, 0.0, piece)
            if turn:
                piece = pltpu.roll(piece, turn, 1)
            wide[:, at * LANES : at * LANES + 768] += piece
        low_sum, high_sum = gather_sequences(wide[...], 24, L_WIDTH, LGRID, 1)
        large_seq[head, 0:1, :] = low_sum
        large_seq[head, 1:2, :] = high_sum
        narrow[...] = jnp.zeros_like(narrow)
        dsum_small[:, SPAD:] = jnp.zeros((SPAD, 384 - SPAD), F32)
        small_lane = iota((SGRID, 384), 1)
        small_column = jnp.zeros((SGRID, 384), F32)
        for block in range(SGRID):
            at, turn = small_window(block)
            piece = dsum_small[pl.ds(1 + SGRID * block, SGRID), :]
            small_column = small_column + piece
            piece = jnp.where(small_lane == 0, 0.0, piece)
            piece = jnp.concatenate([piece, jnp.zeros((2, 384), F32)], axis=0)
            if turn:
                piece = pltpu.roll(piece, turn, 1)
            narrow[:, at * LANES : at * LANES + 384] += piece
        low_sum, high_sum = gather_sequences(narrow[...], 16, S_WIDTH, SGRID, 0)
        small_seq[head, 0:1, :] = low_sum
        small_seq[head, 1:2, :] = high_sum
        edge[head, 0:1, :] = row_sum(class_column)[:, :LANES] + row_sum(small_column)[:, :LANES]
        both_rows = class_row + jnp.concatenate(
            [dsum_small[0:1, :], jnp.zeros((1, 384), F32)], axis=1
        )
        edge[head, 1:2, :] = jnp.broadcast_to(
            jnp.sum(jnp.where(iota((1, 768), 1) == 0, 0.0, both_rows), axis=1, keepdims=True),
            (1, LANES),
        )
        edge[head, 2:3, :] = both_rows[:, :LANES]
        edge[head, 3:8, :] = jnp.zeros((5, LANES), F32)


def qkv_kernel(x, gain, bias, weight, weight_bias, out):
    width = x.shape[1]
    normal, unused = normalized(x[...].astype(F32))
    hidden = (normal * gain[...] + bias[...]).astype(BF16)
    scale = float(width // HEADS) ** (-0.5)
    for part in range(3):
        cols = slice(part * width, (part + 1) * width)
        made = (dot_nn(hidden, weight[:, cols]) + weight_bias[:, cols]).astype(BF16)
        out[:, cols] = made * jnp.asarray(scale, BF16) if part == 0 else made


def gelu_pair(upper):
    normal_cdf = 0.5 * (1.0 + lax.erf(upper * (0.5**0.5)))
    density = jnp.exp(-0.5 * upper * upper) * 0.3989422804014327
    return upper * normal_cdf, normal_cdf + upper * density


def valid_rows(first, count, n_small):
    row = iota((count, 1), 0) + first
    in_small = row < n_small * SPAD
    small_ok = row % SPAD < SGRID * SGRID + 1
    large_ok = (row - n_small * SPAD) % LPAD < LGRID * LGRID + 1
    return jnp.where(in_small, small_ok.astype(F32), large_ok.astype(F32))


def feed_kernel(
    n_small,
    tiles,
    x,
    attended,
    cot,
    w_out,
    w_up,
    w_down,
    vectors,
    up_bias,
    out,
    dresidual,
    dattended,
    vector_grads,
    up_bias_grad,
    g_out,
    g_up,
    g_down,
    active,
    slope,
    acc_out,
    acc_up,
    acc_down,
    stage,
    sems,
):
    step = pl.program_id(0)
    count, width = x.shape
    tile = w_up.shape[1] // tiles

    @pl.when(step == 0)
    def _():
        acc_out[...] = jnp.zeros_like(acc_out)
        acc_up[...] = jnp.zeros_like(acc_up)
        acc_down[...] = jnp.zeros_like(acc_down)
        vector_grads[...] = jnp.zeros_like(vector_grads)
        up_bias_grad[...] = jnp.zeros_like(up_bias_grad)

    out_bias = vectors[0:1, :]
    attend_scale = vectors[1:2, :]
    second_gain = vectors[2:3, :]
    second_bias = vectors[3:4, :]
    down_bias = vectors[4:5, :]
    feed_scale = vectors[5:6, :]

    valid = valid_rows(step * count, count, n_small)
    mixed = attended[...]
    branch = dot_nn(mixed, w_out[...]) + out_bias
    residual = x[...].astype(F32) + attend_scale * branch
    normal, scale = normalized(residual)
    hidden = (normal * second_gain + second_bias).astype(BF16)
    lower = jnp.zeros((count, width), F32)
    for t in range(tiles):
        cols = slice(t * tile, (t + 1) * tile)
        upper = dot_nn(hidden, w_up[:, cols]) + up_bias[:, cols]
        made, rate = gelu_pair(upper)
        made = made.astype(BF16)
        active[:, cols] = made
        slope[:, cols] = rate.astype(BF16)
        lower += dot_nn(made, w_down[cols, :])
    lower += down_bias
    out[...] = ((residual + feed_scale * lower) * valid).astype(BF16)
    upstream = cot[...].astype(F32) * valid
    vector_grads[5:6, :] += row_sum(upstream * lower)
    dlower = (upstream * feed_scale).astype(BF16)
    vector_grads[4:5, :] += row_sum(dlower.astype(F32))
    turned = hidden.T
    dhidden = jnp.zeros((count, width), F32)
    for t in range(tiles):
        cols = slice(t * tile, (t + 1) * tile)
        dupper = (dot_nt(dlower, w_down[cols, :]) * slope[:, cols].astype(F32)).astype(BF16)
        up_bias_grad[:, cols] += row_sum(dupper.astype(F32))
        acc_down[cols, :] += dot_nn(active[:, cols].T, dlower)
        acc_up[:, cols] += dot_nn(turned, dupper)
        dhidden += dot_nt(dupper, w_up[:, cols])
    vector_grads[2:3, :] += row_sum(dhidden * normal)
    vector_grads[3:4, :] += row_sum(dhidden)
    dres = upstream + norm_back(dhidden * second_gain, normal, scale)
    dresidual[...] = dres
    vector_grads[1:2, :] += row_sum(dres * branch)
    dbranch = (dres * attend_scale).astype(BF16)
    vector_grads[0:1, :] += row_sum(dbranch.astype(F32))
    acc_out[...] += dot_nn(mixed.T, dbranch)
    dattended[...] = dot_nt(dbranch, w_out[...]).astype(BF16)

    @pl.when(step == pl.num_programs(0) - 1)
    def _():
        part = stage.shape[1]
        jobs = [
            (source, target, slice(r, r + part), slice(c, c + width))
            for source, target in ((acc_out, g_out), (acc_up, g_up), (acc_down, g_down))
            for r in range(0, source.shape[0], part)
            for c in range(0, source.shape[1], width)
        ]
        flights = []
        for at, (source, target, rows, cols) in enumerate(jobs):
            slot = at % 2
            if at >= 2:
                flights[at - 2].wait()
            stage[slot] = source[rows, cols].astype(BF16)
            flight = pltpu.make_async_copy(stage.at[slot], target.at[rows, cols], sems.at[slot])
            flight.start()
            flights.append(flight)
        for flight in flights[-2:]:
            flight.wait()


def input_kernel(
    x, dquery, dkey, dvalue, dresidual, gain, bias, weight, out, vector_grads, grad, acc
):
    step = pl.program_id(0)
    width = x.shape[1]

    @pl.when(step == 0)
    def _():
        acc[...] = jnp.zeros_like(acc)
        vector_grads[...] = jnp.zeros_like(vector_grads)

    normal, scale = normalized(x[...].astype(F32))
    hidden = (normal * gain[...] + bias[...]).astype(BF16)
    turned = hidden.T
    dhidden = jnp.zeros(normal.shape, F32)
    for part, item in enumerate((dquery, dkey, dvalue)):
        cols = slice(part * width, (part + 1) * width)
        piece = item[...]
        dhidden += dot_nt(piece, weight[:, cols])
        acc[:, cols] += dot_nn(turned, piece)
        if part != 1:
            vector_grads[part : part + 1, :] += row_sum(piece.astype(F32))
    vector_grads[3:4, :] += row_sum(dhidden * normal)
    vector_grads[4:5, :] += row_sum(dhidden)
    out[...] = (dresidual[...] + norm_back(dhidden * gain[...], normal, scale)).astype(BF16)

    @pl.when(step == pl.num_programs(0) - 1)
    def _():
        grad[...] = acc[...].astype(BF16)


def chunk_rows(total):
    return max(size for size in range(16, 481, 16) if total % size == 0)


def params():
    return pltpu.CompilerParams(vmem_limit_bytes=VMEM_BYTES)


def held(shape):
    rank = len(shape)
    return pl.BlockSpec(shape, lambda i: (0,) * rank, pipeline_mode=pl.Buffered(1))


def resident(shape):
    rank = len(shape)
    return pl.BlockSpec(shape, lambda i: (0,) * rank)


def run_qkv(x, gain, bias, weight, weight_bias):
    rows, width = x.shape
    size = chunk_rows(rows)
    wide = weight.shape[1]
    return pl.pallas_call(
        qkv_kernel,
        grid=(rows // size,),
        in_specs=[
            pl.BlockSpec((size, width), lambda i: (i, 0)),
            held((1, width)),
            held((1, width)),
            held(weight.shape),
            held((1, wide)),
        ],
        out_specs=pl.BlockSpec((size, wide), lambda i: (i, 0)),
        out_shape=jax.ShapeDtypeStruct((rows, wide), BF16),
        compiler_params=params(),
        cost_estimate=pl.CostEstimate(
            flops=2 * rows * width * wide, bytes_accessed=rows * wide * 2, transcendentals=0
        ),
    )(x, gain, bias, weight, weight_bias)


def run_attend(qkv, large_seq, small_seq, edge, n_small, n_large):
    rows = qkv.shape[0]
    width = qkv.shape[1] // 3
    pairs = HEADS // 2

    def column(which):
        return pl.BlockSpec((rows, LANES), lambda i: (0, which * pairs + i))

    def per_pair(shape):
        tail = (0,) * (len(shape) - 1)
        return pl.BlockSpec((2,) + shape[1:], lambda i: (i,) + tail)

    return pl.pallas_call(
        functools.partial(attend_kernel, n_small, n_large),
        grid=(pairs,),
        in_specs=[
            per_pair(large_seq.shape),
            per_pair(small_seq.shape),
            per_pair(edge.shape),
            column(0),
            column(1),
            column(2),
        ],
        out_specs=[
            column(0),
            column(0),
            per_pair((HEADS, n_small, SPAD, SPAD)),
            per_pair((HEADS, n_large, LPAD, LPAD)),
        ],
        out_shape=[
            jax.ShapeDtypeStruct((rows, width), BF16),
            jax.ShapeDtypeStruct((rows, width), F32),
            jax.ShapeDtypeStruct((HEADS, n_small, SPAD, SPAD), BF16),
            jax.ShapeDtypeStruct((HEADS, n_large, LPAD, LPAD), BF16),
        ],
        scratch_shapes=[
            pltpu.VMEM((24, L_WIDTH), F32),
            pltpu.VMEM((16, S_WIDTH), F32),
            pltpu.VMEM((LPAD, 640), F32),
            pltpu.VMEM((SPAD, 256), F32),
        ],
        compiler_params=params(),
        cost_estimate=pl.CostEstimate(
            flops=20 * 10**9, bytes_accessed=20 * 10**6, transcendentals=7 * 10**6
        ),
    )(large_seq, small_seq, edge, qkv, qkv, qkv)


def run_attend_back(qkv, dattended, out_wide, probs_small, probs_large, n_small, n_large):
    rows, width = dattended.shape
    pairs = HEADS // 2

    def column(which):
        return pl.BlockSpec((rows, LANES), lambda i: (0, which * pairs + i))

    def per_pair(shape):
        tail = (0,) * (len(shape) - 1)
        return pl.BlockSpec((2,) + shape[1:], lambda i: (i,) + tail)

    grad = jax.ShapeDtypeStruct((rows, width), BF16)
    return pl.pallas_call(
        functools.partial(attend_back_kernel, n_small, n_large),
        grid=(pairs,),
        in_specs=[
            column(0),
            column(1),
            column(2),
            column(0),
            column(0),
            per_pair(probs_small.shape),
            per_pair(probs_large.shape),
        ],
        out_specs=[
            column(0),
            column(0),
            column(0),
            per_pair((HEADS, 2, L_WIDTH)),
            per_pair((HEADS, 2, S_WIDTH)),
            per_pair((HEADS, 8, LANES)),
        ],
        out_shape=[
            grad,
            grad,
            grad,
            jax.ShapeDtypeStruct((HEADS, 2, L_WIDTH), F32),
            jax.ShapeDtypeStruct((HEADS, 2, S_WIDTH), F32),
            jax.ShapeDtypeStruct((HEADS, 8, LANES), F32),
        ],
        scratch_shapes=[
            pltpu.VMEM((24, L_WIDTH), F32),
            pltpu.VMEM((16, S_WIDTH), F32),
            pltpu.VMEM((SPAD, 384), F32),
            pltpu.VMEM((LPAD, 768), F32),
        ],
        compiler_params=params(),
        cost_estimate=pl.CostEstimate(
            flops=30 * 10**9, bytes_accessed=24 * 10**6, transcendentals=0
        ),
    )(qkv, qkv, qkv, dattended, out_wide, probs_small, probs_large)


def run_feed(x, attended, cot, w_out, w_up, w_down, vectors, up_bias, n_small):
    rows, width = x.shape
    size = chunk_rows(rows)
    hidden = w_up.shape[1]
    tiles = hidden // width
    block = pl.BlockSpec((size, width), lambda i: (i, 0))
    anywhere = pl.BlockSpec(memory_space=pl.ANY)
    return pl.pallas_call(
        functools.partial(feed_kernel, n_small, tiles),
        grid=(rows // size,),
        in_specs=[
            block,
            block,
            block,
            held(w_out.shape),
            held(w_up.shape),
            held(w_down.shape),
            held(vectors.shape),
            held(up_bias.shape),
        ],
        out_specs=[
            block,
            block,
            block,
            resident((8, width)),
            resident((1, hidden)),
            anywhere,
            anywhere,
            anywhere,
        ],
        out_shape=[
            jax.ShapeDtypeStruct((rows, width), BF16),
            jax.ShapeDtypeStruct((rows, width), F32),
            jax.ShapeDtypeStruct((rows, width), BF16),
            jax.ShapeDtypeStruct((8, width), F32),
            jax.ShapeDtypeStruct((1, hidden), F32),
            jax.ShapeDtypeStruct((width, width), BF16),
            jax.ShapeDtypeStruct((width, hidden), BF16),
            jax.ShapeDtypeStruct((hidden, width), BF16),
        ],
        scratch_shapes=[
            pltpu.VMEM((size, hidden), BF16),
            pltpu.VMEM((size, hidden), BF16),
            pltpu.VMEM((width, width), F32),
            pltpu.VMEM((width, hidden), F32),
            pltpu.VMEM((hidden, width), F32),
            pltpu.VMEM((2, width // 4, width), BF16),
            pltpu.SemaphoreType.DMA((2,)),
        ],
        compiler_params=params(),
        cost_estimate=pl.CostEstimate(
            flops=6 * rows * width * (width + 2 * hidden),
            bytes_accessed=40 * 10**6,
            transcendentals=2 * rows * hidden,
        ),
    )(x, attended, cot, w_out, w_up, w_down, vectors, up_bias)


def run_input(x, dquery, dkey, dvalue, dresidual, gain, bias, weight):
    rows, width = x.shape
    size = chunk_rows(rows)
    block = pl.BlockSpec((size, width), lambda i: (i, 0))
    return pl.pallas_call(
        input_kernel,
        grid=(rows // size,),
        in_specs=[
            block,
            block,
            block,
            block,
            block,
            held((1, width)),
            held((1, width)),
            held(weight.shape),
        ],
        out_specs=[block, resident((8, width)), resident(weight.shape)],
        out_shape=[
            jax.ShapeDtypeStruct((rows, width), BF16),
            jax.ShapeDtypeStruct((8, width), F32),
            jax.ShapeDtypeStruct(weight.shape, BF16),
        ],
        scratch_shapes=[pltpu.VMEM(weight.shape, F32)],
        compiler_params=params(),
        cost_estimate=pl.CostEstimate(
            flops=12 * rows * width * width, bytes_accessed=20 * 10**6, transcendentals=0
        ),
    )(x, dquery, dkey, dvalue, dresidual, gain, bias, weight)


def shifted(array, axis, by):
    count = lax.axis_size(axis)
    return lax.ppermute(array, axis, [(i, (i + by) % count) for i in range(count)])


def layer_norm(values, gain, bias):
    center = values - jnp.mean(values, axis=-1, keepdims=True)
    spread = jnp.mean(center * center, axis=-1, keepdims=True)
    return center * lax.rsqrt(spread + EPSILON) * gain + bias


def matmul(left, right):
    return jnp.dot(left, right, preferred_element_type=jnp.float32)


def position_bias(table, places, length, grid):
    heads = table.shape[0]
    span = 2 * LGRID - 1
    total_rel = table.shape[1]
    queries_count = places.shape[0]
    grid_table = table[:, : span * span].reshape(heads, span, span)
    patch = places - 1
    query_row = patch // grid
    query_col = patch % grid
    steps_all = jnp.arange(span, dtype=jnp.int32)
    cells = jnp.arange(grid, dtype=jnp.int32)
    row_hot = (
        steps_all[None, :, None] == query_row[:, None, None] - cells[None, None, :] + LGRID - 1
    ).astype(jnp.float32)
    col_hot = (
        steps_all[None, :, None] == query_col[:, None, None] - cells[None, None, :] + LGRID - 1
    ).astype(jnp.float32)
    partial_bias = jnp.einsum("hab,qbc->hqac", grid_table, col_hot, precision=lax.Precision.HIGHEST)
    patches = jnp.einsum(
        "qar,hqac->hqrc", row_hot, partial_bias, precision=lax.Precision.HIGHEST
    ).reshape(heads, queries_count, grid * grid)
    rest = length - 1 - grid * grid
    class_key = jnp.broadcast_to(table[:, total_rel - 2][:, None, None], (heads, queries_count, 1))
    patch_rows = jnp.concatenate(
        [class_key, patches, jnp.zeros((heads, queries_count, rest), jnp.float32)], axis=2
    )
    class_row = jnp.concatenate(
        [
            table[:, total_rel - 1][:, None],
            jnp.broadcast_to(table[:, total_rel - 3][:, None], (heads, grid * grid)),
            jnp.zeros((heads, rest), jnp.float32),
        ],
        axis=1,
    )
    is_class = (places == 0)[None, :, None]
    return jnp.where(is_class, class_row[:, None, :], patch_rows)


def to_heads(block, heads):
    groups, rows, width = block.shape
    return block.reshape(groups, rows, heads, width // heads)


def block_scores(query, key, query_rows, key_rows, length, bias_full):
    size = query.shape[-1] // HEADS
    raw = jnp.einsum(
        "gqhd,gkhd->ghqk",
        to_heads(query, HEADS),
        to_heads(key, HEADS),
        preferred_element_type=jnp.float32,
    )
    key_place = key_rows % length
    select = (key_place[:, None] == jnp.arange(length, dtype=jnp.int32)[None, :]).astype(
        jnp.float32
    )
    bias_block = jnp.einsum("hql,kl->hqk", bias_full, select, precision=lax.Precision.HIGHEST)
    allowed = (query_rows // length)[:, None] == (key_rows // length)[None, :]
    scores = raw * float(size) ** (-0.5) + bias_block[None]
    return (scores, allowed, select)


def key_rows_of(source, count_keys):
    return source * count_keys + jnp.arange(count_keys, dtype=jnp.int32)


def allowed_mask(allowed, key_rows, length, grid):
    return allowed & (key_rows % length < grid * grid + 1)[None, :]


def absorb_one(state, query, key, value, query_rows, key_rows, info):
    length, grid, bias_full = info
    maximum, total, accum = state
    scores, allowed, select = block_scores(query, key, query_rows, key_rows, length, bias_full)
    allowed = allowed_mask(allowed, key_rows, length, grid)
    masked = jnp.where(allowed[None, None], scores, NEGATIVE)
    newmax = jnp.maximum(maximum, jnp.max(masked, axis=-1))
    weights = jnp.where(allowed[None, None], jnp.exp(scores - newmax[..., None]), 0.0)
    factor = jnp.exp(maximum - newmax)
    total = total * factor + jnp.sum(weights, axis=-1)
    accum = accum * factor[..., None] + jnp.einsum(
        "ghqk,gkhd->ghqd",
        weights.astype(jnp.bfloat16),
        to_heads(value, HEADS),
        preferred_element_type=jnp.float32,
    )
    return (newmax, total, accum)


def absorb_cycle(states, queries, moving, members, query_rows, source, info):
    states = list(states)
    for which, offset, rows in members:
        key = moving[0][:, offset : offset + rows]
        value = moving[1][:, offset : offset + rows]
        states[which] = absorb_one(
            states[which],
            queries[which],
            key,
            value,
            query_rows[which],
            key_rows_of(source, rows),
            info[which],
        )
    return tuple(states)


def pass_forward(moving):
    return shifted((moving[0], moving[1]), "seq", 1)


def cycle_forward(queries, cycle_pair, members, query_rows, info):
    position = lax.axis_index("seq")
    count = lax.axis_size("seq")
    states = []
    for which in range(2):
        groups, rows, width = queries[which].shape
        states.append(
            (
                jnp.full((groups, HEADS, rows), NEGATIVE, jnp.float32),
                jnp.zeros((groups, HEADS, rows), jnp.float32),
                jnp.zeros((groups, HEADS, rows, width // HEADS), jnp.float32),
            )
        )
    states = absorb_cycle(tuple(states), queries, cycle_pair, members, query_rows, position, info)

    def turn(step, carry):
        held_states, moving = carry
        moving = tuple(pass_forward(moving))
        held_states = absorb_cycle(
            held_states, queries, moving, members, query_rows, (position - step) % count, info
        )
        return (held_states, moving)

    states, moving = lax.fori_loop(1, count, turn, (states, cycle_pair))
    attended = []
    logsums = []
    for which in range(2):
        maximum, total, accum = states[which]
        groups, heads_count, rows, size = accum.shape
        attended.append(
            jnp.transpose(accum / total[..., None], (0, 2, 1, 3)).reshape(
                groups, rows, heads_count * size
            )
        )
        logsums.append(maximum + jnp.log(total))
    return (tuple(attended), tuple(logsums))


def visit_one(query, dout, logsum, delta, key, value, query_rows, key_rows, info):
    length, grid, bias_full = info
    groups, count_keys, width = key.shape
    scale = float(width // HEADS) ** (-0.5)
    scores, allowed, select = block_scores(query, key, query_rows, key_rows, length, bias_full)
    allowed = allowed_mask(allowed, key_rows, length, grid)
    probs = jnp.where(allowed[None, None], jnp.exp(scores - logsum[..., None]), 0.0)
    dout_heads = to_heads(dout, HEADS)
    dprobs = jnp.einsum(
        "gqhd,gkhd->ghqk", dout_heads, to_heads(value, HEADS), preferred_element_type=jnp.float32
    )
    dscores = (probs * (dprobs - delta[..., None])).astype(jnp.bfloat16)
    dq_term = scale * jnp.einsum(
        "ghqk,gkhd->gqhd", dscores, to_heads(key, HEADS), preferred_element_type=jnp.float32
    )
    dkey_term = jnp.einsum(
        "ghqk,gqhd->gkhd", dscores, to_heads(query, HEADS), preferred_element_type=jnp.float32
    )
    dvalue_term = jnp.einsum(
        "ghqk,gqhd->gkhd",
        probs.astype(jnp.bfloat16),
        dout_heads,
        preferred_element_type=jnp.float32,
    )
    summed = jnp.sum(dscores.astype(jnp.float32), axis=0)
    bias_term = jnp.einsum("hqk,kl->hql", summed, select, precision=lax.Precision.HIGHEST)
    return (
        dq_term,
        scale * dkey_term.reshape(groups, count_keys, width),
        dvalue_term.reshape(groups, count_keys, width),
        bias_term,
    )


def visit_cycle(carry, queries, douts, logsums, deltas, moving, members, query_rows, source, info):
    dqueries, dpair, bias_grads = carry
    dqueries = list(dqueries)
    bias_grads = list(bias_grads)
    key_pieces = []
    value_pieces = []
    for which, offset, rows in members:
        key = moving[0][:, offset : offset + rows]
        value = moving[1][:, offset : offset + rows]
        dq_term, dk_term, dv_term, bias_term = visit_one(
            queries[which],
            douts[which],
            logsums[which],
            deltas[which],
            key,
            value,
            query_rows[which],
            key_rows_of(source, rows),
            info[which],
        )
        dqueries[which] = dqueries[which] + dq_term
        key_pieces.append(dk_term)
        value_pieces.append(dv_term)
        bias_grads[which] = bias_grads[which] + bias_term
    new_pair = (
        dpair[0] + jnp.concatenate(key_pieces, axis=1),
        dpair[1] + jnp.concatenate(value_pieces, axis=1),
    )
    return (tuple(dqueries), new_pair, tuple(bias_grads))


def send_grads(dpair):
    return tuple(shifted((dpair[0], dpair[1]), "seq", 1))


def cycle_backward(queries, douts, logsums, deltas, cycle_pair, members, query_rows, info, start):
    position = lax.axis_index("seq")
    count = lax.axis_size("seq")
    dpair = tuple((jnp.zeros(item.shape, jnp.float32) for item in cycle_pair))

    def turn(step, state):
        carry, moving = state
        carry = visit_cycle(
            carry,
            queries,
            douts,
            logsums,
            deltas,
            moving,
            members,
            query_rows,
            (position - step) % count,
            info,
        )
        moving = tuple(shifted((moving[0], moving[1]), "seq", 1))
        return ((carry[0], send_grads(carry[1]), carry[2]), moving)

    carry, moving = lax.fori_loop(0, count - 1, turn, ((start[0], dpair, start[1]), cycle_pair))
    carry = visit_cycle(
        carry,
        queries,
        douts,
        logsums,
        deltas,
        moving,
        members,
        query_rows,
        (position - count + 1) % count,
        info,
    )
    return (carry[0], send_grads(carry[1]), carry[2])


def general_device(
    small_in,
    large_in,
    small_cot,
    large_cot,
    first_gain,
    first_bias,
    query_weight,
    query_bias,
    key_weight,
    value_weight,
    value_bias,
    out_weight,
    out_bias,
    attend_scale,
    second_gain,
    second_bias,
    up_weight,
    up_bias,
    down_weight,
    down_bias,
    feed_scale,
    rel_table,
):
    groups, small_rows, width = small_in.shape
    large_rows = large_in.shape[1]
    all_rows = small_rows + large_rows
    position = lax.axis_index("seq")
    query_rows = (
        position * small_rows + jnp.arange(small_rows, dtype=jnp.int32),
        position * large_rows + jnp.arange(large_rows, dtype=jnp.int32),
    )
    small_places = query_rows[0] % SLEN
    large_places = query_rows[1] % LLEN

    def make_biases(table):
        return (
            position_bias(table, small_places, SLEN, SGRID),
            position_bias(table, large_places, LLEN, LGRID),
        )

    biases, bias_back = jax.vjp(make_biases, rel_table)
    info = ((SLEN, SGRID, biases[0]), (LLEN, LGRID, biases[1]))
    valid_rows = jnp.concatenate(
        [small_places < SGRID * SGRID + 1, large_places < LGRID * LGRID + 1]
    )
    valid_flat = jnp.broadcast_to(valid_rows[None, :], (groups, all_rows)).reshape(-1)
    w_query, w_key, w_value, w_out, w_up, w_down = (
        lax.all_gather(query_weight, "img", axis=0, tiled=True),
        lax.all_gather(key_weight, "img", axis=0, tiled=True),
        lax.all_gather(value_weight, "img", axis=0, tiled=True),
        lax.all_gather(out_weight, "img", axis=0, tiled=True),
        lax.all_gather(up_weight, "img", axis=0, tiled=True),
        lax.all_gather(down_weight, "img", axis=0, tiled=True),
    )

    def split(rows_array):
        shaped = rows_array.reshape(groups, all_rows, -1)
        return (shaped[:, :small_rows], shaped[:, small_rows:])

    inputs = jnp.concatenate([small_in, large_in], axis=1).astype(jnp.float32).reshape(-1, width)
    hidden = layer_norm(inputs, first_gain, first_bias).astype(jnp.bfloat16)
    query = (matmul(hidden, w_query) + query_bias).astype(jnp.bfloat16)
    key = matmul(hidden, w_key).astype(jnp.bfloat16)
    value = (matmul(hidden, w_value) + value_bias).astype(jnp.bfloat16)
    queries = split(query)
    cycle_pair = (key.reshape(groups, all_rows, width), value.reshape(groups, all_rows, width))
    members = ((0, 0, small_rows), (1, small_rows, large_rows))
    attended, logsums = cycle_forward(queries, cycle_pair, members, query_rows, info)
    mixed = (
        jnp.concatenate([attended[0], attended[1]], axis=1).reshape(-1, width).astype(jnp.bfloat16)
    )
    branch = matmul(mixed, w_out) + out_bias
    residual = inputs + attend_scale * branch
    hidden2 = layer_norm(residual, second_gain, second_bias).astype(jnp.bfloat16)
    upper = matmul(hidden2, w_up) + up_bias
    active = jax.nn.gelu(upper, approximate=False).astype(jnp.bfloat16)
    lower = matmul(active, w_down) + down_bias
    output = jnp.where(valid_flat[:, None], residual + feed_scale * lower, 0.0).astype(jnp.bfloat16)
    small_out, large_out = split(output)
    upstream = (
        jnp.concatenate([small_cot, large_cot], axis=1).astype(jnp.float32).reshape(-1, width)
    )
    upstream = upstream * valid_flat[:, None].astype(jnp.float32)
    grad_feed_scale = jnp.sum(upstream * lower, axis=0)
    dlower = (upstream * feed_scale).astype(jnp.bfloat16)
    grad_down_bias = jnp.sum(dlower.astype(jnp.float32), axis=0)
    grad_down = jnp.einsum("rf,rd->fd", active, dlower, preferred_element_type=jnp.float32)
    dactive = jnp.einsum("rd,fd->rf", dlower, w_down, preferred_element_type=jnp.float32)
    unused, gelu_back = jax.vjp(lambda inner: jax.nn.gelu(inner, approximate=False), upper)
    dupper = gelu_back(dactive)[0].astype(jnp.bfloat16)
    grad_up_bias = jnp.sum(dupper.astype(jnp.float32), axis=0)
    grad_up = jnp.einsum("rd,rf->df", hidden2, dupper, preferred_element_type=jnp.float32)
    dhidden2 = jnp.einsum("rf,df->rd", dupper, w_up, preferred_element_type=jnp.float32)
    unused, second_back = jax.vjp(layer_norm, residual, second_gain, second_bias)
    dres_part, grad_second_gain, grad_second_bias = second_back(dhidden2)
    dresidual = upstream + dres_part
    grad_attend_scale = jnp.sum(dresidual * branch, axis=0)
    dbranch = (dresidual * attend_scale).astype(jnp.bfloat16)
    grad_out_bias = jnp.sum(dbranch.astype(jnp.float32), axis=0)
    grad_out = jnp.einsum("rd,re->de", mixed, dbranch, preferred_element_type=jnp.float32)
    dmixed = jnp.einsum("re,de->rd", dbranch, w_out, preferred_element_type=jnp.float32).astype(
        jnp.bfloat16
    )
    held, held_sums = cycle_forward(queries, cycle_pair, members, query_rows, info)
    douts = split(dmixed)
    deltas = tuple(
        (
            jnp.einsum(
                "gqhd,gqhd->ghq",
                to_heads(douts[which].astype(jnp.float32), HEADS),
                to_heads(held[which], HEADS),
            )
            for which in range(2)
        )
    )
    dq_start = tuple(
        (jnp.zeros(to_heads(queries[which], HEADS).shape, jnp.float32) for which in range(2))
    )
    bias_start = tuple((jnp.zeros(item.shape, jnp.float32) for item in biases))
    dqueries, dpair, bias_grads = cycle_backward(
        queries,
        douts,
        held_sums,
        deltas,
        cycle_pair,
        members,
        query_rows,
        info,
        (dq_start, bias_start),
    )
    table_grad = bias_back(bias_grads)[0]
    dquery = jnp.concatenate(
        [
            dqueries[0].reshape(groups, small_rows, width),
            dqueries[1].reshape(groups, large_rows, width),
        ],
        axis=1,
    )
    dquery = dquery.reshape(-1, width).astype(jnp.bfloat16)
    dkey = dpair[0].reshape(-1, width).astype(jnp.bfloat16)
    dvalue = dpair[1].reshape(-1, width).astype(jnp.bfloat16)
    grad_query_bias = jnp.sum(dquery.astype(jnp.float32), axis=0)
    grad_value_bias = jnp.sum(dvalue.astype(jnp.float32), axis=0)
    grad_query = jnp.einsum("rd,re->de", hidden, dquery, preferred_element_type=jnp.float32)
    grad_key = jnp.einsum("rd,re->de", hidden, dkey, preferred_element_type=jnp.float32)
    grad_value = jnp.einsum("rd,re->de", hidden, dvalue, preferred_element_type=jnp.float32)
    dhidden = (
        jnp.einsum("re,de->rd", dquery, w_query, preferred_element_type=jnp.float32)
        + jnp.einsum("re,de->rd", dkey, w_key, preferred_element_type=jnp.float32)
        + jnp.einsum("re,de->rd", dvalue, w_value, preferred_element_type=jnp.float32)
    )
    unused, first_back = jax.vjp(layer_norm, inputs, first_gain, first_bias)
    dinput_part, grad_first_gain, grad_first_bias = first_back(dhidden)
    dinputs = (dresidual + dinput_part).astype(jnp.bfloat16)
    small_grad, large_grad = split(dinputs)
    shares = (
        lax.psum_scatter(grad_query, "img", scatter_dimension=0, tiled=True),
        lax.psum_scatter(grad_key, "img", scatter_dimension=0, tiled=True),
        lax.psum_scatter(grad_value, "img", scatter_dimension=0, tiled=True),
        lax.psum_scatter(grad_out, "img", scatter_dimension=0, tiled=True),
        lax.psum_scatter(grad_up, "img", scatter_dimension=0, tiled=True),
        lax.psum_scatter(grad_down, "img", scatter_dimension=0, tiled=True),
    )
    shares = lax.psum((shares[0], shares[1], shares[2], shares[3], shares[4], shares[5]), "seq")
    smalls = lax.psum(
        (
            grad_first_gain,
            grad_first_bias,
            grad_query_bias,
            grad_value_bias,
            grad_out_bias,
            grad_attend_scale,
            grad_second_gain,
            grad_second_bias,
            grad_up_bias,
            grad_down_bias,
            grad_feed_scale,
            table_grad,
        ),
        ("img", "seq"),
    )
    return (
        small_out,
        large_out,
        small_grad,
        large_grad,
        smalls[0],
        smalls[1],
        shares[0],
        smalls[2],
        shares[1],
        shares[2],
        smalls[3],
        shares[3],
        smalls[4],
        smalls[5],
        smalls[6],
        smalls[7],
        shares[4],
        smalls[8],
        shares[5],
        smalls[9],
        smalls[10],
        smalls[11],
    )


def exchange_large(part):
    position = lax.axis_index("seq")
    stay = lax.dynamic_index_in_dim(part, position, 0, keepdims=False)
    leave = lax.dynamic_index_in_dim(part, 1 - position, 0, keepdims=False)
    came = shifted(leave, "seq", 1)
    return jnp.where(
        position == 0,
        jnp.concatenate([stay, came], axis=0),
        jnp.concatenate([came, stay], axis=0),
    )


def return_large(whole, rows):
    position = lax.axis_index("seq")
    stay = lax.dynamic_slice_in_dim(whole, position * rows, rows, 0)
    leave = lax.dynamic_slice_in_dim(whole, (1 - position) * rows, rows, 0)
    came = shifted(leave, "seq", 1)
    return jnp.where(position == 0, jnp.stack([stay, came]), jnp.stack([came, stay]))


def image_device(
    small_in,
    large_in,
    small_cot,
    large_cot,
    first_gain,
    first_bias,
    query_weight,
    query_bias,
    key_weight,
    value_weight,
    value_bias,
    out_weight,
    out_bias,
    attend_scale,
    second_gain,
    second_bias,
    up_weight,
    up_bias,
    down_weight,
    down_bias,
    feed_scale,
    rel_table,
):
    groups, small_rows, width = small_in.shape
    large_rows = large_in.shape[1]
    n_small = groups * small_rows // SLEN
    n_large = 1
    small_part = n_small * SPAD

    def compact(small, large):
        return jnp.concatenate(
            [
                small.reshape(n_small, SLEN, width)[:, :SPAD].reshape(small_part, width),
                exchange_large(large)[:LPAD],
            ],
            axis=0,
        )

    def expand_small(rows):
        small = rows[:small_part].reshape(n_small, SPAD, width)
        small = jnp.pad(small, ((0, 0), (0, SLEN - SPAD), (0, 0)))
        return small.reshape(groups, small_rows, width)

    def expand_large(rows):
        large = jnp.pad(rows[small_part:], ((0, LLEN - LPAD), (0, 0)))
        return return_large(large, large_rows)

    qkv_share = jnp.concatenate([query_weight, key_weight, value_weight], axis=1)
    w_qkv = lax.all_gather(qkv_share, "img", axis=0, tiled=True)
    mid_share = jnp.concatenate([out_weight, up_weight], axis=1)
    w_mid = lax.all_gather(mid_share, "img", axis=0, tiled=True)
    w_out, w_up = w_mid[:, :width], w_mid[:, width:]
    w_down = lax.all_gather(down_weight, "img", axis=0, tiled=True)

    large_seq, small_seq, edge = table_sequences(rel_table)
    x = compact(small_in, large_in)
    cot = compact(small_cot, large_cot)
    gain, bias = first_gain[None], first_bias[None]
    qkv_bias = jnp.concatenate([query_bias, jnp.zeros_like(query_bias), value_bias])[None]
    vectors = jnp.stack(
        [out_bias, attend_scale, second_gain, second_bias, down_bias, feed_scale]
        + [feed_scale] * 2
    )

    qkv = run_qkv(x, gain, bias, w_qkv, qkv_bias)
    attended, out_wide, probs_small, probs_large = run_attend(
        qkv, large_seq, small_seq, edge, n_small, n_large
    )
    out, dresidual, dattended, vector_grads, up_bias_grad, g_out, g_up, g_down = run_feed(
        x, attended, cot, w_out, w_up, w_down, vectors, up_bias[None], n_small
    )
    small_out, large_out = expand_small(out), expand_large(out)

    def reduce(share):
        share = lax.psum_scatter(share, "img", scatter_dimension=0, tiled=True)
        return lax.psum(share.astype(F32), "seq")

    g_mid = reduce(jnp.concatenate([g_out, g_up], axis=1))
    g_down = reduce(g_down)
    dquery, dkey, dvalue, d_large, d_small, d_edge = run_attend_back(
        qkv, dattended, out_wide, probs_small, probs_large, n_small, n_large
    )
    dinput, input_grads, g_qkv = run_input(
        x, dquery, dkey, dvalue, dresidual, gain, bias, w_qkv
    )
    small_grad, large_grad = expand_small(dinput), expand_large(dinput)
    g_qkv = reduce(g_qkv)
    edge_grad = jnp.stack([d_edge[:, 0, 0], d_edge[:, 1, 0], d_edge[:, 2, 0]], axis=1)
    vector_grads, up_bias_grad, input_grads, d_large, d_small, edge_grad = lax.psum(
        (vector_grads, up_bias_grad, input_grads, d_large, d_small, edge_grad), ("img", "seq")
    )
    table_grad = table_from_sequences(d_large, d_small, edge_grad)
    return (
        small_out,
        large_out,
        small_grad,
        large_grad,
        input_grads[3],
        input_grads[4],
        g_qkv[:, :width],
        input_grads[0],
        g_qkv[:, width : 2 * width],
        g_qkv[:, 2 * width :],
        input_grads[2],
        g_mid[:, :width],
        vector_grads[0],
        vector_grads[1],
        vector_grads[2],
        vector_grads[3],
        g_mid[:, width:],
        up_bias_grad[0],
        g_down,
        vector_grads[4],
        vector_grads[5],
        table_grad,
    )


def per_device(*args):
    groups, small_rows, unused = args[0].shape
    if lax.axis_size("seq") == 2 and groups == 2 and small_rows % SLEN == 0:
        return image_device(*args)
    return general_device(*args)


def solution(mesh):
    return jax.shard_map(
        per_device,
        mesh=mesh,
        in_specs=(
            P("img", "seq", None),
            P("img", "seq", None),
            P("img", "seq", None),
            P("img", "seq", None),
            P(),
            P(),
            P("img", None),
            P(),
            P("img", None),
            P("img", None),
            P(),
            P("img", None),
            P(),
            P(),
            P(),
            P(),
            P("img", None),
            P(),
            P("img", None),
            P(),
            P(),
            P(),
        ),
        out_specs=(
            P("img", "seq", None),
            P("img", "seq", None),
            P("img", "seq", None),
            P("img", "seq", None),
            P(),
            P(),
            P("img", None),
            P(),
            P("img", None),
            P("img", None),
            P(),
            P("img", None),
            P(),
            P(),
            P(),
            P(),
            P("img", None),
            P(),
            P("img", None),
            P(),
            P(),
            P(),
        ),
        check_vma=False,
    )
```

```python
import functools

import jax
import jax.numpy as jnp
from jax import lax
from jax.experimental import pallas as pl
from jax.experimental.pallas import tpu as pltpu
from jax.sharding import PartitionSpec as P

HEADS = 12
SGRID = 14
LGRID = 24
SLEN = 256
LLEN = 640
SPAD = 208
LPAD = 608
LANES = 128

NEGATIVE = -1e30
EPSILON = 1e-06
F32 = jnp.float32
BF16 = jnp.bfloat16
VMEM_BYTES = 62 << 20


def dot_nn(left, right):
    return lax.dot_general(left, right, (((1,), (0,)), ((), ())), preferred_element_type=F32)


def dot_nt(left, right):
    return lax.dot_general(left, right, (((1,), (1,)), ((), ())), preferred_element_type=F32)


def normalized(values):
    center = values - jnp.mean(values, axis=-1, keepdims=True)
    spread = jnp.mean(center * center, axis=-1, keepdims=True)
    scale = lax.rsqrt(spread + EPSILON)
    return center * scale, scale


def norm_back(grad, normal, scale):
    return scale * (
        grad
        - jnp.mean(grad, axis=-1, keepdims=True)
        - normal * jnp.mean(grad * normal, axis=-1, keepdims=True)
    )


def row_sum(values):
    return jnp.sum(values, axis=0, keepdims=True)


def iota(shape, axis):
    return lax.broadcasted_iota(jnp.int32, shape, axis)


L_WIDTH = 1280
S_WIDTH = 512


def table_sequences(table):
    heads = table.shape[0]
    span = 2 * LGRID - 1
    cells = table[:, : span * span].reshape(heads, span, span)

    def sequences(part, grid, width):
        rows = part.shape[1]
        low = part[:, :, :grid].reshape(heads, rows * grid)
        high = jnp.pad(part[:, :, grid:], ((0, 0), (0, 0), (0, 1))).reshape(heads, rows * grid)
        low = jnp.pad(low, ((0, 0), (0, width - rows * grid)))
        high = jnp.pad(high, ((0, 0), (grid, width - rows * grid - grid)))
        return jnp.stack([low, high], axis=1)

    off = LGRID - SGRID
    large = sequences(cells, LGRID, L_WIDTH)
    small = sequences(cells[:, off : span - off, off : span - off], SGRID, S_WIDTH)
    edge = jnp.broadcast_to(
        jnp.pad(table[:, span * span :], ((0, 0), (0, 5)))[:, :, None], (heads, 8, LANES)
    )
    return large, small, edge


def table_from_sequences(large, small, edge):
    heads = large.shape[0]
    span = 2 * LGRID - 1

    def cells(part, grid):
        rows = 2 * grid - 1
        low = part[:, 0, : rows * grid].reshape(heads, rows, grid)
        high = part[:, 1, grid : grid + rows * grid].reshape(heads, rows, grid)
        return jnp.concatenate([low, high[:, :, : grid - 1]], axis=2)

    off = LGRID - SGRID
    total = cells(large, LGRID) + jnp.pad(
        cells(small, SGRID), ((0, 0), (off, off), (off, off))
    )
    return jnp.concatenate([total.reshape(heads, span * span), edge], axis=1)


def takes_low(rows, width, grid, first):
    step = iota((rows, width), 1) % grid
    row = iota((rows, width), 0)
    low = step >= grid - 1 + first - row
    if first == 1:
        low = low | (row == 0)
    return low


def spread_sequences(seq, rows, width, grid, first):
    low = jnp.broadcast_to(seq[0:1, :], (rows, width))
    high = jnp.broadcast_to(seq[1:2, :], (rows, width))
    chosen = jnp.where(takes_low(rows, width, grid, first), low, high)
    return pltpu.roll(chosen, 1, 1, stride=1, stride_axis=0)


def gather_sequences(spread, rows, width, grid, first):
    row = iota((rows, width), 0) + 1
    for bit in (1, 2, 4, 8, 16):
        spread = jnp.where((row & bit) != 0, pltpu.roll(spread, width - bit, 1), spread)
    low = takes_low(rows, width, grid, first)
    return (
        row_sum(jnp.where(low, spread, 0.0)),
        row_sum(jnp.where(low, 0.0, spread)),
    )


def large_window(block):
    start = (LGRID - block) * LGRID
    return start // LANES, start % LANES


def small_window(block):
    start = (SGRID - 1 - block) * SGRID + SGRID - 1
    return start // LANES, start % LANES


def head_masks():
    lane = iota((1, LANES), 1)
    return (
        jnp.where(lane < LANES // 2, 1.0, 0.0).astype(BF16),
        jnp.where(lane < LANES // 2, 0.0, 1.0).astype(BF16),
    )


def transposed_biases(large_seq, small_seq, edge, wide, narrow, bias_large, bias_small):
    patch_q = edge[0:1, 0:1]
    patch_k = edge[1:2, 0:1]
    both = edge[2:3, 0:1]
    wide[...] = spread_sequences(large_seq, 24, L_WIDTH, LGRID, 1)
    lane = iota((24, LANES), 1)
    row = iota((24, LANES), 0)
    for block in range(LGRID + 1):
        at, turn = large_window(block)
        piece = wide[:, at * LANES : at * LANES + 768]
        if turn:
            piece = pltpu.roll(piece, 768 - turn, 1)
        piece = piece[:, :640]
        if block == 0:
            rest = jnp.where(iota((24, 640), 0) == 0, patch_k, piece)
        elif block == LGRID:
            rest = jnp.where(iota((24, 640), 0) == 0, piece, NEGATIVE)
        else:
            rest = piece
        first = jnp.where(lane == 0, patch_q, rest[:, :LANES])
        if block == 0:
            first = jnp.where((lane == 0) & (row == 0), both, first)
        if block == LGRID:
            first = jnp.where(row == 0, first, NEGATIVE)
        bias_large[pl.ds(block * 24, 24), 0:LANES] = first
        bias_large[pl.ds(block * 24, 24), LANES:640] = rest[:, LANES:]
    bias_large[pl.ds(600, 8), :] = jnp.full((8, 640), NEGATIVE, F32)
    narrow[...] = spread_sequences(small_seq, 16, S_WIDTH, SGRID, 0)
    for block in range(SGRID):
        at, turn = small_window(block)
        piece = narrow[:, at * LANES : at * LANES + 384]
        if turn:
            piece = pltpu.roll(piece, 384 - turn, 1)
        bias_small[pl.ds(1 + SGRID * block, SGRID), :] = piece[:SGRID, :256]
    whole = bias_small[...]
    lane = iota((SPAD, 256), 1)
    row = iota((SPAD, 256), 0)
    whole = jnp.where(lane == 0, patch_q, whole)
    whole = jnp.where(row == 0, patch_k, whole)
    whole = jnp.where((lane == 0) & (row == 0), both, whole)
    bias_small[...] = jnp.where(row > SGRID * SGRID, NEGATIVE, whole)


MESH = pl.DeviceIdType.MESH
ZS = 4


def place():
    img = lax.axis_index("img")
    return img // 4, (img // 2) % 2, img % 2, lax.axis_index("seq")


def device(z, x, c, y):
    return ((z * 2 + x) * 2 + c, y)


def z_peer(z, hop):
    low = (z % 2) * (1 - 2 * (hop % 2)) + hop % 2
    high = (z // 2) * (1 - 2 * (hop // 2)) + hop // 2
    return high * 2 + low


def greet():
    z, x, c, y = place()
    barrier = pltpu.get_barrier_semaphore()
    peers = [device(z_peer(z, hop), x, c, y) for hop in range(1, ZS)]
    peers += [device(z, 1 - x, c, y), device(z, x, c, 1 - y), device(z, x, 1 - c, y)]
    for peer in peers:
        pl.semaphore_signal(barrier, inc=1, device_id=peer, device_id_type=MESH)
    pl.semaphore_wait(barrier, len(peers))


def half_of(width, y):
    return pl.ds(pl.multiple_of(y * (width // 2), 128), width // 2)


class Gather:
    n_sems = 3 + 4 + 4 + 4 + 4

    def __init__(self, share, whole, send, recv, own):
        self.share, self.whole, self.send, self.recv, self.own = share, whole, send, recv, own
        self.width = share.shape[1]
        self.at = place()

    def copy(self, source, target, index, peer):
        return pltpu.make_async_remote_copy(
            src_ref=source,
            dst_ref=target,
            send_sem=self.send.at[index],
            recv_sem=self.recv.at[index],
            device_id=peer,
            device_id_type=MESH,
        )

    def along_z(self, hop):
        z, x, c, y = self.at
        cols = half_of(self.width, y)
        return self.copy(
            self.share.at[:, cols],
            self.whole.at[z, x, c, :, cols],
            hop - 1,
            device(z_peer(z, hop), x, c, y),
        )

    def across(self, hop, axis):
        z, x, c, y = self.at
        cols = half_of(self.width, y)
        source_z = z_peer(z, hop)
        source = self.share.at[:, cols] if hop == 0 else self.whole.at[source_z, x, c, :, cols]
        peer = device(z, 1 - x, c, y) if axis == 0 else device(z, x, c, 1 - y)
        return self.copy(source, self.whole.at[source_z, x, c, :, cols], 3 + 4 * axis + hop, peer)

    def onward(self, hop):
        z, x, c, y = self.at
        source_z = z_peer(z, hop)
        even = 1 if hop == 0 else 1 - source_z % 2
        side = x + even * (1 - 2 * x)
        cols = half_of(self.width, y + (1 - even) * (1 - 2 * y))
        block = self.whole.at[source_z, side, c, :, cols]
        peer = device(z, x + (1 - even) * (1 - 2 * x), c, y + even * (1 - 2 * y))
        return self.copy(block, block, 11 + hop, peer)

    def to_core(self, hop):
        z, x, c, y = self.at
        block = self.whole.at[z_peer(z, hop), :, c]
        return self.copy(block, block, 15 + hop, device(z, x, 1 - c, y))

    def keep_own(self):
        z, x, c, y = self.at
        return pltpu.make_async_copy(self.share, self.whole.at[z, x, c], self.own)

    def begin(self):
        self.keep_own().start()
        self.across(0, 0).start()
        for hop in range(1, ZS):
            self.along_z(hop).start()

    def spread(self):
        for hop in range(1, ZS):
            self.along_z(hop).wait_recv()
            for axis in range(2):
                self.across(hop, axis).start()

    def relay(self):
        for hop in range(ZS):
            for axis in range(2 if hop else 1):
                self.across(hop, axis).wait_recv()
            self.onward(hop).start()

    def share_cores(self):
        self.keep_own().wait()
        for hop in range(ZS):
            self.onward(hop).wait_recv()
            self.to_core(hop).start()

    def finish(self):
        for hop in range(ZS):
            self.to_core(hop).wait()
            self.onward(hop).wait_send()
            for axis in range(2 if hop else 1):
                self.across(hop, axis).wait_send()
        for hop in range(1, ZS):
            self.along_z(hop).wait_send()


def gather_kernel(count, *refs):
    shares, wholes = refs[:count], refs[count : 2 * count]
    send, recv, own = refs[2 * count :]
    greet()
    jobs = [
        Gather(shares[i], wholes[i], send.at[i], recv.at[i], own.at[i]) for i in range(count)
    ]
    for stage in ("begin", "spread", "relay", "share_cores", "finish"):
        for job in jobs:
            getattr(job, stage)()


def run_gather(shares, collective):
    count = len(shares)
    anywhere = pl.BlockSpec(memory_space=pl.ANY)
    sems = pltpu.SemaphoreType.DMA
    wholes = pl.pallas_call(
        functools.partial(gather_kernel, count),
        in_specs=[anywhere] * count,
        out_specs=[anywhere] * count,
        out_shape=[jax.ShapeDtypeStruct((ZS, 2, 2) + s.shape, s.dtype) for s in shares],
        scratch_shapes=[
            sems((count, Gather.n_sems)),
            sems((count, Gather.n_sems)),
            sems((count,)),
        ],
        compiler_params=pltpu.CompilerParams(collective_id=collective, has_side_effects=True),
    )(*shares)
    return [w.reshape(-1, w.shape[-1]) for w in wholes]


def add_rows(target, source, shape):
    rows, cols = shape

    def strip(i, unused):
        at = pl.ds(pl.multiple_of(i * 16, 16), 16)
        target[at, :] = (target[at, :].astype(F32) + source[at, :].astype(F32)).astype(BF16)
        return unused

    lax.fori_loop(0, rows // 16, strip, 0)


class Reduce:
    n_sems = 21
    n_scratch = 6

    def __init__(self, grad, out, held, core, first, second, last, edge, send, recv, own):
        self.grad, self.held, self.core = grad, held, core
        self.first, self.second, self.last, self.edge, self.out = first, second, last, edge, out
        self.send, self.recv, self.own = send, recv, own
        self.rows, self.width = out.shape
        self.at = place()
        self.mine = half_of(self.width, self.at[3])
        self.other = half_of(self.width, 1 - self.at[3])

    @staticmethod
    def scratch(rows, width):
        half = width // 2
        return [
            pltpu.VMEM((ZS, 2, rows, width), BF16),
            pltpu.VMEM((ZS, 2, rows, width), BF16),
            pltpu.VMEM((ZS, 2, rows, half), BF16),
            pltpu.VMEM((ZS, rows, half), BF16),
            pltpu.VMEM((ZS, rows, half), BF16),
            pltpu.VMEM((2, rows, half), BF16),
        ]

    def copy(self, source, target, index, peer):
        return pltpu.make_async_remote_copy(
            src_ref=source,
            dst_ref=target,
            send_sem=self.send.at[index],
            recv_sem=self.recv.at[index],
            device_id=peer,
            device_id_type=MESH,
        )

    def load(self, s):
        return pltpu.make_async_copy(
            self.grad.at[s, :, self.at[2]], self.held.at[s], self.own.at[s]
        )

    def between_cores(self, s):
        z, x, c, y = self.at
        return self.copy(self.grad.at[s, :, 1 - c], self.core.at[s], s, device(z, x, 1 - c, y))

    def leg_one(self, s, i):
        z, x, c, y = self.at
        half = self.width // 2
        if s % 2 == 0:
            source = self.held.at[s, 1 - x, :, pl.ds(i * half, half)]
            peer = device(z, 1 - x, c, y)
        else:
            source = self.held.at[s, i, :, self.other]
            peer = device(z, x, c, 1 - y)
        return self.copy(source, self.first.at[s, i], 4 + 2 * s + i, peer)

    def leg_two(self, s):
        z, x, c, y = self.at
        if s % 2 == 0:
            source = self.held.at[s, x, :, self.other]
            peer = device(z, x, c, 1 - y)
        else:
            source = self.held.at[s, 1 - x, :, self.mine]
            peer = device(z, 1 - x, c, y)
        return self.copy(source, self.second.at[s], 12 + s, peer)

    def leg_three(self, hop):
        z, x, c, y = self.at
        target = z_peer(z, hop)
        source = self.held.at[target, x, :, self.mine]
        return self.copy(source, self.last.at[hop], 16 + hop, device(target, x, c, y))

    def leg_four(self):
        z, x, c, y = self.at
        return self.copy(self.edge.at[0], self.edge.at[1], 20, device(z, x, c, 1 - y))

    def begin(self):
        for s in range(ZS):
            self.between_cores(s).start()
            self.load(s).start()

    def one(self):
        for s in range(ZS):
            self.load(s).wait()
            self.between_cores(s).wait_recv()
            for i in range(2):
                add_rows(self.held.at[s, i], self.core.at[s, i], (self.rows, self.width))
            for i in range(2):
                self.leg_one(s, i).start()

    def two(self):
        x = self.at[1]
        half = self.width // 2
        for s in range(ZS):
            for i in range(2):
                self.leg_one(s, i).wait_recv()
                if s % 2 == 0:
                    target = self.held.at[s, x, :, pl.ds(i * half, half)]
                else:
                    target = self.held.at[s, i, :, self.mine]
                add_rows(target, self.first.at[s, i], (self.rows, half))
            self.leg_two(s).start()

    def three(self):
        x = self.at[1]
        for s in range(ZS):
            self.leg_two(s).wait_recv()
            target = self.held.at[s, x, :, self.mine]
            add_rows(target, self.second.at[s], (self.rows, self.width // 2))
        for hop in range(1, ZS):
            self.leg_three(hop).start()

    def four(self):
        z, x, c, y = self.at
        for hop in range(1, ZS):
            self.leg_three(hop).wait_recv()
        own = self.held.at[z, x, :, self.mine]
        last, edge = self.last, self.edge

        def strip(i, unused):
            at = pl.ds(pl.multiple_of(i * 16, 16), 16)
            total = own[at, :].astype(F32)
            for hop in range(1, ZS):
                total += last[hop, at, :].astype(F32)
            edge[0, at, :] = total.astype(BF16)
            return unused

        lax.fori_loop(0, self.rows // 16, strip, 0)
        self.leg_four().start()
        self.out[:, self.mine] = edge[0].astype(F32)

    def finish(self):
        self.leg_four().wait()
        self.out[:, self.other] = self.edge[1].astype(F32)
        for s in range(ZS):
            self.between_cores(s).wait_send()
            for i in range(2):
                self.leg_one(s, i).wait_send()
            self.leg_two(s).wait_send()
        for hop in range(1, ZS):
            self.leg_three(hop).wait_send()


class Total:
    n_steps = 5

    def __init__(self, part, out, leave, come, send, recv):
        self.part, self.out, self.leave, self.come = part, out, leave, come
        self.send, self.recv = send, recv
        self.at = place()

    @staticmethod
    def scratch(shape):
        return [pltpu.VMEM((Total.n_steps,) + shape, BF16)] * 2

    def copy(self, step):
        z, x, c, y = self.at
        peer = (
            device(z, x, 1 - c, y),
            device(z, 1 - x, c, y),
            device(z, x, c, 1 - y),
            device(z_peer(z, 1), x, c, y),
            device(z_peer(z, 2), x, c, y),
        )[step]
        return pltpu.make_async_remote_copy(
            src_ref=self.leave.at[step],
            dst_ref=self.come.at[step],
            send_sem=self.send.at[step],
            recv_sem=self.recv.at[step],
            device_id=peer,
            device_id_type=MESH,
        )

    def begin(self):
        self.leave[0] = self.part[...].astype(BF16)
        self.copy(0).start()

    def advance(self, step):
        self.copy(step).wait()
        total = self.leave[step].astype(F32) + self.come[step].astype(F32)
        if step + 1 < self.n_steps:
            self.leave[step + 1] = total.astype(BF16)
            self.copy(step + 1).start()
        else:
            self.out[...] = total


def reduce_kernel(n_grads, n_small, *refs):
    refs = list(refs)

    def take(count):
        taken = refs[:count]
        del refs[:count]
        return taken

    grads, parts = take(n_grads), take(n_small)
    outs, totals = take(n_grads), take(n_small)
    grad_scratch = [take(Reduce.n_scratch) for unused in grads]
    small_scratch = [take(2) for unused in parts]
    send, recv, own = take(3)
    small_send, small_recv = take(2) if n_small else (None, None)
    greet()
    jobs = [
        Reduce(grads[i], outs[i], *grad_scratch[i], send.at[i], recv.at[i], own.at[i])
        for i in range(n_grads)
    ]
    sums = [
        Total(parts[i], totals[i], *small_scratch[i], small_send.at[i], small_recv.at[i])
        for i in range(n_small)
    ]
    for item in jobs + sums:
        item.begin()
    for step, stage in enumerate(("one", "two", "three", "four", "finish")):
        for job in jobs:
            getattr(job, stage)()
        for item in sums:
            item.advance(step)


def run_reduce(grads, smalls, collective):
    anywhere = pl.BlockSpec(memory_space=pl.ANY)
    inside = pl.BlockSpec(memory_space=pltpu.VMEM)
    sems = pltpu.SemaphoreType.DMA
    count = len(grads)
    shares = [(g.shape[0] // 16, g.shape[1]) for g in grads]
    scratch = []
    for shape in shares:
        scratch += Reduce.scratch(*shape)
    for small in smalls:
        scratch += Total.scratch(small.shape)
    scratch += [
        sems((count, Reduce.n_sems)),
        sems((count, Reduce.n_sems)),
        sems((count, ZS)),
    ]
    if smalls:
        scratch += [sems((len(smalls), Total.n_steps))] * 2
    made = pl.pallas_call(
        functools.partial(reduce_kernel, count, len(smalls)),
        in_specs=[anywhere] * count + [inside] * len(smalls),
        out_specs=[inside] * (count + len(smalls)),
        out_shape=[jax.ShapeDtypeStruct(s, F32) for s in shares]
        + [jax.ShapeDtypeStruct(s.shape, F32) for s in smalls],
        scratch_shapes=scratch,
        compiler_params=pltpu.CompilerParams(
            collective_id=collective, has_side_effects=True, vmem_limit_bytes=62 << 20
        ),
    )(*[g.reshape(ZS, 2, 2, g.shape[0] // 16, g.shape[1]) for g in grads], *smalls)
    return made[:count], made[count:]


def attend_kernel(
    n_small,
    n_large,
    large_seq,
    small_seq,
    edge,
    query,
    key,
    value,
    mid_share,
    down_share,
    out,
    out_wide,
    probs_small,
    probs_large,
    mid_whole,
    down_whole,
    wide,
    narrow,
    bias_large,
    bias_small,
    send,
    recv,
    own,
):
    masks = head_masks()
    jobs = [
        Gather(mid_share, mid_whole, send.at[0], recv.at[0], own.at[0]),
        Gather(down_share, down_whole, send.at[1], recv.at[1], own.at[1]),
    ]

    @pl.when(pl.program_id(0) == 0)
    def _():
        greet()
        for job in jobs:
            job.begin()

    @pl.when(pl.program_id(0) == 0)
    def _():
        bias_small[...] = jnp.zeros_like(bias_small)

    members = [(i * SPAD, SPAD, bias_small, probs_small, i) for i in range(n_small)]
    members += [
        (n_small * SPAD + i * LPAD, LPAD, bias_large, probs_large, i) for i in range(n_large)
    ]
    halves = [[] for _ in members]
    for head in range(2):
        transposed_biases(
            large_seq[head], small_seq[head], edge[head], wide, narrow, bias_large, bias_small
        )
        for at, (start, count, bias, probs, which) in enumerate(members):
            rows = pl.ds(start, count)
            scores = dot_nt(key[rows, :], query[rows, :] * masks[head]) + bias[:, :count]
            top = jnp.max(scores, axis=0, keepdims=True)
            weights = jnp.exp(scores - top)
            total = jnp.sum(weights, axis=0, keepdims=True)
            prob = (weights * (1.0 / total)).astype(BF16)
            probs[head, which] = prob
            turned = value[rows, :].T
            halves[at].append(dot_nn(turned[head * 64 : head * 64 + 64, :], prob))
    for at, (start, count, bias, probs, which) in enumerate(members):
        both = jnp.concatenate(halves[at], axis=0).T
        out[pl.ds(start, count), :] = both.astype(BF16)
        out_wide[pl.ds(start, count), :] = both
    for stage, step in (("spread", 2), ("relay", 4), ("share_cores", 5), ("finish", 5)):

        @pl.when(pl.program_id(0) == step)
        def _():
            for job in jobs:
                getattr(job, stage)()


def attend_back_kernel(
    n_small,
    n_large,
    query,
    key,
    value,
    dout,
    out_wide,
    probs_small,
    probs_large,
    g_mid,
    g_down,
    dquery,
    dkey,
    dvalue,
    large_seq,
    small_seq,
    mid_out,
    down_out,
    wide,
    narrow,
    dsum_small,
    dscore_large,
    *scratch,
):
    masks = head_masks()
    send, recv, own = scratch[-3:]
    count = Reduce.n_scratch
    jobs = [
        Reduce(g_mid, mid_out, *scratch[:count], send.at[0], recv.at[0], own.at[0]),
        Reduce(g_down, down_out, *scratch[count : 2 * count], send.at[1], recv.at[1], own.at[1]),
    ]

    @pl.when(pl.program_id(0) == 0)
    def _():
        greet()
        for job in jobs:
            job.begin()
    lane = iota((1, LANES), 1)
    scale = float(64) ** (-0.5)
    members = [(i * SPAD, SPAD, probs_small, i) for i in range(n_small)]
    members += [(n_small * SPAD + i * LPAD, LPAD, probs_large, i) for i in range(n_large)]
    keep = []
    for head in range(2):
        spot = 64 * (1 - head)
        minus = jnp.where((lane == spot) | (lane == spot + 1), -1.0, 0.0).astype(BF16)
        mask32 = masks[head].astype(F32)
        for at, (start, count, probs, which) in enumerate(members):
            rows = pl.ds(start, count)
            grad = dout[rows, :]
            grad32 = grad.astype(F32) * mask32
            delta = jnp.sum(grad32 * out_wide[rows, :], axis=1, keepdims=True)
            coarse = delta.astype(BF16).astype(F32)
            fine = delta - coarse
            side = jnp.where(lane == spot, coarse, jnp.where(lane == spot + 1, fine, grad32))
            values = value[rows, :] * masks[head] + minus
            prob = probs[head, which]
            dscore = prob.astype(F32) * dot_nt(values, side.astype(BF16))
            if count == SPAD:
                if which == 0:
                    dsum_small[:, :SPAD] = dscore
                else:
                    dsum_small[:, :SPAD] += dscore
            elif which == 0:
                dscore_large[:, :LPAD] = dscore
            else:
                dscore_large[:, :LPAD] += dscore
            low = dscore.astype(BF16)
            turned = key[rows, :].T
            dq = dot_nn(turned[head * 64 : head * 64 + 64, :], low)
            dk = dot_nn(low, query[rows, :])
            dv = dot_nn(prob, grad)
            if head == 0:
                keep.append((dq, dk, dv))
            else:
                first = iota((count, LANES), 1) < 64
                dq0, dk0, dv0 = keep[at]
                dquery[rows, :] = (jnp.concatenate([dq0, dq], axis=0).T * scale).astype(BF16)
                dkey[rows, :] = jnp.where(first, dk0, dk).astype(BF16)
                dvalue[rows, :] = jnp.where(first, dv0, dv).astype(BF16)
        wide[...] = jnp.zeros_like(wide)
        dscore_large[:, LPAD:] = jnp.zeros((LPAD, 768 - LPAD), F32)
        edge_lane = iota((24, 768), 1)
        edge_row = iota((24, 768), 0)
        class_column = jnp.zeros((24, 768), F32)
        class_row = None
        for block in range(LGRID + 1):
            at, turn = large_window(block)
            piece = dscore_large[pl.ds(block * 24, 24), :]
            if block == 0:
                class_row = piece[0:1, :]
                piece = jnp.where(edge_row == 0, 0.0, piece)
            class_column = class_column + piece
            piece = jnp.where(edge_lane == 0, 0.0, piece)
            if turn:
                piece = pltpu.roll(piece, turn, 1)
            wide[:, at * LANES : at * LANES + 768] += piece
        low_sum, high_sum = gather_sequences(wide[...], 24, L_WIDTH, LGRID, 1)
        large_seq[head, 0:1, :] = low_sum
        large_seq[head, 1:2, :] = high_sum
        narrow[...] = jnp.zeros_like(narrow)
        dsum_small[:, SPAD:] = jnp.zeros((SPAD, 384 - SPAD), F32)
        small_lane = iota((SGRID, 384), 1)
        small_column = jnp.zeros((SGRID, 384), F32)
        for block in range(SGRID):
            at, turn = small_window(block)
            piece = dsum_small[pl.ds(1 + SGRID * block, SGRID), :]
            small_column = small_column + piece
            piece = jnp.where(small_lane == 0, 0.0, piece)
            piece = jnp.concatenate([piece, jnp.zeros((2, 384), F32)], axis=0)
            if turn:
                piece = pltpu.roll(piece, turn, 1)
            narrow[:, at * LANES : at * LANES + 384] += piece
        low_sum, high_sum = gather_sequences(narrow[...], 16, S_WIDTH, SGRID, 0)
        by_query = row_sum(class_column)[:, :LANES] + row_sum(small_column)[:, :LANES]
        both_rows = class_row + jnp.concatenate(
            [dsum_small[0:1, :], jnp.zeros((1, 384), F32)], axis=1
        )
        class_key = jnp.sum(
            jnp.where(iota((1, 768), 1) == 0, 0.0, both_rows), axis=1, keepdims=True
        )
        spot = iota((1, S_WIDTH), 1)
        low_sum = jnp.where(spot == S_WIDTH - 3, by_query[:, 0:1], low_sum)
        low_sum = jnp.where(spot == S_WIDTH - 2, class_key, low_sum)
        low_sum = jnp.where(spot == S_WIDTH - 1, both_rows[:, 0:1], low_sum)
        small_seq[head, 0:1, :] = low_sum
        small_seq[head, 1:2, :] = high_sum
    for stage, step in (("one", 1), ("two", 3), ("three", 4), ("four", 5), ("finish", 5)):

        @pl.when(pl.program_id(0) == step)
        def _():
            for job in jobs:
                getattr(job, stage)()


def qkv_kernel(x, gain, bias, weight, weight_bias, out):
    width = x.shape[1]
    normal, unused = normalized(x[...].astype(F32))
    hidden = (normal * gain[...] + bias[...]).astype(BF16)
    scale = float(width // HEADS) ** (-0.5)
    for part in range(3):
        cols = slice(part * width, (part + 1) * width)
        made = (dot_nn(hidden, weight[:, cols]) + weight_bias[:, cols]).astype(BF16)
        out[:, cols] = made * jnp.asarray(scale, BF16) if part == 0 else made


def gelu_pair(upper):
    normal_cdf = 0.5 * (1.0 + lax.erf(upper * (0.5**0.5)))
    density = jnp.exp(-0.5 * upper * upper) * 0.3989422804014327
    return upper * normal_cdf, normal_cdf + upper * density


def valid_rows(first, count, n_small):
    row = iota((count, 1), 0) + first
    in_small = row < n_small * SPAD
    small_ok = row % SPAD < SGRID * SGRID + 1
    large_ok = (row - n_small * SPAD) % LPAD < LGRID * LGRID + 1
    return jnp.where(in_small, small_ok.astype(F32), large_ok.astype(F32))


def feed_kernel(
    n_small,
    tiles,
    x,
    attended,
    cot,
    w_mid,
    w_down,
    vectors,
    up_bias,
    out,
    dresidual,
    dattended,
    vector_grads,
    g_mid,
    g_down,
    active,
    slope,
    acc_out,
    acc_up,
    acc_down,
    stage,
    sems,
):
    step = pl.program_id(0)
    count, width = x.shape
    w_out = w_mid.at[:, :width]
    w_up = w_mid.at[:, width:]
    tile = w_up.shape[1] // tiles

    @pl.when(step == 0)
    def _():
        acc_out[...] = jnp.zeros_like(acc_out)
        acc_up[...] = jnp.zeros_like(acc_up)
        acc_down[...] = jnp.zeros_like(acc_down)
        vector_grads[...] = jnp.zeros_like(vector_grads)

    out_bias = vectors[0:1, :]
    attend_scale = vectors[1:2, :]
    second_gain = vectors[2:3, :]
    second_bias = vectors[3:4, :]
    down_bias = vectors[4:5, :]
    feed_scale = vectors[5:6, :]

    valid = valid_rows(step * count, count, n_small)
    mixed = attended[...]
    branch = dot_nn(mixed, w_out[...]) + out_bias
    residual = x[...].astype(F32) + attend_scale * branch
    normal, scale = normalized(residual)
    hidden = (normal * second_gain + second_bias).astype(BF16)
    lower = jnp.zeros((count, width), F32)
    for t in range(tiles):
        cols = slice(t * tile, (t + 1) * tile)
        upper = dot_nn(hidden, w_up[:, cols]) + up_bias[:, cols]
        made, rate = gelu_pair(upper)
        made = made.astype(BF16)
        active[:, cols] = made
        slope[:, cols] = rate.astype(BF16)
        lower += dot_nn(made, w_down[cols, :])
    lower += down_bias
    out[...] = ((residual + feed_scale * lower) * valid).astype(BF16)
    upstream = cot[...].astype(F32) * valid
    vector_grads[5:6, :] += row_sum(upstream * lower)
    dlower = (upstream * feed_scale).astype(BF16)
    vector_grads[4:5, :] += row_sum(dlower.astype(F32))
    turned = hidden.T
    dhidden = jnp.zeros((count, width), F32)
    for t in range(tiles):
        cols = slice(t * tile, (t + 1) * tile)
        dupper = (dot_nt(dlower, w_down[cols, :]) * slope[:, cols].astype(F32)).astype(BF16)
        vector_grads[8 + t : 9 + t, :] += row_sum(dupper.astype(F32))
        acc_down[cols, :] += dot_nn(active[:, cols].T, dlower)
        acc_up[:, cols] += dot_nn(turned, dupper)
        dhidden += dot_nt(dupper, w_up[:, cols])
    vector_grads[2:3, :] += row_sum(dhidden * normal)
    vector_grads[3:4, :] += row_sum(dhidden)
    dres = upstream + norm_back(dhidden * second_gain, normal, scale)
    dresidual[...] = dres
    vector_grads[1:2, :] += row_sum(dres * branch)
    dbranch = (dres * attend_scale).astype(BF16)
    vector_grads[0:1, :] += row_sum(dbranch.astype(F32))
    acc_out[...] += dot_nn(mixed.T, dbranch)
    dattended[...] = dot_nt(dbranch, w_out[...]).astype(BF16)

    @pl.when(step == pl.num_programs(0) - 1)
    def _():
        part = stage.shape[1]
        jobs = [
            (source, target, slice(r, r + part), c, shift)
            for source, target, shift in (
                (acc_out, g_mid, 0),
                (acc_up, g_mid, width),
                (acc_down, g_down, 0),
            )
            for r in range(0, source.shape[0], part)
            for c in range(0, source.shape[1], width)
        ]
        flights = []
        for at, (source, target, rows, col, shift) in enumerate(jobs):
            slot = at % 2
            if at >= 2:
                flights[at - 2].wait()
            stage[slot] = source[rows, col : col + width].astype(BF16)
            flight = pltpu.make_async_copy(
                stage.at[slot],
                target.at[rows, col + shift : col + shift + width],
                sems.at[slot],
            )
            flight.start()
            flights.append(flight)
        for flight in flights[-2:]:
            flight.wait()


def input_kernel(
    x, dquery, dkey, dvalue, dresidual, gain, bias, weight, out, vector_grads, grad, acc
):
    step = pl.program_id(0)
    width = x.shape[1]

    @pl.when(step == 0)
    def _():
        acc[...] = jnp.zeros_like(acc)
        vector_grads[...] = jnp.zeros_like(vector_grads)

    normal, scale = normalized(x[...].astype(F32))
    hidden = (normal * gain[...] + bias[...]).astype(BF16)
    turned = hidden.T
    dhidden = jnp.zeros(normal.shape, F32)
    for part, item in enumerate((dquery, dkey, dvalue)):
        cols = slice(part * width, (part + 1) * width)
        piece = item[...]
        dhidden += dot_nt(piece, weight[:, cols])
        acc[:, cols] += dot_nn(turned, piece)
        if part != 1:
            vector_grads[part : part + 1, :] += row_sum(piece.astype(F32))
    vector_grads[3:4, :] += row_sum(dhidden * normal)
    vector_grads[4:5, :] += row_sum(dhidden)
    out[...] = (dresidual[...] + norm_back(dhidden * gain[...], normal, scale)).astype(BF16)

    @pl.when(step == pl.num_programs(0) - 1)
    def _():
        grad[...] = acc[...].astype(BF16)


def chunk_rows(total):
    return max(size for size in range(16, 481, 16) if total % size == 0)


def params(collective=None):
    if collective is None:
        return pltpu.CompilerParams(vmem_limit_bytes=VMEM_BYTES)
    return pltpu.CompilerParams(
        vmem_limit_bytes=VMEM_BYTES, collective_id=collective, has_side_effects=True
    )


def held(shape):
    rank = len(shape)
    return pl.BlockSpec(shape, lambda i: (0,) * rank, pipeline_mode=pl.Buffered(1))


def resident(shape):
    rank = len(shape)
    return pl.BlockSpec(shape, lambda i: (0,) * rank)


def run_qkv(x, gain, bias, weight, weight_bias):
    rows, width = x.shape
    size = chunk_rows(rows)
    wide = weight.shape[1]
    return pl.pallas_call(
        qkv_kernel,
        grid=(rows // size,),
        in_specs=[
            pl.BlockSpec((size, width), lambda i: (i, 0)),
            held((1, width)),
            held((1, width)),
            held(weight.shape),
            held((1, wide)),
        ],
        out_specs=pl.BlockSpec((size, wide), lambda i: (i, 0)),
        out_shape=jax.ShapeDtypeStruct((rows, wide), BF16),
        compiler_params=params(),
        cost_estimate=pl.CostEstimate(
            flops=2 * rows * width * wide, bytes_accessed=rows * wide * 2, transcendentals=0
        ),
    )(x, gain, bias, weight, weight_bias)


def run_attend(qkv, large_seq, small_seq, edge, n_small, n_large, shares, collective):
    rows = qkv.shape[0]
    width = qkv.shape[1] // 3
    pairs = HEADS // 2

    def column(which):
        return pl.BlockSpec((rows, LANES), lambda i: (0, which * pairs + i))

    def per_pair(shape):
        tail = (0,) * (len(shape) - 1)
        return pl.BlockSpec((2,) + shape[1:], lambda i: (i,) + tail)

    anywhere = pl.BlockSpec(memory_space=pl.ANY)
    wholes = [(ZS, 2, 2) + s.shape for s in shares]
    sems = pltpu.SemaphoreType.DMA
    made = pl.pallas_call(
        functools.partial(attend_kernel, n_small, n_large),
        grid=(pairs,),
        in_specs=[
            per_pair(large_seq.shape),
            per_pair(small_seq.shape),
            per_pair(edge.shape),
            column(0),
            column(1),
            column(2),
            anywhere,
            anywhere,
        ],
        out_specs=[
            column(0),
            column(0),
            per_pair((HEADS, n_small, SPAD, SPAD)),
            per_pair((HEADS, n_large, LPAD, LPAD)),
            anywhere,
            anywhere,
        ],
        out_shape=[
            jax.ShapeDtypeStruct((rows, width), BF16),
            jax.ShapeDtypeStruct((rows, width), F32),
            jax.ShapeDtypeStruct((HEADS, n_small, SPAD, SPAD), BF16),
            jax.ShapeDtypeStruct((HEADS, n_large, LPAD, LPAD), BF16),
        ]
        + [jax.ShapeDtypeStruct(w, BF16) for w in wholes],
        scratch_shapes=[
            pltpu.VMEM((24, L_WIDTH), F32),
            pltpu.VMEM((16, S_WIDTH), F32),
            pltpu.VMEM((LPAD, 640), F32),
            pltpu.VMEM((SPAD, 256), F32),
            sems((2, Gather.n_sems)),
            sems((2, Gather.n_sems)),
            sems((2,)),
        ],
        compiler_params=params(collective),
        cost_estimate=pl.CostEstimate(
            flops=20 * 10**9, bytes_accessed=20 * 10**6, transcendentals=7 * 10**6
        ),
    )(large_seq, small_seq, edge, qkv, qkv, qkv, *shares)
    return made[:4], [w.reshape(-1, w.shape[-1]) for w in made[4:]]


def run_attend_back(qkv, dattended, out_wide, probs_small, probs_large, n_small, n_large, grads, collective):
    rows, width = dattended.shape
    pairs = HEADS // 2

    def column(which):
        return pl.BlockSpec((rows, LANES), lambda i: (0, which * pairs + i))

    def per_pair(shape):
        tail = (0,) * (len(shape) - 1)
        return pl.BlockSpec((2,) + shape[1:], lambda i: (i,) + tail)

    grad = jax.ShapeDtypeStruct((rows, width), BF16)
    anywhere = pl.BlockSpec(memory_space=pl.ANY)
    inside = pl.BlockSpec(memory_space=pltpu.VMEM)
    shares = [(g.shape[0] // 16, g.shape[1]) for g in grads]
    sems = pltpu.SemaphoreType.DMA
    return pl.pallas_call(
        functools.partial(attend_back_kernel, n_small, n_large),
        grid=(pairs,),
        in_specs=[
            column(0),
            column(1),
            column(2),
            column(0),
            column(0),
            per_pair(probs_small.shape),
            per_pair(probs_large.shape),
            anywhere,
            anywhere,
        ],
        out_specs=[
            column(0),
            column(0),
            column(0),
            per_pair((HEADS, 2, L_WIDTH)),
            per_pair((HEADS, 2, S_WIDTH)),
            inside,
            inside,
        ],
        out_shape=[
            grad,
            grad,
            grad,
            jax.ShapeDtypeStruct((HEADS, 2, L_WIDTH), F32),
            jax.ShapeDtypeStruct((HEADS, 2, S_WIDTH), F32),
        ]
        + [jax.ShapeDtypeStruct(s, F32) for s in shares],
        scratch_shapes=[
            pltpu.VMEM((24, L_WIDTH), F32),
            pltpu.VMEM((16, S_WIDTH), F32),
            pltpu.VMEM((SPAD, 384), F32),
            pltpu.VMEM((LPAD, 768), F32),
        ]
        + Reduce.scratch(*shares[0])
        + Reduce.scratch(*shares[1])
        + [sems((2, Reduce.n_sems)), sems((2, Reduce.n_sems)), sems((2, ZS))],
        compiler_params=params(collective),
        cost_estimate=pl.CostEstimate(
            flops=30 * 10**9, bytes_accessed=24 * 10**6, transcendentals=0
        ),
    )(
        qkv,
        qkv,
        qkv,
        dattended,
        out_wide,
        probs_small,
        probs_large,
        *[g.reshape((ZS, 2, 2) + s) for g, s in zip(grads, shares)],
    )


def run_feed(x, attended, cot, w_mid, w_down, vectors, up_bias, n_small):
    rows, width = x.shape
    size = chunk_rows(rows)
    hidden = w_down.shape[0]
    tiles = hidden // width
    block = pl.BlockSpec((size, width), lambda i: (i, 0))
    anywhere = pl.BlockSpec(memory_space=pl.ANY)
    return pl.pallas_call(
        functools.partial(feed_kernel, n_small, tiles),
        grid=(rows // size,),
        in_specs=[
            block,
            block,
            block,
            held(w_mid.shape),
            held(w_down.shape),
            held(vectors.shape),
            held(up_bias.shape),
        ],
        out_specs=[
            block,
            block,
            block,
            resident((16, width)),
            anywhere,
            anywhere,
        ],
        out_shape=[
            jax.ShapeDtypeStruct((rows, width), BF16),
            jax.ShapeDtypeStruct((rows, width), F32),
            jax.ShapeDtypeStruct((rows, width), BF16),
            jax.ShapeDtypeStruct((16, width), F32),
            jax.ShapeDtypeStruct((width, width + hidden), BF16),
            jax.ShapeDtypeStruct((hidden, width), BF16),
        ],
        scratch_shapes=[
            pltpu.VMEM((size, hidden), BF16),
            pltpu.VMEM((size, hidden), BF16),
            pltpu.VMEM((width, width), F32),
            pltpu.VMEM((width, hidden), F32),
            pltpu.VMEM((hidden, width), F32),
            pltpu.VMEM((2, width // 4, width), BF16),
            pltpu.SemaphoreType.DMA((2,)),
        ],
        compiler_params=params(),
        cost_estimate=pl.CostEstimate(
            flops=6 * rows * width * (width + 2 * hidden),
            bytes_accessed=40 * 10**6,
            transcendentals=2 * rows * hidden,
        ),
    )(x, attended, cot, w_mid, w_down, vectors, up_bias)


def run_input(x, dquery, dkey, dvalue, dresidual, gain, bias, weight):
    rows, width = x.shape
    size = chunk_rows(rows)
    block = pl.BlockSpec((size, width), lambda i: (i, 0))
    return pl.pallas_call(
        input_kernel,
        grid=(rows // size,),
        in_specs=[
            block,
            block,
            block,
            block,
            block,
            held((1, width)),
            held((1, width)),
            held(weight.shape),
        ],
        out_specs=[block, resident((8, width)), resident(weight.shape)],
        out_shape=[
            jax.ShapeDtypeStruct((rows, width), BF16),
            jax.ShapeDtypeStruct((8, width), F32),
            jax.ShapeDtypeStruct(weight.shape, BF16),
        ],
        scratch_shapes=[pltpu.VMEM(weight.shape, F32)],
        compiler_params=params(),
        cost_estimate=pl.CostEstimate(
            flops=12 * rows * width * width, bytes_accessed=20 * 10**6, transcendentals=0
        ),
    )(x, dquery, dkey, dvalue, dresidual, gain, bias, weight)


def shifted(array, axis, by):
    count = lax.axis_size(axis)
    return lax.ppermute(array, axis, [(i, (i + by) % count) for i in range(count)])


def layer_norm(values, gain, bias):
    center = values - jnp.mean(values, axis=-1, keepdims=True)
    spread = jnp.mean(center * center, axis=-1, keepdims=True)
    return center * lax.rsqrt(spread + EPSILON) * gain + bias


def matmul(left, right):
    return jnp.dot(left, right, preferred_element_type=jnp.float32)


def position_bias(table, places, length, grid):
    heads = table.shape[0]
    span = 2 * LGRID - 1
    total_rel = table.shape[1]
    queries_count = places.shape[0]
    grid_table = table[:, : span * span].reshape(heads, span, span)
    patch = places - 1
    query_row = patch // grid
    query_col = patch % grid
    steps_all = jnp.arange(span, dtype=jnp.int32)
    cells = jnp.arange(grid, dtype=jnp.int32)
    row_hot = (
        steps_all[None, :, None] == query_row[:, None, None] - cells[None, None, :] + LGRID - 1
    ).astype(jnp.float32)
    col_hot = (
        steps_all[None, :, None] == query_col[:, None, None] - cells[None, None, :] + LGRID - 1
    ).astype(jnp.float32)
    partial_bias = jnp.einsum("hab,qbc->hqac", grid_table, col_hot, precision=lax.Precision.HIGHEST)
    patches = jnp.einsum(
        "qar,hqac->hqrc", row_hot, partial_bias, precision=lax.Precision.HIGHEST
    ).reshape(heads, queries_count, grid * grid)
    rest = length - 1 - grid * grid
    class_key = jnp.broadcast_to(table[:, total_rel - 2][:, None, None], (heads, queries_count, 1))
    patch_rows = jnp.concatenate(
        [class_key, patches, jnp.zeros((heads, queries_count, rest), jnp.float32)], axis=2
    )
    class_row = jnp.concatenate(
        [
            table[:, total_rel - 1][:, None],
            jnp.broadcast_to(table[:, total_rel - 3][:, None], (heads, grid * grid)),
            jnp.zeros((heads, rest), jnp.float32),
        ],
        axis=1,
    )
    is_class = (places == 0)[None, :, None]
    return jnp.where(is_class, class_row[:, None, :], patch_rows)


def to_heads(block, heads):
    groups, rows, width = block.shape
    return block.reshape(groups, rows, heads, width // heads)


def block_scores(query, key, query_rows, key_rows, length, bias_full):
    size = query.shape[-1] // HEADS
    raw = jnp.einsum(
        "gqhd,gkhd->ghqk",
        to_heads(query, HEADS),
        to_heads(key, HEADS),
        preferred_element_type=jnp.float32,
    )
    key_place = key_rows % length
    select = (key_place[:, None] == jnp.arange(length, dtype=jnp.int32)[None, :]).astype(
        jnp.float32
    )
    bias_block = jnp.einsum("hql,kl->hqk", bias_full, select, precision=lax.Precision.HIGHEST)
    allowed = (query_rows // length)[:, None] == (key_rows // length)[None, :]
    scores = raw * float(size) ** (-0.5) + bias_block[None]
    return (scores, allowed, select)


def key_rows_of(source, count_keys):
    return source * count_keys + jnp.arange(count_keys, dtype=jnp.int32)


def allowed_mask(allowed, key_rows, length, grid):
    return allowed & (key_rows % length < grid * grid + 1)[None, :]


def absorb_one(state, query, key, value, query_rows, key_rows, info):
    length, grid, bias_full = info
    maximum, total, accum = state
    scores, allowed, select = block_scores(query, key, query_rows, key_rows, length, bias_full)
    allowed = allowed_mask(allowed, key_rows, length, grid)
    masked = jnp.where(allowed[None, None], scores, NEGATIVE)
    newmax = jnp.maximum(maximum, jnp.max(masked, axis=-1))
    weights = jnp.where(allowed[None, None], jnp.exp(scores - newmax[..., None]), 0.0)
    factor = jnp.exp(maximum - newmax)
    total = total * factor + jnp.sum(weights, axis=-1)
    accum = accum * factor[..., None] + jnp.einsum(
        "ghqk,gkhd->ghqd",
        weights.astype(jnp.bfloat16),
        to_heads(value, HEADS),
        preferred_element_type=jnp.float32,
    )
    return (newmax, total, accum)


def absorb_cycle(states, queries, moving, members, query_rows, source, info):
    states = list(states)
    for which, offset, rows in members:
        key = moving[0][:, offset : offset + rows]
        value = moving[1][:, offset : offset + rows]
        states[which] = absorb_one(
            states[which],
            queries[which],
            key,
            value,
            query_rows[which],
            key_rows_of(source, rows),
            info[which],
        )
    return tuple(states)


def pass_forward(moving):
    return shifted((moving[0], moving[1]), "seq", 1)


def cycle_forward(queries, cycle_pair, members, query_rows, info):
    position = lax.axis_index("seq")
    count = lax.axis_size("seq")
    states = []
    for which in range(2):
        groups, rows, width = queries[which].shape
        states.append(
            (
                jnp.full((groups, HEADS, rows), NEGATIVE, jnp.float32),
                jnp.zeros((groups, HEADS, rows), jnp.float32),
                jnp.zeros((groups, HEADS, rows, width // HEADS), jnp.float32),
            )
        )
    states = absorb_cycle(tuple(states), queries, cycle_pair, members, query_rows, position, info)

    def turn(step, carry):
        held_states, moving = carry
        moving = tuple(pass_forward(moving))
        held_states = absorb_cycle(
            held_states, queries, moving, members, query_rows, (position - step) % count, info
        )
        return (held_states, moving)

    states, moving = lax.fori_loop(1, count, turn, (states, cycle_pair))
    attended = []
    logsums = []
    for which in range(2):
        maximum, total, accum = states[which]
        groups, heads_count, rows, size = accum.shape
        attended.append(
            jnp.transpose(accum / total[..., None], (0, 2, 1, 3)).reshape(
                groups, rows, heads_count * size
            )
        )
        logsums.append(maximum + jnp.log(total))
    return (tuple(attended), tuple(logsums))


def visit_one(query, dout, logsum, delta, key, value, query_rows, key_rows, info):
    length, grid, bias_full = info
    groups, count_keys, width = key.shape
    scale = float(width // HEADS) ** (-0.5)
    scores, allowed, select = block_scores(query, key, query_rows, key_rows, length, bias_full)
    allowed = allowed_mask(allowed, key_rows, length, grid)
    probs = jnp.where(allowed[None, None], jnp.exp(scores - logsum[..., None]), 0.0)
    dout_heads = to_heads(dout, HEADS)
    dprobs = jnp.einsum(
        "gqhd,gkhd->ghqk", dout_heads, to_heads(value, HEADS), preferred_element_type=jnp.float32
    )
    dscores = (probs * (dprobs - delta[..., None])).astype(jnp.bfloat16)
    dq_term = scale * jnp.einsum(
        "ghqk,gkhd->gqhd", dscores, to_heads(key, HEADS), preferred_element_type=jnp.float32
    )
    dkey_term = jnp.einsum(
        "ghqk,gqhd->gkhd", dscores, to_heads(query, HEADS), preferred_element_type=jnp.float32
    )
    dvalue_term = jnp.einsum(
        "ghqk,gqhd->gkhd",
        probs.astype(jnp.bfloat16),
        dout_heads,
        preferred_element_type=jnp.float32,
    )
    summed = jnp.sum(dscores.astype(jnp.float32), axis=0)
    bias_term = jnp.einsum("hqk,kl->hql", summed, select, precision=lax.Precision.HIGHEST)
    return (
        dq_term,
        scale * dkey_term.reshape(groups, count_keys, width),
        dvalue_term.reshape(groups, count_keys, width),
        bias_term,
    )


def visit_cycle(carry, queries, douts, logsums, deltas, moving, members, query_rows, source, info):
    dqueries, dpair, bias_grads = carry
    dqueries = list(dqueries)
    bias_grads = list(bias_grads)
    key_pieces = []
    value_pieces = []
    for which, offset, rows in members:
        key = moving[0][:, offset : offset + rows]
        value = moving[1][:, offset : offset + rows]
        dq_term, dk_term, dv_term, bias_term = visit_one(
            queries[which],
            douts[which],
            logsums[which],
            deltas[which],
            key,
            value,
            query_rows[which],
            key_rows_of(source, rows),
            info[which],
        )
        dqueries[which] = dqueries[which] + dq_term
        key_pieces.append(dk_term)
        value_pieces.append(dv_term)
        bias_grads[which] = bias_grads[which] + bias_term
    new_pair = (
        dpair[0] + jnp.concatenate(key_pieces, axis=1),
        dpair[1] + jnp.concatenate(value_pieces, axis=1),
    )
    return (tuple(dqueries), new_pair, tuple(bias_grads))


def send_grads(dpair):
    return tuple(shifted((dpair[0], dpair[1]), "seq", 1))


def cycle_backward(queries, douts, logsums, deltas, cycle_pair, members, query_rows, info, start):
    position = lax.axis_index("seq")
    count = lax.axis_size("seq")
    dpair = tuple((jnp.zeros(item.shape, jnp.float32) for item in cycle_pair))

    def turn(step, state):
        carry, moving = state
        carry = visit_cycle(
            carry,
            queries,
            douts,
            logsums,
            deltas,
            moving,
            members,
            query_rows,
            (position - step) % count,
            info,
        )
        moving = tuple(shifted((moving[0], moving[1]), "seq", 1))
        return ((carry[0], send_grads(carry[1]), carry[2]), moving)

    carry, moving = lax.fori_loop(0, count - 1, turn, ((start[0], dpair, start[1]), cycle_pair))
    carry = visit_cycle(
        carry,
        queries,
        douts,
        logsums,
        deltas,
        moving,
        members,
        query_rows,
        (position - count + 1) % count,
        info,
    )
    return (carry[0], send_grads(carry[1]), carry[2])


def general_device(
    small_in,
    large_in,
    small_cot,
    large_cot,
    first_gain,
    first_bias,
    query_weight,
    query_bias,
    key_weight,
    value_weight,
    value_bias,
    out_weight,
    out_bias,
    attend_scale,
    second_gain,
    second_bias,
    up_weight,
    up_bias,
    down_weight,
    down_bias,
    feed_scale,
    rel_table,
):
    groups, small_rows, width = small_in.shape
    large_rows = large_in.shape[1]
    all_rows = small_rows + large_rows
    position = lax.axis_index("seq")
    query_rows = (
        position * small_rows + jnp.arange(small_rows, dtype=jnp.int32),
        position * large_rows + jnp.arange(large_rows, dtype=jnp.int32),
    )
    small_places = query_rows[0] % SLEN
    large_places = query_rows[1] % LLEN

    def make_biases(table):
        return (
            position_bias(table, small_places, SLEN, SGRID),
            position_bias(table, large_places, LLEN, LGRID),
        )

    biases, bias_back = jax.vjp(make_biases, rel_table)
    info = ((SLEN, SGRID, biases[0]), (LLEN, LGRID, biases[1]))
    valid_rows = jnp.concatenate(
        [small_places < SGRID * SGRID + 1, large_places < LGRID * LGRID + 1]
    )
    valid_flat = jnp.broadcast_to(valid_rows[None, :], (groups, all_rows)).reshape(-1)
    w_query, w_key, w_value, w_out, w_up, w_down = (
        lax.all_gather(query_weight, "img", axis=0, tiled=True),
        lax.all_gather(key_weight, "img", axis=0, tiled=True),
        lax.all_gather(value_weight, "img", axis=0, tiled=True),
        lax.all_gather(out_weight, "img", axis=0, tiled=True),
        lax.all_gather(up_weight, "img", axis=0, tiled=True),
        lax.all_gather(down_weight, "img", axis=0, tiled=True),
    )

    def split(rows_array):
        shaped = rows_array.reshape(groups, all_rows, -1)
        return (shaped[:, :small_rows], shaped[:, small_rows:])

    inputs = jnp.concatenate([small_in, large_in], axis=1).astype(jnp.float32).reshape(-1, width)
    hidden = layer_norm(inputs, first_gain, first_bias).astype(jnp.bfloat16)
    query = (matmul(hidden, w_query) + query_bias).astype(jnp.bfloat16)
    key = matmul(hidden, w_key).astype(jnp.bfloat16)
    value = (matmul(hidden, w_value) + value_bias).astype(jnp.bfloat16)
    queries = split(query)
    cycle_pair = (key.reshape(groups, all_rows, width), value.reshape(groups, all_rows, width))
    members = ((0, 0, small_rows), (1, small_rows, large_rows))
    attended, logsums = cycle_forward(queries, cycle_pair, members, query_rows, info)
    mixed = (
        jnp.concatenate([attended[0], attended[1]], axis=1).reshape(-1, width).astype(jnp.bfloat16)
    )
    branch = matmul(mixed, w_out) + out_bias
    residual = inputs + attend_scale * branch
    hidden2 = layer_norm(residual, second_gain, second_bias).astype(jnp.bfloat16)
    upper = matmul(hidden2, w_up) + up_bias
    active = jax.nn.gelu(upper, approximate=False).astype(jnp.bfloat16)
    lower = matmul(active, w_down) + down_bias
    output = jnp.where(valid_flat[:, None], residual + feed_scale * lower, 0.0).astype(jnp.bfloat16)
    small_out, large_out = split(output)
    upstream = (
        jnp.concatenate([small_cot, large_cot], axis=1).astype(jnp.float32).reshape(-1, width)
    )
    upstream = upstream * valid_flat[:, None].astype(jnp.float32)
    grad_feed_scale = jnp.sum(upstream * lower, axis=0)
    dlower = (upstream * feed_scale).astype(jnp.bfloat16)
    grad_down_bias = jnp.sum(dlower.astype(jnp.float32), axis=0)
    grad_down = jnp.einsum("rf,rd->fd", active, dlower, preferred_element_type=jnp.float32)
    dactive = jnp.einsum("rd,fd->rf", dlower, w_down, preferred_element_type=jnp.float32)
    unused, gelu_back = jax.vjp(lambda inner: jax.nn.gelu(inner, approximate=False), upper)
    dupper = gelu_back(dactive)[0].astype(jnp.bfloat16)
    grad_up_bias = jnp.sum(dupper.astype(jnp.float32), axis=0)
    grad_up = jnp.einsum("rd,rf->df", hidden2, dupper, preferred_element_type=jnp.float32)
    dhidden2 = jnp.einsum("rf,df->rd", dupper, w_up, preferred_element_type=jnp.float32)
    unused, second_back = jax.vjp(layer_norm, residual, second_gain, second_bias)
    dres_part, grad_second_gain, grad_second_bias = second_back(dhidden2)
    dresidual = upstream + dres_part
    grad_attend_scale = jnp.sum(dresidual * branch, axis=0)
    dbranch = (dresidual * attend_scale).astype(jnp.bfloat16)
    grad_out_bias = jnp.sum(dbranch.astype(jnp.float32), axis=0)
    grad_out = jnp.einsum("rd,re->de", mixed, dbranch, preferred_element_type=jnp.float32)
    dmixed = jnp.einsum("re,de->rd", dbranch, w_out, preferred_element_type=jnp.float32).astype(
        jnp.bfloat16
    )
    held, held_sums = cycle_forward(queries, cycle_pair, members, query_rows, info)
    douts = split(dmixed)
    deltas = tuple(
        (
            jnp.einsum(
                "gqhd,gqhd->ghq",
                to_heads(douts[which].astype(jnp.float32), HEADS),
                to_heads(held[which], HEADS),
            )
            for which in range(2)
        )
    )
    dq_start = tuple(
        (jnp.zeros(to_heads(queries[which], HEADS).shape, jnp.float32) for which in range(2))
    )
    bias_start = tuple((jnp.zeros(item.shape, jnp.float32) for item in biases))
    dqueries, dpair, bias_grads = cycle_backward(
        queries,
        douts,
        held_sums,
        deltas,
        cycle_pair,
        members,
        query_rows,
        info,
        (dq_start, bias_start),
    )
    table_grad = bias_back(bias_grads)[0]
    dquery = jnp.concatenate(
        [
            dqueries[0].reshape(groups, small_rows, width),
            dqueries[1].reshape(groups, large_rows, width),
        ],
        axis=1,
    )
    dquery = dquery.reshape(-1, width).astype(jnp.bfloat16)
    dkey = dpair[0].reshape(-1, width).astype(jnp.bfloat16)
    dvalue = dpair[1].reshape(-1, width).astype(jnp.bfloat16)
    grad_query_bias = jnp.sum(dquery.astype(jnp.float32), axis=0)
    grad_value_bias = jnp.sum(dvalue.astype(jnp.float32), axis=0)
    grad_query = jnp.einsum("rd,re->de", hidden, dquery, preferred_element_type=jnp.float32)
    grad_key = jnp.einsum("rd,re->de", hidden, dkey, preferred_element_type=jnp.float32)
    grad_value = jnp.einsum("rd,re->de", hidden, dvalue, preferred_element_type=jnp.float32)
    dhidden = (
        jnp.einsum("re,de->rd", dquery, w_query, preferred_element_type=jnp.float32)
        + jnp.einsum("re,de->rd", dkey, w_key, preferred_element_type=jnp.float32)
        + jnp.einsum("re,de->rd", dvalue, w_value, preferred_element_type=jnp.float32)
    )
    unused, first_back = jax.vjp(layer_norm, inputs, first_gain, first_bias)
    dinput_part, grad_first_gain, grad_first_bias = first_back(dhidden)
    dinputs = (dresidual + dinput_part).astype(jnp.bfloat16)
    small_grad, large_grad = split(dinputs)
    shares = (
        lax.psum_scatter(grad_query, "img", scatter_dimension=0, tiled=True),
        lax.psum_scatter(grad_key, "img", scatter_dimension=0, tiled=True),
        lax.psum_scatter(grad_value, "img", scatter_dimension=0, tiled=True),
        lax.psum_scatter(grad_out, "img", scatter_dimension=0, tiled=True),
        lax.psum_scatter(grad_up, "img", scatter_dimension=0, tiled=True),
        lax.psum_scatter(grad_down, "img", scatter_dimension=0, tiled=True),
    )
    shares = lax.psum((shares[0], shares[1], shares[2], shares[3], shares[4], shares[5]), "seq")
    smalls = lax.psum(
        (
            grad_first_gain,
            grad_first_bias,
            grad_query_bias,
            grad_value_bias,
            grad_out_bias,
            grad_attend_scale,
            grad_second_gain,
            grad_second_bias,
            grad_up_bias,
            grad_down_bias,
            grad_feed_scale,
            table_grad,
        ),
        ("img", "seq"),
    )
    return (
        small_out,
        large_out,
        small_grad,
        large_grad,
        smalls[0],
        smalls[1],
        shares[0],
        smalls[2],
        shares[1],
        shares[2],
        smalls[3],
        shares[3],
        smalls[4],
        smalls[5],
        smalls[6],
        smalls[7],
        shares[4],
        smalls[8],
        shares[5],
        smalls[9],
        smalls[10],
        smalls[11],
    )


def exchange_large(part):
    position = lax.axis_index("seq")
    stay = lax.dynamic_index_in_dim(part, position, 0, keepdims=False)
    leave = lax.dynamic_index_in_dim(part, 1 - position, 0, keepdims=False)
    came = shifted(leave, "seq", 1)
    return jnp.where(
        position == 0,
        jnp.concatenate([stay, came], axis=0),
        jnp.concatenate([came, stay], axis=0),
    )


def return_large(whole, rows):
    position = lax.axis_index("seq")
    stay = lax.dynamic_slice_in_dim(whole, position * rows, rows, 0)
    leave = lax.dynamic_slice_in_dim(whole, (1 - position) * rows, rows, 0)
    came = shifted(leave, "seq", 1)
    return jnp.where(position == 0, jnp.stack([stay, came]), jnp.stack([came, stay]))


def image_device(
    small_in,
    large_in,
    small_cot,
    large_cot,
    first_gain,
    first_bias,
    query_weight,
    query_bias,
    key_weight,
    value_weight,
    value_bias,
    out_weight,
    out_bias,
    attend_scale,
    second_gain,
    second_bias,
    up_weight,
    up_bias,
    down_weight,
    down_bias,
    feed_scale,
    rel_table,
):
    groups, small_rows, width = small_in.shape
    large_rows = large_in.shape[1]
    n_small = groups * small_rows // SLEN
    n_large = 1
    small_part = n_small * SPAD

    def compact(small, large):
        return jnp.concatenate(
            [
                small.reshape(n_small, SLEN, width)[:, :SPAD].reshape(small_part, width),
                exchange_large(large)[:LPAD],
            ],
            axis=0,
        )

    def expand_small(rows):
        small = rows[:small_part].reshape(n_small, SPAD, width)
        small = jnp.pad(small, ((0, 0), (0, SLEN - SPAD), (0, 0)))
        return small.reshape(groups, small_rows, width)

    def expand_large(rows):
        large = jnp.pad(rows[small_part:], ((0, LLEN - LPAD), (0, 0)))
        return return_large(large, large_rows)

    qkv_share = jnp.concatenate([query_weight, key_weight, value_weight], axis=1)
    (w_qkv,) = run_gather([qkv_share], 1)
    mid_share = jnp.concatenate([out_weight, up_weight], axis=1)

    large_seq, small_seq, edge = table_sequences(rel_table)
    x = compact(small_in, large_in)
    cot = compact(small_cot, large_cot)
    gain, bias = first_gain[None], first_bias[None]
    qkv_bias = jnp.concatenate([query_bias, jnp.zeros_like(query_bias), value_bias])[None]
    vectors = jnp.stack(
        [out_bias, attend_scale, second_gain, second_bias, down_bias, feed_scale]
        + [feed_scale] * 2
    )

    qkv = run_qkv(x, gain, bias, w_qkv, qkv_bias)
    (attended, out_wide, probs_small, probs_large), (w_mid, w_down) = run_attend(
        qkv, large_seq, small_seq, edge, n_small, n_large, [mid_share, down_weight], 2
    )
    out, dresidual, dattended, vector_grads, g_mid, g_down = run_feed(
        x, attended, cot, w_mid, w_down, vectors, up_bias[None], n_small
    )
    small_out, large_out = expand_small(out), expand_large(out)

    dquery, dkey, dvalue, d_large, d_small, g_mid, g_down = run_attend_back(
        qkv, dattended, out_wide, probs_small, probs_large, n_small, n_large, [g_mid, g_down], 3
    )
    dinput, input_grads, g_qkv = run_input(
        x, dquery, dkey, dvalue, dresidual, gain, bias, w_qkv
    )
    small_grad, large_grad = expand_small(dinput), expand_large(dinput)
    heads = d_large.shape[0]
    (g_qkv,), (vector_grads, input_grads, d_large, d_small) = run_reduce(
        [g_qkv],
        [
            vector_grads,
            input_grads,
            d_large.reshape(2 * heads, L_WIDTH),
            d_small.reshape(2 * heads, S_WIDTH),
        ],
        4,
    )
    d_large = d_large.reshape(heads, 2, L_WIDTH)
    d_small = d_small.reshape(heads, 2, S_WIDTH)
    edge_grad = d_small[:, 0, S_WIDTH - 3 :]
    table_grad = table_from_sequences(d_large, d_small, edge_grad)
    return (
        small_out,
        large_out,
        small_grad,
        large_grad,
        input_grads[3],
        input_grads[4],
        g_qkv[:, :width],
        input_grads[0],
        g_qkv[:, width : 2 * width],
        g_qkv[:, 2 * width :],
        input_grads[2],
        g_mid[:, :width],
        vector_grads[0],
        vector_grads[1],
        vector_grads[2],
        vector_grads[3],
        g_mid[:, width:],
        vector_grads[8:12].reshape(-1),
        g_down,
        vector_grads[4],
        vector_grads[5],
        table_grad,
    )


def per_device(*args):
    groups, small_rows, unused = args[0].shape
    if lax.axis_size("seq") == 2 and groups == 2 and small_rows % SLEN == 0:
        return image_device(*args)
    return general_device(*args)


def solution(mesh):
    return jax.shard_map(
        per_device,
        mesh=mesh,
        in_specs=(
            P("img", "seq", None),
            P("img", "seq", None),
            P("img", "seq", None),
            P("img", "seq", None),
            P(),
            P(),
            P("img", None),
            P(),
            P("img", None),
            P("img", None),
            P(),
            P("img", None),
            P(),
            P(),
            P(),
            P(),
            P("img", None),
            P(),
            P("img", None),
            P(),
            P(),
            P(),
        ),
        out_specs=(
            P("img", "seq", None),
            P("img", "seq", None),
            P("img", "seq", None),
            P("img", "seq", None),
            P(),
            P(),
            P("img", None),
            P(),
            P("img", None),
            P("img", None),
            P(),
            P("img", None),
            P(),
            P(),
            P(),
            P(),
            P("img", None),
            P(),
            P("img", None),
            P(),
            P(),
            P(),
        ),
        check_vma=False,
    )
```

```python
import functools

import jax
import jax.numpy as jnp
from jax import lax
from jax.experimental import pallas as pl
from jax.experimental.pallas import tpu as pltpu
from jax.sharding import PartitionSpec as P

HEADS = 12
SGRID = 14
LGRID = 24
SLEN = 256
LLEN = 640
SPAD = 208
LPAD = 608
LANES = 128

NEGATIVE = -1e30
EPSILON = 1e-06
F32 = jnp.float32
BF16 = jnp.bfloat16
VMEM_BYTES = 62 << 20


def dot_nn(left, right):
    return lax.dot_general(left, right, (((1,), (0,)), ((), ())), preferred_element_type=F32)


def dot_nt(left, right):
    return lax.dot_general(left, right, (((1,), (1,)), ((), ())), preferred_element_type=F32)


def normalized(values):
    center = values - jnp.mean(values, axis=-1, keepdims=True)
    spread = jnp.mean(center * center, axis=-1, keepdims=True)
    scale = lax.rsqrt(spread + EPSILON)
    return center * scale, scale


def norm_back(grad, normal, scale):
    return scale * (
        grad
        - jnp.mean(grad, axis=-1, keepdims=True)
        - normal * jnp.mean(grad * normal, axis=-1, keepdims=True)
    )


def row_sum(values):
    return jnp.sum(values, axis=0, keepdims=True)


def iota(shape, axis):
    return lax.broadcasted_iota(jnp.int32, shape, axis)


L_WIDTH = 1280
S_WIDTH = 512


def table_sequences(table):
    heads = table.shape[0]
    span = 2 * LGRID - 1
    cells = table[:, : span * span].reshape(heads, span, span)

    def sequences(part, grid, width):
        rows = part.shape[1]
        low = part[:, :, :grid].reshape(heads, rows * grid)
        high = jnp.pad(part[:, :, grid:], ((0, 0), (0, 0), (0, 1))).reshape(heads, rows * grid)
        low = jnp.pad(low, ((0, 0), (0, width - rows * grid)))
        high = jnp.pad(high, ((0, 0), (grid, width - rows * grid - grid)))
        return jnp.stack([low, high], axis=1)

    off = LGRID - SGRID
    large = sequences(cells, LGRID, L_WIDTH)
    small = sequences(cells[:, off : span - off, off : span - off], SGRID, S_WIDTH)
    edge = jnp.broadcast_to(
        jnp.pad(table[:, span * span :], ((0, 0), (0, 5)))[:, :, None], (heads, 8, LANES)
    )
    return large, small, edge


def table_from_sequences(large, small, edge):
    heads = large.shape[0]
    span = 2 * LGRID - 1

    def cells(part, grid):
        rows = 2 * grid - 1
        low = part[:, 0, : rows * grid].reshape(heads, rows, grid)
        high = part[:, 1, grid : grid + rows * grid].reshape(heads, rows, grid)
        return jnp.concatenate([low, high[:, :, : grid - 1]], axis=2)

    off = LGRID - SGRID
    total = cells(large, LGRID) + jnp.pad(
        cells(small, SGRID), ((0, 0), (off, off), (off, off))
    )
    return jnp.concatenate([total.reshape(heads, span * span), edge], axis=1)


def takes_low(rows, width, grid, first):
    step = iota((rows, width), 1) % grid
    row = iota((rows, width), 0)
    low = step >= grid - 1 + first - row
    if first == 1:
        low = low | (row == 0)
    return low


def spread_sequences(seq, rows, width, grid, first):
    low = jnp.broadcast_to(seq[0:1, :], (rows, width))
    high = jnp.broadcast_to(seq[1:2, :], (rows, width))
    chosen = jnp.where(takes_low(rows, width, grid, first), low, high)
    return pltpu.roll(chosen, 1, 1, stride=1, stride_axis=0)


def gather_sequences(spread, rows, width, grid, first):
    row = iota((rows, width), 0) + 1
    for bit in (1, 2, 4, 8, 16):
        spread = jnp.where((row & bit) != 0, pltpu.roll(spread, width - bit, 1), spread)
    low = takes_low(rows, width, grid, first)
    return (
        row_sum(jnp.where(low, spread, 0.0)),
        row_sum(jnp.where(low, 0.0, spread)),
    )


def large_window(block):
    start = (LGRID - block) * LGRID
    return start // LANES, start % LANES


def small_window(block):
    start = (SGRID - 1 - block) * SGRID + SGRID - 1
    return start // LANES, start % LANES


def head_masks():
    lane = iota((1, LANES), 1)
    return (
        jnp.where(lane < LANES // 2, 1.0, 0.0).astype(BF16),
        jnp.where(lane < LANES // 2, 0.0, 1.0).astype(BF16),
    )


def transposed_biases(large_seq, small_seq, edge, wide, narrow, bias_large, bias_small):
    patch_q = edge[0:1, 0:1]
    patch_k = edge[1:2, 0:1]
    both = edge[2:3, 0:1]
    wide[...] = spread_sequences(large_seq, 24, L_WIDTH, LGRID, 1)
    lane = iota((24, LANES), 1)
    row = iota((24, LANES), 0)
    for block in range(LGRID + 1):
        at, turn = large_window(block)
        piece = wide[:, at * LANES : at * LANES + 768]
        if turn:
            piece = pltpu.roll(piece, 768 - turn, 1)
        piece = piece[:, :640]
        if block == 0:
            rest = jnp.where(iota((24, 640), 0) == 0, patch_k, piece)
        elif block == LGRID:
            rest = jnp.where(iota((24, 640), 0) == 0, piece, NEGATIVE)
        else:
            rest = piece
        first = jnp.where(lane == 0, patch_q, rest[:, :LANES])
        if block == 0:
            first = jnp.where((lane == 0) & (row == 0), both, first)
        if block == LGRID:
            first = jnp.where(row == 0, first, NEGATIVE)
        bias_large[pl.ds(block * 24, 24), 0:LANES] = first
        bias_large[pl.ds(block * 24, 24), LANES:640] = rest[:, LANES:]
    bias_large[pl.ds(600, 8), :] = jnp.full((8, 640), NEGATIVE, F32)
    narrow[...] = spread_sequences(small_seq, 16, S_WIDTH, SGRID, 0)
    for block in range(SGRID):
        at, turn = small_window(block)
        piece = narrow[:, at * LANES : at * LANES + 384]
        if turn:
            piece = pltpu.roll(piece, 384 - turn, 1)
        bias_small[pl.ds(1 + SGRID * block, SGRID), :] = piece[:SGRID, :256]
    whole = bias_small[...]
    lane = iota((SPAD, 256), 1)
    row = iota((SPAD, 256), 0)
    whole = jnp.where(lane == 0, patch_q, whole)
    whole = jnp.where(row == 0, patch_k, whole)
    whole = jnp.where((lane == 0) & (row == 0), both, whole)
    bias_small[...] = jnp.where(row > SGRID * SGRID, NEGATIVE, whole)


MESH = pl.DeviceIdType.MESH
ZS = 4


def place():
    img = lax.axis_index("img")
    return img // 4, (img // 2) % 2, img % 2, lax.axis_index("seq")


def device(z, x, c, y):
    return ((z * 2 + x) * 2 + c, y)


def z_peer(z, hop):
    low = (z % 2) * (1 - 2 * (hop % 2)) + hop % 2
    high = (z // 2) * (1 - 2 * (hop // 2)) + hop // 2
    return high * 2 + low


def greet():
    z, x, c, y = place()
    barrier = pltpu.get_barrier_semaphore()
    peers = [device(z_peer(z, hop), x, c, y) for hop in range(1, ZS)]
    peers += [device(z, 1 - x, c, y), device(z, x, c, 1 - y), device(z, x, 1 - c, y)]
    for peer in peers:
        pl.semaphore_signal(barrier, inc=1, device_id=peer, device_id_type=MESH)
    pl.semaphore_wait(barrier, len(peers))


def half_of(width, y):
    return pl.ds(pl.multiple_of(y * (width // 2), 128), width // 2)


class Gather:
    n_sems = 3 + 4 + 4 + 4 + 4

    def __init__(self, share, whole, send, recv, own):
        self.share, self.whole, self.send, self.recv, self.own = share, whole, send, recv, own
        self.width = share.shape[1]
        self.at = place()

    def copy(self, source, target, index, peer):
        return pltpu.make_async_remote_copy(
            src_ref=source,
            dst_ref=target,
            send_sem=self.send.at[index],
            recv_sem=self.recv.at[index],
            device_id=peer,
            device_id_type=MESH,
        )

    def along_z(self, hop):
        z, x, c, y = self.at
        cols = half_of(self.width, y)
        return self.copy(
            self.share.at[:, cols],
            self.whole.at[z, x, c, :, cols],
            hop - 1,
            device(z_peer(z, hop), x, c, y),
        )

    def across(self, hop, axis):
        z, x, c, y = self.at
        cols = half_of(self.width, y)
        source_z = z_peer(z, hop)
        source = self.share.at[:, cols] if hop == 0 else self.whole.at[source_z, x, c, :, cols]
        peer = device(z, 1 - x, c, y) if axis == 0 else device(z, x, c, 1 - y)
        return self.copy(source, self.whole.at[source_z, x, c, :, cols], 3 + 4 * axis + hop, peer)

    def onward(self, hop):
        z, x, c, y = self.at
        source_z = z_peer(z, hop)
        even = 1 if hop == 0 else 1 - source_z % 2
        side = x + even * (1 - 2 * x)
        cols = half_of(self.width, y + (1 - even) * (1 - 2 * y))
        block = self.whole.at[source_z, side, c, :, cols]
        peer = device(z, x + (1 - even) * (1 - 2 * x), c, y + even * (1 - 2 * y))
        return self.copy(block, block, 11 + hop, peer)

    def to_core(self, hop):
        z, x, c, y = self.at
        block = self.whole.at[z_peer(z, hop), :, c]
        return self.copy(block, block, 15 + hop, device(z, x, 1 - c, y))

    def keep_own(self):
        z, x, c, y = self.at
        return pltpu.make_async_copy(self.share, self.whole.at[z, x, c], self.own)

    def begin(self):
        self.keep_own().start()
        self.across(0, 0).start()
        for hop in range(1, ZS):
            self.along_z(hop).start()

    def spread(self):
        for hop in range(1, ZS):
            self.along_z(hop).wait_recv()
            for axis in range(2):
                self.across(hop, axis).start()

    def relay(self):
        for hop in range(ZS):
            for axis in range(2 if hop else 1):
                self.across(hop, axis).wait_recv()
            self.onward(hop).start()

    def share_cores(self):
        self.keep_own().wait()
        for hop in range(ZS):
            self.onward(hop).wait_recv()
            self.to_core(hop).start()

    def finish(self):
        for hop in range(ZS):
            self.to_core(hop).wait()
            self.onward(hop).wait_send()
            for axis in range(2 if hop else 1):
                self.across(hop, axis).wait_send()
        for hop in range(1, ZS):
            self.along_z(hop).wait_send()


def gather_kernel(count, *refs):
    shares, wholes = refs[:count], refs[count : 2 * count]
    send, recv, own = refs[2 * count :]
    greet()
    jobs = [
        Gather(shares[i], wholes[i], send.at[i], recv.at[i], own.at[i]) for i in range(count)
    ]
    for stage in ("begin", "spread", "relay", "share_cores", "finish"):
        for job in jobs:
            getattr(job, stage)()


def run_gather(shares, collective):
    count = len(shares)
    anywhere = pl.BlockSpec(memory_space=pl.ANY)
    sems = pltpu.SemaphoreType.DMA
    wholes = pl.pallas_call(
        functools.partial(gather_kernel, count),
        in_specs=[anywhere] * count,
        out_specs=[anywhere] * count,
        out_shape=[jax.ShapeDtypeStruct((ZS, 2, 2) + s.shape, s.dtype) for s in shares],
        scratch_shapes=[
            sems((count, Gather.n_sems)),
            sems((count, Gather.n_sems)),
            sems((count,)),
        ],
        compiler_params=pltpu.CompilerParams(collective_id=collective, has_side_effects=True),
    )(*shares)
    return [w.reshape(-1, w.shape[-1]) for w in wholes]


def add_rows(target, source, shape):
    rows, cols = shape

    def strip(i, unused):
        at = pl.ds(pl.multiple_of(i * 16, 16), 16)
        target[at, :] = (target[at, :].astype(F32) + source[at, :].astype(F32)).astype(BF16)
        return unused

    lax.fori_loop(0, rows // 16, strip, 0)


class Reduce:
    n_sems = 21
    n_scratch = 6

    def __init__(self, grad, out, held, core, first, second, last, edge, send, recv, own):
        self.grad, self.held, self.core = grad, held, core
        self.first, self.second, self.last, self.edge, self.out = first, second, last, edge, out
        self.send, self.recv, self.own = send, recv, own
        self.rows, self.width = out.shape
        self.at = place()
        self.mine = half_of(self.width, self.at[3])
        self.other = half_of(self.width, 1 - self.at[3])

    @staticmethod
    def scratch(rows, width):
        half = width // 2
        return [
            pltpu.VMEM((ZS, 2, rows, width), BF16),
            pltpu.VMEM((ZS, 2, rows, width), BF16),
            pltpu.VMEM((ZS, 2, rows, half), BF16),
            pltpu.VMEM((ZS, rows, half), BF16),
            pltpu.VMEM((ZS, rows, half), BF16),
            pltpu.VMEM((2, rows, half), BF16),
        ]

    def copy(self, source, target, index, peer):
        return pltpu.make_async_remote_copy(
            src_ref=source,
            dst_ref=target,
            send_sem=self.send.at[index],
            recv_sem=self.recv.at[index],
            device_id=peer,
            device_id_type=MESH,
        )

    def load(self, s):
        return pltpu.make_async_copy(
            self.grad.at[s, :, self.at[2]], self.held.at[s], self.own.at[s]
        )

    def between_cores(self, s):
        z, x, c, y = self.at
        return self.copy(self.grad.at[s, :, 1 - c], self.core.at[s], s, device(z, x, 1 - c, y))

    def leg_one(self, s, i):
        z, x, c, y = self.at
        half = self.width // 2
        if s % 2 == 0:
            source = self.held.at[s, 1 - x, :, pl.ds(i * half, half)]
            peer = device(z, 1 - x, c, y)
        else:
            source = self.held.at[s, i, :, self.other]
            peer = device(z, x, c, 1 - y)
        return self.copy(source, self.first.at[s, i], 4 + 2 * s + i, peer)

    def leg_two(self, s):
        z, x, c, y = self.at
        if s % 2 == 0:
            source = self.held.at[s, x, :, self.other]
            peer = device(z, x, c, 1 - y)
        else:
            source = self.held.at[s, 1 - x, :, self.mine]
            peer = device(z, 1 - x, c, y)
        return self.copy(source, self.second.at[s], 12 + s, peer)

    def leg_three(self, hop):
        z, x, c, y = self.at
        target = z_peer(z, hop)
        source = self.held.at[target, x, :, self.mine]
        return self.copy(source, self.last.at[hop], 16 + hop, device(target, x, c, y))

    def leg_four(self):
        z, x, c, y = self.at
        return self.copy(self.edge.at[0], self.edge.at[1], 20, device(z, x, c, 1 - y))

    def begin(self):
        for s in range(ZS):
            self.between_cores(s).start()
            self.load(s).start()

    def one(self):
        for s in range(ZS):
            self.load(s).wait()
            self.between_cores(s).wait_recv()
            for i in range(2):
                add_rows(self.held.at[s, i], self.core.at[s, i], (self.rows, self.width))
            for i in range(2):
                self.leg_one(s, i).start()

    def two(self):
        x = self.at[1]
        half = self.width // 2
        for s in range(ZS):
            for i in range(2):
                self.leg_one(s, i).wait_recv()
                if s % 2 == 0:
                    target = self.held.at[s, x, :, pl.ds(i * half, half)]
                else:
                    target = self.held.at[s, i, :, self.mine]
                add_rows(target, self.first.at[s, i], (self.rows, half))
            self.leg_two(s).start()

    def three(self):
        x = self.at[1]
        for s in range(ZS):
            self.leg_two(s).wait_recv()
            target = self.held.at[s, x, :, self.mine]
            add_rows(target, self.second.at[s], (self.rows, self.width // 2))
        for hop in range(1, ZS):
            self.leg_three(hop).start()

    def four(self):
        z, x, c, y = self.at
        for hop in range(1, ZS):
            self.leg_three(hop).wait_recv()
        own = self.held.at[z, x, :, self.mine]
        last, edge = self.last, self.edge

        def strip(i, unused):
            at = pl.ds(pl.multiple_of(i * 16, 16), 16)
            total = own[at, :].astype(F32)
            for hop in range(1, ZS):
                total += last[hop, at, :].astype(F32)
            edge[0, at, :] = total.astype(BF16)
            return unused

        lax.fori_loop(0, self.rows // 16, strip, 0)
        self.leg_four().start()
        self.out[:, self.mine] = edge[0].astype(F32)

    def finish(self):
        self.leg_four().wait()
        self.out[:, self.other] = self.edge[1].astype(F32)
        for s in range(ZS):
            self.between_cores(s).wait_send()
            for i in range(2):
                self.leg_one(s, i).wait_send()
            self.leg_two(s).wait_send()
        for hop in range(1, ZS):
            self.leg_three(hop).wait_send()


class Total:
    n_steps = 5

    def __init__(self, part, out, leave, come, send, recv):
        self.part, self.out, self.leave, self.come = part, out, leave, come
        self.send, self.recv = send, recv
        self.at = place()

    @staticmethod
    def scratch(shape):
        return [pltpu.VMEM((Total.n_steps,) + shape, BF16)] * 2

    def copy(self, step):
        z, x, c, y = self.at
        peer = (
            device(z, x, 1 - c, y),
            device(z, 1 - x, c, y),
            device(z, x, c, 1 - y),
            device(z_peer(z, 1), x, c, y),
            device(z_peer(z, 2), x, c, y),
        )[step]
        return pltpu.make_async_remote_copy(
            src_ref=self.leave.at[step],
            dst_ref=self.come.at[step],
            send_sem=self.send.at[step],
            recv_sem=self.recv.at[step],
            device_id=peer,
            device_id_type=MESH,
        )

    def begin(self):
        self.leave[0] = self.part[...].astype(BF16)
        self.copy(0).start()

    def advance(self, step):
        self.copy(step).wait()
        total = self.leave[step].astype(F32) + self.come[step].astype(F32)
        if step + 1 < self.n_steps:
            self.leave[step + 1] = total.astype(BF16)
            self.copy(step + 1).start()
        else:
            self.out[...] = total


def reduce_kernel(n_grads, n_small, *refs):
    refs = list(refs)

    def take(count):
        taken = refs[:count]
        del refs[:count]
        return taken

    grads, parts = take(n_grads), take(n_small)
    outs, totals = take(n_grads), take(n_small)
    grad_scratch = [take(Reduce.n_scratch) for unused in grads]
    small_scratch = [take(2) for unused in parts]
    send, recv, own = take(3)
    small_send, small_recv = take(2) if n_small else (None, None)
    greet()
    jobs = [
        Reduce(grads[i], outs[i], *grad_scratch[i], send.at[i], recv.at[i], own.at[i])
        for i in range(n_grads)
    ]
    sums = [
        Total(parts[i], totals[i], *small_scratch[i], small_send.at[i], small_recv.at[i])
        for i in range(n_small)
    ]
    for item in jobs + sums:
        item.begin()
    for step, stage in enumerate(("one", "two", "three", "four", "finish")):
        for job in jobs:
            getattr(job, stage)()
        for item in sums:
            item.advance(step)


def run_reduce(grads, smalls, collective):
    anywhere = pl.BlockSpec(memory_space=pl.ANY)
    inside = pl.BlockSpec(memory_space=pltpu.VMEM)
    sems = pltpu.SemaphoreType.DMA
    count = len(grads)
    shares = [(g.shape[0] // 16, g.shape[1]) for g in grads]
    scratch = []
    for shape in shares:
        scratch += Reduce.scratch(*shape)
    for small in smalls:
        scratch += Total.scratch(small.shape)
    scratch += [
        sems((count, Reduce.n_sems)),
        sems((count, Reduce.n_sems)),
        sems((count, ZS)),
    ]
    if smalls:
        scratch += [sems((len(smalls), Total.n_steps))] * 2
    made = pl.pallas_call(
        functools.partial(reduce_kernel, count, len(smalls)),
        in_specs=[anywhere] * count + [inside] * len(smalls),
        out_specs=[inside] * (count + len(smalls)),
        out_shape=[jax.ShapeDtypeStruct(s, F32) for s in shares]
        + [jax.ShapeDtypeStruct(s.shape, F32) for s in smalls],
        scratch_shapes=scratch,
        compiler_params=pltpu.CompilerParams(
            collective_id=collective, has_side_effects=True, vmem_limit_bytes=62 << 20
        ),
    )(*[g.reshape(ZS, 2, 2, g.shape[0] // 16, g.shape[1]) for g in grads], *smalls)
    return made[:count], made[count:]


def attend_kernel(
    n_small,
    n_large,
    large_seq,
    small_seq,
    edge,
    query,
    key,
    value,
    mid_share,
    down_share,
    out,
    out_wide,
    probs_small,
    probs_large,
    mid_whole,
    down_whole,
    wide,
    narrow,
    bias_large,
    bias_small,
    send,
    recv,
    own,
):
    masks = head_masks()
    jobs = [
        Gather(mid_share, mid_whole, send.at[0], recv.at[0], own.at[0]),
        Gather(down_share, down_whole, send.at[1], recv.at[1], own.at[1]),
    ]

    @pl.when(pl.program_id(0) == 0)
    def _():
        greet()
        for job in jobs:
            job.begin()

    @pl.when(pl.program_id(0) == 0)
    def _():
        bias_small[...] = jnp.zeros_like(bias_small)

    members = [(i * SPAD, SPAD, bias_small, probs_small, i) for i in range(n_small)]
    members += [
        (n_small * SPAD + i * LPAD, LPAD, bias_large, probs_large, i) for i in range(n_large)
    ]
    halves = [[] for _ in members]
    for head in range(2):
        transposed_biases(
            large_seq[head], small_seq[head], edge[head], wide, narrow, bias_large, bias_small
        )
        for at, (start, count, bias, probs, which) in enumerate(members):
            rows = pl.ds(start, count)
            scores = dot_nt(key[rows, :], query[rows, :] * masks[head]) + bias[:, :count]
            top = jnp.max(scores, axis=0, keepdims=True)
            weights = jnp.exp(scores - top)
            total = jnp.sum(weights, axis=0, keepdims=True)
            prob = (weights * (1.0 / total)).astype(BF16)
            probs[head, which] = prob
            turned = value[rows, :].T
            halves[at].append(dot_nn(turned[head * 64 : head * 64 + 64, :], prob))
    for at, (start, count, bias, probs, which) in enumerate(members):
        both = jnp.concatenate(halves[at], axis=0).T
        out[pl.ds(start, count), :] = both.astype(BF16)
        out_wide[pl.ds(start, count), :] = both
    for stage, step in (("spread", 2), ("relay", 4), ("share_cores", 5), ("finish", 5)):

        @pl.when(pl.program_id(0) == step)
        def _():
            for job in jobs:
                getattr(job, stage)()


def attend_back_kernel(
    n_small,
    n_large,
    query,
    key,
    value,
    dout,
    out_wide,
    probs_small,
    probs_large,
    g_mid,
    g_down,
    dquery,
    dkey,
    dvalue,
    large_seq,
    small_seq,
    mid_out,
    down_out,
    wide,
    narrow,
    dsum_small,
    dscore_large,
    *scratch,
):
    masks = head_masks()
    send, recv, own = scratch[-3:]
    count = Reduce.n_scratch
    jobs = [
        Reduce(g_mid, mid_out, *scratch[:count], send.at[0], recv.at[0], own.at[0]),
        Reduce(g_down, down_out, *scratch[count : 2 * count], send.at[1], recv.at[1], own.at[1]),
    ]

    @pl.when(pl.program_id(0) == 0)
    def _():
        greet()
        for job in jobs:
            job.begin()
    lane = iota((1, LANES), 1)
    scale = float(64) ** (-0.5)
    members = [(i * SPAD, SPAD, probs_small, i) for i in range(n_small)]
    members += [(n_small * SPAD + i * LPAD, LPAD, probs_large, i) for i in range(n_large)]
    keep = []
    for head in range(2):
        spot = 64 * (1 - head)
        minus = jnp.where((lane == spot) | (lane == spot + 1), -1.0, 0.0).astype(BF16)
        mask32 = masks[head].astype(F32)
        for at, (start, count, probs, which) in enumerate(members):
            rows = pl.ds(start, count)
            grad = dout[rows, :]
            grad32 = grad.astype(F32) * mask32
            delta = jnp.sum(grad32 * out_wide[rows, :], axis=1, keepdims=True)
            coarse = delta.astype(BF16).astype(F32)
            fine = delta - coarse
            side = jnp.where(lane == spot, coarse, jnp.where(lane == spot + 1, fine, grad32))
            values = value[rows, :] * masks[head] + minus
            prob = probs[head, which]
            dscore = prob.astype(F32) * dot_nt(values, side.astype(BF16))
            if count == SPAD:
                if which == 0:
                    dsum_small[:, :SPAD] = dscore
                else:
                    dsum_small[:, :SPAD] += dscore
            elif which == 0:
                dscore_large[:, :LPAD] = dscore
            else:
                dscore_large[:, :LPAD] += dscore
            low = dscore.astype(BF16)
            turned = key[rows, :].T
            dq = dot_nn(turned[head * 64 : head * 64 + 64, :], low)
            dk = dot_nn(low, query[rows, :])
            dv = dot_nn(prob, grad)
            if head == 0:
                keep.append((dq, dk, dv))
            else:
                first = iota((count, LANES), 1) < 64
                dq0, dk0, dv0 = keep[at]
                dquery[rows, :] = (jnp.concatenate([dq0, dq], axis=0).T * scale).astype(BF16)
                dkey[rows, :] = jnp.where(first, dk0, dk).astype(BF16)
                dvalue[rows, :] = jnp.where(first, dv0, dv).astype(BF16)
        wide[...] = jnp.zeros_like(wide)
        dscore_large[:, LPAD:] = jnp.zeros((LPAD, 768 - LPAD), F32)
        edge_lane = iota((24, 768), 1)
        edge_row = iota((24, 768), 0)
        class_column = jnp.zeros((24, 768), F32)
        class_row = None
        for block in range(LGRID + 1):
            at, turn = large_window(block)
            piece = dscore_large[pl.ds(block * 24, 24), :]
            if block == 0:
                class_row = piece[0:1, :]
                piece = jnp.where(edge_row == 0, 0.0, piece)
            class_column = class_column + piece
            piece = jnp.where(edge_lane == 0, 0.0, piece)
            if turn:
                piece = pltpu.roll(piece, turn, 1)
            wide[:, at * LANES : at * LANES + 768] += piece
        low_sum, high_sum = gather_sequences(wide[...], 24, L_WIDTH, LGRID, 1)
        large_seq[head, 0:1, :] = low_sum
        large_seq[head, 1:2, :] = high_sum
        narrow[...] = jnp.zeros_like(narrow)
        dsum_small[:, SPAD:] = jnp.zeros((SPAD, 384 - SPAD), F32)
        small_lane = iota((SGRID, 384), 1)
        small_column = jnp.zeros((SGRID, 384), F32)
        for block in range(SGRID):
            at, turn = small_window(block)
            piece = dsum_small[pl.ds(1 + SGRID * block, SGRID), :]
            small_column = small_column + piece
            piece = jnp.where(small_lane == 0, 0.0, piece)
            piece = jnp.concatenate([piece, jnp.zeros((2, 384), F32)], axis=0)
            if turn:
                piece = pltpu.roll(piece, turn, 1)
            narrow[:, at * LANES : at * LANES + 384] += piece
        low_sum, high_sum = gather_sequences(narrow[...], 16, S_WIDTH, SGRID, 0)
        by_query = row_sum(class_column)[:, :LANES] + row_sum(small_column)[:, :LANES]
        both_rows = class_row + jnp.concatenate(
            [dsum_small[0:1, :], jnp.zeros((1, 384), F32)], axis=1
        )
        class_key = jnp.sum(
            jnp.where(iota((1, 768), 1) == 0, 0.0, both_rows), axis=1, keepdims=True
        )
        spot = iota((1, S_WIDTH), 1)
        low_sum = jnp.where(spot == S_WIDTH - 3, by_query[:, 0:1], low_sum)
        low_sum = jnp.where(spot == S_WIDTH - 2, class_key, low_sum)
        low_sum = jnp.where(spot == S_WIDTH - 1, both_rows[:, 0:1], low_sum)
        small_seq[head, 0:1, :] = low_sum
        small_seq[head, 1:2, :] = high_sum
    for stage, step in (("one", 1), ("two", 3), ("three", 4), ("four", 5), ("finish", 5)):

        @pl.when(pl.program_id(0) == step)
        def _():
            for job in jobs:
                getattr(job, stage)()


def qkv_kernel(x, gain, bias, weight, weight_bias, out):
    width = x.shape[1]
    normal, unused = normalized(x[...].astype(F32))
    hidden = (normal * gain[...] + bias[...]).astype(BF16)
    scale = float(width // HEADS) ** (-0.5)
    for part in range(3):
        cols = slice(part * width, (part + 1) * width)
        made = (dot_nn(hidden, weight[:, cols]) + weight_bias[:, cols]).astype(BF16)
        out[:, cols] = made * jnp.asarray(scale, BF16) if part == 0 else made


def gelu_pair(upper):
    normal_cdf = 0.5 * (1.0 + lax.erf(upper * (0.5**0.5)))
    density = jnp.exp(-0.5 * upper * upper) * 0.3989422804014327
    return upper * normal_cdf, normal_cdf + upper * density


def valid_rows(first, count, n_small):
    row = iota((count, 1), 0) + first
    in_small = row < n_small * SPAD
    small_ok = row % SPAD < SGRID * SGRID + 1
    large_ok = (row - n_small * SPAD) % LPAD < LGRID * LGRID + 1
    return jnp.where(in_small, small_ok.astype(F32), large_ok.astype(F32))


def feed_kernel(
    n_small,
    tiles,
    x,
    attended,
    cot,
    mid_hbm,
    down_hbm,
    vectors,
    up_bias,
    out,
    dresidual,
    dattended,
    vector_grads,
    g_mid,
    g_down,
    w_mid,
    w_down,
    active,
    slope,
    acc_out,
    acc_up,
    acc_down,
    sems,
):
    step = pl.program_id(0)
    count, width = x.shape
    w_out = w_mid.at[:, :width]
    w_up = w_mid.at[:, width:]
    tile = w_up.shape[1] // tiles

    final = pl.num_programs(0) - 1
    pieces = [(mid_hbm, w_mid, g_mid, (slice(None), slice(0, width)))]
    for t in range(tiles):
        cols = slice(width + t * tile, width + (t + 1) * tile)
        pieces.append((mid_hbm, w_mid, g_mid, (slice(None), cols)))
    for t in range(tiles):
        rows = slice(t * tile, (t + 1) * tile)
        pieces.append((down_hbm, w_down, g_down, (rows, slice(None))))

    def load(at):
        source, held, target, where = pieces[at]
        return pltpu.make_async_copy(source.at[where], held.at[where], sems.at[at])

    def store(at):
        source, held, target, where = pieces[at]
        return pltpu.make_async_copy(held.at[where], target.at[where], sems.at[at])

    @pl.when(step == 0)
    def _():
        for at in range(len(pieces)):
            load(at).start()
        acc_out[...] = jnp.zeros_like(acc_out)
        acc_up[...] = jnp.zeros_like(acc_up)
        acc_down[...] = jnp.zeros_like(acc_down)
        vector_grads[...] = jnp.zeros_like(vector_grads)
        load(0).wait()

    out_bias = vectors[0:1, :]
    attend_scale = vectors[1:2, :]
    second_gain = vectors[2:3, :]
    second_bias = vectors[3:4, :]
    down_bias = vectors[4:5, :]
    feed_scale = vectors[5:6, :]

    valid = valid_rows(step * count, count, n_small)
    mixed = attended[...]
    branch = dot_nn(mixed, w_out[...]) + out_bias
    residual = x[...].astype(F32) + attend_scale * branch
    normal, scale = normalized(residual)
    hidden = (normal * second_gain + second_bias).astype(BF16)

    @pl.when(step == 0)
    def _():
        for at in range(1, len(pieces)):
            load(at).wait()

    lower = jnp.zeros((count, width), F32)
    for t in range(tiles):
        cols = slice(t * tile, (t + 1) * tile)
        upper = dot_nn(hidden, w_up[:, cols]) + up_bias[:, cols]
        made, rate = gelu_pair(upper)
        made = made.astype(BF16)
        active[:, cols] = made
        slope[:, cols] = rate.astype(BF16)
        lower += dot_nn(made, w_down[cols, :])
    lower += down_bias
    out[...] = ((residual + feed_scale * lower) * valid).astype(BF16)
    upstream = cot[...].astype(F32) * valid
    vector_grads[5:6, :] += row_sum(upstream * lower)
    dlower = (upstream * feed_scale).astype(BF16)
    vector_grads[4:5, :] += row_sum(dlower.astype(F32))
    turned = hidden.T
    dhidden = jnp.zeros((count, width), F32)
    for t in range(tiles):
        cols = slice(t * tile, (t + 1) * tile)
        dupper = (dot_nt(dlower, w_down[cols, :]) * slope[:, cols].astype(F32)).astype(BF16)
        vector_grads[8 + t : 9 + t, :] += row_sum(dupper.astype(F32))
        acc_down[cols, :] += dot_nn(active[:, cols].T, dlower)
        acc_up[:, cols] += dot_nn(turned, dupper)
        dhidden += dot_nt(dupper, w_up[:, cols])

    @pl.when(step == final)
    def _():
        for t in range(tiles):
            cols = slice(t * tile, (t + 1) * tile)
            w_up[:, cols] = acc_up[:, cols].astype(BF16)
            store(1 + t).start()
            w_down[cols, :] = acc_down[cols, :].astype(BF16)
            store(1 + tiles + t).start()

    vector_grads[2:3, :] += row_sum(dhidden * normal)
    vector_grads[3:4, :] += row_sum(dhidden)
    dres = upstream + norm_back(dhidden * second_gain, normal, scale)
    dresidual[...] = dres
    vector_grads[1:2, :] += row_sum(dres * branch)
    dbranch = (dres * attend_scale).astype(BF16)
    vector_grads[0:1, :] += row_sum(dbranch.astype(F32))
    acc_out[...] += dot_nn(mixed.T, dbranch)
    dattended[...] = dot_nt(dbranch, w_out[...]).astype(BF16)

    @pl.when(step == final)
    def _():
        w_out[...] = acc_out[...].astype(BF16)
        store(0).start()
        for at in range(len(pieces)):
            store(at).wait()


def input_kernel(
    x, dquery, dkey, dvalue, dresidual, gain, bias, weight, out, vector_grads, grad, acc
):
    step = pl.program_id(0)
    width = x.shape[1]

    @pl.when(step == 0)
    def _():
        acc[...] = jnp.zeros_like(acc)
        vector_grads[...] = jnp.zeros_like(vector_grads)

    normal, scale = normalized(x[...].astype(F32))
    hidden = (normal * gain[...] + bias[...]).astype(BF16)
    turned = hidden.T
    dhidden = jnp.zeros(normal.shape, F32)
    for part, item in enumerate((dquery, dkey, dvalue)):
        cols = slice(part * width, (part + 1) * width)
        piece = item[...]
        dhidden += dot_nt(piece, weight[:, cols])
        acc[:, cols] += dot_nn(turned, piece)
        if part != 1:
            vector_grads[part : part + 1, :] += row_sum(piece.astype(F32))
    vector_grads[3:4, :] += row_sum(dhidden * normal)
    vector_grads[4:5, :] += row_sum(dhidden)
    out[...] = (dresidual[...] + norm_back(dhidden * gain[...], normal, scale)).astype(BF16)

    @pl.when(step == pl.num_programs(0) - 1)
    def _():
        grad[...] = acc[...].astype(BF16)


def chunk_rows(total):
    return max(size for size in range(16, 481, 16) if total % size == 0)


def params(collective=None):
    if collective is None:
        return pltpu.CompilerParams(vmem_limit_bytes=VMEM_BYTES)
    return pltpu.CompilerParams(
        vmem_limit_bytes=VMEM_BYTES, collective_id=collective, has_side_effects=True
    )


def held(shape):
    rank = len(shape)
    return pl.BlockSpec(shape, lambda i: (0,) * rank, pipeline_mode=pl.Buffered(1))


def resident(shape):
    rank = len(shape)
    return pl.BlockSpec(shape, lambda i: (0,) * rank)


def run_qkv(x, gain, bias, weight, weight_bias):
    rows, width = x.shape
    size = chunk_rows(rows)
    wide = weight.shape[1]
    return pl.pallas_call(
        qkv_kernel,
        grid=(rows // size,),
        in_specs=[
            pl.BlockSpec((size, width), lambda i: (i, 0)),
            held((1, width)),
            held((1, width)),
            held(weight.shape),
            held((1, wide)),
        ],
        out_specs=pl.BlockSpec((size, wide), lambda i: (i, 0)),
        out_shape=jax.ShapeDtypeStruct((rows, wide), BF16),
        compiler_params=params(),
        cost_estimate=pl.CostEstimate(
            flops=2 * rows * width * wide, bytes_accessed=rows * wide * 2, transcendentals=0
        ),
    )(x, gain, bias, weight, weight_bias)


def run_attend(qkv, large_seq, small_seq, edge, n_small, n_large, shares, collective):
    rows = qkv.shape[0]
    width = qkv.shape[1] // 3
    pairs = HEADS // 2

    def column(which):
        return pl.BlockSpec((rows, LANES), lambda i: (0, which * pairs + i))

    def per_pair(shape):
        tail = (0,) * (len(shape) - 1)
        return pl.BlockSpec((2,) + shape[1:], lambda i: (i,) + tail)

    anywhere = pl.BlockSpec(memory_space=pl.ANY)
    wholes = [(ZS, 2, 2) + s.shape for s in shares]
    sems = pltpu.SemaphoreType.DMA
    made = pl.pallas_call(
        functools.partial(attend_kernel, n_small, n_large),
        grid=(pairs,),
        in_specs=[
            per_pair(large_seq.shape),
            per_pair(small_seq.shape),
            per_pair(edge.shape),
            column(0),
            column(1),
            column(2),
            anywhere,
            anywhere,
        ],
        out_specs=[
            column(0),
            column(0),
            per_pair((HEADS, n_small, SPAD, SPAD)),
            per_pair((HEADS, n_large, LPAD, LPAD)),
            anywhere,
            anywhere,
        ],
        out_shape=[
            jax.ShapeDtypeStruct((rows, width), BF16),
            jax.ShapeDtypeStruct((rows, width), F32),
            jax.ShapeDtypeStruct((HEADS, n_small, SPAD, SPAD), BF16),
            jax.ShapeDtypeStruct((HEADS, n_large, LPAD, LPAD), BF16),
        ]
        + [jax.ShapeDtypeStruct(w, BF16) for w in wholes],
        scratch_shapes=[
            pltpu.VMEM((24, L_WIDTH), F32),
            pltpu.VMEM((16, S_WIDTH), F32),
            pltpu.VMEM((LPAD, 640), F32),
            pltpu.VMEM((SPAD, 256), F32),
            sems((2, Gather.n_sems)),
            sems((2, Gather.n_sems)),
            sems((2,)),
        ],
        compiler_params=params(collective),
        cost_estimate=pl.CostEstimate(
            flops=20 * 10**9, bytes_accessed=20 * 10**6, transcendentals=7 * 10**6
        ),
    )(large_seq, small_seq, edge, qkv, qkv, qkv, *shares)
    return made[:4], [w.reshape(-1, w.shape[-1]) for w in made[4:]]


def run_attend_back(qkv, dattended, out_wide, probs_small, probs_large, n_small, n_large, grads, collective):
    rows, width = dattended.shape
    pairs = HEADS // 2

    def column(which):
        return pl.BlockSpec((rows, LANES), lambda i: (0, which * pairs + i))

    def per_pair(shape):
        tail = (0,) * (len(shape) - 1)
        return pl.BlockSpec((2,) + shape[1:], lambda i: (i,) + tail)

    grad = jax.ShapeDtypeStruct((rows, width), BF16)
    anywhere = pl.BlockSpec(memory_space=pl.ANY)
    inside = pl.BlockSpec(memory_space=pltpu.VMEM)
    shares = [(g.shape[0] // 16, g.shape[1]) for g in grads]
    sems = pltpu.SemaphoreType.DMA
    return pl.pallas_call(
        functools.partial(attend_back_kernel, n_small, n_large),
        grid=(pairs,),
        in_specs=[
            column(0),
            column(1),
            column(2),
            column(0),
            column(0),
            per_pair(probs_small.shape),
            per_pair(probs_large.shape),
            anywhere,
            anywhere,
        ],
        out_specs=[
            column(0),
            column(0),
            column(0),
            per_pair((HEADS, 2, L_WIDTH)),
            per_pair((HEADS, 2, S_WIDTH)),
            inside,
            inside,
        ],
        out_shape=[
            grad,
            grad,
            grad,
            jax.ShapeDtypeStruct((HEADS, 2, L_WIDTH), F32),
            jax.ShapeDtypeStruct((HEADS, 2, S_WIDTH), F32),
        ]
        + [jax.ShapeDtypeStruct(s, F32) for s in shares],
        scratch_shapes=[
            pltpu.VMEM((24, L_WIDTH), F32),
            pltpu.VMEM((16, S_WIDTH), F32),
            pltpu.VMEM((SPAD, 384), F32),
            pltpu.VMEM((LPAD, 768), F32),
        ]
        + Reduce.scratch(*shares[0])
        + Reduce.scratch(*shares[1])
        + [sems((2, Reduce.n_sems)), sems((2, Reduce.n_sems)), sems((2, ZS))],
        compiler_params=params(collective),
        cost_estimate=pl.CostEstimate(
            flops=30 * 10**9, bytes_accessed=24 * 10**6, transcendentals=0
        ),
    )(
        qkv,
        qkv,
        qkv,
        dattended,
        out_wide,
        probs_small,
        probs_large,
        *[g.reshape((ZS, 2, 2) + s) for g, s in zip(grads, shares)],
    )


def run_feed(x, attended, cot, w_mid, w_down, vectors, up_bias, n_small):
    rows, width = x.shape
    size = chunk_rows(rows)
    hidden = w_down.shape[0]
    tiles = hidden // width
    block = pl.BlockSpec((size, width), lambda i: (i, 0))
    anywhere = pl.BlockSpec(memory_space=pl.ANY)
    return pl.pallas_call(
        functools.partial(feed_kernel, n_small, tiles),
        grid=(rows // size,),
        in_specs=[
            block,
            block,
            block,
            anywhere,
            anywhere,
            held(vectors.shape),
            held(up_bias.shape),
        ],
        out_specs=[
            block,
            block,
            block,
            resident((16, width)),
            anywhere,
            anywhere,
        ],
        out_shape=[
            jax.ShapeDtypeStruct((rows, width), BF16),
            jax.ShapeDtypeStruct((rows, width), F32),
            jax.ShapeDtypeStruct((rows, width), BF16),
            jax.ShapeDtypeStruct((16, width), F32),
            jax.ShapeDtypeStruct((width, width + hidden), BF16),
            jax.ShapeDtypeStruct((hidden, width), BF16),
        ],
        scratch_shapes=[
            pltpu.VMEM((width, width + hidden), BF16),
            pltpu.VMEM((hidden, width), BF16),
            pltpu.VMEM((size, hidden), BF16),
            pltpu.VMEM((size, hidden), BF16),
            pltpu.VMEM((width, width), F32),
            pltpu.VMEM((width, hidden), F32),
            pltpu.VMEM((hidden, width), F32),
            pltpu.SemaphoreType.DMA((1 + 2 * tiles,)),
        ],
        compiler_params=params(),
        cost_estimate=pl.CostEstimate(
            flops=6 * rows * width * (width + 2 * hidden),
            bytes_accessed=40 * 10**6,
            transcendentals=2 * rows * hidden,
        ),
    )(x, attended, cot, w_mid, w_down, vectors, up_bias)


def run_input(x, dquery, dkey, dvalue, dresidual, gain, bias, weight):
    rows, width = x.shape
    size = chunk_rows(rows)
    block = pl.BlockSpec((size, width), lambda i: (i, 0))
    return pl.pallas_call(
        input_kernel,
        grid=(rows // size,),
        in_specs=[
            block,
            block,
            block,
            block,
            block,
            held((1, width)),
            held((1, width)),
            held(weight.shape),
        ],
        out_specs=[block, resident((8, width)), resident(weight.shape)],
        out_shape=[
            jax.ShapeDtypeStruct((rows, width), BF16),
            jax.ShapeDtypeStruct((8, width), F32),
            jax.ShapeDtypeStruct(weight.shape, BF16),
        ],
        scratch_shapes=[pltpu.VMEM(weight.shape, F32)],
        compiler_params=params(),
        cost_estimate=pl.CostEstimate(
            flops=12 * rows * width * width, bytes_accessed=20 * 10**6, transcendentals=0
        ),
    )(x, dquery, dkey, dvalue, dresidual, gain, bias, weight)


def shifted(array, axis, by):
    count = lax.axis_size(axis)
    return lax.ppermute(array, axis, [(i, (i + by) % count) for i in range(count)])


def layer_norm(values, gain, bias):
    center = values - jnp.mean(values, axis=-1, keepdims=True)
    spread = jnp.mean(center * center, axis=-1, keepdims=True)
    return center * lax.rsqrt(spread + EPSILON) * gain + bias


def matmul(left, right):
    return jnp.dot(left, right, preferred_element_type=jnp.float32)


def position_bias(table, places, length, grid):
    heads = table.shape[0]
    span = 2 * LGRID - 1
    total_rel = table.shape[1]
    queries_count = places.shape[0]
    grid_table = table[:, : span * span].reshape(heads, span, span)
    patch = places - 1
    query_row = patch // grid
    query_col = patch % grid
    steps_all = jnp.arange(span, dtype=jnp.int32)
    cells = jnp.arange(grid, dtype=jnp.int32)
    row_hot = (
        steps_all[None, :, None] == query_row[:, None, None] - cells[None, None, :] + LGRID - 1
    ).astype(jnp.float32)
    col_hot = (
        steps_all[None, :, None] == query_col[:, None, None] - cells[None, None, :] + LGRID - 1
    ).astype(jnp.float32)
    partial_bias = jnp.einsum("hab,qbc->hqac", grid_table, col_hot, precision=lax.Precision.HIGHEST)
    patches = jnp.einsum(
        "qar,hqac->hqrc", row_hot, partial_bias, precision=lax.Precision.HIGHEST
    ).reshape(heads, queries_count, grid * grid)
    rest = length - 1 - grid * grid
    class_key = jnp.broadcast_to(table[:, total_rel - 2][:, None, None], (heads, queries_count, 1))
    patch_rows = jnp.concatenate(
        [class_key, patches, jnp.zeros((heads, queries_count, rest), jnp.float32)], axis=2
    )
    class_row = jnp.concatenate(
        [
            table[:, total_rel - 1][:, None],
            jnp.broadcast_to(table[:, total_rel - 3][:, None], (heads, grid * grid)),
            jnp.zeros((heads, rest), jnp.float32),
        ],
        axis=1,
    )
    is_class = (places == 0)[None, :, None]
    return jnp.where(is_class, class_row[:, None, :], patch_rows)


def to_heads(block, heads):
    groups, rows, width = block.shape
    return block.reshape(groups, rows, heads, width // heads)


def block_scores(query, key, query_rows, key_rows, length, bias_full):
    size = query.shape[-1] // HEADS
    raw = jnp.einsum(
        "gqhd,gkhd->ghqk",
        to_heads(query, HEADS),
        to_heads(key, HEADS),
        preferred_element_type=jnp.float32,
    )
    key_place = key_rows % length
    select = (key_place[:, None] == jnp.arange(length, dtype=jnp.int32)[None, :]).astype(
        jnp.float32
    )
    bias_block = jnp.einsum("hql,kl->hqk", bias_full, select, precision=lax.Precision.HIGHEST)
    allowed = (query_rows // length)[:, None] == (key_rows // length)[None, :]
    scores = raw * float(size) ** (-0.5) + bias_block[None]
    return (scores, allowed, select)


def key_rows_of(source, count_keys):
    return source * count_keys + jnp.arange(count_keys, dtype=jnp.int32)


def allowed_mask(allowed, key_rows, length, grid):
    return allowed & (key_rows % length < grid * grid + 1)[None, :]


def absorb_one(state, query, key, value, query_rows, key_rows, info):
    length, grid, bias_full = info
    maximum, total, accum = state
    scores, allowed, select = block_scores(query, key, query_rows, key_rows, length, bias_full)
    allowed = allowed_mask(allowed, key_rows, length, grid)
    masked = jnp.where(allowed[None, None], scores, NEGATIVE)
    newmax = jnp.maximum(maximum, jnp.max(masked, axis=-1))
    weights = jnp.where(allowed[None, None], jnp.exp(scores - newmax[..., None]), 0.0)
    factor = jnp.exp(maximum - newmax)
    total = total * factor + jnp.sum(weights, axis=-1)
    accum = accum * factor[..., None] + jnp.einsum(
        "ghqk,gkhd->ghqd",
        weights.astype(jnp.bfloat16),
        to_heads(value, HEADS),
        preferred_element_type=jnp.float32,
    )
    return (newmax, total, accum)


def absorb_cycle(states, queries, moving, members, query_rows, source, info):
    states = list(states)
    for which, offset, rows in members:
        key = moving[0][:, offset : offset + rows]
        value = moving[1][:, offset : offset + rows]
        states[which] = absorb_one(
            states[which],
            queries[which],
            key,
            value,
            query_rows[which],
            key_rows_of(source, rows),
            info[which],
        )
    return tuple(states)


def pass_forward(moving):
    return shifted((moving[0], moving[1]), "seq", 1)


def cycle_forward(queries, cycle_pair, members, query_rows, info):
    position = lax.axis_index("seq")
    count = lax.axis_size("seq")
    states = []
    for which in range(2):
        groups, rows, width = queries[which].shape
        states.append(
            (
                jnp.full((groups, HEADS, rows), NEGATIVE, jnp.float32),
                jnp.zeros((groups, HEADS, rows), jnp.float32),
                jnp.zeros((groups, HEADS, rows, width // HEADS), jnp.float32),
            )
        )
    states = absorb_cycle(tuple(states), queries, cycle_pair, members, query_rows, position, info)

    def turn(step, carry):
        held_states, moving = carry
        moving = tuple(pass_forward(moving))
        held_states = absorb_cycle(
            held_states, queries, moving, members, query_rows, (position - step) % count, info
        )
        return (held_states, moving)

    states, moving = lax.fori_loop(1, count, turn, (states, cycle_pair))
    attended = []
    logsums = []
    for which in range(2):
        maximum, total, accum = states[which]
        groups, heads_count, rows, size = accum.shape
        attended.append(
            jnp.transpose(accum / total[..., None], (0, 2, 1, 3)).reshape(
                groups, rows, heads_count * size
            )
        )
        logsums.append(maximum + jnp.log(total))
    return (tuple(attended), tuple(logsums))


def visit_one(query, dout, logsum, delta, key, value, query_rows, key_rows, info):
    length, grid, bias_full = info
    groups, count_keys, width = key.shape
    scale = float(width // HEADS) ** (-0.5)
    scores, allowed, select = block_scores(query, key, query_rows, key_rows, length, bias_full)
    allowed = allowed_mask(allowed, key_rows, length, grid)
    probs = jnp.where(allowed[None, None], jnp.exp(scores - logsum[..., None]), 0.0)
    dout_heads = to_heads(dout, HEADS)
    dprobs = jnp.einsum(
        "gqhd,gkhd->ghqk", dout_heads, to_heads(value, HEADS), preferred_element_type=jnp.float32
    )
    dscores = (probs * (dprobs - delta[..., None])).astype(jnp.bfloat16)
    dq_term = scale * jnp.einsum(
        "ghqk,gkhd->gqhd", dscores, to_heads(key, HEADS), preferred_element_type=jnp.float32
    )
    dkey_term = jnp.einsum(
        "ghqk,gqhd->gkhd", dscores, to_heads(query, HEADS), preferred_element_type=jnp.float32
    )
    dvalue_term = jnp.einsum(
        "ghqk,gqhd->gkhd",
        probs.astype(jnp.bfloat16),
        dout_heads,
        preferred_element_type=jnp.float32,
    )
    summed = jnp.sum(dscores.astype(jnp.float32), axis=0)
    bias_term = jnp.einsum("hqk,kl->hql", summed, select, precision=lax.Precision.HIGHEST)
    return (
        dq_term,
        scale * dkey_term.reshape(groups, count_keys, width),
        dvalue_term.reshape(groups, count_keys, width),
        bias_term,
    )


def visit_cycle(carry, queries, douts, logsums, deltas, moving, members, query_rows, source, info):
    dqueries, dpair, bias_grads = carry
    dqueries = list(dqueries)
    bias_grads = list(bias_grads)
    key_pieces = []
    value_pieces = []
    for which, offset, rows in members:
        key = moving[0][:, offset : offset + rows]
        value = moving[1][:, offset : offset + rows]
        dq_term, dk_term, dv_term, bias_term = visit_one(
            queries[which],
            douts[which],
            logsums[which],
            deltas[which],
            key,
            value,
            query_rows[which],
            key_rows_of(source, rows),
            info[which],
        )
        dqueries[which] = dqueries[which] + dq_term
        key_pieces.append(dk_term)
        value_pieces.append(dv_term)
        bias_grads[which] = bias_grads[which] + bias_term
    new_pair = (
        dpair[0] + jnp.concatenate(key_pieces, axis=1),
        dpair[1] + jnp.concatenate(value_pieces, axis=1),
    )
    return (tuple(dqueries), new_pair, tuple(bias_grads))


def send_grads(dpair):
    return tuple(shifted((dpair[0], dpair[1]), "seq", 1))


def cycle_backward(queries, douts, logsums, deltas, cycle_pair, members, query_rows, info, start):
    position = lax.axis_index("seq")
    count = lax.axis_size("seq")
    dpair = tuple((jnp.zeros(item.shape, jnp.float32) for item in cycle_pair))

    def turn(step, state):
        carry, moving = state
        carry = visit_cycle(
            carry,
            queries,
            douts,
            logsums,
            deltas,
            moving,
            members,
            query_rows,
            (position - step) % count,
            info,
        )
        moving = tuple(shifted((moving[0], moving[1]), "seq", 1))
        return ((carry[0], send_grads(carry[1]), carry[2]), moving)

    carry, moving = lax.fori_loop(0, count - 1, turn, ((start[0], dpair, start[1]), cycle_pair))
    carry = visit_cycle(
        carry,
        queries,
        douts,
        logsums,
        deltas,
        moving,
        members,
        query_rows,
        (position - count + 1) % count,
        info,
    )
    return (carry[0], send_grads(carry[1]), carry[2])


def general_device(
    small_in,
    large_in,
    small_cot,
    large_cot,
    first_gain,
    first_bias,
    query_weight,
    query_bias,
    key_weight,
    value_weight,
    value_bias,
    out_weight,
    out_bias,
    attend_scale,
    second_gain,
    second_bias,
    up_weight,
    up_bias,
    down_weight,
    down_bias,
    feed_scale,
    rel_table,
):
    groups, small_rows, width = small_in.shape
    large_rows = large_in.shape[1]
    all_rows = small_rows + large_rows
    position = lax.axis_index("seq")
    query_rows = (
        position * small_rows + jnp.arange(small_rows, dtype=jnp.int32),
        position * large_rows + jnp.arange(large_rows, dtype=jnp.int32),
    )
    small_places = query_rows[0] % SLEN
    large_places = query_rows[1] % LLEN

    def make_biases(table):
        return (
            position_bias(table, small_places, SLEN, SGRID),
            position_bias(table, large_places, LLEN, LGRID),
        )

    biases, bias_back = jax.vjp(make_biases, rel_table)
    info = ((SLEN, SGRID, biases[0]), (LLEN, LGRID, biases[1]))
    valid_rows = jnp.concatenate(
        [small_places < SGRID * SGRID + 1, large_places < LGRID * LGRID + 1]
    )
    valid_flat = jnp.broadcast_to(valid_rows[None, :], (groups, all_rows)).reshape(-1)
    w_query, w_key, w_value, w_out, w_up, w_down = (
        lax.all_gather(query_weight, "img", axis=0, tiled=True),
        lax.all_gather(key_weight, "img", axis=0, tiled=True),
        lax.all_gather(value_weight, "img", axis=0, tiled=True),
        lax.all_gather(out_weight, "img", axis=0, tiled=True),
        lax.all_gather(up_weight, "img", axis=0, tiled=True),
        lax.all_gather(down_weight, "img", axis=0, tiled=True),
    )

    def split(rows_array):
        shaped = rows_array.reshape(groups, all_rows, -1)
        return (shaped[:, :small_rows], shaped[:, small_rows:])

    inputs = jnp.concatenate([small_in, large_in], axis=1).astype(jnp.float32).reshape(-1, width)
    hidden = layer_norm(inputs, first_gain, first_bias).astype(jnp.bfloat16)
    query = (matmul(hidden, w_query) + query_bias).astype(jnp.bfloat16)
    key = matmul(hidden, w_key).astype(jnp.bfloat16)
    value = (matmul(hidden, w_value) + value_bias).astype(jnp.bfloat16)
    queries = split(query)
    cycle_pair = (key.reshape(groups, all_rows, width), value.reshape(groups, all_rows, width))
    members = ((0, 0, small_rows), (1, small_rows, large_rows))
    attended, logsums = cycle_forward(queries, cycle_pair, members, query_rows, info)
    mixed = (
        jnp.concatenate([attended[0], attended[1]], axis=1).reshape(-1, width).astype(jnp.bfloat16)
    )
    branch = matmul(mixed, w_out) + out_bias
    residual = inputs + attend_scale * branch
    hidden2 = layer_norm(residual, second_gain, second_bias).astype(jnp.bfloat16)
    upper = matmul(hidden2, w_up) + up_bias
    active = jax.nn.gelu(upper, approximate=False).astype(jnp.bfloat16)
    lower = matmul(active, w_down) + down_bias
    output = jnp.where(valid_flat[:, None], residual + feed_scale * lower, 0.0).astype(jnp.bfloat16)
    small_out, large_out = split(output)
    upstream = (
        jnp.concatenate([small_cot, large_cot], axis=1).astype(jnp.float32).reshape(-1, width)
    )
    upstream = upstream * valid_flat[:, None].astype(jnp.float32)
    grad_feed_scale = jnp.sum(upstream * lower, axis=0)
    dlower = (upstream * feed_scale).astype(jnp.bfloat16)
    grad_down_bias = jnp.sum(dlower.astype(jnp.float32), axis=0)
    grad_down = jnp.einsum("rf,rd->fd", active, dlower, preferred_element_type=jnp.float32)
    dactive = jnp.einsum("rd,fd->rf", dlower, w_down, preferred_element_type=jnp.float32)
    unused, gelu_back = jax.vjp(lambda inner: jax.nn.gelu(inner, approximate=False), upper)
    dupper = gelu_back(dactive)[0].astype(jnp.bfloat16)
    grad_up_bias = jnp.sum(dupper.astype(jnp.float32), axis=0)
    grad_up = jnp.einsum("rd,rf->df", hidden2, dupper, preferred_element_type=jnp.float32)
    dhidden2 = jnp.einsum("rf,df->rd", dupper, w_up, preferred_element_type=jnp.float32)
    unused, second_back = jax.vjp(layer_norm, residual, second_gain, second_bias)
    dres_part, grad_second_gain, grad_second_bias = second_back(dhidden2)
    dresidual = upstream + dres_part
    grad_attend_scale = jnp.sum(dresidual * branch, axis=0)
    dbranch = (dresidual * attend_scale).astype(jnp.bfloat16)
    grad_out_bias = jnp.sum(dbranch.astype(jnp.float32), axis=0)
    grad_out = jnp.einsum("rd,re->de", mixed, dbranch, preferred_element_type=jnp.float32)
    dmixed = jnp.einsum("re,de->rd", dbranch, w_out, preferred_element_type=jnp.float32).astype(
        jnp.bfloat16
    )
    held, held_sums = cycle_forward(queries, cycle_pair, members, query_rows, info)
    douts = split(dmixed)
    deltas = tuple(
        (
            jnp.einsum(
                "gqhd,gqhd->ghq",
                to_heads(douts[which].astype(jnp.float32), HEADS),
                to_heads(held[which], HEADS),
            )
            for which in range(2)
        )
    )
    dq_start = tuple(
        (jnp.zeros(to_heads(queries[which], HEADS).shape, jnp.float32) for which in range(2))
    )
    bias_start = tuple((jnp.zeros(item.shape, jnp.float32) for item in biases))
    dqueries, dpair, bias_grads = cycle_backward(
        queries,
        douts,
        held_sums,
        deltas,
        cycle_pair,
        members,
        query_rows,
        info,
        (dq_start, bias_start),
    )
    table_grad = bias_back(bias_grads)[0]
    dquery = jnp.concatenate(
        [
            dqueries[0].reshape(groups, small_rows, width),
            dqueries[1].reshape(groups, large_rows, width),
        ],
        axis=1,
    )
    dquery = dquery.reshape(-1, width).astype(jnp.bfloat16)
    dkey = dpair[0].reshape(-1, width).astype(jnp.bfloat16)
    dvalue = dpair[1].reshape(-1, width).astype(jnp.bfloat16)
    grad_query_bias = jnp.sum(dquery.astype(jnp.float32), axis=0)
    grad_value_bias = jnp.sum(dvalue.astype(jnp.float32), axis=0)
    grad_query = jnp.einsum("rd,re->de", hidden, dquery, preferred_element_type=jnp.float32)
    grad_key = jnp.einsum("rd,re->de", hidden, dkey, preferred_element_type=jnp.float32)
    grad_value = jnp.einsum("rd,re->de", hidden, dvalue, preferred_element_type=jnp.float32)
    dhidden = (
        jnp.einsum("re,de->rd", dquery, w_query, preferred_element_type=jnp.float32)
        + jnp.einsum("re,de->rd", dkey, w_key, preferred_element_type=jnp.float32)
        + jnp.einsum("re,de->rd", dvalue, w_value, preferred_element_type=jnp.float32)
    )
    unused, first_back = jax.vjp(layer_norm, inputs, first_gain, first_bias)
    dinput_part, grad_first_gain, grad_first_bias = first_back(dhidden)
    dinputs = (dresidual + dinput_part).astype(jnp.bfloat16)
    small_grad, large_grad = split(dinputs)
    shares = (
        lax.psum_scatter(grad_query, "img", scatter_dimension=0, tiled=True),
        lax.psum_scatter(grad_key, "img", scatter_dimension=0, tiled=True),
        lax.psum_scatter(grad_value, "img", scatter_dimension=0, tiled=True),
        lax.psum_scatter(grad_out, "img", scatter_dimension=0, tiled=True),
        lax.psum_scatter(grad_up, "img", scatter_dimension=0, tiled=True),
        lax.psum_scatter(grad_down, "img", scatter_dimension=0, tiled=True),
    )
    shares = lax.psum((shares[0], shares[1], shares[2], shares[3], shares[4], shares[5]), "seq")
    smalls = lax.psum(
        (
            grad_first_gain,
            grad_first_bias,
            grad_query_bias,
            grad_value_bias,
            grad_out_bias,
            grad_attend_scale,
            grad_second_gain,
            grad_second_bias,
            grad_up_bias,
            grad_down_bias,
            grad_feed_scale,
            table_grad,
        ),
        ("img", "seq"),
    )
    return (
        small_out,
        large_out,
        small_grad,
        large_grad,
        smalls[0],
        smalls[1],
        shares[0],
        smalls[2],
        shares[1],
        shares[2],
        smalls[3],
        shares[3],
        smalls[4],
        smalls[5],
        smalls[6],
        smalls[7],
        shares[4],
        smalls[8],
        shares[5],
        smalls[9],
        smalls[10],
        smalls[11],
    )


def exchange_large(part):
    position = lax.axis_index("seq")
    stay = lax.dynamic_index_in_dim(part, position, 0, keepdims=False)
    leave = lax.dynamic_index_in_dim(part, 1 - position, 0, keepdims=False)
    came = shifted(leave, "seq", 1)
    return jnp.where(
        position == 0,
        jnp.concatenate([stay, came], axis=0),
        jnp.concatenate([came, stay], axis=0),
    )


def return_large(whole, rows):
    position = lax.axis_index("seq")
    stay = lax.dynamic_slice_in_dim(whole, position * rows, rows, 0)
    leave = lax.dynamic_slice_in_dim(whole, (1 - position) * rows, rows, 0)
    came = shifted(leave, "seq", 1)
    return jnp.where(position == 0, jnp.stack([stay, came]), jnp.stack([came, stay]))


def image_device(
    small_in,
    large_in,
    small_cot,
    large_cot,
    first_gain,
    first_bias,
    query_weight,
    query_bias,
    key_weight,
    value_weight,
    value_bias,
    out_weight,
    out_bias,
    attend_scale,
    second_gain,
    second_bias,
    up_weight,
    up_bias,
    down_weight,
    down_bias,
    feed_scale,
    rel_table,
):
    groups, small_rows, width = small_in.shape
    large_rows = large_in.shape[1]
    n_small = groups * small_rows // SLEN
    n_large = 1
    small_part = n_small * SPAD

    def compact(small, large):
        return jnp.concatenate(
            [
                small.reshape(n_small, SLEN, width)[:, :SPAD].reshape(small_part, width),
                exchange_large(large)[:LPAD],
            ],
            axis=0,
        )

    def expand_small(rows):
        small = rows[:small_part].reshape(n_small, SPAD, width)
        small = jnp.pad(small, ((0, 0), (0, SLEN - SPAD), (0, 0)))
        return small.reshape(groups, small_rows, width)

    def expand_large(rows):
        large = jnp.pad(rows[small_part:], ((0, LLEN - LPAD), (0, 0)))
        return return_large(large, large_rows)

    qkv_share = jnp.concatenate([query_weight, key_weight, value_weight], axis=1)
    (w_qkv,) = run_gather([qkv_share], 1)
    mid_share = jnp.concatenate([out_weight, up_weight], axis=1)

    large_seq, small_seq, edge = table_sequences(rel_table)
    x = compact(small_in, large_in)
    cot = compact(small_cot, large_cot)
    gain, bias = first_gain[None], first_bias[None]
    qkv_bias = jnp.concatenate([query_bias, jnp.zeros_like(query_bias), value_bias])[None]
    vectors = jnp.stack(
        [out_bias, attend_scale, second_gain, second_bias, down_bias, feed_scale]
        + [feed_scale] * 2
    )

    qkv = run_qkv(x, gain, bias, w_qkv, qkv_bias)
    (attended, out_wide, probs_small, probs_large), (w_mid, w_down) = run_attend(
        qkv, large_seq, small_seq, edge, n_small, n_large, [mid_share, down_weight], 2
    )
    out, dresidual, dattended, vector_grads, g_mid, g_down = run_feed(
        x, attended, cot, w_mid, w_down, vectors, up_bias[None], n_small
    )
    small_out, large_out = expand_small(out), expand_large(out)

    dquery, dkey, dvalue, d_large, d_small, g_mid, g_down = run_attend_back(
        qkv, dattended, out_wide, probs_small, probs_large, n_small, n_large, [g_mid, g_down], 3
    )
    dinput, input_grads, g_qkv = run_input(
        x, dquery, dkey, dvalue, dresidual, gain, bias, w_qkv
    )
    small_grad, large_grad = expand_small(dinput), expand_large(dinput)
    heads = d_large.shape[0]
    (g_qkv,), (vector_grads, input_grads, d_large, d_small) = run_reduce(
        [g_qkv],
        [
            vector_grads,
            input_grads,
            d_large.reshape(2 * heads, L_WIDTH),
            d_small.reshape(2 * heads, S_WIDTH),
        ],
        4,
    )
    d_large = d_large.reshape(heads, 2, L_WIDTH)
    d_small = d_small.reshape(heads, 2, S_WIDTH)
    edge_grad = d_small[:, 0, S_WIDTH - 3 :]
    table_grad = table_from_sequences(d_large, d_small, edge_grad)
    return (
        small_out,
        large_out,
        small_grad,
        large_grad,
        input_grads[3],
        input_grads[4],
        g_qkv[:, :width],
        input_grads[0],
        g_qkv[:, width : 2 * width],
        g_qkv[:, 2 * width :],
        input_grads[2],
        g_mid[:, :width],
        vector_grads[0],
        vector_grads[1],
        vector_grads[2],
        vector_grads[3],
        g_mid[:, width:],
        vector_grads[8:12].reshape(-1),
        g_down,
        vector_grads[4],
        vector_grads[5],
        table_grad,
    )


def per_device(*args):
    groups, small_rows, unused = args[0].shape
    if lax.axis_size("seq") == 2 and groups == 2 and small_rows % SLEN == 0:
        return image_device(*args)
    return general_device(*args)


def solution(mesh):
    return jax.shard_map(
        per_device,
        mesh=mesh,
        in_specs=(
            P("img", "seq", None),
            P("img", "seq", None),
            P("img", "seq", None),
            P("img", "seq", None),
            P(),
            P(),
            P("img", None),
            P(),
            P("img", None),
            P("img", None),
            P(),
            P("img", None),
            P(),
            P(),
            P(),
            P(),
            P("img", None),
            P(),
            P("img", None),
            P(),
            P(),
            P(),
        ),
        out_specs=(
            P("img", "seq", None),
            P("img", "seq", None),
            P("img", "seq", None),
            P("img", "seq", None),
            P(),
            P(),
            P("img", None),
            P(),
            P("img", None),
            P("img", None),
            P(),
            P("img", None),
            P(),
            P(),
            P(),
            P(),
            P("img", None),
            P(),
            P("img", None),
            P(),
            P(),
            P(),
        ),
        check_vma=False,
    )
```

```python
import functools

import jax
import jax.numpy as jnp
from jax import lax
from jax.experimental import pallas as pl
from jax.experimental.pallas import tpu as pltpu
from jax.sharding import PartitionSpec as P

HEADS = 12
SGRID = 14
LGRID = 24
SLEN = 256
LLEN = 640
SPAD = 208
LPAD = 608
LANES = 128

NEGATIVE = -1e30
EPSILON = 1e-06
F32 = jnp.float32
BF16 = jnp.bfloat16
VMEM_BYTES = 62 << 20


def dot_nn(left, right):
    return lax.dot_general(left, right, (((1,), (0,)), ((), ())), preferred_element_type=F32)


def dot_nt(left, right):
    return lax.dot_general(left, right, (((1,), (1,)), ((), ())), preferred_element_type=F32)


def normalized(values):
    center = values - jnp.mean(values, axis=-1, keepdims=True)
    spread = jnp.mean(center * center, axis=-1, keepdims=True)
    scale = lax.rsqrt(spread + EPSILON)
    return center * scale, scale


def norm_back(grad, normal, scale):
    return scale * (
        grad
        - jnp.mean(grad, axis=-1, keepdims=True)
        - normal * jnp.mean(grad * normal, axis=-1, keepdims=True)
    )


def row_sum(values):
    return jnp.sum(values, axis=0, keepdims=True)


def iota(shape, axis):
    return lax.broadcasted_iota(jnp.int32, shape, axis)


L_WIDTH = 1280
S_WIDTH = 512


def table_sequences(table):
    heads = table.shape[0]
    span = 2 * LGRID - 1
    cells = table[:, : span * span].reshape(heads, span, span)

    def sequences(part, grid, width):
        rows = part.shape[1]
        low = part[:, :, :grid].reshape(heads, rows * grid)
        high = jnp.pad(part[:, :, grid:], ((0, 0), (0, 0), (0, 1))).reshape(heads, rows * grid)
        low = jnp.pad(low, ((0, 0), (0, width - rows * grid)))
        high = jnp.pad(high, ((0, 0), (grid, width - rows * grid - grid)))
        return jnp.stack([low, high], axis=1)

    off = LGRID - SGRID
    large = sequences(cells, LGRID, L_WIDTH)
    small = sequences(cells[:, off : span - off, off : span - off], SGRID, S_WIDTH)
    edge = jnp.broadcast_to(
        jnp.pad(table[:, span * span :], ((0, 0), (0, 5)))[:, :, None], (heads, 8, LANES)
    )
    return large, small, edge


def table_from_sequences(large, small, edge):
    heads = large.shape[0]
    span = 2 * LGRID - 1

    def cells(part, grid):
        rows = 2 * grid - 1
        low = part[:, 0, : rows * grid].reshape(heads, rows, grid)
        high = part[:, 1, grid : grid + rows * grid].reshape(heads, rows, grid)
        return jnp.concatenate([low, high[:, :, : grid - 1]], axis=2)

    off = LGRID - SGRID
    total = cells(large, LGRID) + jnp.pad(
        cells(small, SGRID), ((0, 0), (off, off), (off, off))
    )
    return jnp.concatenate([total.reshape(heads, span * span), edge], axis=1)


def takes_low(rows, width, grid, first):
    step = iota((rows, width), 1) % grid
    row = iota((rows, width), 0)
    low = step >= grid - 1 + first - row
    if first == 1:
        low = low | (row == 0)
    return low


def spread_sequences(seq, rows, width, grid, first):
    low = jnp.broadcast_to(seq[0:1, :], (rows, width))
    high = jnp.broadcast_to(seq[1:2, :], (rows, width))
    chosen = jnp.where(takes_low(rows, width, grid, first), low, high)
    return pltpu.roll(chosen, 1, 1, stride=1, stride_axis=0)


def gather_sequences(spread, rows, width, grid, first):
    row = iota((rows, width), 0) + 1
    for bit in (1, 2, 4, 8, 16):
        spread = jnp.where((row & bit) != 0, pltpu.roll(spread, width - bit, 1), spread)
    low = takes_low(rows, width, grid, first)
    return (
        row_sum(jnp.where(low, spread, 0.0)),
        row_sum(jnp.where(low, 0.0, spread)),
    )


def large_window(block):
    start = (LGRID - block) * LGRID
    return start // LANES, start % LANES


def small_window(block):
    start = (SGRID - 1 - block) * SGRID + SGRID - 1
    return start // LANES, start % LANES


def head_masks():
    lane = iota((1, LANES), 1)
    return (
        jnp.where(lane < LANES // 2, 1.0, 0.0).astype(BF16),
        jnp.where(lane < LANES // 2, 0.0, 1.0).astype(BF16),
    )


def transposed_biases(large_seq, small_seq, edge, wide, narrow, bias_large, bias_small):
    patch_q = edge[0:1, 0:1]
    patch_k = edge[1:2, 0:1]
    both = edge[2:3, 0:1]
    wide[...] = spread_sequences(large_seq, 24, L_WIDTH, LGRID, 1)
    lane = iota((24, LANES), 1)
    row = iota((24, LANES), 0)
    for block in range(LGRID + 1):
        at, turn = large_window(block)
        piece = wide[:, at * LANES : at * LANES + 768]
        if turn:
            piece = pltpu.roll(piece, 768 - turn, 1)
        piece = piece[:, :640]
        if block == 0:
            rest = jnp.where(iota((24, 640), 0) == 0, patch_k, piece)
        elif block == LGRID:
            rest = jnp.where(iota((24, 640), 0) == 0, piece, NEGATIVE)
        else:
            rest = piece
        first = jnp.where(lane == 0, patch_q, rest[:, :LANES])
        if block == 0:
            first = jnp.where((lane == 0) & (row == 0), both, first)
        if block == LGRID:
            first = jnp.where(row == 0, first, NEGATIVE)
        bias_large[pl.ds(block * 24, 24), 0:LANES] = first
        bias_large[pl.ds(block * 24, 24), LANES:640] = rest[:, LANES:]
    bias_large[pl.ds(600, 8), :] = jnp.full((8, 640), NEGATIVE, F32)
    narrow[...] = spread_sequences(small_seq, 16, S_WIDTH, SGRID, 0)
    for block in range(SGRID):
        at, turn = small_window(block)
        piece = narrow[:, at * LANES : at * LANES + 384]
        if turn:
            piece = pltpu.roll(piece, 384 - turn, 1)
        bias_small[pl.ds(1 + SGRID * block, SGRID), :] = piece[:SGRID, :256]
    whole = bias_small[...]
    lane = iota((SPAD, 256), 1)
    row = iota((SPAD, 256), 0)
    whole = jnp.where(lane == 0, patch_q, whole)
    whole = jnp.where(row == 0, patch_k, whole)
    whole = jnp.where((lane == 0) & (row == 0), both, whole)
    bias_small[...] = jnp.where(row > SGRID * SGRID, NEGATIVE, whole)


MESH = pl.DeviceIdType.MESH
ZS = 4


def place():
    img = lax.axis_index("img")
    return img // 4, (img // 2) % 2, img % 2, lax.axis_index("seq")


def device(z, x, c, y):
    return ((z * 2 + x) * 2 + c, y)


def z_peer(z, hop):
    low = (z % 2) * (1 - 2 * (hop % 2)) + hop % 2
    high = (z // 2) * (1 - 2 * (hop // 2)) + hop // 2
    return high * 2 + low


def greet():
    z, x, c, y = place()
    barrier = pltpu.get_barrier_semaphore()
    peers = [device(z_peer(z, hop), x, c, y) for hop in range(1, ZS)]
    peers += [device(z, 1 - x, c, y), device(z, x, c, 1 - y), device(z, x, 1 - c, y)]
    for peer in peers:
        pl.semaphore_signal(barrier, inc=1, device_id=peer, device_id_type=MESH)
    pl.semaphore_wait(barrier, len(peers))


def half_of(width, y):
    return pl.ds(pl.multiple_of(y * (width // 2), 128), width // 2)


class Gather:
    n_sems = 21

    def __init__(self, share, whole, send, recv, own, spare_seq):
        self.share, self.whole, self.send, self.recv, self.own = share, whole, send, recv, own
        self.spare_seq = spare_seq
        self.width = share.shape[1]
        self.at = z, x, c, y = place()
        self.inner = z % 3 != 0

    def copy(self, source, target, index, peer, recv=None):
        return pltpu.make_async_remote_copy(
            src_ref=source,
            dst_ref=target,
            send_sem=self.send.at[index],
            recv_sem=self.recv.at[index if recv is None else recv],
            device_id=peer,
            device_id_type=MESH,
        )

    def source_z(self, turn):
        z = self.at[0]
        is_inner = jnp.minimum(z % 3, 1)
        hop = (0, 1, 2 + is_inner, 3 - is_inner)[turn]
        return z_peer(z, hop)

    def along_z(self, turn, onto, recv):
        z, x, c, y = self.at
        cols = half_of(self.width, y)
        target = self.whole.at[self.source_z(turn), x, c, :, cols]
        source = self.share.at[:, cols] if turn == 0 else target
        index = {(0, 1): 0, (0, 3): 1, (1, 3): 2, (2, 1): 19, (3, 1): 20}[turn, onto]
        return self.copy(source, target, index, device(z_peer(z, onto), x, c, y), recv - 1)

    def from_z(self, turn):
        z, x, c, y = self.at
        cols = half_of(self.width, y)
        block = self.whole.at[self.source_z(turn), x, c, :, cols]
        return self.copy(block, block, turn - 1, device(z_peer(z, 1), x, c, y))

    def across(self, turn, axis):
        z, x, c, y = self.at
        cols = half_of(self.width, y)
        target = self.whole.at[self.source_z(turn), x, c, :, cols]
        source = self.share.at[:, cols] if turn == 0 else target
        peer = device(z, 1 - x, c, y) if axis == 0 else device(z, x, c, 1 - y)
        return self.copy(source, target, 3 + 4 * axis + turn, peer)

    def onward(self, turn):
        z, x, c, y = self.at
        source_z = self.source_z(turn)
        even = 1 if turn == 0 else 0 if self.spare_seq else 1 - source_z % 2
        side = x + even * (1 - 2 * x)
        cols = half_of(self.width, y + (1 - even) * (1 - 2 * y))
        block = self.whole.at[source_z, side, c, :, cols]
        peer = device(z, x + (1 - even) * (1 - 2 * x), c, y + even * (1 - 2 * y))
        return self.copy(block, block, 11 + turn, peer)

    def to_core(self, turn):
        z, x, c, y = self.at
        block = self.whole.at[self.source_z(turn), :, c]
        return self.copy(block, block, 15 + turn, device(z, x, 1 - c, y))

    def keep_own(self):
        z, x, c, y = self.at
        return pltpu.make_async_copy(self.share, self.whole.at[z, x, c], self.own)

    def begin(self):
        self.keep_own().start()
        self.across(0, 0).start()
        self.along_z(0, 1, 1).start()

        @pl.when(self.inner)
        def _():
            self.along_z(0, 3, 2).start()

    def come(self, hop):
        self.from_z(hop).wait_recv()

        @pl.when(self.inner)
        def _():
            if hop == 1:
                self.along_z(1, 3, 3).start()
            else:
                self.along_z(hop, 1, hop).start()

        for axis in range(2):
            self.across(hop, axis).start()

    def pass_on(self, hop):
        for axis in range(2 if hop else 1):
            self.across(hop, axis).wait_recv()
        self.onward(hop).start()

    def give(self, hop):
        if hop == 0:
            self.keep_own().wait()
        self.onward(hop).wait_recv()
        self.to_core(hop).start()

    def turn(self, at):
        stage, hop = (
            (self.come, 1),
            (self.pass_on, 0),
            (self.come, 2),
            (self.pass_on, 1),
            (self.come, 3),
            (self.pass_on, 2),
            (self.give, 0),
            (self.pass_on, 3),
            (self.give, 1),
            (self.give, 2),
            (self.give, 3),
        )[at]
        stage(hop)

    def arrive(self):
        for hop in range(ZS):
            self.to_core(hop).wait_recv()

    def drain(self):
        for hop in range(ZS):
            self.to_core(hop).wait_send()
            self.onward(hop).wait_send()
            for axis in range(2 if hop else 1):
                self.across(hop, axis).wait_send()
        self.along_z(0, 1, 1).wait_send()

        @pl.when(self.inner)
        def _():
            self.along_z(0, 3, 2).wait_send()
            self.along_z(1, 3, 3).wait_send()
            self.along_z(2, 1, 2).wait_send()
            self.along_z(3, 1, 3).wait_send()


class Rows:
    n_sems = 2

    def __init__(self, small, large, line, sems, send, recv):
        self.small, self.large, self.line = small, large, line
        self.sems, self.send, self.recv = sems, send, recv
        self.at = place()
        self.n_small = small.shape[0]
        self.base = self.n_small * SPAD
        self.rows = large.shape[1]

    def spot(self):
        start = self.base + self.rows * self.at[3]
        return self.line.at[pl.ds(pl.multiple_of(start, 16), self.rows)]

    def local(self, i):
        if i < self.n_small:
            return pltpu.make_async_copy(
                self.small.at[i, pl.ds(0, SPAD)],
                self.line.at[pl.ds(i * SPAD, SPAD)],
                self.sems.at[i],
            )
        return pltpu.make_async_copy(self.large.at[self.at[3]], self.spot(), self.sems.at[i])

    def remote(self):
        z, x, c, y = self.at
        return pltpu.make_async_remote_copy(
            src_ref=self.large.at[1 - y],
            dst_ref=self.spot(),
            send_sem=self.send,
            recv_sem=self.recv,
            device_id=device(z, x, c, 1 - y),
            device_id_type=MESH,
        )

    def begin(self):
        self.remote().start()
        for i in range(self.n_small + 1):
            self.local(i).start()

    def wait_small(self):
        for i in range(self.n_small):
            self.local(i).wait()

    def wait_large(self):
        self.local(self.n_small).wait()
        self.remote().wait()


def add_rows(target, source, shape):
    rows, cols = shape

    def strip(i, unused):
        at = pl.ds(pl.multiple_of(i * 16, 16), 16)
        target[at, :] = (target[at, :].astype(F32) + source[at, :].astype(F32)).astype(BF16)
        return unused

    lax.fori_loop(0, rows // 16, strip, 0)


class Reduce:
    n_sems = 21
    n_scratch = 6

    def __init__(self, grad, out, held, core, first, second, last, edge, send, recv, own, x_first):
        self.x_first = x_first
        self.grad, self.held, self.core = grad, held, core
        self.first, self.second, self.last, self.edge, self.out = first, second, last, edge, out
        self.send, self.recv, self.own = send, recv, own
        self.rows, self.width = out.shape
        self.at = place()
        self.mine = half_of(self.width, self.at[3])
        self.other = half_of(self.width, 1 - self.at[3])

    @staticmethod
    def scratch(rows, width):
        half = width // 2
        return [
            pltpu.VMEM((ZS, 2, rows, width), BF16),
            pltpu.VMEM((ZS, 2, rows, width), BF16),
            pltpu.VMEM((ZS, 2, rows, half), BF16),
            pltpu.VMEM((ZS, rows, half), BF16),
            pltpu.VMEM((ZS, rows, half), BF16),
            pltpu.VMEM((2, rows, half), BF16),
        ]

    def copy(self, source, target, index, peer):
        return pltpu.make_async_remote_copy(
            src_ref=source,
            dst_ref=target,
            send_sem=self.send.at[index],
            recv_sem=self.recv.at[index],
            device_id=peer,
            device_id_type=MESH,
        )

    def load(self, s):
        return pltpu.make_async_copy(
            self.grad.at[s, :, self.at[2]], self.held.at[s], self.own.at[s]
        )

    def between_cores(self, s):
        z, x, c, y = self.at
        return self.copy(self.grad.at[s, :, 1 - c], self.core.at[s], s, device(z, x, 1 - c, y))

    def leg_one(self, s, i):
        z, x, c, y = self.at
        half = self.width // 2
        if s in self.x_first:
            source = self.held.at[s, 1 - x, :, pl.ds(i * half, half)]
            peer = device(z, 1 - x, c, y)
        else:
            source = self.held.at[s, i, :, self.other]
            peer = device(z, x, c, 1 - y)
        return self.copy(source, self.first.at[s, i], 4 + 2 * s + i, peer)

    def leg_two(self, s):
        z, x, c, y = self.at
        if s in self.x_first:
            source = self.held.at[s, x, :, self.other]
            peer = device(z, x, c, 1 - y)
        else:
            source = self.held.at[s, 1 - x, :, self.mine]
            peer = device(z, 1 - x, c, y)
        return self.copy(source, self.second.at[s], 12 + s, peer)

    def leg_three(self, hop):
        z, x, c, y = self.at
        target = z_peer(z, hop)
        source = self.held.at[target, x, :, self.mine]
        return self.copy(source, self.last.at[hop], 16 + hop, device(target, x, c, y))

    def leg_four(self):
        z, x, c, y = self.at
        return self.copy(self.edge.at[0], self.edge.at[1], 20, device(z, x, c, 1 - y))

    def begin(self):
        for s in range(ZS):
            self.between_cores(s).start()
            self.load(s).start()

    def one(self, s):
        self.load(s).wait()
        self.between_cores(s).wait_recv()
        for i in range(2):
            add_rows(self.held.at[s, i], self.core.at[s, i], (self.rows, self.width))
        for i in range(2):
            self.leg_one(s, i).start()

    def two(self, s):
        x = self.at[1]
        half = self.width // 2
        for i in range(2):
            self.leg_one(s, i).wait_recv()
            if s in self.x_first:
                target = self.held.at[s, x, :, pl.ds(i * half, half)]
            else:
                target = self.held.at[s, i, :, self.mine]
            add_rows(target, self.first.at[s, i], (self.rows, half))
        self.leg_two(s).start()

    def three(self, s):
        x = self.at[1]
        self.leg_two(s).wait_recv()
        target = self.held.at[s, x, :, self.mine]
        add_rows(target, self.second.at[s], (self.rows, self.width // 2))
        if s == ZS - 1:
            for hop in range(1, ZS):
                self.leg_three(hop).start()

    def four(self):
        z, x, c, y = self.at
        for hop in range(1, ZS):
            self.leg_three(hop).wait_recv()
        own = self.held.at[z, x, :, self.mine]
        last, edge = self.last, self.edge

        def strip(i, unused):
            at = pl.ds(pl.multiple_of(i * 16, 16), 16)
            total = own[at, :].astype(F32)
            for hop in range(1, ZS):
                total += last[hop, at, :].astype(F32)
            edge[0, at, :] = total.astype(BF16)
            return unused

        lax.fori_loop(0, self.rows // 16, strip, 0)
        self.leg_four().start()
        self.out[:, self.mine] = edge[0].astype(F32)

    def finish(self):
        self.leg_four().wait()
        self.out[:, self.other] = self.edge[1].astype(F32)
        for s in range(ZS):
            self.between_cores(s).wait_send()
            for i in range(2):
                self.leg_one(s, i).wait_send()
            self.leg_two(s).wait_send()
        for hop in range(1, ZS):
            self.leg_three(hop).wait_send()


class Total:
    n_steps = 5

    def __init__(self, part, out, leave, come, send, recv):
        self.part, self.out, self.leave, self.come = part, out, leave, come
        self.send, self.recv = send, recv
        self.at = place()

    @staticmethod
    def scratch(shape):
        return [pltpu.VMEM((Total.n_steps,) + shape, BF16)] * 2

    def copy(self, step):
        z, x, c, y = self.at
        peer = (
            device(z, x, 1 - c, y),
            device(z, 1 - x, c, y),
            device(z, x, c, 1 - y),
            device(z_peer(z, 1), x, c, y),
            device(z_peer(z, 2), x, c, y),
        )[step]
        return pltpu.make_async_remote_copy(
            src_ref=self.leave.at[step],
            dst_ref=self.come.at[step],
            send_sem=self.send.at[step],
            recv_sem=self.recv.at[step],
            device_id=peer,
            device_id_type=MESH,
        )

    def begin(self):
        self.leave[0] = self.part[...].astype(BF16)
        self.copy(0).start()

    def advance(self, step):
        self.copy(step).wait()
        total = self.leave[step].astype(F32) + self.come[step].astype(F32)
        if step + 1 < self.n_steps:
            self.leave[step + 1] = total.astype(BF16)
            self.copy(step + 1).start()
        else:
            self.out[...] = total


class RowsBack:
    n_sems = 3

    def __init__(self, line, blank, small, large, sems, send, recv):
        self.line, self.blank, self.small, self.large = line, blank, small, large
        self.sems, self.send, self.recv = sems, send, recv
        self.at = place()
        self.n_small = small.shape[0]
        self.rows = large.shape[1]

    def half(self, y):
        start = self.n_small * SPAD + self.rows * y
        return self.line.at[pl.ds(pl.multiple_of(start, 16), self.rows)]

    def local(self, i):
        n = self.n_small
        if i < n:
            source, target = self.line.at[pl.ds(i * SPAD, SPAD)], self.small.at[i, pl.ds(0, SPAD)]
        elif i < 2 * n:
            source, target = self.blank, self.small.at[i - n, pl.ds(SPAD, SLEN - SPAD)]
        else:
            y = self.at[3]
            source, target = self.half(y), self.large.at[y]
        return pltpu.make_async_copy(source, target, self.sems.at[i])

    def remote(self):
        z, x, c, y = self.at
        return pltpu.make_async_remote_copy(
            src_ref=self.half(1 - y),
            dst_ref=self.large.at[y],
            send_sem=self.send,
            recv_sem=self.recv,
            device_id=device(z, x, c, 1 - y),
            device_id_type=MESH,
        )

    def begin(self):
        self.remote().start()
        for i in range(2 * self.n_small + 1):
            self.local(i).start()

    def finish(self):
        for i in range(2 * self.n_small + 1):
            self.local(i).wait()
        self.remote().wait()


def begin_kernel(
    n_small,
    n_large,
    qkv_share,
    mid_share,
    down_share,
    small_in,
    large_in,
    small_cot,
    large_cot,
    large_seq,
    small_seq,
    edge,
    gain,
    gain_bias,
    qkv_bias,
    x_out,
    cot_out,
    qkv_out,
    turned_out,
    w_out,
    mid_whole,
    down_whole,
    out,
    out_wide,
    probs_small,
    probs_large,
    line,
    cot_line,
    hidden,
    turned,
    qkv,
    w_qkv,
    wide,
    narrow,
    bias_large,
    bias_small,
    send,
    recv,
    own,
    row_sems,
    row_send,
    row_recv,
    keep_sems,
):
    step = pl.program_id(0)
    pairs = pl.num_programs(0)
    width = hidden.shape[1]
    count = qkv.shape[1]
    masks = head_masks()
    first = Gather(qkv_share, w_qkv, send.at[0], recv.at[0], own.at[0], True)
    mid = Gather(mid_share, mid_whole, send.at[1], recv.at[1], own.at[1], False)
    down = Gather(down_share, down_whole, send.at[2], recv.at[2], own.at[2], True)
    x_rows = Rows(small_in, large_in, line, row_sems.at[0], row_send.at[0], row_recv.at[0])
    cot_rows = Rows(small_cot, large_cot, cot_line, row_sems.at[1], row_send.at[1], row_recv.at[1])
    keeps = [
        pltpu.make_async_copy(line, x_out, keep_sems.at[0]),
        pltpu.make_async_copy(qkv, qkv_out, keep_sems.at[1]),
        pltpu.make_async_copy(w_qkv, w_out, keep_sems.at[2]),
        pltpu.make_async_copy(cot_line, cot_out, keep_sems.at[3]),
        pltpu.make_async_copy(turned, turned_out, keep_sems.at[4]),
    ]

    early = (
        ((mid, 0), (mid, 1), (down, 0), (down, 1)),
        ((mid, 2),),
        ((mid, 3),),
    )
    slots = (
        ((down, 2),),
        ((down, 3),),
        (),
        (),
        ((mid, 4),),
        ((mid, 5), (mid, 6)),
        ((down, 4),),
        ((mid, 7), (down, 5), (down, 6)),
        ((mid, 8), (mid, 9)),
        ((down, 7), (down, 8)),
        ((mid, 10), (down, 9)),
        ((down, 10),),
    )

    @pl.when(step == 0)
    def _():
        greet()
        first.begin()
        x_rows.begin()
        part = chunk_rows(count)
        chunks = [pl.ds(at, part) for at in range(0, count, part)]

        def norm(rows):
            normal, unused = normalized(line[rows, :].astype(F32))
            hidden[rows, :] = (normal * gain[...] + gain_bias[...]).astype(BF16)

        x_rows.wait_small()
        norm(chunks[0])
        for at in range(5):
            first.turn(at)
        for at in range(5, 8):
            first.turn(at)
        x_rows.wait_large()
        for rows in chunks[1:]:
            norm(rows)
        keeps[0].start()
        for at in range(8, 11):
            first.turn(at)
        first.arrive()
        mid.begin()
        down.begin()
        cot_rows.begin()
        keeps[2].start()
        scale = jnp.asarray(float(width // HEADS) ** (-0.5), BF16)
        for at, rows in enumerate(chunks):
            for kind in range(3):
                cols = slice(kind * width, (kind + 1) * width)
                weight = w_qkv[:, :, :, :, cols].reshape(width, width)
                made = (dot_nn(hidden[rows, :], weight) + qkv_bias[:, cols]).astype(BF16)
                if kind == 0:
                    made = made * scale
                for j in range(HEADS // 2):
                    qkv[kind * (HEADS // 2) + j, rows, :] = made[:, j * LANES : (j + 1) * LANES]
            for job, turn in early[at]:
                job.turn(turn)
        keeps[1].start()
        turned[...] = hidden[...].T
        keeps[4].start()

    query = qkv.at[step]
    key = qkv.at[pairs + step]
    value = qkv.at[2 * pairs + step]

    @pl.when(pl.program_id(0) == 0)
    def _():
        bias_small[...] = jnp.zeros_like(bias_small)

    members = [(i * SPAD, SPAD, bias_small, probs_small, i) for i in range(n_small)]
    members += [
        (n_small * SPAD + i * LPAD, LPAD, bias_large, probs_large, i) for i in range(n_large)
    ]
    halves = [[] for _ in members]
    for head in range(2):
        transposed_biases(
            large_seq[head], small_seq[head], edge[head], wide, narrow, bias_large, bias_small
        )
        for at, (start, count, bias, probs, which) in enumerate(members):
            rows = pl.ds(start, count)
            scores = dot_nt(key[rows, :], query[rows, :] * masks[head]) + bias[:, :count]
            top = jnp.max(scores, axis=0, keepdims=True)
            weights = jnp.exp(scores - top)
            total = jnp.sum(weights, axis=0, keepdims=True)
            prob = (weights * (1.0 / total)).astype(BF16)
            probs[head, which] = prob
            turned = value[rows, :].T
            halves[at].append(dot_nn(turned[head * 64 : head * 64 + 64, :], prob))
        for at in range(HEADS // 2):
            if slots[2 * at + head]:

                @pl.when(step == at)
                def _():
                    for job, turn in slots[2 * at + head]:
                        job.turn(turn)

    for at, (start, count, bias, probs, which) in enumerate(members):
        both = jnp.concatenate(halves[at], axis=0).T
        out[pl.ds(start, count), :] = both.astype(BF16)
        out_wide[pl.ds(start, count), :] = both

    @pl.when(step == pairs - 3)
    def _():
        cot_rows.wait_small()
        cot_rows.wait_large()
        keeps[3].start()

    @pl.when(step == pairs - 1)
    def _():
        for job in (mid, down):
            job.arrive()
        for job in (first, mid, down):
            job.drain()
        for keep in keeps:
            keep.wait()


EARLY = 4


def end_kernel(
    n_small,
    n_large,
    query,
    key,
    value,
    dout,
    out_wide,
    probs_small,
    probs_large,
    g_mid,
    g_down,
    x_hbm,
    turned_hbm,
    w_hbm,
    dres_hbm,
    out_hbm,
    feed_grads,
    gain,
    small_out,
    large_out,
    small_grad,
    large_grad,
    mid_out,
    down_out,
    early_out,
    late_out,
    feed_total,
    input_total,
    large_total,
    small_total,
    *scratch,
):
    scratch = list(scratch)

    def take(count):
        taken = scratch[:count]
        del scratch[:count]
        return taken

    wide, narrow, dsum_small, dscore_large, dqkv, hidden_turned, w_qkv, line, blank = take(9)
    early_grad, late_grad, input_part, large_part, small_part = take(5)
    mid_bufs, down_bufs, early_bufs, late_bufs = [take(Reduce.n_scratch) for unused in range(4)]
    feed_bufs, input_bufs, large_bufs, small_bufs = [take(2) for unused in range(4)]
    send, recv, own, total_send, total_recv, load_sems, row_sems, row_send, row_recv = scratch

    step = pl.program_id(0)
    pairs = HEADS // 2
    width = x_hbm.shape[1]
    all_rows = dqkv.shape[1]
    masks = head_masks()
    query, key, value = query.at[0], key.at[0], value.at[0]
    both_ways, mostly_x = (0, 2), (0, 1, 2)
    mid = Reduce(g_mid, mid_out, *mid_bufs, send.at[0], recv.at[0], own.at[0], both_ways)
    down = Reduce(g_down, down_out, *down_bufs, send.at[1], recv.at[1], own.at[1], both_ways)
    early = Reduce(early_grad, early_out, *early_bufs, send.at[2], recv.at[2], own.at[2], mostly_x)
    late = Reduce(late_grad, late_out, *late_bufs, send.at[3], recv.at[3], own.at[3], mostly_x)
    sums = [
        Total(part, total, *bufs, total_send.at[i], total_recv.at[i])
        for i, (part, total, bufs) in enumerate(
            (
                (feed_grads, feed_total, feed_bufs),
                (input_part, input_total, input_bufs),
                (large_part, large_total, large_bufs),
                (small_part, small_total, small_bufs),
            )
        )
    ]
    feed_sum, input_sum, large_sum, small_sum = sums
    out_rows = RowsBack(
        line, blank, small_out, large_out, row_sems.at[0], row_send.at[0], row_recv.at[0]
    )
    grad_rows = RowsBack(
        line, blank, small_grad, large_grad, row_sems.at[1], row_send.at[1], row_recv.at[1]
    )
    load_out = pltpu.make_async_copy(out_hbm, line.at[pl.ds(0, all_rows)], load_sems.at[0])
    load_x = pltpu.make_async_copy(x_hbm, line, load_sems.at[1])
    load_turned = pltpu.make_async_copy(turned_hbm, hidden_turned, load_sems.at[2])
    load_w = pltpu.make_async_copy(w_hbm, w_qkv, load_sems.at[3])

    def take_turns(by_step):
        for at, turns in enumerate(by_step):
            if turns:

                @pl.when(step == at)
                def _():
                    for turn in turns:
                        turn[0](*turn[1:])

    slots = (
        ([(mid.one, 0), (mid.one, 1)], [(down.one, 0), (down.one, 1)], [(feed_sum.advance, 1)], [(mid.two, 2), (mid.two, 3)], [(down.two, 0), (down.two, 1), (early.one, 0)], [(mid.three, 0), (mid.three, 1), (mid.three, 2), (mid.three, 3)]),
        ([(mid.one, 2), (mid.one, 3)], [(down.one, 2), (down.one, 3)], [], [], [(down.two, 2), (down.two, 3), (early.one, 1)], []),
        ([], [], [(mid.two, 0), (mid.two, 1)], [(feed_sum.advance, 3)], [(early.one, 2)], [(down.three, 0), (down.three, 1), (down.three, 2), (down.three, 3)]),
        ([(feed_sum.advance, 0)], [], [(feed_sum.advance, 2)], [], [(early.one, 3)], [(feed_sum.advance, 4)]),
    )

    @pl.when(step == 0)
    def _():
        greet()
        mid.begin()
        down.begin()
        load_out.start()
        load_turned.start()
        blank[...] = jnp.zeros_like(blank)
        line[pl.ds(all_rows, line.shape[0] - all_rows), :] = jnp.zeros(
            (line.shape[0] - all_rows, width), BF16
        )
        feed_sum.begin()
        load_out.wait()
        out_rows.begin()

    lane = iota((1, LANES), 1)
    scale = float(64) ** (-0.5)
    members = [(i * SPAD, SPAD, probs_small, i) for i in range(n_small)]
    members += [(n_small * SPAD + i * LPAD, LPAD, probs_large, i) for i in range(n_large)]
    keep = []
    for head in range(2):
        spot = 64 * (1 - head)
        minus = jnp.where((lane == spot) | (lane == spot + 1), -1.0, 0.0).astype(BF16)
        mask32 = masks[head].astype(F32)
        for at, (start, count, probs, which) in enumerate(members):
            rows = pl.ds(start, count)
            grad = dout[rows, :]
            grad32 = grad.astype(F32) * mask32
            delta = jnp.sum(grad32 * out_wide[rows, :], axis=1, keepdims=True)
            coarse = delta.astype(BF16).astype(F32)
            fine = delta - coarse
            side = jnp.where(lane == spot, coarse, jnp.where(lane == spot + 1, fine, grad32))
            values = value[rows, :] * masks[head] + minus
            prob = probs[head, which]
            dscore = prob.astype(F32) * dot_nt(values, side.astype(BF16))
            if count == SPAD:
                if which == 0:
                    dsum_small[:, :SPAD] = dscore
                else:
                    dsum_small[:, :SPAD] += dscore
            elif which == 0:
                dscore_large[:, :LPAD] = dscore
            else:
                dscore_large[:, :LPAD] += dscore
            low = dscore.astype(BF16)
            turned = key[rows, :].T
            dq = dot_nn(turned[head * 64 : head * 64 + 64, :], low)
            dk = dot_nn(low, query[rows, :])
            dv = dot_nn(prob, grad)
            if head == 0:
                keep.append((dq, dk, dv))
            else:
                first = iota((count, LANES), 1) < 64
                dq0, dk0, dv0 = keep[at]
                dqkv[step, rows, :] = (jnp.concatenate([dq0, dq], axis=0).T * scale).astype(BF16)
                dqkv[pairs + step, rows, :] = jnp.where(first, dk0, dk).astype(BF16)
                dqkv[2 * pairs + step, rows, :] = jnp.where(first, dv0, dv).astype(BF16)
        take_turns(slots[2 * head])
        wide[...] = jnp.zeros_like(wide)
        dscore_large[:, LPAD:] = jnp.zeros((LPAD, 768 - LPAD), F32)
        edge_lane = iota((24, 768), 1)
        edge_row = iota((24, 768), 0)
        class_column = jnp.zeros((24, 768), F32)
        class_row = None
        for block in range(LGRID + 1):
            at, turn = large_window(block)
            piece = dscore_large[pl.ds(block * 24, 24), :]
            if block == 0:
                class_row = piece[0:1, :]
                piece = jnp.where(edge_row == 0, 0.0, piece)
            class_column = class_column + piece
            piece = jnp.where(edge_lane == 0, 0.0, piece)
            if turn:
                piece = pltpu.roll(piece, turn, 1)
            wide[:, at * LANES : at * LANES + 768] += piece
        low_sum, high_sum = gather_sequences(wide[...], 24, L_WIDTH, LGRID, 1)
        spot_row = step * 4 + head * 2
        large_part[pl.ds(spot_row, 1), :] = low_sum
        large_part[pl.ds(spot_row + 1, 1), :] = high_sum
        narrow[...] = jnp.zeros_like(narrow)
        dsum_small[:, SPAD:] = jnp.zeros((SPAD, 384 - SPAD), F32)
        small_lane = iota((SGRID, 384), 1)
        small_column = jnp.zeros((SGRID, 384), F32)
        for block in range(SGRID):
            at, turn = small_window(block)
            piece = dsum_small[pl.ds(1 + SGRID * block, SGRID), :]
            small_column = small_column + piece
            piece = jnp.where(small_lane == 0, 0.0, piece)
            piece = jnp.concatenate([piece, jnp.zeros((2, 384), F32)], axis=0)
            if turn:
                piece = pltpu.roll(piece, turn, 1)
            narrow[:, at * LANES : at * LANES + 384] += piece
        low_sum, high_sum = gather_sequences(narrow[...], 16, S_WIDTH, SGRID, 0)
        by_query = row_sum(class_column)[:, :LANES] + row_sum(small_column)[:, :LANES]
        both_rows = class_row + jnp.concatenate(
            [dsum_small[0:1, :], jnp.zeros((1, 384), F32)], axis=1
        )
        class_key = jnp.sum(
            jnp.where(iota((1, 768), 1) == 0, 0.0, both_rows), axis=1, keepdims=True
        )
        spot = iota((1, S_WIDTH), 1)
        low_sum = jnp.where(spot == S_WIDTH - 3, by_query[:, 0:1], low_sum)
        low_sum = jnp.where(spot == S_WIDTH - 2, class_key, low_sum)
        low_sum = jnp.where(spot == S_WIDTH - 1, both_rows[:, 0:1], low_sum)
        small_part[pl.ds(spot_row, 1), :] = low_sum
        small_part[pl.ds(spot_row + 1, 1), :] = high_sum
        take_turns(slots[1 + 2 * head])

    @pl.when(step == 0)
    def _():
        load_turned.wait()

    made = [dot_nn(hidden_turned[...], dqkv[kind * pairs + step]).astype(BF16) for kind in range(3)]
    made = [item.reshape(ZS, 2, 2, width // 16, LANES) for item in made]
    for grad, first, many in ((early_grad, 0, EARLY), (late_grad, EARLY, pairs - EARLY)):
        for at in range(many):

            @pl.when(step == first + at)
            def _():
                for kind in range(3):
                    cols = slice((3 * at + kind) * LANES, (3 * at + kind + 1) * LANES)
                    grad[:, :, :, :, cols] = made[kind]

    @pl.when(step == EARLY - 1)
    def _():
        early.begin()
        out_rows.finish()
        load_x.start()
        load_w.start()

    @pl.when(step == pairs - 1)
    def _():
        late.begin()
        large_sum.begin()
        small_sum.begin()
        load_x.wait()
        load_w.wait()
        part = chunk_rows(all_rows)
        zeros = jnp.zeros((1, width), F32)
        input_part[...] = jnp.zeros_like(input_part)
        end_turns = (
            [(late.one, 0), (late.one, 1), (late.one, 2), (late.one, 3), (large_sum.advance, 0), (small_sum.advance, 0)],
            [(early.two, 0), (early.two, 1), (early.two, 2), (early.two, 3), (mid.four,), (large_sum.advance, 1), (small_sum.advance, 1)],
            [(late.two, 0), (late.two, 1), (late.two, 2), (late.two, 3), (down.four,), (large_sum.advance, 2), (small_sum.advance, 2)],
        )
        for at, first in enumerate(range(0, all_rows, part)):
            rows = pl.ds(first, part)
            load_dres = pltpu.make_async_copy(
                dres_hbm.at[rows], dscore_large.at[pl.ds(0, part)], load_sems.at[4]
            )
            load_dres.start()
            dhidden = jnp.zeros((part, width), F32)
            for kind in range(3):
                piece = jnp.concatenate(
                    [dqkv[kind * pairs + j, rows, :] for j in range(pairs)], axis=1
                )
                weight = w_qkv[:, :, :, :, kind * width : (kind + 1) * width]
                dhidden += dot_nt(piece, weight.reshape(width, width))
                if kind != 1:
                    input_part[kind : kind + 1, :] += row_sum(piece.astype(F32))
            normal, rate = normalized(line[rows, :].astype(F32))
            input_part[3:4, :] += row_sum(dhidden * normal)
            input_part[4:5, :] += row_sum(dhidden)
            back = norm_back(dhidden * gain[...], normal, rate)
            load_dres.wait()
            line[rows, :] = (dscore_large[pl.ds(0, part), :] + back).astype(BF16)
            for turn in end_turns[at]:
                turn[0](*turn[1:])
        line[pl.ds(all_rows, line.shape[0] - all_rows), :] = jnp.zeros(
            (line.shape[0] - all_rows, width), BF16
        )
        grad_rows.begin()
        input_sum.begin()
        for turn in (
            [(input_sum.advance, 0)] + [(early.three, i) for i in range(ZS)]
            + [(large_sum.advance, 3), (small_sum.advance, 3), (input_sum.advance, 1)]
            + [(late.three, i) for i in range(ZS)]
            + [(input_sum.advance, 2), (early.four,)]
            + [(large_sum.advance, 4), (small_sum.advance, 4)]
            + [(input_sum.advance, 3), (late.four,), (input_sum.advance, 4)]
        ):
            turn[0](*turn[1:])
        grad_rows.finish()
        for job in (mid, down, early, late):
            job.finish()


def gelu_pair(upper):
    normal_cdf = 0.5 * (1.0 + lax.erf(upper * (0.5**0.5)))
    density = jnp.exp(-0.5 * upper * upper) * 0.3989422804014327
    return upper * normal_cdf, normal_cdf + upper * density


def valid_rows(first, count, n_small):
    row = iota((count, 1), 0) + first
    in_small = row < n_small * SPAD
    small_ok = row % SPAD < SGRID * SGRID + 1
    large_ok = (row - n_small * SPAD) % LPAD < LGRID * LGRID + 1
    return jnp.where(in_small, small_ok.astype(F32), large_ok.astype(F32))


def feed_kernel(
    n_small,
    tiles,
    x,
    attended,
    cot,
    mid_hbm,
    down_hbm,
    vectors,
    up_bias,
    out,
    dresidual,
    dattended,
    vector_grads,
    g_mid,
    g_down,
    w_mid,
    w_down,
    active,
    slope,
    acc_out,
    acc_up,
    acc_down,
    sems,
):
    step = pl.program_id(0)
    count, width = x.shape
    w_out = w_mid.at[:, :width]
    w_up = w_mid.at[:, width:]
    tile = w_up.shape[1] // tiles

    final = pl.num_programs(0) - 1
    pieces = [(mid_hbm, w_mid, g_mid, (slice(None), slice(0, width)))]
    for t in range(tiles):
        cols = slice(width + t * tile, width + (t + 1) * tile)
        pieces.append((mid_hbm, w_mid, g_mid, (slice(None), cols)))
    for t in range(tiles):
        rows = slice(t * tile, (t + 1) * tile)
        pieces.append((down_hbm, w_down, g_down, (rows, slice(None))))

    def load(at):
        source, held, target, where = pieces[at]
        return pltpu.make_async_copy(source.at[where], held.at[where], sems.at[at])

    def store(at):
        source, held, target, where = pieces[at]
        return pltpu.make_async_copy(held.at[where], target.at[where], sems.at[at])

    @pl.when(step == 0)
    def _():
        for at in range(len(pieces)):
            load(at).start()
        acc_out[...] = jnp.zeros_like(acc_out)
        acc_up[...] = jnp.zeros_like(acc_up)
        acc_down[...] = jnp.zeros_like(acc_down)
        vector_grads[...] = jnp.zeros_like(vector_grads)
        load(0).wait()

    out_bias = vectors[0:1, :]
    attend_scale = vectors[1:2, :]
    second_gain = vectors[2:3, :]
    second_bias = vectors[3:4, :]
    down_bias = vectors[4:5, :]
    feed_scale = vectors[5:6, :]

    valid = valid_rows(step * count, count, n_small)
    mixed = attended[...]
    branch = dot_nn(mixed, w_out[...]) + out_bias
    residual = x[...].astype(F32) + attend_scale * branch
    normal, scale = normalized(residual)
    hidden = (normal * second_gain + second_bias).astype(BF16)

    @pl.when(step == 0)
    def _():
        for at in range(1, len(pieces)):
            load(at).wait()

    lower = jnp.zeros((count, width), F32)
    for t in range(tiles):
        cols = slice(t * tile, (t + 1) * tile)
        upper = dot_nn(hidden, w_up[:, cols]) + up_bias[:, cols]
        made, rate = gelu_pair(upper)
        made = made.astype(BF16)
        active[:, cols] = made
        slope[:, cols] = rate.astype(BF16)
        lower += dot_nn(made, w_down[cols, :])
    lower += down_bias
    out[...] = ((residual + feed_scale * lower) * valid).astype(BF16)
    upstream = cot[...].astype(F32) * valid
    vector_grads[5:6, :] += row_sum(upstream * lower)
    dlower = (upstream * feed_scale).astype(BF16)
    vector_grads[4:5, :] += row_sum(dlower.astype(F32))
    turned = hidden.T
    dhidden = jnp.zeros((count, width), F32)
    for t in range(tiles):
        cols = slice(t * tile, (t + 1) * tile)
        dupper = (dot_nt(dlower, w_down[cols, :]) * slope[:, cols].astype(F32)).astype(BF16)
        vector_grads[8 + t : 9 + t, :] += row_sum(dupper.astype(F32))
        acc_down[cols, :] += dot_nn(active[:, cols].T, dlower)
        acc_up[:, cols] += dot_nn(turned, dupper)
        dhidden += dot_nt(dupper, w_up[:, cols])

    @pl.when(step == final)
    def _():
        for t in range(tiles):
            cols = slice(t * tile, (t + 1) * tile)
            w_up[:, cols] = acc_up[:, cols].astype(BF16)
            store(1 + t).start()
            w_down[cols, :] = acc_down[cols, :].astype(BF16)
            store(1 + tiles + t).start()

    vector_grads[2:3, :] += row_sum(dhidden * normal)
    vector_grads[3:4, :] += row_sum(dhidden)
    dres = upstream + norm_back(dhidden * second_gain, normal, scale)
    dresidual[...] = dres
    vector_grads[1:2, :] += row_sum(dres * branch)
    dbranch = (dres * attend_scale).astype(BF16)
    vector_grads[0:1, :] += row_sum(dbranch.astype(F32))
    acc_out[...] += dot_nn(mixed.T, dbranch)
    dattended[...] = dot_nt(dbranch, w_out[...]).astype(BF16)

    @pl.when(step == final)
    def _():
        w_out[...] = acc_out[...].astype(BF16)
        store(0).start()
        for at in range(len(pieces)):
            store(at).wait()


def chunk_rows(total):
    return max(size for size in range(16, 481, 16) if total % size == 0)


def params(collective=None):
    if collective is None:
        return pltpu.CompilerParams(vmem_limit_bytes=VMEM_BYTES)
    return pltpu.CompilerParams(
        vmem_limit_bytes=VMEM_BYTES, collective_id=collective, has_side_effects=True
    )


def held(shape):
    rank = len(shape)
    return pl.BlockSpec(shape, lambda i: (0,) * rank, pipeline_mode=pl.Buffered(1))


def resident(shape):
    rank = len(shape)
    return pl.BlockSpec(shape, lambda i: (0,) * rank)


def run_begin(shares, rows, sequences, gain, bias, qkv_bias, collective):
    small, large = rows[:2]
    n_small, n_large = small.shape[0], 1
    width = small.shape[-1]
    pairs = HEADS // 2
    count = n_small * SPAD + n_large * LPAD
    line = n_small * SPAD + n_large * LLEN
    anywhere = pl.BlockSpec(memory_space=pl.ANY)
    sems = pltpu.SemaphoreType.DMA
    column = pl.BlockSpec((count, LANES), lambda i: (0, i))
    wholes = [(ZS, 2, 2) + s.shape for s in shares]

    def per_pair(shape):
        tail = (0,) * (len(shape) - 1)
        return pl.BlockSpec((2,) + shape[1:], lambda i: (i,) + tail)

    probs = [(HEADS, n_small, SPAD, SPAD), (HEADS, n_large, LPAD, LPAD)]
    return pl.pallas_call(
        functools.partial(begin_kernel, n_small, n_large),
        grid=(pairs,),
        in_specs=[anywhere] * 7
        + [per_pair(s.shape) for s in sequences]
        + [held(gain.shape), held(bias.shape), held(qkv_bias.shape)],
        out_specs=[anywhere] * 7 + [column, column] + [per_pair(p) for p in probs],
        out_shape=[
            jax.ShapeDtypeStruct((line, width), BF16),
            jax.ShapeDtypeStruct((line, width), BF16),
            jax.ShapeDtypeStruct((3 * pairs, count, LANES), BF16),
            jax.ShapeDtypeStruct((width, count), BF16),
        ]
        + [jax.ShapeDtypeStruct(w, BF16) for w in wholes]
        + [
            jax.ShapeDtypeStruct((count, width), BF16),
            jax.ShapeDtypeStruct((count, width), F32),
        ]
        + [jax.ShapeDtypeStruct(p, BF16) for p in probs],
        scratch_shapes=[
            pltpu.VMEM((line, width), BF16),
            pltpu.VMEM((line, width), BF16),
            pltpu.VMEM((count, width), BF16),
            pltpu.VMEM((width, count), BF16),
            pltpu.VMEM((3 * pairs, count, LANES), BF16),
            pltpu.VMEM(wholes[0], BF16),
            pltpu.VMEM((24, L_WIDTH), F32),
            pltpu.VMEM((16, S_WIDTH), F32),
            pltpu.VMEM((LPAD, 640), F32),
            pltpu.VMEM((SPAD, 256), F32),
            sems((3, Gather.n_sems)),
            sems((3, Gather.n_sems)),
            sems((3,)),
            sems((2, n_small + 1)),
            sems((2,)),
            sems((2,)),
            sems((5,)),
        ],
        compiler_params=params(collective),
    )(*shares, *rows, *sequences, gain, bias, qkv_bias)


def run_end(qkv, dattended, out_wide, probs, grads, rows, feed_grads, gain, n_small, collective):
    count, width = dattended.shape
    pairs = HEADS // 2
    line = rows[0].shape[0]
    anywhere = pl.BlockSpec(memory_space=pl.ANY)
    inside = pl.BlockSpec(memory_space=pltpu.VMEM)
    sems = pltpu.SemaphoreType.DMA
    column = pl.BlockSpec((count, LANES), lambda i: (0, i))
    shares = [(g.shape[0] // 16, g.shape[1]) for g in grads]
    shares += [(width // 16, 3 * LANES * many) for many in (EARLY, pairs - EARLY)]
    smalls = [feed_grads.shape, (8, width), (2 * HEADS, L_WIDTH), (2 * HEADS, S_WIDTH)]

    def third(which):
        return pl.BlockSpec((1, count, LANES), lambda i: (which * pairs + i, 0, 0))

    def per_pair(shape):
        tail = (0,) * (len(shape) - 1)
        return pl.BlockSpec((2,) + shape[1:], lambda i: (i,) + tail)

    scratch = [
        pltpu.VMEM((24, L_WIDTH), F32),
        pltpu.VMEM((16, S_WIDTH), F32),
        pltpu.VMEM((SPAD, 384), F32),
        pltpu.VMEM((LPAD, 768), F32),
        pltpu.VMEM((3 * pairs, count, LANES), BF16),
        pltpu.VMEM((width, count), BF16),
        pltpu.VMEM((ZS, 2, 2, width // 16, 3 * width), BF16),
        pltpu.VMEM((line, width), BF16),
        pltpu.VMEM((SLEN - SPAD, width), BF16),
        pltpu.VMEM((ZS, 2, 2) + shares[2], BF16),
        pltpu.VMEM((ZS, 2, 2) + shares[3], BF16),
        pltpu.VMEM(smalls[1], F32),
        pltpu.VMEM(smalls[2], F32),
        pltpu.VMEM(smalls[3], F32),
    ]
    for shape in shares:
        scratch += Reduce.scratch(*shape)
    for shape in smalls:
        scratch += Total.scratch(shape)
    scratch += [
        sems((4, Reduce.n_sems)),
        sems((4, Reduce.n_sems)),
        sems((4, ZS)),
        sems((4, Total.n_steps)),
        sems((4, Total.n_steps)),
        sems((5,)),
        sems((2, 2 * n_small + 1)),
        sems((2,)),
        sems((2,)),
    ]
    small = jax.ShapeDtypeStruct((n_small, SLEN, width), BF16)
    large = jax.ShapeDtypeStruct((2, LLEN // 2, width), BF16)
    return pl.pallas_call(
        functools.partial(end_kernel, n_small, 1),
        grid=(pairs,),
        in_specs=[third(0), third(1), third(2), column, column]
        + [per_pair(p.shape) for p in probs]
        + [anywhere] * 7
        + [held(feed_grads.shape), held(gain.shape)],
        out_specs=[anywhere] * 4 + [inside] * 8,
        out_shape=[small, large, small, large]
        + [jax.ShapeDtypeStruct(s, F32) for s in shares + smalls],
        scratch_shapes=scratch,
        compiler_params=params(collective),
        cost_estimate=pl.CostEstimate(
            flops=40 * 10**9, bytes_accessed=50 * 10**6, transcendentals=0
        ),
    )(
        qkv,
        qkv,
        qkv,
        dattended,
        out_wide,
        *probs,
        *[g.reshape((ZS, 2, 2) + s) for g, s in zip(grads, shares)],
        *rows,
        feed_grads,
        gain,
    )


def run_feed(x, attended, cot, w_mid, w_down, vectors, up_bias, n_small):
    rows, width = attended.shape
    size = chunk_rows(rows)
    hidden = w_down.shape[0]
    tiles = hidden // width
    block = pl.BlockSpec((size, width), lambda i: (i, 0))
    anywhere = pl.BlockSpec(memory_space=pl.ANY)
    return pl.pallas_call(
        functools.partial(feed_kernel, n_small, tiles),
        grid=(rows // size,),
        in_specs=[
            block,
            block,
            block,
            anywhere,
            anywhere,
            held(vectors.shape),
            held(up_bias.shape),
        ],
        out_specs=[
            block,
            block,
            block,
            resident((16, width)),
            anywhere,
            anywhere,
        ],
        out_shape=[
            jax.ShapeDtypeStruct((rows, width), BF16),
            jax.ShapeDtypeStruct((rows, width), F32),
            jax.ShapeDtypeStruct((rows, width), BF16),
            jax.ShapeDtypeStruct((16, width), F32),
            jax.ShapeDtypeStruct((width, width + hidden), BF16),
            jax.ShapeDtypeStruct((hidden, width), BF16),
        ],
        scratch_shapes=[
            pltpu.VMEM((width, width + hidden), BF16),
            pltpu.VMEM((hidden, width), BF16),
            pltpu.VMEM((size, hidden), BF16),
            pltpu.VMEM((size, hidden), BF16),
            pltpu.VMEM((width, width), F32),
            pltpu.VMEM((width, hidden), F32),
            pltpu.VMEM((hidden, width), F32),
            pltpu.SemaphoreType.DMA((1 + 2 * tiles,)),
        ],
        compiler_params=params(),
        cost_estimate=pl.CostEstimate(
            flops=6 * rows * width * (width + 2 * hidden),
            bytes_accessed=40 * 10**6,
            transcendentals=2 * rows * hidden,
        ),
    )(x, attended, cot, w_mid, w_down, vectors, up_bias)


def shifted(array, axis, by):
    count = lax.axis_size(axis)
    return lax.ppermute(array, axis, [(i, (i + by) % count) for i in range(count)])


def layer_norm(values, gain, bias):
    center = values - jnp.mean(values, axis=-1, keepdims=True)
    spread = jnp.mean(center * center, axis=-1, keepdims=True)
    return center * lax.rsqrt(spread + EPSILON) * gain + bias


def matmul(left, right):
    return jnp.dot(left, right, preferred_element_type=jnp.float32)


def position_bias(table, places, length, grid):
    heads = table.shape[0]
    span = 2 * LGRID - 1
    total_rel = table.shape[1]
    queries_count = places.shape[0]
    grid_table = table[:, : span * span].reshape(heads, span, span)
    patch = places - 1
    query_row = patch // grid
    query_col = patch % grid
    steps_all = jnp.arange(span, dtype=jnp.int32)
    cells = jnp.arange(grid, dtype=jnp.int32)
    row_hot = (
        steps_all[None, :, None] == query_row[:, None, None] - cells[None, None, :] + LGRID - 1
    ).astype(jnp.float32)
    col_hot = (
        steps_all[None, :, None] == query_col[:, None, None] - cells[None, None, :] + LGRID - 1
    ).astype(jnp.float32)
    partial_bias = jnp.einsum("hab,qbc->hqac", grid_table, col_hot, precision=lax.Precision.HIGHEST)
    patches = jnp.einsum(
        "qar,hqac->hqrc", row_hot, partial_bias, precision=lax.Precision.HIGHEST
    ).reshape(heads, queries_count, grid * grid)
    rest = length - 1 - grid * grid
    class_key = jnp.broadcast_to(table[:, total_rel - 2][:, None, None], (heads, queries_count, 1))
    patch_rows = jnp.concatenate(
        [class_key, patches, jnp.zeros((heads, queries_count, rest), jnp.float32)], axis=2
    )
    class_row = jnp.concatenate(
        [
            table[:, total_rel - 1][:, None],
            jnp.broadcast_to(table[:, total_rel - 3][:, None], (heads, grid * grid)),
            jnp.zeros((heads, rest), jnp.float32),
        ],
        axis=1,
    )
    is_class = (places == 0)[None, :, None]
    return jnp.where(is_class, class_row[:, None, :], patch_rows)


def to_heads(block, heads):
    groups, rows, width = block.shape
    return block.reshape(groups, rows, heads, width // heads)


def block_scores(query, key, query_rows, key_rows, length, bias_full):
    size = query.shape[-1] // HEADS
    raw = jnp.einsum(
        "gqhd,gkhd->ghqk",
        to_heads(query, HEADS),
        to_heads(key, HEADS),
        preferred_element_type=jnp.float32,
    )
    key_place = key_rows % length
    select = (key_place[:, None] == jnp.arange(length, dtype=jnp.int32)[None, :]).astype(
        jnp.float32
    )
    bias_block = jnp.einsum("hql,kl->hqk", bias_full, select, precision=lax.Precision.HIGHEST)
    allowed = (query_rows // length)[:, None] == (key_rows // length)[None, :]
    scores = raw * float(size) ** (-0.5) + bias_block[None]
    return (scores, allowed, select)


def key_rows_of(source, count_keys):
    return source * count_keys + jnp.arange(count_keys, dtype=jnp.int32)


def allowed_mask(allowed, key_rows, length, grid):
    return allowed & (key_rows % length < grid * grid + 1)[None, :]


def absorb_one(state, query, key, value, query_rows, key_rows, info):
    length, grid, bias_full = info
    maximum, total, accum = state
    scores, allowed, select = block_scores(query, key, query_rows, key_rows, length, bias_full)
    allowed = allowed_mask(allowed, key_rows, length, grid)
    masked = jnp.where(allowed[None, None], scores, NEGATIVE)
    newmax = jnp.maximum(maximum, jnp.max(masked, axis=-1))
    weights = jnp.where(allowed[None, None], jnp.exp(scores - newmax[..., None]), 0.0)
    factor = jnp.exp(maximum - newmax)
    total = total * factor + jnp.sum(weights, axis=-1)
    accum = accum * factor[..., None] + jnp.einsum(
        "ghqk,gkhd->ghqd",
        weights.astype(jnp.bfloat16),
        to_heads(value, HEADS),
        preferred_element_type=jnp.float32,
    )
    return (newmax, total, accum)


def absorb_cycle(states, queries, moving, members, query_rows, source, info):
    states = list(states)
    for which, offset, rows in members:
        key = moving[0][:, offset : offset + rows]
        value = moving[1][:, offset : offset + rows]
        states[which] = absorb_one(
            states[which],
            queries[which],
            key,
            value,
            query_rows[which],
            key_rows_of(source, rows),
            info[which],
        )
    return tuple(states)


def pass_forward(moving):
    return shifted((moving[0], moving[1]), "seq", 1)


def cycle_forward(queries, cycle_pair, members, query_rows, info):
    position = lax.axis_index("seq")
    count = lax.axis_size("seq")
    states = []
    for which in range(2):
        groups, rows, width = queries[which].shape
        states.append(
            (
                jnp.full((groups, HEADS, rows), NEGATIVE, jnp.float32),
                jnp.zeros((groups, HEADS, rows), jnp.float32),
                jnp.zeros((groups, HEADS, rows, width // HEADS), jnp.float32),
            )
        )
    states = absorb_cycle(tuple(states), queries, cycle_pair, members, query_rows, position, info)

    def turn(step, carry):
        held_states, moving = carry
        moving = tuple(pass_forward(moving))
        held_states = absorb_cycle(
            held_states, queries, moving, members, query_rows, (position - step) % count, info
        )
        return (held_states, moving)

    states, moving = lax.fori_loop(1, count, turn, (states, cycle_pair))
    attended = []
    logsums = []
    for which in range(2):
        maximum, total, accum = states[which]
        groups, heads_count, rows, size = accum.shape
        attended.append(
            jnp.transpose(accum / total[..., None], (0, 2, 1, 3)).reshape(
                groups, rows, heads_count * size
            )
        )
        logsums.append(maximum + jnp.log(total))
    return (tuple(attended), tuple(logsums))


def visit_one(query, dout, logsum, delta, key, value, query_rows, key_rows, info):
    length, grid, bias_full = info
    groups, count_keys, width = key.shape
    scale = float(width // HEADS) ** (-0.5)
    scores, allowed, select = block_scores(query, key, query_rows, key_rows, length, bias_full)
    allowed = allowed_mask(allowed, key_rows, length, grid)
    probs = jnp.where(allowed[None, None], jnp.exp(scores - logsum[..., None]), 0.0)
    dout_heads = to_heads(dout, HEADS)
    dprobs = jnp.einsum(
        "gqhd,gkhd->ghqk", dout_heads, to_heads(value, HEADS), preferred_element_type=jnp.float32
    )
    dscores = (probs * (dprobs - delta[..., None])).astype(jnp.bfloat16)
    dq_term = scale * jnp.einsum(
        "ghqk,gkhd->gqhd", dscores, to_heads(key, HEADS), preferred_element_type=jnp.float32
    )
    dkey_term = jnp.einsum(
        "ghqk,gqhd->gkhd", dscores, to_heads(query, HEADS), preferred_element_type=jnp.float32
    )
    dvalue_term = jnp.einsum(
        "ghqk,gqhd->gkhd",
        probs.astype(jnp.bfloat16),
        dout_heads,
        preferred_element_type=jnp.float32,
    )
    summed = jnp.sum(dscores.astype(jnp.float32), axis=0)
    bias_term = jnp.einsum("hqk,kl->hql", summed, select, precision=lax.Precision.HIGHEST)
    return (
        dq_term,
        scale * dkey_term.reshape(groups, count_keys, width),
        dvalue_term.reshape(groups, count_keys, width),
        bias_term,
    )


def visit_cycle(carry, queries, douts, logsums, deltas, moving, members, query_rows, source, info):
    dqueries, dpair, bias_grads = carry
    dqueries = list(dqueries)
    bias_grads = list(bias_grads)
    key_pieces = []
    value_pieces = []
    for which, offset, rows in members:
        key = moving[0][:, offset : offset + rows]
        value = moving[1][:, offset : offset + rows]
        dq_term, dk_term, dv_term, bias_term = visit_one(
            queries[which],
            douts[which],
            logsums[which],
            deltas[which],
            key,
            value,
            query_rows[which],
            key_rows_of(source, rows),
            info[which],
        )
        dqueries[which] = dqueries[which] + dq_term
        key_pieces.append(dk_term)
        value_pieces.append(dv_term)
        bias_grads[which] = bias_grads[which] + bias_term
    new_pair = (
        dpair[0] + jnp.concatenate(key_pieces, axis=1),
        dpair[1] + jnp.concatenate(value_pieces, axis=1),
    )
    return (tuple(dqueries), new_pair, tuple(bias_grads))


def send_grads(dpair):
    return tuple(shifted((dpair[0], dpair[1]), "seq", 1))


def cycle_backward(queries, douts, logsums, deltas, cycle_pair, members, query_rows, info, start):
    position = lax.axis_index("seq")
    count = lax.axis_size("seq")
    dpair = tuple((jnp.zeros(item.shape, jnp.float32) for item in cycle_pair))

    def turn(step, state):
        carry, moving = state
        carry = visit_cycle(
            carry,
            queries,
            douts,
            logsums,
            deltas,
            moving,
            members,
            query_rows,
            (position - step) % count,
            info,
        )
        moving = tuple(shifted((moving[0], moving[1]), "seq", 1))
        return ((carry[0], send_grads(carry[1]), carry[2]), moving)

    carry, moving = lax.fori_loop(0, count - 1, turn, ((start[0], dpair, start[1]), cycle_pair))
    carry = visit_cycle(
        carry,
        queries,
        douts,
        logsums,
        deltas,
        moving,
        members,
        query_rows,
        (position - count + 1) % count,
        info,
    )
    return (carry[0], send_grads(carry[1]), carry[2])


def general_device(
    small_in,
    large_in,
    small_cot,
    large_cot,
    first_gain,
    first_bias,
    query_weight,
    query_bias,
    key_weight,
    value_weight,
    value_bias,
    out_weight,
    out_bias,
    attend_scale,
    second_gain,
    second_bias,
    up_weight,
    up_bias,
    down_weight,
    down_bias,
    feed_scale,
    rel_table,
):
    groups, small_rows, width = small_in.shape
    large_rows = large_in.shape[1]
    all_rows = small_rows + large_rows
    position = lax.axis_index("seq")
    query_rows = (
        position * small_rows + jnp.arange(small_rows, dtype=jnp.int32),
        position * large_rows + jnp.arange(large_rows, dtype=jnp.int32),
    )
    small_places = query_rows[0] % SLEN
    large_places = query_rows[1] % LLEN

    def make_biases(table):
        return (
            position_bias(table, small_places, SLEN, SGRID),
            position_bias(table, large_places, LLEN, LGRID),
        )

    biases, bias_back = jax.vjp(make_biases, rel_table)
    info = ((SLEN, SGRID, biases[0]), (LLEN, LGRID, biases[1]))
    valid_rows = jnp.concatenate(
        [small_places < SGRID * SGRID + 1, large_places < LGRID * LGRID + 1]
    )
    valid_flat = jnp.broadcast_to(valid_rows[None, :], (groups, all_rows)).reshape(-1)
    w_query, w_key, w_value, w_out, w_up, w_down = (
        lax.all_gather(query_weight, "img", axis=0, tiled=True),
        lax.all_gather(key_weight, "img", axis=0, tiled=True),
        lax.all_gather(value_weight, "img", axis=0, tiled=True),
        lax.all_gather(out_weight, "img", axis=0, tiled=True),
        lax.all_gather(up_weight, "img", axis=0, tiled=True),
        lax.all_gather(down_weight, "img", axis=0, tiled=True),
    )

    def split(rows_array):
        shaped = rows_array.reshape(groups, all_rows, -1)
        return (shaped[:, :small_rows], shaped[:, small_rows:])

    inputs = jnp.concatenate([small_in, large_in], axis=1).astype(jnp.float32).reshape(-1, width)
    hidden = layer_norm(inputs, first_gain, first_bias).astype(jnp.bfloat16)
    query = (matmul(hidden, w_query) + query_bias).astype(jnp.bfloat16)
    key = matmul(hidden, w_key).astype(jnp.bfloat16)
    value = (matmul(hidden, w_value) + value_bias).astype(jnp.bfloat16)
    queries = split(query)
    cycle_pair = (key.reshape(groups, all_rows, width), value.reshape(groups, all_rows, width))
    members = ((0, 0, small_rows), (1, small_rows, large_rows))
    attended, logsums = cycle_forward(queries, cycle_pair, members, query_rows, info)
    mixed = (
        jnp.concatenate([attended[0], attended[1]], axis=1).reshape(-1, width).astype(jnp.bfloat16)
    )
    branch = matmul(mixed, w_out) + out_bias
    residual = inputs + attend_scale * branch
    hidden2 = layer_norm(residual, second_gain, second_bias).astype(jnp.bfloat16)
    upper = matmul(hidden2, w_up) + up_bias
    active = jax.nn.gelu(upper, approximate=False).astype(jnp.bfloat16)
    lower = matmul(active, w_down) + down_bias
    output = jnp.where(valid_flat[:, None], residual + feed_scale * lower, 0.0).astype(jnp.bfloat16)
    small_out, large_out = split(output)
    upstream = (
        jnp.concatenate([small_cot, large_cot], axis=1).astype(jnp.float32).reshape(-1, width)
    )
    upstream = upstream * valid_flat[:, None].astype(jnp.float32)
    grad_feed_scale = jnp.sum(upstream * lower, axis=0)
    dlower = (upstream * feed_scale).astype(jnp.bfloat16)
    grad_down_bias = jnp.sum(dlower.astype(jnp.float32), axis=0)
    grad_down = jnp.einsum("rf,rd->fd", active, dlower, preferred_element_type=jnp.float32)
    dactive = jnp.einsum("rd,fd->rf", dlower, w_down, preferred_element_type=jnp.float32)
    unused, gelu_back = jax.vjp(lambda inner: jax.nn.gelu(inner, approximate=False), upper)
    dupper = gelu_back(dactive)[0].astype(jnp.bfloat16)
    grad_up_bias = jnp.sum(dupper.astype(jnp.float32), axis=0)
    grad_up = jnp.einsum("rd,rf->df", hidden2, dupper, preferred_element_type=jnp.float32)
    dhidden2 = jnp.einsum("rf,df->rd", dupper, w_up, preferred_element_type=jnp.float32)
    unused, second_back = jax.vjp(layer_norm, residual, second_gain, second_bias)
    dres_part, grad_second_gain, grad_second_bias = second_back(dhidden2)
    dresidual = upstream + dres_part
    grad_attend_scale = jnp.sum(dresidual * branch, axis=0)
    dbranch = (dresidual * attend_scale).astype(jnp.bfloat16)
    grad_out_bias = jnp.sum(dbranch.astype(jnp.float32), axis=0)
    grad_out = jnp.einsum("rd,re->de", mixed, dbranch, preferred_element_type=jnp.float32)
    dmixed = jnp.einsum("re,de->rd", dbranch, w_out, preferred_element_type=jnp.float32).astype(
        jnp.bfloat16
    )
    held, held_sums = cycle_forward(queries, cycle_pair, members, query_rows, info)
    douts = split(dmixed)
    deltas = tuple(
        (
            jnp.einsum(
                "gqhd,gqhd->ghq",
                to_heads(douts[which].astype(jnp.float32), HEADS),
                to_heads(held[which], HEADS),
            )
            for which in range(2)
        )
    )
    dq_start = tuple(
        (jnp.zeros(to_heads(queries[which], HEADS).shape, jnp.float32) for which in range(2))
    )
    bias_start = tuple((jnp.zeros(item.shape, jnp.float32) for item in biases))
    dqueries, dpair, bias_grads = cycle_backward(
        queries,
        douts,
        held_sums,
        deltas,
        cycle_pair,
        members,
        query_rows,
        info,
        (dq_start, bias_start),
    )
    table_grad = bias_back(bias_grads)[0]
    dquery = jnp.concatenate(
        [
            dqueries[0].reshape(groups, small_rows, width),
            dqueries[1].reshape(groups, large_rows, width),
        ],
        axis=1,
    )
    dquery = dquery.reshape(-1, width).astype(jnp.bfloat16)
    dkey = dpair[0].reshape(-1, width).astype(jnp.bfloat16)
    dvalue = dpair[1].reshape(-1, width).astype(jnp.bfloat16)
    grad_query_bias = jnp.sum(dquery.astype(jnp.float32), axis=0)
    grad_value_bias = jnp.sum(dvalue.astype(jnp.float32), axis=0)
    grad_query = jnp.einsum("rd,re->de", hidden, dquery, preferred_element_type=jnp.float32)
    grad_key = jnp.einsum("rd,re->de", hidden, dkey, preferred_element_type=jnp.float32)
    grad_value = jnp.einsum("rd,re->de", hidden, dvalue, preferred_element_type=jnp.float32)
    dhidden = (
        jnp.einsum("re,de->rd", dquery, w_query, preferred_element_type=jnp.float32)
        + jnp.einsum("re,de->rd", dkey, w_key, preferred_element_type=jnp.float32)
        + jnp.einsum("re,de->rd", dvalue, w_value, preferred_element_type=jnp.float32)
    )
    unused, first_back = jax.vjp(layer_norm, inputs, first_gain, first_bias)
    dinput_part, grad_first_gain, grad_first_bias = first_back(dhidden)
    dinputs = (dresidual + dinput_part).astype(jnp.bfloat16)
    small_grad, large_grad = split(dinputs)
    shares = (
        lax.psum_scatter(grad_query, "img", scatter_dimension=0, tiled=True),
        lax.psum_scatter(grad_key, "img", scatter_dimension=0, tiled=True),
        lax.psum_scatter(grad_value, "img", scatter_dimension=0, tiled=True),
        lax.psum_scatter(grad_out, "img", scatter_dimension=0, tiled=True),
        lax.psum_scatter(grad_up, "img", scatter_dimension=0, tiled=True),
        lax.psum_scatter(grad_down, "img", scatter_dimension=0, tiled=True),
    )
    shares = lax.psum((shares[0], shares[1], shares[2], shares[3], shares[4], shares[5]), "seq")
    smalls = lax.psum(
        (
            grad_first_gain,
            grad_first_bias,
            grad_query_bias,
            grad_value_bias,
            grad_out_bias,
            grad_attend_scale,
            grad_second_gain,
            grad_second_bias,
            grad_up_bias,
            grad_down_bias,
            grad_feed_scale,
            table_grad,
        ),
        ("img", "seq"),
    )
    return (
        small_out,
        large_out,
        small_grad,
        large_grad,
        smalls[0],
        smalls[1],
        shares[0],
        smalls[2],
        shares[1],
        shares[2],
        smalls[3],
        shares[3],
        smalls[4],
        smalls[5],
        smalls[6],
        smalls[7],
        shares[4],
        smalls[8],
        shares[5],
        smalls[9],
        smalls[10],
        smalls[11],
    )


def image_device(
    small_in,
    large_in,
    small_cot,
    large_cot,
    first_gain,
    first_bias,
    query_weight,
    query_bias,
    key_weight,
    value_weight,
    value_bias,
    out_weight,
    out_bias,
    attend_scale,
    second_gain,
    second_bias,
    up_weight,
    up_bias,
    down_weight,
    down_bias,
    feed_scale,
    rel_table,
):
    groups, small_rows, width = small_in.shape
    large_rows = large_in.shape[1]
    n_small = groups * small_rows // SLEN
    n_large = 1
    small_part = n_small * SPAD

    qkv_share = jnp.concatenate([query_weight, key_weight, value_weight], axis=1)
    mid_share = jnp.concatenate([out_weight, up_weight], axis=1)
    gain, bias = first_gain[None], first_bias[None]
    qkv_bias = jnp.concatenate([query_bias, jnp.zeros_like(query_bias), value_bias])[None]
    vectors = jnp.stack(
        [out_bias, attend_scale, second_gain, second_bias, down_bias, feed_scale]
        + [feed_scale] * 2
    )
    x, cot, qkv, turned, w_qkv, w_mid, w_down, attended, out_wide, *probs = run_begin(
        [qkv_share, mid_share, down_weight],
        [
            small_in.reshape(n_small, SLEN, width),
            large_in,
            small_cot.reshape(n_small, SLEN, width),
            large_cot,
        ],
        table_sequences(rel_table),
        gain,
        bias,
        qkv_bias,
        1,
    )
    w_mid, w_down = (w.reshape(-1, w.shape[-1]) for w in (w_mid, w_down))
    out, dresidual, dattended, vector_grads, g_mid, g_down = run_feed(
        x, attended, cot, w_mid, w_down, vectors, up_bias[None], n_small
    )
    (
        small_out,
        large_out,
        small_grad,
        large_grad,
        g_mid,
        g_down,
        g_early,
        g_late,
        vector_grads,
        input_grads,
        d_large,
        d_small,
    ) = run_end(
        qkv,
        dattended,
        out_wide,
        probs,
        [g_mid, g_down],
        [x, turned, w_qkv, dresidual, out],
        vector_grads,
        gain,
        n_small,
        2,
    )
    small_out, small_grad = (v.reshape(groups, small_rows, width) for v in (small_out, small_grad))
    parts = (g.reshape(g.shape[0], -1, 3, LANES) for g in (g_early, g_late))
    g_query, g_key, g_value = (
        jnp.moveaxis(jnp.concatenate(list(parts), axis=1), 2, 0).reshape(3, -1, width)
    )
    heads = HEADS
    d_large = d_large.reshape(heads, 2, L_WIDTH)
    d_small = d_small.reshape(heads, 2, S_WIDTH)
    edge_grad = d_small[:, 0, S_WIDTH - 3 :]
    table_grad = table_from_sequences(d_large, d_small, edge_grad)
    return (
        small_out,
        large_out,
        small_grad,
        large_grad,
        input_grads[3],
        input_grads[4],
        g_query,
        input_grads[0],
        g_key,
        g_value,
        input_grads[2],
        g_mid[:, :width],
        vector_grads[0],
        vector_grads[1],
        vector_grads[2],
        vector_grads[3],
        g_mid[:, width:],
        vector_grads[8:12].reshape(-1),
        g_down,
        vector_grads[4],
        vector_grads[5],
        table_grad,
    )


def per_device(*args):
    groups, small_rows, unused = args[0].shape
    if lax.axis_size("seq") == 2 and groups == 2 and small_rows % SLEN == 0:
        return image_device(*args)
    return general_device(*args)


def solution(mesh):
    return jax.shard_map(
        per_device,
        mesh=mesh,
        in_specs=(
            P("img", "seq", None),
            P("img", "seq", None),
            P("img", "seq", None),
            P("img", "seq", None),
            P(),
            P(),
            P("img", None),
            P(),
            P("img", None),
            P("img", None),
            P(),
            P("img", None),
            P(),
            P(),
            P(),
            P(),
            P("img", None),
            P(),
            P("img", None),
            P(),
            P(),
            P(),
        ),
        out_specs=(
            P("img", "seq", None),
            P("img", "seq", None),
            P("img", "seq", None),
            P("img", "seq", None),
            P(),
            P(),
            P("img", None),
            P(),
            P("img", None),
            P("img", None),
            P(),
            P("img", None),
            P(),
            P(),
            P(),
            P(),
            P("img", None),
            P(),
            P("img", None),
            P(),
            P(),
            P(),
        ),
        check_vma=False,
    )
```

```python
import functools

import jax
import jax.numpy as jnp
from jax import lax
from jax.experimental import pallas as pl
from jax.experimental.pallas import tpu as pltpu
from jax.sharding import PartitionSpec as P

HEADS = 12
SGRID = 14
LGRID = 24
SLEN = 256
LLEN = 640
SPAD = 208
LPAD = 608
LANES = 128

NEGATIVE = -1e30
EPSILON = 1e-06
F32 = jnp.float32
BF16 = jnp.bfloat16
VMEM_BYTES = 62 << 20


def dot_nn(left, right):
    return lax.dot_general(left, right, (((1,), (0,)), ((), ())), preferred_element_type=F32)


def dot_nt(left, right):
    return lax.dot_general(left, right, (((1,), (1,)), ((), ())), preferred_element_type=F32)


def normalized(values):
    center = values - jnp.mean(values, axis=-1, keepdims=True)
    spread = jnp.mean(center * center, axis=-1, keepdims=True)
    scale = lax.rsqrt(spread + EPSILON)
    return center * scale, scale


def norm_back(grad, normal, scale):
    return scale * (
        grad
        - jnp.mean(grad, axis=-1, keepdims=True)
        - normal * jnp.mean(grad * normal, axis=-1, keepdims=True)
    )


def row_sum(values):
    return jnp.sum(values, axis=0, keepdims=True)


def iota(shape, axis):
    return lax.broadcasted_iota(jnp.int32, shape, axis)


L_WIDTH = 1280
S_WIDTH = 512


SPAN = 2 * LGRID - 1
CELLS = SPAN * SPAN
T_WIDTH = 2304


def row_moves():
    off = LGRID - SGRID
    moves = []
    for m in range(SPAN):
        moves.append((m * SPAN, m * LGRID, LGRID, False, True))
        moves.append((m * SPAN + LGRID, (m + 1) * LGRID, LGRID - 1, True, True))
    for m in range(2 * SGRID - 1):
        start = (m + off) * SPAN + off
        moves.append((start, m * SGRID, SGRID, False, False))
        moves.append((start + SGRID, (m + 1) * SGRID, SGRID - 1, True, False))
    return moves


def moved(source, start, target, width, count):
    source_tile = min(start // LANES, source.shape[1] // LANES - 2)
    target_tile = min(target // LANES, width // LANES - 2)
    piece = source[:, source_tile * LANES : source_tile * LANES + 256]
    turn = (target - target_tile * LANES - start + source_tile * LANES) % 256
    if turn:
        piece = pltpu.roll(piece, turn, 1)
    lane = iota(piece.shape, 1) - (target - target_tile * LANES)
    return slice(target_tile * LANES, target_tile * LANES + 256), piece, (lane >= 0) & (lane < count)


def table_sequences(table, wide_table, lows, highs):
    heads, entries = table.shape
    wide_table[...] = jnp.zeros_like(wide_table)
    wide_table[pl.ds(0, heads), pl.ds(0, entries)] = table[...]
    for ref in lows + highs:
        ref[...] = jnp.zeros_like(ref)
    for start, place_at, count, high, large in row_moves():
        ref = (highs if high else lows)[0 if large else 1]
        where, piece, inside = moved(wide_table, start, place_at, ref.shape[1], count)
        ref[:, where] = jnp.where(inside, piece, ref[:, where])


def table_from_sequences(lows, highs, wide_table):
    wide_table[...] = jnp.zeros_like(wide_table)
    for start, place_at, count, high, large in row_moves():
        ref = (highs if high else lows)[0 if large else 1]
        where, piece, inside = moved(ref, place_at, start, T_WIDTH, count)
        wide_table[:, where] += jnp.where(inside, piece, 0.0)
    where, piece, inside = moved(lows[1], S_WIDTH - 3, CELLS, T_WIDTH, 3)
    wide_table[:, where] += jnp.where(inside, piece, 0.0)


def one_entry(row, place_at):
    return jnp.sum(jnp.where(iota(row.shape, 1) == place_at, row, 0.0), axis=1, keepdims=True)


def takes_low(rows, width, grid, first):
    step = iota((rows, width), 1) % grid
    row = iota((rows, width), 0)
    low = step >= grid - 1 + first - row
    if first == 1:
        low = low | (row == 0)
    return low


def spread_sequences(low, high, rows, width, grid, first):
    low = jnp.broadcast_to(low, (rows, width))
    high = jnp.broadcast_to(high, (rows, width))
    chosen = jnp.where(takes_low(rows, width, grid, first), low, high)
    return pltpu.roll(chosen, 1, 1, stride=1, stride_axis=0)


def gather_sequences(spread, rows, width, grid, first):
    row = iota((rows, width), 0) + 1
    for bit in (1, 2, 4, 8, 16):
        spread = jnp.where((row & bit) != 0, pltpu.roll(spread, width - bit, 1), spread)
    low = takes_low(rows, width, grid, first)
    return (
        row_sum(jnp.where(low, spread, 0.0)),
        row_sum(jnp.where(low, 0.0, spread)),
    )


def large_window(block):
    start = (LGRID - block) * LGRID
    return start // LANES, start % LANES


def small_window(block):
    start = (SGRID - 1 - block) * SGRID + SGRID - 1
    return start // LANES, start % LANES


def head_masks():
    lane = iota((1, LANES), 1)
    return (
        jnp.where(lane < LANES // 2, 1.0, 0.0).astype(BF16),
        jnp.where(lane < LANES // 2, 0.0, 1.0).astype(BF16),
    )


def transposed_biases(large_seq, small_seq, entries, wide, narrow, bias_large, bias_small):
    patch_q, patch_k, both = (one_entry(entries, CELLS + i - T_WIDTH + 256) for i in range(3))
    wide[...] = spread_sequences(*large_seq, 24, L_WIDTH, LGRID, 1)
    lane = iota((24, LANES), 1)
    row = iota((24, LANES), 0)
    for block in range(LGRID + 1):
        at, turn = large_window(block)
        piece = wide[:, at * LANES : at * LANES + 768]
        if turn:
            piece = pltpu.roll(piece, 768 - turn, 1)
        piece = piece[:, :640]
        if block == 0:
            rest = jnp.where(iota((24, 640), 0) == 0, patch_k, piece)
        elif block == LGRID:
            rest = jnp.where(iota((24, 640), 0) == 0, piece, NEGATIVE)
        else:
            rest = piece
        first = jnp.where(lane == 0, patch_q, rest[:, :LANES])
        if block == 0:
            first = jnp.where((lane == 0) & (row == 0), both, first)
        if block == LGRID:
            first = jnp.where(row == 0, first, NEGATIVE)
        bias_large[pl.ds(block * 24, 24), 0:LANES] = first
        bias_large[pl.ds(block * 24, 24), LANES:640] = rest[:, LANES:]
    bias_large[pl.ds(600, 8), :] = jnp.full((8, 640), NEGATIVE, F32)
    narrow[...] = spread_sequences(*small_seq, 16, S_WIDTH, SGRID, 0)
    for block in range(SGRID):
        at, turn = small_window(block)
        piece = narrow[:, at * LANES : at * LANES + 384]
        if turn:
            piece = pltpu.roll(piece, 384 - turn, 1)
        bias_small[pl.ds(1 + SGRID * block, SGRID), :] = piece[:SGRID, :256]
    whole = bias_small[...]
    lane = iota((SPAD, 256), 1)
    row = iota((SPAD, 256), 0)
    whole = jnp.where(lane == 0, patch_q, whole)
    whole = jnp.where(row == 0, patch_k, whole)
    whole = jnp.where((lane == 0) & (row == 0), both, whole)
    bias_small[...] = jnp.where(row > SGRID * SGRID, NEGATIVE, whole)


MESH = pl.DeviceIdType.MESH
ZS = 4


def place():
    img = lax.axis_index("img")
    return img // 4, (img // 2) % 2, img % 2, lax.axis_index("seq")


def device(z, x, c, y):
    return ((z * 2 + x) * 2 + c, y)


def z_peer(z, hop):
    low = (z % 2) * (1 - 2 * (hop % 2)) + hop % 2
    high = (z // 2) * (1 - 2 * (hop // 2)) + hop // 2
    return high * 2 + low


def greet():
    z, x, c, y = place()
    barrier = pltpu.get_barrier_semaphore()
    peers = [device(z_peer(z, hop), x, c, y) for hop in range(1, ZS)]
    for flip in range(1, 8):
        peers.append(
            device(
                z,
                1 - x if flip & 1 else x,
                1 - c if flip & 2 else c,
                1 - y if flip & 4 else y,
            )
        )
    for peer in peers:
        pl.semaphore_signal(barrier, inc=1, device_id=peer, device_id_type=MESH)
    pl.semaphore_wait(barrier, len(peers))


def half_of(width, y):
    return pl.ds(pl.multiple_of(y * (width // 2), 128), width // 2)


class Gather:
    n_sems = 21

    def __init__(self, share, whole, send, recv, own, spare_seq):
        self.share, self.whole, self.send, self.recv, self.own = share, whole, send, recv, own
        self.spare_seq = spare_seq
        self.width = share.shape[1]
        self.at = z, x, c, y = place()
        self.inner = z % 3 != 0

    def copy(self, source, target, index, peer, recv=None):
        return pltpu.make_async_remote_copy(
            src_ref=source,
            dst_ref=target,
            send_sem=self.send.at[index],
            recv_sem=self.recv.at[index if recv is None else recv],
            device_id=peer,
            device_id_type=MESH,
        )

    def source_z(self, turn):
        z = self.at[0]
        is_inner = jnp.minimum(z % 3, 1)
        hop = (0, 1, 2 + is_inner, 3 - is_inner)[turn]
        return z_peer(z, hop)

    def along_z(self, turn, onto, recv):
        z, x, c, y = self.at
        cols = half_of(self.width, y)
        target = self.whole.at[self.source_z(turn), x, c, :, cols]
        source = self.share.at[:, cols] if turn == 0 else target
        index = {(0, 1): 0, (0, 3): 1, (1, 3): 2, (2, 1): 19, (3, 1): 20}[turn, onto]
        return self.copy(source, target, index, device(z_peer(z, onto), x, c, y), recv - 1)

    def from_z(self, turn):
        z, x, c, y = self.at
        cols = half_of(self.width, y)
        block = self.whole.at[self.source_z(turn), x, c, :, cols]
        return self.copy(block, block, turn - 1, device(z_peer(z, 1), x, c, y))

    def across(self, turn, axis):
        z, x, c, y = self.at
        cols = half_of(self.width, y)
        target = self.whole.at[self.source_z(turn), x, c, :, cols]
        source = self.share.at[:, cols] if turn == 0 else target
        peer = device(z, 1 - x, c, y) if axis == 0 else device(z, x, c, 1 - y)
        return self.copy(source, target, 3 + 4 * axis + turn, peer)

    def onward(self, turn):
        z, x, c, y = self.at
        source_z = self.source_z(turn)
        even = 1 if turn == 0 else 0 if self.spare_seq else 1 - source_z % 2
        side = x + even * (1 - 2 * x)
        cols = half_of(self.width, y + (1 - even) * (1 - 2 * y))
        block = self.whole.at[source_z, side, c, :, cols]
        peer = device(z, x + (1 - even) * (1 - 2 * x), c, y + even * (1 - 2 * y))
        return self.copy(block, block, 11 + turn, peer)

    def to_core(self, turn):
        z, x, c, y = self.at
        block = self.whole.at[self.source_z(turn), :, c]
        return self.copy(block, block, 15 + turn, device(z, x, 1 - c, y))

    def keep_own(self):
        z, x, c, y = self.at
        return pltpu.make_async_copy(self.share, self.whole.at[z, x, c], self.own)

    def begin(self):
        self.keep_own().start()
        self.across(0, 0).start()
        self.along_z(0, 1, 1).start()

        @pl.when(self.inner)
        def _():
            self.along_z(0, 3, 2).start()

    def come(self, hop):
        self.from_z(hop).wait_recv()

        @pl.when(self.inner)
        def _():
            if hop == 1:
                self.along_z(1, 3, 3).start()
            else:
                self.along_z(hop, 1, hop).start()

        for axis in range(2):
            self.across(hop, axis).start()

    def pass_on(self, hop):
        for axis in range(2 if hop else 1):
            self.across(hop, axis).wait_recv()
        self.onward(hop).start()

    def give(self, hop):
        if hop == 0:
            self.keep_own().wait()
        self.onward(hop).wait_recv()
        self.to_core(hop).start()

    def turn(self, at):
        stage, hop = (
            (self.come, 1),
            (self.pass_on, 0),
            (self.come, 2),
            (self.pass_on, 1),
            (self.come, 3),
            (self.pass_on, 2),
            (self.give, 0),
            (self.pass_on, 3),
            (self.give, 1),
            (self.give, 2),
            (self.give, 3),
        )[at]
        stage(hop)

    def arrive(self):
        for hop in range(ZS):
            self.to_core(hop).wait_recv()

    def drain(self):
        for hop in range(ZS):
            self.to_core(hop).wait_send()
            self.onward(hop).wait_send()
            for axis in range(2 if hop else 1):
                self.across(hop, axis).wait_send()
        self.along_z(0, 1, 1).wait_send()

        @pl.when(self.inner)
        def _():
            self.along_z(0, 3, 2).wait_send()
            self.along_z(1, 3, 3).wait_send()
            self.along_z(2, 1, 2).wait_send()
            self.along_z(3, 1, 3).wait_send()


class Rows:
    n_sems = 2

    def __init__(self, small, large, line, sems, send, recv):
        self.small, self.large, self.line = small, large, line
        self.sems, self.send, self.recv = sems, send, recv
        self.at = place()
        self.n_small = small.shape[0]
        self.base = self.n_small * SPAD
        self.rows = large.shape[1]

    def spot(self):
        start = self.base + self.rows * self.at[3]
        return self.line.at[pl.ds(pl.multiple_of(start, 16), self.rows)]

    def local(self, i):
        if i < self.n_small:
            return pltpu.make_async_copy(
                self.small.at[i, pl.ds(0, SPAD)],
                self.line.at[pl.ds(i * SPAD, SPAD)],
                self.sems.at[i],
            )
        return pltpu.make_async_copy(self.large.at[self.at[3]], self.spot(), self.sems.at[i])

    def remote(self):
        z, x, c, y = self.at
        return pltpu.make_async_remote_copy(
            src_ref=self.large.at[1 - y],
            dst_ref=self.spot(),
            send_sem=self.send,
            recv_sem=self.recv,
            device_id=device(z, x, c, 1 - y),
            device_id_type=MESH,
        )

    def begin(self):
        self.remote().start()
        for i in range(self.n_small + 1):
            self.local(i).start()

    def wait_small(self):
        for i in range(self.n_small):
            self.local(i).wait()

    def wait_large(self):
        self.local(self.n_small).wait()
        self.remote().wait()


def add_rows(target, source, shape):
    rows, cols = shape
    many = max(n for n in range(16, rows + 1, 16) if rows % n == 0 and n * cols <= 65536)

    def strip(i, unused):
        at = pl.ds(pl.multiple_of(i * many, 16), many)
        target[at, :] = (target[at, :].astype(F32) + source[at, :].astype(F32)).astype(BF16)
        return unused

    lax.fori_loop(0, rows // many, strip, 0)


class Reduce:
    n_sems = 21
    n_scratch = 6

    def __init__(self, grad, out, held, core, first, second, last, edge, send, recv, own, x_first):
        self.x_first = x_first
        self.grad, self.held, self.core = grad, held, core
        self.first, self.second, self.last, self.edge, self.out = first, second, last, edge, out
        self.send, self.recv, self.own = send, recv, own
        self.rows, self.width = out.shape
        self.at = place()
        self.mine = half_of(self.width, self.at[3])
        self.other = half_of(self.width, 1 - self.at[3])

    @staticmethod
    def scratch(rows, width):
        half = width // 2
        return [
            pltpu.VMEM((ZS, 2, rows, width), BF16),
            pltpu.VMEM((ZS, 2, rows, width), BF16),
            pltpu.VMEM((ZS, 2, rows, half), BF16),
            pltpu.VMEM((ZS, rows, half), BF16),
            pltpu.VMEM((ZS, rows, half), BF16),
            pltpu.VMEM((2, rows, half), BF16),
        ]

    def copy(self, source, target, index, peer):
        return pltpu.make_async_remote_copy(
            src_ref=source,
            dst_ref=target,
            send_sem=self.send.at[index],
            recv_sem=self.recv.at[index],
            device_id=peer,
            device_id_type=MESH,
        )

    def load(self, s):
        return pltpu.make_async_copy(
            self.grad.at[s, :, self.at[2]], self.held.at[s], self.own.at[s]
        )

    def between_cores(self, s):
        z, x, c, y = self.at
        return self.copy(self.grad.at[s, :, 1 - c], self.core.at[s], s, device(z, x, 1 - c, y))

    def leg_one(self, s, i):
        z, x, c, y = self.at
        half = self.width // 2
        if s in self.x_first:
            source = self.held.at[s, 1 - x, :, pl.ds(i * half, half)]
            peer = device(z, 1 - x, c, y)
        else:
            source = self.held.at[s, i, :, self.other]
            peer = device(z, x, c, 1 - y)
        return self.copy(source, self.first.at[s, i], 4 + 2 * s + i, peer)

    def leg_two(self, s):
        z, x, c, y = self.at
        if s in self.x_first:
            source = self.held.at[s, x, :, self.other]
            peer = device(z, x, c, 1 - y)
        else:
            source = self.held.at[s, 1 - x, :, self.mine]
            peer = device(z, 1 - x, c, y)
        return self.copy(source, self.second.at[s], 12 + s, peer)

    def leg_three(self, s):
        z, x, c, y = self.at
        hop = (z + s) % 2 + 2 * ((z // 2 + s // 2) % 2)
        source = self.held.at[s, x, :, self.mine]
        return self.copy(source, self.last.at[hop], 16 + hop, device(s, x, c, y))

    def from_z(self, hop):
        z, x, c, y = self.at
        slot = self.last.at[hop]
        return self.copy(slot, slot, 16 + hop, device(z_peer(z, hop), x, c, y))

    def leg_four(self):
        z, x, c, y = self.at
        return self.copy(self.edge.at[0], self.edge.at[1], 20, device(z, x, c, 1 - y))

    def begin(self):
        for s in (0, 3, 1, 2):
            self.between_cores(s).start()
            self.load(s).start()

    def one(self, s):
        self.load(s).wait()
        self.between_cores(s).wait_recv()
        for i in range(2):
            add_rows(self.held.at[s, i], self.core.at[s, i], (self.rows, self.width))
        for i in range(2):
            self.leg_one(s, i).start()

    def two(self, s):
        x = self.at[1]
        half = self.width // 2
        for i in range(2):
            self.leg_one(s, i).wait_recv()
            if s in self.x_first:
                target = self.held.at[s, x, :, pl.ds(i * half, half)]
            else:
                target = self.held.at[s, i, :, self.mine]
            add_rows(target, self.first.at[s, i], (self.rows, half))
        self.leg_two(s).start()

    def three(self, s):
        x = self.at[1]
        self.leg_two(s).wait_recv()
        target = self.held.at[s, x, :, self.mine]
        add_rows(target, self.second.at[s], (self.rows, self.width // 2))

        @pl.when(self.at[0] != s)
        def _():
            self.leg_three(s).start()

    def four(self):
        z, x, c, y = self.at
        for hop in range(1, ZS):
            self.from_z(hop).wait_recv()
        own = self.held.at[z, x, :, self.mine]
        last, edge = self.last, self.edge

        def strip(i, unused):
            at = pl.ds(pl.multiple_of(i * 16, 16), 16)
            total = own[at, :].astype(F32)
            for hop in range(1, ZS):
                total += last[hop, at, :].astype(F32)
            edge[0, at, :] = total.astype(BF16)
            return unused

        lax.fori_loop(0, self.rows // 16, strip, 0)
        self.leg_four().start()
        self.out[:, self.mine] = edge[0].astype(F32)

    def finish(self):
        self.leg_four().wait()
        self.out[:, self.other] = self.edge[1].astype(F32)
        for s in range(ZS):
            self.between_cores(s).wait_send()
            for i in range(2):
                self.leg_one(s, i).wait_send()
            self.leg_two(s).wait_send()

            @pl.when(self.at[0] != s)
            def _():
                self.leg_three(s).wait_send()


class Total:
    long = (("c",), ("x",), ("y",), ("z",))
    short = (("c", "x", "y"), ("z",))
    n_slots = 12

    def __init__(self, part, out, leave, come, send, recv, rounds):
        self.part, self.out, self.leave, self.come = part, out, leave, come
        self.send, self.recv, self.rounds = send, recv, rounds
        self.at = place()

    @staticmethod
    def scratch(shape, kind):
        return [pltpu.VMEM((4,) + shape, kind), pltpu.VMEM((Total.n_slots,) + shape, kind)]

    def group(self, step):
        z, x, c, y = self.at
        axes = self.rounds[step]
        if axes == ("z",):
            members = [device(i, x, c, y) for i in range(ZS)]
            return 8, z, members
        number, members = 0, []
        for axis in axes:
            number = number * 2 + {"c": c, "x": x, "y": y}[axis]
        for i in range(2 ** len(axes)):
            bits = {axis: (i >> (len(axes) - 1 - k)) % 2 for k, axis in enumerate(axes)}
            members.append(device(z, bits.get("x", x), bits.get("c", c), bits.get("y", y)))
        return 2 * step, number, members

    def copy(self, step, to, source):
        first, number, members = self.group(step)
        return pltpu.make_async_remote_copy(
            src_ref=self.leave.at[step],
            dst_ref=self.come.at[first + source],
            send_sem=self.send.at[first + to],
            recv_sem=self.recv.at[first + source],
            device_id=members[to],
            device_id_type=MESH,
        )

    def give(self, step, values):
        first, number, members = self.group(step)
        low = values.astype(self.leave.dtype)
        self.leave[step] = low
        self.come[first + number] = low
        for to in range(len(members)):

            @pl.when(number != to)
            def _():
                self.copy(step, to, number).start()

    def begin(self):
        self.give(0, self.part[...])

    def advance(self, step):
        first, number, members = self.group(step)
        for other in range(len(members)):

            @pl.when(number != other)
            def _():
                self.copy(step, other, other).wait_recv()
                self.copy(step, other, number).wait_send()

        total = self.come[first].astype(F32)
        for other in range(1, len(members)):
            total += self.come[first + other].astype(F32)
        if step + 1 < len(self.rounds):
            self.give(step + 1, total)
        else:
            self.out[...] = total


class RowsBack:
    n_sems = 3

    def __init__(self, line, blank, small, large, sems, send, recv):
        self.line, self.blank, self.small, self.large = line, blank, small, large
        self.sems, self.send, self.recv = sems, send, recv
        self.at = place()
        self.n_small = small.shape[0]
        self.rows = large.shape[1]

    def half(self, y):
        start = self.n_small * SPAD + self.rows * y
        return self.line.at[pl.ds(pl.multiple_of(start, 16), self.rows)]

    def local(self, i):
        n = self.n_small
        if i < n:
            source, target = self.line.at[pl.ds(i * SPAD, SPAD)], self.small.at[i, pl.ds(0, SPAD)]
        elif i < 2 * n:
            source, target = self.blank, self.small.at[i - n, pl.ds(SPAD, SLEN - SPAD)]
        else:
            y = self.at[3]
            source, target = self.half(y), self.large.at[y]
        return pltpu.make_async_copy(source, target, self.sems.at[i])

    def remote(self):
        z, x, c, y = self.at
        return pltpu.make_async_remote_copy(
            src_ref=self.half(1 - y),
            dst_ref=self.large.at[y],
            send_sem=self.send,
            recv_sem=self.recv,
            device_id=device(z, x, c, 1 - y),
            device_id_type=MESH,
        )

    def begin_large(self):
        self.remote().start()
        self.local(2 * self.n_small).start()

    def begin_small(self):
        for i in range(2 * self.n_small):
            self.local(i).start()

    def finish(self):
        for i in range(2 * self.n_small + 1):
            self.local(i).wait()
        self.remote().wait()


def begin_kernel(
    n_small,
    n_large,
    query_weight,
    key_weight,
    value_weight,
    out_weight,
    up_weight,
    down_share,
    small_in,
    large_in,
    small_cot,
    large_cot,
    table,
    gain,
    gain_bias,
    query_bias,
    value_bias,
    x_out,
    cot_out,
    qkv_out,
    turned_out,
    w_out,
    mid_whole,
    down_whole,
    out,
    out_wide,
    probs_small,
    probs_large,
    line,
    cot_line,
    hidden,
    turned,
    qkv,
    w_qkv,
    wide,
    narrow,
    bias_large,
    bias_small,
    send,
    recv,
    own,
    row_sems,
    row_send,
    row_recv,
    keep_sems,
    qkv_share,
    mid_share,
    share_sems,
    wide_table,
    low_large,
    low_small,
    high_large,
    high_small,
):
    step = pl.program_id(0)
    pairs = pl.num_programs(0)
    lows, highs = (low_large, low_small), (high_large, high_small)
    shares = []
    for target, weights in (
        (qkv_share, (query_weight, key_weight, value_weight)),
        (mid_share, (out_weight, up_weight)),
    ):
        col = 0
        for weight in weights:
            cols = slice(col, col + weight.shape[1])
            shares.append(
                pltpu.make_async_copy(weight, target.at[:, cols], share_sems.at[len(shares)])
            )
            col += weight.shape[1]
    width = hidden.shape[1]
    count = qkv.shape[1]
    masks = head_masks()
    first = Gather(qkv_share, w_qkv, send.at[0], recv.at[0], own.at[0], True)
    mid = Gather(mid_share, mid_whole, send.at[1], recv.at[1], own.at[1], False)
    down = Gather(down_share, down_whole, send.at[2], recv.at[2], own.at[2], True)
    x_rows = Rows(small_in, large_in, line, row_sems.at[0], row_send.at[0], row_recv.at[0])
    cot_rows = Rows(small_cot, large_cot, cot_line, row_sems.at[1], row_send.at[1], row_recv.at[1])
    keeps = [
        pltpu.make_async_copy(line, x_out, keep_sems.at[0]),
        pltpu.make_async_copy(qkv, qkv_out, keep_sems.at[1]),
        pltpu.make_async_copy(w_qkv, w_out, keep_sems.at[2]),
        pltpu.make_async_copy(cot_line, cot_out, keep_sems.at[3]),
        pltpu.make_async_copy(turned, turned_out, keep_sems.at[4]),
    ]

    early = (
        ((mid, 0), (mid, 1), (down, 0), (down, 1)),
        ((mid, 2),),
        ((mid, 3),),
    )
    slots = (
        ((down, 2),),
        ((down, 3),),
        (),
        (),
        ((mid, 4),),
        ((mid, 5), (mid, 6)),
        ((down, 4),),
        ((mid, 7), (down, 5), (down, 6)),
        ((mid, 8), (mid, 9)),
        ((down, 7), (down, 8)),
        ((mid, 10), (down, 9)),
        ((down, 10),),
    )

    @pl.when(step == 0)
    def _():
        for share in shares:
            share.start()
        greet()
        for share in shares:
            share.wait()
        first.begin()
        x_rows.begin()
        table_sequences(table, wide_table, lows, highs)
        part = chunk_rows(count)
        chunks = [pl.ds(at, part) for at in range(0, count, part)]

        def norm(rows):
            normal, unused = normalized(line[rows, :].astype(F32))
            hidden[rows, :] = (normal * gain[...][None, :] + gain_bias[...][None, :]).astype(BF16)

        x_rows.wait_small()
        norm(chunks[0])
        for at in range(5):
            first.turn(at)
        for at in range(5, 8):
            first.turn(at)
        x_rows.wait_large()
        for rows in chunks[1:]:
            norm(rows)
        keeps[0].start()
        for at in range(8, 11):
            first.turn(at)
        first.arrive()
        mid.begin()
        down.begin()
        cot_rows.begin()
        keeps[2].start()
        scale = jnp.asarray(float(width // HEADS) ** (-0.5), BF16)
        for at, rows in enumerate(chunks):
            for kind in range(3):
                cols = slice(kind * width, (kind + 1) * width)
                weight = w_qkv[:, :, :, :, cols].reshape(width, width)
                made = dot_nn(hidden[rows, :], weight)
                if kind != 1:
                    made += (query_bias, None, value_bias)[kind][...][None, :]
                made = made.astype(BF16)
                if kind == 0:
                    made = made * scale
                for j in range(HEADS // 2):
                    qkv[kind * (HEADS // 2) + j, rows, :] = made[:, j * LANES : (j + 1) * LANES]
            for job, turn in early[at]:
                job.turn(turn)
        keeps[1].start()
        turned[...] = hidden[...].T
        keeps[4].start()

    query = qkv.at[step]
    key = qkv.at[pairs + step]
    value = qkv.at[2 * pairs + step]

    @pl.when(pl.program_id(0) == 0)
    def _():
        bias_small[...] = jnp.zeros_like(bias_small)

    members = [(i * SPAD, SPAD, bias_small, probs_small, i) for i in range(n_small)]
    members += [
        (n_small * SPAD + i * LPAD, LPAD, bias_large, probs_large, i) for i in range(n_large)
    ]
    halves = [[] for _ in members]
    for head in range(2):
        at_head = pl.ds(2 * step + head, 1)
        transposed_biases(
            (lows[0][at_head, :], highs[0][at_head, :]),
            (lows[1][at_head, :], highs[1][at_head, :]),
            wide_table[at_head, T_WIDTH - 256 :],
            wide,
            narrow,
            bias_large,
            bias_small,
        )
        for at, (start, count, bias, probs, which) in enumerate(members):
            rows = pl.ds(start, count)
            scores = dot_nt(key[rows, :], query[rows, :] * masks[head]) + bias[:, :count]
            top = jnp.max(scores, axis=0, keepdims=True)
            weights = jnp.exp(scores - top)
            total = jnp.sum(weights, axis=0, keepdims=True)
            prob = (weights * (1.0 / total)).astype(BF16)
            probs[head, which] = prob
            turned = value[rows, :].T
            halves[at].append(dot_nn(turned[head * 64 : head * 64 + 64, :], prob))
        for at in range(HEADS // 2):
            if slots[2 * at + head]:

                @pl.when(step == at)
                def _():
                    for job, turn in slots[2 * at + head]:
                        job.turn(turn)

    for at, (start, count, bias, probs, which) in enumerate(members):
        both = jnp.concatenate(halves[at], axis=0).T
        out[pl.ds(start, count), :] = both.astype(BF16)
        out_wide[pl.ds(start, count), :] = both

    @pl.when(step == pairs - 3)
    def _():
        cot_rows.wait_small()
        cot_rows.wait_large()
        keeps[3].start()

    @pl.when(step == pairs - 1)
    def _():
        for job in (mid, down):
            job.arrive()
        for job in (first, mid, down):
            job.drain()
        for keep in keeps:
            keep.wait()


EARLY = 4


def end_kernel(
    n_small,
    n_large,
    query,
    key,
    value,
    dout,
    out_wide,
    probs_small,
    probs_large,
    g_mid,
    g_down,
    x_hbm,
    turned_hbm,
    w_hbm,
    dres_hbm,
    out_hbm,
    feed_grads,
    gain,
    small_out,
    large_out,
    small_grad,
    large_grad,
    mid_out,
    down_out,
    early_out,
    late_out,
    feed_total,
    input_total,
    table_total,
    *scratch,
):
    scratch = list(scratch)

    def take(count):
        taken = scratch[:count]
        del scratch[:count]
        return taken

    wide, narrow, dsum_small, dscore_large, dqkv, hidden_turned, w_qkv, line, blank = take(9)
    early_grad, late_grad, input_part, table_part = take(4)
    large_part = table_part.at[:, :L_WIDTH]
    small_part = table_part.at[:, L_WIDTH:]
    mid_bufs, down_bufs, early_bufs, late_bufs = [take(Reduce.n_scratch) for unused in range(4)]
    feed_bufs, input_bufs, table_bufs = [take(2) for unused in range(3)]
    send, recv, own, total_send, total_recv, load_sems, row_sems, row_send, row_recv = scratch

    step = pl.program_id(0)
    pairs = HEADS // 2
    width = x_hbm.shape[1]
    all_rows = dqkv.shape[1]
    masks = head_masks()
    query, key, value = query.at[0], key.at[0], value.at[0]
    both_ways, mostly_x = (0, 1), (0, 1)
    mid = Reduce(g_mid, mid_out, *mid_bufs, send.at[0], recv.at[0], own.at[0], both_ways)
    down = Reduce(g_down, down_out, *down_bufs, send.at[1], recv.at[1], own.at[1], both_ways)
    early = Reduce(early_grad, early_out, *early_bufs, send.at[2], recv.at[2], own.at[2], mostly_x)
    late = Reduce(late_grad, late_out, *late_bufs, send.at[3], recv.at[3], own.at[3], mostly_x)
    sums = [
        Total(part, total, *bufs, total_send.at[i], total_recv.at[i], rounds)
        for i, (part, total, bufs, rounds) in enumerate(
            (
                (feed_grads, feed_total, feed_bufs, Total.long),
                (input_part, input_total, input_bufs, Total.short),
                (table_part, table_total, table_bufs, Total.long),
            )
        )
    ]
    feed_sum, input_sum, table_sum = sums
    out_rows = RowsBack(
        line, blank, small_out, large_out, row_sems.at[0], row_send.at[0], row_recv.at[0]
    )
    grad_rows = RowsBack(
        line, blank, small_grad, large_grad, row_sems.at[1], row_send.at[1], row_recv.at[1]
    )
    load_out = pltpu.make_async_copy(out_hbm, line.at[pl.ds(0, all_rows)], load_sems.at[0])
    load_x = pltpu.make_async_copy(x_hbm, line, load_sems.at[1])
    load_turned = pltpu.make_async_copy(turned_hbm, hidden_turned, load_sems.at[2])
    load_w = pltpu.make_async_copy(w_hbm, w_qkv, load_sems.at[3])

    def take_turns(by_step):
        for at, turns in enumerate(by_step):
            if turns:

                @pl.when(step == at)
                def _():
                    for turn in turns:
                        turn[0](*turn[1:])

    slots = (
        ([(mid.one, 0), (mid.one, 3)], [], [], [(mid.three, 0), (mid.three, 3), (down.one, 1), (down.one, 2)], [(mid.three, 1), (mid.three, 2)], [(down.three, 0), (down.three, 3), (early.one, 1), (early.one, 2)]),
        ([], [(mid.one, 1), (mid.one, 2)], [(down.one, 0), (down.one, 3)], [], [], []),
        ([], [(feed_sum.advance, 1)], [(feed_sum.advance, 2)], [(down.two, 0), (down.two, 3)], [(down.two, 1), (down.two, 2), (early.one, 0), (early.one, 3)], [(early.two, 0), (early.two, 3), (down.three, 1), (down.three, 2)]),
        ([(feed_sum.advance, 0)], [(mid.two, 0), (mid.two, 3)], [(mid.two, 1), (mid.two, 2)], [(feed_sum.advance, 3)], [], []),
    )

    @pl.when(step == 0)
    def _():
        greet()
        mid.begin()
        down.begin()
        load_out.start()
        load_turned.start()
        blank[...] = jnp.zeros_like(blank)
        line[pl.ds(all_rows, line.shape[0] - all_rows), :] = jnp.zeros(
            (line.shape[0] - all_rows, width), BF16
        )
        table_part[...] = jnp.zeros_like(table_part)
        feed_sum.begin()
        load_out.wait()
        out_rows.begin_large()
        out_rows.begin_small()

    lane = iota((1, LANES), 1)
    scale = float(64) ** (-0.5)
    members = [(i * SPAD, SPAD, probs_small, i) for i in range(n_small)]
    members += [(n_small * SPAD + i * LPAD, LPAD, probs_large, i) for i in range(n_large)]
    keep = []
    for head in range(2):
        spot = 64 * (1 - head)
        minus = jnp.where((lane == spot) | (lane == spot + 1), -1.0, 0.0).astype(BF16)
        mask32 = masks[head].astype(F32)
        for at, (start, count, probs, which) in enumerate(members):
            rows = pl.ds(start, count)
            grad = dout[rows, :]
            grad32 = grad.astype(F32) * mask32
            delta = jnp.sum(grad32 * out_wide[rows, :], axis=1, keepdims=True)
            coarse = delta.astype(BF16).astype(F32)
            fine = delta - coarse
            side = jnp.where(lane == spot, coarse, jnp.where(lane == spot + 1, fine, grad32))
            values = value[rows, :] * masks[head] + minus
            prob = probs[head, which]
            dscore = prob.astype(F32) * dot_nt(values, side.astype(BF16))
            if count == SPAD:
                if which == 0:
                    dsum_small[:, :SPAD] = dscore
                else:
                    dsum_small[:, :SPAD] += dscore
            elif which == 0:
                dscore_large[:, :LPAD] = dscore
            else:
                dscore_large[:, :LPAD] += dscore
            low = dscore.astype(BF16)
            turned = key[rows, :].T
            dq = dot_nn(turned[head * 64 : head * 64 + 64, :], low)
            dk = dot_nn(low, query[rows, :])
            dv = dot_nn(prob, grad)
            if head == 0:
                keep.append((dq, dk, dv))
            else:
                first = iota((count, LANES), 1) < 64
                dq0, dk0, dv0 = keep[at]
                dqkv[step, rows, :] = (jnp.concatenate([dq0, dq], axis=0).T * scale).astype(BF16)
                dqkv[pairs + step, rows, :] = jnp.where(first, dk0, dk).astype(BF16)
                dqkv[2 * pairs + step, rows, :] = jnp.where(first, dv0, dv).astype(BF16)
        take_turns(slots[2 * head])
        wide[...] = jnp.zeros_like(wide)
        dscore_large[:, LPAD:] = jnp.zeros((LPAD, 768 - LPAD), F32)
        edge_lane = iota((24, 768), 1)
        edge_row = iota((24, 768), 0)
        class_column = jnp.zeros((24, 768), F32)
        class_row = None
        for block in range(LGRID + 1):
            at, turn = large_window(block)
            piece = dscore_large[pl.ds(block * 24, 24), :]
            if block == 0:
                class_row = piece[0:1, :]
                piece = jnp.where(edge_row == 0, 0.0, piece)
            class_column = class_column + piece
            piece = jnp.where(edge_lane == 0, 0.0, piece)
            if turn:
                piece = pltpu.roll(piece, turn, 1)
            wide[:, at * LANES : at * LANES + 768] += piece
        low_sum, high_sum = gather_sequences(wide[...], 24, L_WIDTH, LGRID, 1)
        spot_row = step * 2 + head
        large_part[pl.ds(spot_row, 1), :] = low_sum
        large_part[pl.ds(16 + spot_row, 1), :] = high_sum
        narrow[...] = jnp.zeros_like(narrow)
        dsum_small[:, SPAD:] = jnp.zeros((SPAD, 384 - SPAD), F32)
        small_lane = iota((SGRID, 384), 1)
        small_column = jnp.zeros((SGRID, 384), F32)
        for block in range(SGRID):
            at, turn = small_window(block)
            piece = dsum_small[pl.ds(1 + SGRID * block, SGRID), :]
            small_column = small_column + piece
            piece = jnp.where(small_lane == 0, 0.0, piece)
            piece = jnp.concatenate([piece, jnp.zeros((2, 384), F32)], axis=0)
            if turn:
                piece = pltpu.roll(piece, turn, 1)
            narrow[:, at * LANES : at * LANES + 384] += piece
        low_sum, high_sum = gather_sequences(narrow[...], 16, S_WIDTH, SGRID, 0)
        by_query = row_sum(class_column)[:, :LANES] + row_sum(small_column)[:, :LANES]
        both_rows = class_row + jnp.concatenate(
            [dsum_small[0:1, :], jnp.zeros((1, 384), F32)], axis=1
        )
        class_key = jnp.sum(
            jnp.where(iota((1, 768), 1) == 0, 0.0, both_rows), axis=1, keepdims=True
        )
        spot = iota((1, S_WIDTH), 1)
        low_sum = jnp.where(spot == S_WIDTH - 3, by_query[:, 0:1], low_sum)
        low_sum = jnp.where(spot == S_WIDTH - 2, class_key, low_sum)
        low_sum = jnp.where(spot == S_WIDTH - 1, both_rows[:, 0:1], low_sum)
        small_part[pl.ds(spot_row, 1), :] = low_sum
        small_part[pl.ds(16 + spot_row, 1), :] = high_sum
        take_turns(slots[1 + 2 * head])

    @pl.when(step == 0)
    def _():
        load_turned.wait()

    @pl.when(step % 2 == 1)
    def _():
        pieces = [dqkv[kind * pairs + step - 1 + i] for i in range(2) for kind in range(3)]
        made = dot_nn(hidden_turned[...], jnp.concatenate(pieces, axis=1)).astype(BF16)
        made = made.reshape(ZS, 2, 2, width // 16, width)
        for at in range(pairs // 2):

            @pl.when(step == 2 * at + 1)
            def _():
                if at < EARLY // 2:
                    early_grad[:, :, :, :, at * width : (at + 1) * width] = made
                else:
                    late_grad[...] = made

    @pl.when(step == EARLY - 1)
    def _():
        early.begin()
        out_rows.finish()
        load_x.start()
        load_w.start()

    @pl.when(step == pairs - 1)
    def _():
        late.begin()
        table_sum.begin()
        load_x.wait()
        load_w.wait()
        part = chunk_rows(all_rows)
        zeros = jnp.zeros((1, width), F32)
        input_part[...] = jnp.zeros_like(input_part)
        end_turns = (
            [(late.one, 0), (late.one, 3), (late.one, 1), (late.one, 2), (early.two, 1), (early.two, 2), (table_sum.advance, 0)],
            [(mid.four,), (late.two, 0), (late.two, 3), (early.three, 0), (early.three, 3), (table_sum.advance, 1)],
            [(late.two, 1), (late.two, 2), (early.three, 1), (early.three, 2), (down.four,), (table_sum.advance, 2)],
        )
        for at, first in enumerate(reversed(range(0, all_rows, part))):
            rows = pl.ds(first, part)
            load_dres = pltpu.make_async_copy(
                dres_hbm.at[rows], dscore_large.at[pl.ds(0, part)], load_sems.at[4]
            )
            load_dres.start()
            dhidden = jnp.zeros((part, width), F32)
            for kind in range(3):
                piece = jnp.concatenate(
                    [dqkv[kind * pairs + j, rows, :] for j in range(pairs)], axis=1
                )
                weight = w_qkv[:, :, :, :, kind * width : (kind + 1) * width]
                dhidden += dot_nt(piece, weight.reshape(width, width))
                if kind != 1:
                    input_part[kind : kind + 1, :] += row_sum(piece.astype(F32))
            normal, rate = normalized(line[rows, :].astype(F32))
            input_part[3:4, :] += row_sum(dhidden * normal)
            input_part[4:5, :] += row_sum(dhidden)
            back = norm_back(dhidden * gain[...][None, :], normal, rate)
            load_dres.wait()
            line[rows, :] = (dscore_large[pl.ds(0, part), :] + back).astype(BF16)
            if at == 0:
                line[pl.ds(all_rows, line.shape[0] - all_rows), :] = jnp.zeros(
                    (line.shape[0] - all_rows, width), BF16
                )
            if first <= n_small * SPAD < first + part:
                grad_rows.begin_large()
            for turn in end_turns[at]:
                turn[0](*turn[1:])
        grad_rows.begin_small()
        input_sum.begin()
        for turn in (
            [(input_sum.advance, 0), (late.three, 0), (late.three, 3), (late.three, 1), (late.three, 2), (table_sum.advance, 3), (early.four,), (input_sum.advance, 1), (late.four,)]
        ):
            turn[0](*turn[1:])
        grad_rows.finish()
        for job in (mid, down, early, late):
            job.finish()


def gelu_pair(upper):
    normal_cdf = 0.5 * (1.0 + lax.erf(upper * (0.5**0.5)))
    density = jnp.exp(-0.5 * upper * upper) * 0.3989422804014327
    return upper * normal_cdf, normal_cdf + upper * density


def valid_rows(first, count, n_small):
    row = iota((count, 1), 0) + first
    in_small = row < n_small * SPAD
    small_ok = row % SPAD < SGRID * SGRID + 1
    large_ok = (row - n_small * SPAD) % LPAD < LGRID * LGRID + 1
    return jnp.where(in_small, small_ok.astype(F32), large_ok.astype(F32))


def feed_kernel(
    n_small,
    tiles,
    x,
    attended,
    cot,
    mid_hbm,
    down_hbm,
    out_bias,
    attend_scale,
    second_gain,
    second_bias,
    down_bias,
    feed_scale,
    up_bias,
    out,
    dresidual,
    dattended,
    vector_grads,
    g_mid,
    g_down,
    w_mid,
    w_down,
    active,
    slope,
    acc_out,
    acc_up,
    acc_down,
    sems,
):
    step = pl.program_id(0)
    count, width = x.shape
    w_out = w_mid.at[:, :width]
    w_up = w_mid.at[:, width:]
    tile = w_up.shape[1] // tiles

    final = pl.num_programs(0) - 1
    pieces = [(mid_hbm, w_mid, g_mid, (slice(None), slice(0, width)))]
    for t in range(tiles):
        cols = slice(width + t * tile, width + (t + 1) * tile)
        pieces.append((mid_hbm, w_mid, g_mid, (slice(None), cols)))
    for t in range(tiles):
        rows = slice(t * tile, (t + 1) * tile)
        pieces.append((down_hbm, w_down, g_down, (rows, slice(None))))

    def load(at):
        source, held, target, where = pieces[at]
        return pltpu.make_async_copy(source.at[where], held.at[where], sems.at[at])

    def store(at):
        source, held, target, where = pieces[at]
        return pltpu.make_async_copy(held.at[where], target.at[where], sems.at[at])

    @pl.when(step == 0)
    def _():
        for at in range(len(pieces)):
            load(at).start()
        acc_out[...] = jnp.zeros_like(acc_out)
        acc_up[...] = jnp.zeros_like(acc_up)
        acc_down[...] = jnp.zeros_like(acc_down)
        vector_grads[...] = jnp.zeros_like(vector_grads)
        load(0).wait()

    out_bias, attend_scale, second_gain, second_bias, down_bias, feed_scale = (
        v[...][None, :]
        for v in (out_bias, attend_scale, second_gain, second_bias, down_bias, feed_scale)
    )

    valid = valid_rows(step * count, count, n_small)
    mixed = attended[...]
    branch = dot_nn(mixed, w_out[...]) + out_bias
    residual = x[...].astype(F32) + attend_scale * branch
    normal, scale = normalized(residual)
    hidden = (normal * second_gain + second_bias).astype(BF16)

    @pl.when(step == 0)
    def _():
        for at in range(1, len(pieces)):
            load(at).wait()

    lower = jnp.zeros((count, width), F32)
    for t in range(tiles):
        cols = slice(t * tile, (t + 1) * tile)
        upper = dot_nn(hidden, w_up[:, cols]) + up_bias[cols][None, :]
        made, rate = gelu_pair(upper)
        made = made.astype(BF16)
        active[:, cols] = made
        slope[:, cols] = rate.astype(BF16)
        lower += dot_nn(made, w_down[cols, :])
    lower += down_bias
    out[...] = ((residual + feed_scale * lower) * valid).astype(BF16)
    upstream = cot[...].astype(F32) * valid
    vector_grads[5:6, :] += row_sum(upstream * lower)
    dlower = (upstream * feed_scale).astype(BF16)
    vector_grads[4:5, :] += row_sum(dlower.astype(F32))
    turned = hidden.T
    dhidden = jnp.zeros((count, width), F32)
    for t in range(tiles):
        cols = slice(t * tile, (t + 1) * tile)
        dupper = (dot_nt(dlower, w_down[cols, :]) * slope[:, cols].astype(F32)).astype(BF16)
        vector_grads[8 + t : 9 + t, :] += row_sum(dupper.astype(F32))
        acc_down[cols, :] += dot_nn(active[:, cols].T, dlower)
        acc_up[:, cols] += dot_nn(turned, dupper)
        dhidden += dot_nt(dupper, w_up[:, cols])

    @pl.when(step == final)
    def _():
        for t in range(tiles):
            cols = slice(t * tile, (t + 1) * tile)
            w_up[:, cols] = acc_up[:, cols].astype(BF16)
            store(1 + t).start()
            w_down[cols, :] = acc_down[cols, :].astype(BF16)
            store(1 + tiles + t).start()

    vector_grads[2:3, :] += row_sum(dhidden * normal)
    vector_grads[3:4, :] += row_sum(dhidden)
    dres = upstream + norm_back(dhidden * second_gain, normal, scale)
    dresidual[...] = dres
    vector_grads[1:2, :] += row_sum(dres * branch)
    dbranch = (dres * attend_scale).astype(BF16)
    vector_grads[0:1, :] += row_sum(dbranch.astype(F32))
    acc_out[...] += dot_nn(mixed.T, dbranch)
    dattended[...] = dot_nt(dbranch, w_out[...]).astype(BF16)

    @pl.when(step == final)
    def _():
        w_out[...] = acc_out[...].astype(BF16)
        store(0).start()
        for at in range(len(pieces)):
            store(at).wait()


def chunk_rows(total):
    return max(size for size in range(16, 481, 16) if total % size == 0)


def params(collective=None):
    if collective is None:
        return pltpu.CompilerParams(vmem_limit_bytes=VMEM_BYTES)
    return pltpu.CompilerParams(
        vmem_limit_bytes=VMEM_BYTES, collective_id=collective, has_side_effects=True
    )


def held(shape):
    rank = len(shape)
    return pl.BlockSpec(shape, lambda i: (0,) * rank, pipeline_mode=pl.Buffered(1))


def resident(shape):
    rank = len(shape)
    return pl.BlockSpec(shape, lambda i: (0,) * rank)


def run_begin(weights, rows, table, vectors, collective):
    small, large = rows[:2]
    n_small, n_large = small.shape[0], 1
    width = small.shape[-1]
    pairs = HEADS // 2
    count = n_small * SPAD + n_large * LPAD
    line = n_small * SPAD + n_large * LLEN
    anywhere = pl.BlockSpec(memory_space=pl.ANY)
    sems = pltpu.SemaphoreType.DMA
    column = pl.BlockSpec((count, LANES), lambda i: (0, i))
    strip = width // 16
    qkv_share, mid_share = (strip, 3 * width), (strip, width + weights[4].shape[1])
    wholes = [(ZS, 2, 2) + s for s in (qkv_share, mid_share, weights[5].shape)]

    def per_pair(shape):
        tail = (0,) * (len(shape) - 1)
        return pl.BlockSpec((2,) + shape[1:], lambda i: (i,) + tail)

    probs = [(HEADS, n_small, SPAD, SPAD), (HEADS, n_large, LPAD, LPAD)]
    return pl.pallas_call(
        functools.partial(begin_kernel, n_small, n_large),
        grid=(pairs,),
        in_specs=[anywhere] * 10 + [held(v.shape) for v in (table,) + vectors],
        out_specs=[anywhere] * 7 + [column, column] + [per_pair(p) for p in probs],
        out_shape=[
            jax.ShapeDtypeStruct((line, width), BF16),
            jax.ShapeDtypeStruct((line, width), BF16),
            jax.ShapeDtypeStruct((3 * pairs, count, LANES), BF16),
            jax.ShapeDtypeStruct((width, count), BF16),
        ]
        + [jax.ShapeDtypeStruct(w, BF16) for w in wholes]
        + [
            jax.ShapeDtypeStruct((count, width), BF16),
            jax.ShapeDtypeStruct((count, width), F32),
        ]
        + [jax.ShapeDtypeStruct(p, BF16) for p in probs],
        scratch_shapes=[
            pltpu.VMEM((line, width), BF16),
            pltpu.VMEM((line, width), BF16),
            pltpu.VMEM((count, width), BF16),
            pltpu.VMEM((width, count), BF16),
            pltpu.VMEM((3 * pairs, count, LANES), BF16),
            pltpu.VMEM(wholes[0], BF16),
            pltpu.VMEM((24, L_WIDTH), F32),
            pltpu.VMEM((16, S_WIDTH), F32),
            pltpu.VMEM((LPAD, 640), F32),
            pltpu.VMEM((SPAD, 256), F32),
            sems((3, Gather.n_sems)),
            sems((3, Gather.n_sems)),
            sems((3,)),
            sems((2, n_small + 1)),
            sems((2,)),
            sems((2,)),
            sems((5,)),
            pltpu.VMEM(qkv_share, BF16),
            pltpu.VMEM(mid_share, BF16),
            sems((5,)),
            pltpu.VMEM((16, T_WIDTH), F32),
            pltpu.VMEM((16, L_WIDTH), F32),
            pltpu.VMEM((16, S_WIDTH), F32),
            pltpu.VMEM((16, L_WIDTH), F32),
            pltpu.VMEM((16, S_WIDTH), F32),
        ],
        compiler_params=params(collective),
    )(*weights, *rows, table, *vectors)


def run_end(qkv, dattended, out_wide, probs, grads, rows, feed_grads, gain, n_small, collective):
    count, width = dattended.shape
    pairs = HEADS // 2
    line = rows[0].shape[0]
    anywhere = pl.BlockSpec(memory_space=pl.ANY)
    inside = pl.BlockSpec(memory_space=pltpu.VMEM)
    sems = pltpu.SemaphoreType.DMA
    column = pl.BlockSpec((count, LANES), lambda i: (0, i))
    shares = [(g.shape[0] // 16, g.shape[1]) for g in grads]
    shares += [(width // 16, 3 * LANES * many) for many in (EARLY, pairs - EARLY)]
    smalls = [feed_grads.shape, (8, width), (32, L_WIDTH + S_WIDTH)]

    def third(which):
        return pl.BlockSpec((1, count, LANES), lambda i: (which * pairs + i, 0, 0))

    def per_pair(shape):
        tail = (0,) * (len(shape) - 1)
        return pl.BlockSpec((2,) + shape[1:], lambda i: (i,) + tail)

    scratch = [
        pltpu.VMEM((24, L_WIDTH), F32),
        pltpu.VMEM((16, S_WIDTH), F32),
        pltpu.VMEM((SPAD, 384), F32),
        pltpu.VMEM((LPAD, 768), F32),
        pltpu.VMEM((3 * pairs, count, LANES), BF16),
        pltpu.VMEM((width, count), BF16),
        pltpu.VMEM((ZS, 2, 2, width // 16, 3 * width), BF16),
        pltpu.VMEM((line, width), BF16),
        pltpu.VMEM((SLEN - SPAD, width), BF16),
        pltpu.VMEM((ZS, 2, 2) + shares[2], BF16),
        pltpu.VMEM((ZS, 2, 2) + shares[3], BF16),
        pltpu.VMEM(smalls[1], F32),
        pltpu.VMEM(smalls[2], F32),
    ]
    for shape in shares:
        scratch += Reduce.scratch(*shape)
    for shape, kind in zip(smalls, (F32, F32, BF16)):
        scratch += Total.scratch(shape, kind)
    scratch += [
        sems((4, Reduce.n_sems)),
        sems((4, Reduce.n_sems)),
        sems((4, ZS)),
        sems((3, Total.n_slots)),
        sems((3, Total.n_slots)),
        sems((5,)),
        sems((2, 2 * n_small + 1)),
        sems((2,)),
        sems((2,)),
    ]
    small = jax.ShapeDtypeStruct((n_small, SLEN, width), BF16)
    large = jax.ShapeDtypeStruct((2, LLEN // 2, width), BF16)
    return pl.pallas_call(
        functools.partial(end_kernel, n_small, 1),
        grid=(pairs,),
        in_specs=[third(0), third(1), third(2), column, column]
        + [per_pair(p.shape) for p in probs]
        + [anywhere] * 7
        + [held(feed_grads.shape), held(gain.shape)],
        out_specs=[anywhere] * 4 + [inside] * 7,
        out_shape=[small, large, small, large]
        + [jax.ShapeDtypeStruct(s, F32) for s in shares + smalls],
        scratch_shapes=scratch,
        compiler_params=params(collective),
        cost_estimate=pl.CostEstimate(
            flops=40 * 10**9, bytes_accessed=50 * 10**6, transcendentals=0
        ),
    )(
        qkv,
        qkv,
        qkv,
        dattended,
        out_wide,
        *probs,
        *[g.reshape((ZS, 2, 2) + s) for g, s in zip(grads, shares)],
        *rows,
        feed_grads,
        gain,
    )


def run_feed(x, attended, cot, w_mid, w_down, vectors, n_small):
    rows, width = attended.shape
    size = chunk_rows(rows)
    hidden = w_down.shape[0]
    tiles = hidden // width
    block = pl.BlockSpec((size, width), lambda i: (i, 0))
    anywhere = pl.BlockSpec(memory_space=pl.ANY)
    return pl.pallas_call(
        functools.partial(feed_kernel, n_small, tiles),
        grid=(rows // size,),
        in_specs=[
            block,
            block,
            block,
            anywhere,
            anywhere,
        ]
        + [held(v.shape) for v in vectors],
        out_specs=[
            block,
            block,
            block,
            resident((16, width)),
            anywhere,
            anywhere,
        ],
        out_shape=[
            jax.ShapeDtypeStruct((rows, width), BF16),
            jax.ShapeDtypeStruct((rows, width), F32),
            jax.ShapeDtypeStruct((rows, width), BF16),
            jax.ShapeDtypeStruct((16, width), F32),
            jax.ShapeDtypeStruct((width, width + hidden), BF16),
            jax.ShapeDtypeStruct((hidden, width), BF16),
        ],
        scratch_shapes=[
            pltpu.VMEM((width, width + hidden), BF16),
            pltpu.VMEM((hidden, width), BF16),
            pltpu.VMEM((size, hidden), BF16),
            pltpu.VMEM((size, hidden), BF16),
            pltpu.VMEM((width, width), F32),
            pltpu.VMEM((width, hidden), F32),
            pltpu.VMEM((hidden, width), F32),
            pltpu.SemaphoreType.DMA((1 + 2 * tiles,)),
        ],
        compiler_params=params(),
        cost_estimate=pl.CostEstimate(
            flops=6 * rows * width * (width + 2 * hidden),
            bytes_accessed=40 * 10**6,
            transcendentals=2 * rows * hidden,
        ),
    )(x, attended, cot, w_mid, w_down, *vectors)


def finish_kernel(
    feed_total,
    input_total,
    table_total,
    mid_share,
    down_share,
    early_share,
    late_share,
    first_gain,
    first_bias,
    query,
    query_bias,
    key,
    value,
    value_bias,
    out,
    out_bias,
    attend_scale,
    second_gain,
    second_bias,
    up,
    up_bias,
    down,
    down_bias,
    feed_scale,
    table,
    wide_table,
):
    width = out.shape[1]
    for at, ref in enumerate(
        (out_bias, attend_scale, second_gain, second_bias, down_bias, feed_scale)
    ):
        ref[...] = feed_total[at, :]
    for t in range(up_bias.shape[0] // width):
        up_bias[t * width : (t + 1) * width] = feed_total[8 + t, :]
    for at, ref in ((0, query_bias), (2, value_bias), (3, first_gain), (4, first_bias)):
        ref[...] = input_total[at, :]
    out[...] = mid_share[:, :width]
    up[...] = mid_share[:, width:]
    down[...] = down_share[...]
    pair = 0
    for share in (early_share, late_share):
        for at in range(share.shape[1] // (3 * LANES)):
            for kind, ref in enumerate((query, key, value)):
                place_at = (3 * at + kind) * LANES
                ref[:, pair * LANES : (pair + 1) * LANES] = share[:, place_at : place_at + LANES]
            pair += 1
    lows = (table_total.at[pl.ds(0, 16), :L_WIDTH], table_total.at[pl.ds(0, 16), L_WIDTH:])
    highs = (table_total.at[pl.ds(16, 16), :L_WIDTH], table_total.at[pl.ds(16, 16), L_WIDTH:])
    table_from_sequences(lows, highs, wide_table)
    table[...] = wide_table[pl.ds(0, table.shape[0]), pl.ds(0, table.shape[1])]


def run_finish(totals, shares, entries):
    width = totals[0].shape[1]
    strip, hidden = shares[0].shape[0], shares[0].shape[1] - width
    vector = jax.ShapeDtypeStruct((width,), F32)
    square = jax.ShapeDtypeStruct((strip, width), F32)
    inside = pl.BlockSpec(memory_space=pltpu.VMEM)
    out_shape = [vector, vector, square, vector, square, square, vector, square]
    out_shape += [vector, vector, vector, vector]
    out_shape += [jax.ShapeDtypeStruct((strip, hidden), F32), jax.ShapeDtypeStruct((hidden,), F32)]
    out_shape += [jax.ShapeDtypeStruct(shares[1].shape, F32), vector, vector]
    out_shape += [jax.ShapeDtypeStruct((HEADS, entries), F32)]
    return pl.pallas_call(
        finish_kernel,
        in_specs=[inside] * 7,
        out_specs=[inside] * len(out_shape),
        out_shape=out_shape,
        scratch_shapes=[pltpu.VMEM((16, T_WIDTH), F32)],
        compiler_params=params(),
    )(*totals, *shares)


def shifted(array, axis, by):
    count = lax.axis_size(axis)
    return lax.ppermute(array, axis, [(i, (i + by) % count) for i in range(count)])


def layer_norm(values, gain, bias):
    center = values - jnp.mean(values, axis=-1, keepdims=True)
    spread = jnp.mean(center * center, axis=-1, keepdims=True)
    return center * lax.rsqrt(spread + EPSILON) * gain + bias


def matmul(left, right):
    return jnp.dot(left, right, preferred_element_type=jnp.float32)


def position_bias(table, places, length, grid):
    heads = table.shape[0]
    span = 2 * LGRID - 1
    total_rel = table.shape[1]
    queries_count = places.shape[0]
    grid_table = table[:, : span * span].reshape(heads, span, span)
    patch = places - 1
    query_row = patch // grid
    query_col = patch % grid
    steps_all = jnp.arange(span, dtype=jnp.int32)
    cells = jnp.arange(grid, dtype=jnp.int32)
    row_hot = (
        steps_all[None, :, None] == query_row[:, None, None] - cells[None, None, :] + LGRID - 1
    ).astype(jnp.float32)
    col_hot = (
        steps_all[None, :, None] == query_col[:, None, None] - cells[None, None, :] + LGRID - 1
    ).astype(jnp.float32)
    partial_bias = jnp.einsum("hab,qbc->hqac", grid_table, col_hot, precision=lax.Precision.HIGHEST)
    patches = jnp.einsum(
        "qar,hqac->hqrc", row_hot, partial_bias, precision=lax.Precision.HIGHEST
    ).reshape(heads, queries_count, grid * grid)
    rest = length - 1 - grid * grid
    class_key = jnp.broadcast_to(table[:, total_rel - 2][:, None, None], (heads, queries_count, 1))
    patch_rows = jnp.concatenate(
        [class_key, patches, jnp.zeros((heads, queries_count, rest), jnp.float32)], axis=2
    )
    class_row = jnp.concatenate(
        [
            table[:, total_rel - 1][:, None],
            jnp.broadcast_to(table[:, total_rel - 3][:, None], (heads, grid * grid)),
            jnp.zeros((heads, rest), jnp.float32),
        ],
        axis=1,
    )
    is_class = (places == 0)[None, :, None]
    return jnp.where(is_class, class_row[:, None, :], patch_rows)


def to_heads(block, heads):
    groups, rows, width = block.shape
    return block.reshape(groups, rows, heads, width // heads)


def block_scores(query, key, query_rows, key_rows, length, bias_full):
    size = query.shape[-1] // HEADS
    raw = jnp.einsum(
        "gqhd,gkhd->ghqk",
        to_heads(query, HEADS),
        to_heads(key, HEADS),
        preferred_element_type=jnp.float32,
    )
    key_place = key_rows % length
    select = (key_place[:, None] == jnp.arange(length, dtype=jnp.int32)[None, :]).astype(
        jnp.float32
    )
    bias_block = jnp.einsum("hql,kl->hqk", bias_full, select, precision=lax.Precision.HIGHEST)
    allowed = (query_rows // length)[:, None] == (key_rows // length)[None, :]
    scores = raw * float(size) ** (-0.5) + bias_block[None]
    return (scores, allowed, select)


def key_rows_of(source, count_keys):
    return source * count_keys + jnp.arange(count_keys, dtype=jnp.int32)


def allowed_mask(allowed, key_rows, length, grid):
    return allowed & (key_rows % length < grid * grid + 1)[None, :]


def absorb_one(state, query, key, value, query_rows, key_rows, info):
    length, grid, bias_full = info
    maximum, total, accum = state
    scores, allowed, select = block_scores(query, key, query_rows, key_rows, length, bias_full)
    allowed = allowed_mask(allowed, key_rows, length, grid)
    masked = jnp.where(allowed[None, None], scores, NEGATIVE)
    newmax = jnp.maximum(maximum, jnp.max(masked, axis=-1))
    weights = jnp.where(allowed[None, None], jnp.exp(scores - newmax[..., None]), 0.0)
    factor = jnp.exp(maximum - newmax)
    total = total * factor + jnp.sum(weights, axis=-1)
    accum = accum * factor[..., None] + jnp.einsum(
        "ghqk,gkhd->ghqd",
        weights.astype(jnp.bfloat16),
        to_heads(value, HEADS),
        preferred_element_type=jnp.float32,
    )
    return (newmax, total, accum)


def absorb_cycle(states, queries, moving, members, query_rows, source, info):
    states = list(states)
    for which, offset, rows in members:
        key = moving[0][:, offset : offset + rows]
        value = moving[1][:, offset : offset + rows]
        states[which] = absorb_one(
            states[which],
            queries[which],
            key,
            value,
            query_rows[which],
            key_rows_of(source, rows),
            info[which],
        )
    return tuple(states)


def pass_forward(moving):
    return shifted((moving[0], moving[1]), "seq", 1)


def cycle_forward(queries, cycle_pair, members, query_rows, info):
    position = lax.axis_index("seq")
    count = lax.axis_size("seq")
    states = []
    for which in range(2):
        groups, rows, width = queries[which].shape
        states.append(
            (
                jnp.full((groups, HEADS, rows), NEGATIVE, jnp.float32),
                jnp.zeros((groups, HEADS, rows), jnp.float32),
                jnp.zeros((groups, HEADS, rows, width // HEADS), jnp.float32),
            )
        )
    states = absorb_cycle(tuple(states), queries, cycle_pair, members, query_rows, position, info)

    def turn(step, carry):
        held_states, moving = carry
        moving = tuple(pass_forward(moving))
        held_states = absorb_cycle(
            held_states, queries, moving, members, query_rows, (position - step) % count, info
        )
        return (held_states, moving)

    states, moving = lax.fori_loop(1, count, turn, (states, cycle_pair))
    attended = []
    logsums = []
    for which in range(2):
        maximum, total, accum = states[which]
        groups, heads_count, rows, size = accum.shape
        attended.append(
            jnp.transpose(accum / total[..., None], (0, 2, 1, 3)).reshape(
                groups, rows, heads_count * size
            )
        )
        logsums.append(maximum + jnp.log(total))
    return (tuple(attended), tuple(logsums))


def visit_one(query, dout, logsum, delta, key, value, query_rows, key_rows, info):
    length, grid, bias_full = info
    groups, count_keys, width = key.shape
    scale = float(width // HEADS) ** (-0.5)
    scores, allowed, select = block_scores(query, key, query_rows, key_rows, length, bias_full)
    allowed = allowed_mask(allowed, key_rows, length, grid)
    probs = jnp.where(allowed[None, None], jnp.exp(scores - logsum[..., None]), 0.0)
    dout_heads = to_heads(dout, HEADS)
    dprobs = jnp.einsum(
        "gqhd,gkhd->ghqk", dout_heads, to_heads(value, HEADS), preferred_element_type=jnp.float32
    )
    dscores = (probs * (dprobs - delta[..., None])).astype(jnp.bfloat16)
    dq_term = scale * jnp.einsum(
        "ghqk,gkhd->gqhd", dscores, to_heads(key, HEADS), preferred_element_type=jnp.float32
    )
    dkey_term = jnp.einsum(
        "ghqk,gqhd->gkhd", dscores, to_heads(query, HEADS), preferred_element_type=jnp.float32
    )
    dvalue_term = jnp.einsum(
        "ghqk,gqhd->gkhd",
        probs.astype(jnp.bfloat16),
        dout_heads,
        preferred_element_type=jnp.float32,
    )
    summed = jnp.sum(dscores.astype(jnp.float32), axis=0)
    bias_term = jnp.einsum("hqk,kl->hql", summed, select, precision=lax.Precision.HIGHEST)
    return (
        dq_term,
        scale * dkey_term.reshape(groups, count_keys, width),
        dvalue_term.reshape(groups, count_keys, width),
        bias_term,
    )


def visit_cycle(carry, queries, douts, logsums, deltas, moving, members, query_rows, source, info):
    dqueries, dpair, bias_grads = carry
    dqueries = list(dqueries)
    bias_grads = list(bias_grads)
    key_pieces = []
    value_pieces = []
    for which, offset, rows in members:
        key = moving[0][:, offset : offset + rows]
        value = moving[1][:, offset : offset + rows]
        dq_term, dk_term, dv_term, bias_term = visit_one(
            queries[which],
            douts[which],
            logsums[which],
            deltas[which],
            key,
            value,
            query_rows[which],
            key_rows_of(source, rows),
            info[which],
        )
        dqueries[which] = dqueries[which] + dq_term
        key_pieces.append(dk_term)
        value_pieces.append(dv_term)
        bias_grads[which] = bias_grads[which] + bias_term
    new_pair = (
        dpair[0] + jnp.concatenate(key_pieces, axis=1),
        dpair[1] + jnp.concatenate(value_pieces, axis=1),
    )
    return (tuple(dqueries), new_pair, tuple(bias_grads))


def send_grads(dpair):
    return tuple(shifted((dpair[0], dpair[1]), "seq", 1))


def cycle_backward(queries, douts, logsums, deltas, cycle_pair, members, query_rows, info, start):
    position = lax.axis_index("seq")
    count = lax.axis_size("seq")
    dpair = tuple((jnp.zeros(item.shape, jnp.float32) for item in cycle_pair))

    def turn(step, state):
        carry, moving = state
        carry = visit_cycle(
            carry,
            queries,
            douts,
            logsums,
            deltas,
            moving,
            members,
            query_rows,
            (position - step) % count,
            info,
        )
        moving = tuple(shifted((moving[0], moving[1]), "seq", 1))
        return ((carry[0], send_grads(carry[1]), carry[2]), moving)

    carry, moving = lax.fori_loop(0, count - 1, turn, ((start[0], dpair, start[1]), cycle_pair))
    carry = visit_cycle(
        carry,
        queries,
        douts,
        logsums,
        deltas,
        moving,
        members,
        query_rows,
        (position - count + 1) % count,
        info,
    )
    return (carry[0], send_grads(carry[1]), carry[2])


def general_device(
    small_in,
    large_in,
    small_cot,
    large_cot,
    first_gain,
    first_bias,
    query_weight,
    query_bias,
    key_weight,
    value_weight,
    value_bias,
    out_weight,
    out_bias,
    attend_scale,
    second_gain,
    second_bias,
    up_weight,
    up_bias,
    down_weight,
    down_bias,
    feed_scale,
    rel_table,
):
    groups, small_rows, width = small_in.shape
    large_rows = large_in.shape[1]
    all_rows = small_rows + large_rows
    position = lax.axis_index("seq")
    query_rows = (
        position * small_rows + jnp.arange(small_rows, dtype=jnp.int32),
        position * large_rows + jnp.arange(large_rows, dtype=jnp.int32),
    )
    small_places = query_rows[0] % SLEN
    large_places = query_rows[1] % LLEN

    def make_biases(table):
        return (
            position_bias(table, small_places, SLEN, SGRID),
            position_bias(table, large_places, LLEN, LGRID),
        )

    biases, bias_back = jax.vjp(make_biases, rel_table)
    info = ((SLEN, SGRID, biases[0]), (LLEN, LGRID, biases[1]))
    valid_rows = jnp.concatenate(
        [small_places < SGRID * SGRID + 1, large_places < LGRID * LGRID + 1]
    )
    valid_flat = jnp.broadcast_to(valid_rows[None, :], (groups, all_rows)).reshape(-1)
    w_query, w_key, w_value, w_out, w_up, w_down = (
        lax.all_gather(query_weight, "img", axis=0, tiled=True),
        lax.all_gather(key_weight, "img", axis=0, tiled=True),
        lax.all_gather(value_weight, "img", axis=0, tiled=True),
        lax.all_gather(out_weight, "img", axis=0, tiled=True),
        lax.all_gather(up_weight, "img", axis=0, tiled=True),
        lax.all_gather(down_weight, "img", axis=0, tiled=True),
    )

    def split(rows_array):
        shaped = rows_array.reshape(groups, all_rows, -1)
        return (shaped[:, :small_rows], shaped[:, small_rows:])

    inputs = jnp.concatenate([small_in, large_in], axis=1).astype(jnp.float32).reshape(-1, width)
    hidden = layer_norm(inputs, first_gain, first_bias).astype(jnp.bfloat16)
    query = (matmul(hidden, w_query) + query_bias).astype(jnp.bfloat16)
    key = matmul(hidden, w_key).astype(jnp.bfloat16)
    value = (matmul(hidden, w_value) + value_bias).astype(jnp.bfloat16)
    queries = split(query)
    cycle_pair = (key.reshape(groups, all_rows, width), value.reshape(groups, all_rows, width))
    members = ((0, 0, small_rows), (1, small_rows, large_rows))
    attended, logsums = cycle_forward(queries, cycle_pair, members, query_rows, info)
    mixed = (
        jnp.concatenate([attended[0], attended[1]], axis=1).reshape(-1, width).astype(jnp.bfloat16)
    )
    branch = matmul(mixed, w_out) + out_bias
    residual = inputs + attend_scale * branch
    hidden2 = layer_norm(residual, second_gain, second_bias).astype(jnp.bfloat16)
    upper = matmul(hidden2, w_up) + up_bias
    active = jax.nn.gelu(upper, approximate=False).astype(jnp.bfloat16)
    lower = matmul(active, w_down) + down_bias
    output = jnp.where(valid_flat[:, None], residual + feed_scale * lower, 0.0).astype(jnp.bfloat16)
    small_out, large_out = split(output)
    upstream = (
        jnp.concatenate([small_cot, large_cot], axis=1).astype(jnp.float32).reshape(-1, width)
    )
    upstream = upstream * valid_flat[:, None].astype(jnp.float32)
    grad_feed_scale = jnp.sum(upstream * lower, axis=0)
    dlower = (upstream * feed_scale).astype(jnp.bfloat16)
    grad_down_bias = jnp.sum(dlower.astype(jnp.float32), axis=0)
    grad_down = jnp.einsum("rf,rd->fd", active, dlower, preferred_element_type=jnp.float32)
    dactive = jnp.einsum("rd,fd->rf", dlower, w_down, preferred_element_type=jnp.float32)
    unused, gelu_back = jax.vjp(lambda inner: jax.nn.gelu(inner, approximate=False), upper)
    dupper = gelu_back(dactive)[0].astype(jnp.bfloat16)
    grad_up_bias = jnp.sum(dupper.astype(jnp.float32), axis=0)
    grad_up = jnp.einsum("rd,rf->df", hidden2, dupper, preferred_element_type=jnp.float32)
    dhidden2 = jnp.einsum("rf,df->rd", dupper, w_up, preferred_element_type=jnp.float32)
    unused, second_back = jax.vjp(layer_norm, residual, second_gain, second_bias)
    dres_part, grad_second_gain, grad_second_bias = second_back(dhidden2)
    dresidual = upstream + dres_part
    grad_attend_scale = jnp.sum(dresidual * branch, axis=0)
    dbranch = (dresidual * attend_scale).astype(jnp.bfloat16)
    grad_out_bias = jnp.sum(dbranch.astype(jnp.float32), axis=0)
    grad_out = jnp.einsum("rd,re->de", mixed, dbranch, preferred_element_type=jnp.float32)
    dmixed = jnp.einsum("re,de->rd", dbranch, w_out, preferred_element_type=jnp.float32).astype(
        jnp.bfloat16
    )
    held, held_sums = cycle_forward(queries, cycle_pair, members, query_rows, info)
    douts = split(dmixed)
    deltas = tuple(
        (
            jnp.einsum(
                "gqhd,gqhd->ghq",
                to_heads(douts[which].astype(jnp.float32), HEADS),
                to_heads(held[which], HEADS),
            )
            for which in range(2)
        )
    )
    dq_start = tuple(
        (jnp.zeros(to_heads(queries[which], HEADS).shape, jnp.float32) for which in range(2))
    )
    bias_start = tuple((jnp.zeros(item.shape, jnp.float32) for item in biases))
    dqueries, dpair, bias_grads = cycle_backward(
        queries,
        douts,
        held_sums,
        deltas,
        cycle_pair,
        members,
        query_rows,
        info,
        (dq_start, bias_start),
    )
    table_grad = bias_back(bias_grads)[0]
    dquery = jnp.concatenate(
        [
            dqueries[0].reshape(groups, small_rows, width),
            dqueries[1].reshape(groups, large_rows, width),
        ],
        axis=1,
    )
    dquery = dquery.reshape(-1, width).astype(jnp.bfloat16)
    dkey = dpair[0].reshape(-1, width).astype(jnp.bfloat16)
    dvalue = dpair[1].reshape(-1, width).astype(jnp.bfloat16)
    grad_query_bias = jnp.sum(dquery.astype(jnp.float32), axis=0)
    grad_value_bias = jnp.sum(dvalue.astype(jnp.float32), axis=0)
    grad_query = jnp.einsum("rd,re->de", hidden, dquery, preferred_element_type=jnp.float32)
    grad_key = jnp.einsum("rd,re->de", hidden, dkey, preferred_element_type=jnp.float32)
    grad_value = jnp.einsum("rd,re->de", hidden, dvalue, preferred_element_type=jnp.float32)
    dhidden = (
        jnp.einsum("re,de->rd", dquery, w_query, preferred_element_type=jnp.float32)
        + jnp.einsum("re,de->rd", dkey, w_key, preferred_element_type=jnp.float32)
        + jnp.einsum("re,de->rd", dvalue, w_value, preferred_element_type=jnp.float32)
    )
    unused, first_back = jax.vjp(layer_norm, inputs, first_gain, first_bias)
    dinput_part, grad_first_gain, grad_first_bias = first_back(dhidden)
    dinputs = (dresidual + dinput_part).astype(jnp.bfloat16)
    small_grad, large_grad = split(dinputs)
    shares = (
        lax.psum_scatter(grad_query, "img", scatter_dimension=0, tiled=True),
        lax.psum_scatter(grad_key, "img", scatter_dimension=0, tiled=True),
        lax.psum_scatter(grad_value, "img", scatter_dimension=0, tiled=True),
        lax.psum_scatter(grad_out, "img", scatter_dimension=0, tiled=True),
        lax.psum_scatter(grad_up, "img", scatter_dimension=0, tiled=True),
        lax.psum_scatter(grad_down, "img", scatter_dimension=0, tiled=True),
    )
    shares = lax.psum((shares[0], shares[1], shares[2], shares[3], shares[4], shares[5]), "seq")
    smalls = lax.psum(
        (
            grad_first_gain,
            grad_first_bias,
            grad_query_bias,
            grad_value_bias,
            grad_out_bias,
            grad_attend_scale,
            grad_second_gain,
            grad_second_bias,
            grad_up_bias,
            grad_down_bias,
            grad_feed_scale,
            table_grad,
        ),
        ("img", "seq"),
    )
    return (
        small_out,
        large_out,
        small_grad,
        large_grad,
        smalls[0],
        smalls[1],
        shares[0],
        smalls[2],
        shares[1],
        shares[2],
        smalls[3],
        shares[3],
        smalls[4],
        smalls[5],
        smalls[6],
        smalls[7],
        shares[4],
        smalls[8],
        shares[5],
        smalls[9],
        smalls[10],
        smalls[11],
    )


def image_device(
    small_in,
    large_in,
    small_cot,
    large_cot,
    first_gain,
    first_bias,
    query_weight,
    query_bias,
    key_weight,
    value_weight,
    value_bias,
    out_weight,
    out_bias,
    attend_scale,
    second_gain,
    second_bias,
    up_weight,
    up_bias,
    down_weight,
    down_bias,
    feed_scale,
    rel_table,
):
    groups, small_rows, width = small_in.shape
    n_small = groups * small_rows // SLEN

    x, cot, qkv, turned, w_qkv, w_mid, w_down, attended, out_wide, *probs = run_begin(
        (query_weight, key_weight, value_weight, out_weight, up_weight, down_weight),
        (
            small_in.reshape(n_small, SLEN, width),
            large_in,
            small_cot.reshape(n_small, SLEN, width),
            large_cot,
        ),
        rel_table,
        (first_gain, first_bias, query_bias, value_bias),
        1,
    )
    w_mid, w_down = (w.reshape(-1, w.shape[-1]) for w in (w_mid, w_down))
    out, dresidual, dattended, feed_grads, g_mid, g_down = run_feed(
        x,
        attended,
        cot,
        w_mid,
        w_down,
        (out_bias, attend_scale, second_gain, second_bias, down_bias, feed_scale, up_bias),
        n_small,
    )
    small_out, large_out, small_grad, large_grad, *made = run_end(
        qkv,
        dattended,
        out_wide,
        probs,
        [g_mid, g_down],
        [x, turned, w_qkv, dresidual, out],
        feed_grads,
        first_gain,
        n_small,
        2,
    )
    grads = run_finish(made[4:], made[:4], rel_table.shape[1])
    small_out, small_grad = (v.reshape(groups, small_rows, width) for v in (small_out, small_grad))
    return (small_out, large_out, small_grad, large_grad, *grads)


def per_device(*args):
    groups, small_rows, unused = args[0].shape
    if lax.axis_size("seq") == 2 and groups == 2 and small_rows % SLEN == 0:
        return image_device(*args)
    return general_device(*args)


def solution(mesh):
    return jax.shard_map(
        per_device,
        mesh=mesh,
        in_specs=(
            P("img", "seq", None),
            P("img", "seq", None),
            P("img", "seq", None),
            P("img", "seq", None),
            P(),
            P(),
            P("img", None),
            P(),
            P("img", None),
            P("img", None),
            P(),
            P("img", None),
            P(),
            P(),
            P(),
            P(),
            P("img", None),
            P(),
            P("img", None),
            P(),
            P(),
            P(),
        ),
        out_specs=(
            P("img", "seq", None),
            P("img", "seq", None),
            P("img", "seq", None),
            P("img", "seq", None),
            P(),
            P(),
            P("img", None),
            P(),
            P("img", None),
            P("img", None),
            P(),
            P("img", None),
            P(),
            P(),
            P(),
            P(),
            P("img", None),
            P(),
            P("img", None),
            P(),
            P(),
            P(),
        ),
        check_vma=False,
    )
```

```python
import functools

import jax
import jax.numpy as jnp
from jax import lax
from jax.experimental import pallas as pl
from jax.experimental.pallas import tpu as pltpu
from jax.sharding import PartitionSpec as P

HEADS = 12
SGRID = 14
LGRID = 24
SLEN = 256
LLEN = 640
SPAD = 208
LPAD = 608
LANES = 128

NEGATIVE = -1e30
EPSILON = 1e-06
F32 = jnp.float32
BF16 = jnp.bfloat16
VMEM_BYTES = 62 << 20


def dot_nn(left, right):
    return lax.dot_general(left, right, (((1,), (0,)), ((), ())), preferred_element_type=F32)


def dot_nt(left, right):
    return lax.dot_general(left, right, (((1,), (1,)), ((), ())), preferred_element_type=F32)


def normalized(values):
    center = values - jnp.mean(values, axis=-1, keepdims=True)
    spread = jnp.mean(center * center, axis=-1, keepdims=True)
    scale = lax.rsqrt(spread + EPSILON)
    return center * scale, scale


def norm_back(grad, normal, scale):
    return scale * (
        grad
        - jnp.mean(grad, axis=-1, keepdims=True)
        - normal * jnp.mean(grad * normal, axis=-1, keepdims=True)
    )


def row_sum(values):
    return jnp.sum(values, axis=0, keepdims=True)


def iota(shape, axis):
    return lax.broadcasted_iota(jnp.int32, shape, axis)


L_WIDTH = 1280
S_WIDTH = 512


SPAN = 2 * LGRID - 1
CELLS = SPAN * SPAN
T_WIDTH = 2304


def row_moves():
    off = LGRID - SGRID
    moves = []
    for m in range(SPAN):
        moves.append((m * SPAN, m * LGRID, LGRID, False, True))
        moves.append((m * SPAN + LGRID, (m + 1) * LGRID, LGRID - 1, True, True))
    for m in range(2 * SGRID - 1):
        start = (m + off) * SPAN + off
        moves.append((start, m * SGRID, SGRID, False, False))
        moves.append((start + SGRID, (m + 1) * SGRID, SGRID - 1, True, False))
    return moves


def moved(source, start, target, width, count):
    source_tile = min(start // LANES, source.shape[1] // LANES - 2)
    target_tile = min(target // LANES, width // LANES - 2)
    piece = source[:, source_tile * LANES : source_tile * LANES + 256]
    turn = (target - target_tile * LANES - start + source_tile * LANES) % 256
    if turn:
        piece = pltpu.roll(piece, turn, 1)
    lane = iota(piece.shape, 1) - (target - target_tile * LANES)
    return slice(target_tile * LANES, target_tile * LANES + 256), piece, (lane >= 0) & (lane < count)


def table_sequences(table, wide_table, lows, highs):
    heads, entries = table.shape
    wide_table[...] = jnp.zeros_like(wide_table)
    wide_table[pl.ds(0, heads), pl.ds(0, entries)] = table[...]
    for ref in lows + highs:
        ref[...] = jnp.zeros_like(ref)
    for start, place_at, count, high, large in row_moves():
        ref = (highs if high else lows)[0 if large else 1]
        where, piece, inside = moved(wide_table, start, place_at, ref.shape[1], count)
        ref[:, where] = jnp.where(inside, piece, ref[:, where])


def table_from_sequences(lows, highs, wide_table):
    wide_table[...] = jnp.zeros_like(wide_table)
    for start, place_at, count, high, large in row_moves():
        ref = (highs if high else lows)[0 if large else 1]
        where, piece, inside = moved(ref, place_at, start, T_WIDTH, count)
        wide_table[:, where] += jnp.where(inside, piece, 0.0)
    where, piece, inside = moved(lows[1], S_WIDTH - 3, CELLS, T_WIDTH, 3)
    wide_table[:, where] += jnp.where(inside, piece, 0.0)


def one_entry(row, place_at):
    return jnp.sum(jnp.where(iota(row.shape, 1) == place_at, row, 0.0), axis=1, keepdims=True)


def takes_low(rows, width, grid, first):
    step = iota((rows, width), 1) % grid
    row = iota((rows, width), 0)
    low = step >= grid - 1 + first - row
    if first == 1:
        low = low | (row == 0)
    return low


def spread_sequences(low, high, rows, width, grid, first):
    low = jnp.broadcast_to(low, (rows, width))
    high = jnp.broadcast_to(high, (rows, width))
    chosen = jnp.where(takes_low(rows, width, grid, first), low, high)
    return pltpu.roll(chosen, 1, 1, stride=1, stride_axis=0)


def gather_sequences(spread, rows, width, grid, first):
    row = iota((rows, width), 0) + 1
    for bit in (1, 2, 4, 8, 16):
        spread = jnp.where((row & bit) != 0, pltpu.roll(spread, width - bit, 1), spread)
    low = takes_low(rows, width, grid, first)
    return (
        row_sum(jnp.where(low, spread, 0.0)),
        row_sum(jnp.where(low, 0.0, spread)),
    )


def large_window(block):
    start = (LGRID - block) * LGRID
    return start // LANES, start % LANES


def small_window(block):
    start = (SGRID - 1 - block) * SGRID + SGRID - 1
    return start // LANES, start % LANES


def head_masks():
    lane = iota((1, LANES), 1)
    return (
        jnp.where(lane < LANES // 2, 1.0, 0.0).astype(BF16),
        jnp.where(lane < LANES // 2, 0.0, 1.0).astype(BF16),
    )


def transposed_biases(large_seq, small_seq, entries, wide, narrow, bias_large, bias_small):
    patch_q, patch_k, both = (one_entry(entries, CELLS + i - T_WIDTH + 256) for i in range(3))
    wide[...] = spread_sequences(*large_seq, 24, L_WIDTH, LGRID, 1)
    lane = iota((24, LANES), 1)
    row = iota((24, LANES), 0)
    for block in range(LGRID + 1):
        at, turn = large_window(block)
        piece = wide[:, at * LANES : at * LANES + 768]
        if turn:
            piece = pltpu.roll(piece, 768 - turn, 1)
        piece = piece[:, :640]
        if block == 0:
            rest = jnp.where(iota((24, 640), 0) == 0, patch_k, piece)
        elif block == LGRID:
            rest = jnp.where(iota((24, 640), 0) == 0, piece, NEGATIVE)
        else:
            rest = piece
        first = jnp.where(lane == 0, patch_q, rest[:, :LANES])
        if block == 0:
            first = jnp.where((lane == 0) & (row == 0), both, first)
        if block == LGRID:
            first = jnp.where(row == 0, first, NEGATIVE)
        bias_large[pl.ds(block * 24, 24), 0:LANES] = first
        bias_large[pl.ds(block * 24, 24), LANES:640] = rest[:, LANES:]
    bias_large[pl.ds(600, 8), :] = jnp.full((8, 640), NEGATIVE, F32)
    narrow[...] = spread_sequences(*small_seq, 16, S_WIDTH, SGRID, 0)
    for block in range(SGRID):
        at, turn = small_window(block)
        piece = narrow[:, at * LANES : at * LANES + 384]
        if turn:
            piece = pltpu.roll(piece, 384 - turn, 1)
        bias_small[pl.ds(1 + SGRID * block, SGRID), :] = piece[:SGRID, :256]
    whole = bias_small[...]
    lane = iota((SPAD, 256), 1)
    row = iota((SPAD, 256), 0)
    whole = jnp.where(lane == 0, patch_q, whole)
    whole = jnp.where(row == 0, patch_k, whole)
    whole = jnp.where((lane == 0) & (row == 0), both, whole)
    bias_small[...] = jnp.where(row > SGRID * SGRID, NEGATIVE, whole)


MESH = pl.DeviceIdType.MESH
ZS = 4


def place():
    img = lax.axis_index("img")
    return img // 4, (img // 2) % 2, img % 2, lax.axis_index("seq")


def device(z, x, c, y):
    return ((z * 2 + x) * 2 + c, y)


def z_peer(z, hop):
    low = (z % 2) * (1 - 2 * (hop % 2)) + hop % 2
    high = (z // 2) * (1 - 2 * (hop // 2)) + hop // 2
    return high * 2 + low


def greet():
    z, x, c, y = place()
    barrier = pltpu.get_barrier_semaphore()
    peers = [device(z_peer(z, hop), x, c, y) for hop in range(1, ZS)]
    for flip in range(1, 8):
        peers.append(
            device(
                z,
                1 - x if flip & 1 else x,
                1 - c if flip & 2 else c,
                1 - y if flip & 4 else y,
            )
        )
    for peer in peers:
        pl.semaphore_signal(barrier, inc=1, device_id=peer, device_id_type=MESH)
    pl.semaphore_wait(barrier, len(peers))


def greet_seq():
    z, x, c, y = place()
    barrier = pltpu.get_barrier_semaphore()
    pl.semaphore_signal(barrier, inc=1, device_id=device(z, x, c, 1 - y), device_id_type=MESH)
    pl.semaphore_wait(barrier, 1)


def half_of(width, y):
    return pl.ds(pl.multiple_of(y * (width // 2), 128), width // 2)


class Gather:
    n_sems = 21

    def __init__(self, share, whole, send, recv, own, spare_seq):
        self.share, self.whole, self.send, self.recv, self.own = share, whole, send, recv, own
        self.spare_seq = spare_seq
        self.width = share.shape[1]
        self.at = z, x, c, y = place()
        self.inner = z % 3 != 0

    def copy(self, source, target, index, peer, recv=None):
        return pltpu.make_async_remote_copy(
            src_ref=source,
            dst_ref=target,
            send_sem=self.send.at[index],
            recv_sem=self.recv.at[index if recv is None else recv],
            device_id=peer,
            device_id_type=MESH,
        )

    def source_z(self, turn):
        z = self.at[0]
        is_inner = jnp.minimum(z % 3, 1)
        hop = (0, 1, 2 + is_inner, 3 - is_inner)[turn]
        return z_peer(z, hop)

    def along_z(self, turn, onto, recv):
        z, x, c, y = self.at
        cols = half_of(self.width, y)
        target = self.whole.at[self.source_z(turn), x, c, :, cols]
        source = self.share.at[:, cols] if turn == 0 else target
        index = {(0, 1): 0, (0, 3): 1, (1, 3): 2, (2, 1): 19, (3, 1): 20}[turn, onto]
        return self.copy(source, target, index, device(z_peer(z, onto), x, c, y), recv - 1)

    def from_z(self, turn):
        z, x, c, y = self.at
        cols = half_of(self.width, y)
        block = self.whole.at[self.source_z(turn), x, c, :, cols]
        return self.copy(block, block, turn - 1, device(z_peer(z, 1), x, c, y))

    def across(self, turn, axis):
        z, x, c, y = self.at
        cols = half_of(self.width, y)
        target = self.whole.at[self.source_z(turn), x, c, :, cols]
        source = self.share.at[:, cols] if turn == 0 else target
        peer = device(z, 1 - x, c, y) if axis == 0 else device(z, x, c, 1 - y)
        return self.copy(source, target, 3 + 4 * axis + turn, peer)

    def onward(self, turn):
        z, x, c, y = self.at
        source_z = self.source_z(turn)
        even = 1 if turn == 0 else 0 if self.spare_seq else 1 - source_z % 2
        side = x + even * (1 - 2 * x)
        cols = half_of(self.width, y + (1 - even) * (1 - 2 * y))
        block = self.whole.at[source_z, side, c, :, cols]
        peer = device(z, x + (1 - even) * (1 - 2 * x), c, y + even * (1 - 2 * y))
        return self.copy(block, block, 11 + turn, peer)

    def to_core(self, turn):
        z, x, c, y = self.at
        block = self.whole.at[self.source_z(turn), :, c]
        return self.copy(block, block, 15 + turn, device(z, x, 1 - c, y))

    def keep_own(self):
        z, x, c, y = self.at
        return pltpu.make_async_copy(self.share, self.whole.at[z, x, c], self.own)

    def begin(self):
        self.begin_z()
        self.begin_across()

    def begin_across(self):
        self.keep_own().start()
        self.across(0, 0).start()

    def begin_z(self):
        self.along_z(0, 1, 1).start()

        @pl.when(self.inner)
        def _():
            self.along_z(0, 3, 2).start()

    def come(self, hop):
        self.from_z(hop).wait_recv()

        @pl.when(self.inner)
        def _():
            if hop == 1:
                self.along_z(1, 3, 3).start()
            else:
                self.along_z(hop, 1, hop).start()

        for axis in range(2):
            self.across(hop, axis).start()

    def pass_on(self, hop):
        for axis in range(2 if hop else 1):
            self.across(hop, axis).wait_recv()
        self.onward(hop).start()

    def give(self, hop):
        if hop == 0:
            self.keep_own().wait()
        self.onward(hop).wait_recv()
        self.to_core(hop).start()

    def turn(self, at):
        stage, hop = (
            (self.come, 1),
            (self.pass_on, 0),
            (self.come, 2),
            (self.pass_on, 1),
            (self.come, 3),
            (self.pass_on, 2),
            (self.give, 0),
            (self.pass_on, 3),
            (self.give, 1),
            (self.give, 2),
            (self.give, 3),
        )[at]
        stage(hop)

    def arrive(self):
        for hop in range(ZS):
            self.to_core(hop).wait_recv()

    def drain(self):
        for hop in range(ZS):
            self.to_core(hop).wait_send()
            self.onward(hop).wait_send()
            for axis in range(2 if hop else 1):
                self.across(hop, axis).wait_send()
        self.along_z(0, 1, 1).wait_send()

        @pl.when(self.inner)
        def _():
            self.along_z(0, 3, 2).wait_send()
            self.along_z(1, 3, 3).wait_send()
            self.along_z(2, 1, 2).wait_send()
            self.along_z(3, 1, 3).wait_send()


class Rows:
    n_sems = 2

    def __init__(self, small, large, line, sems, send, recv):
        self.small, self.large, self.line = small, large, line
        self.sems, self.send, self.recv = sems, send, recv
        self.at = place()
        self.n_small = small.shape[0]
        self.base = self.n_small * SPAD
        self.rows = large.shape[1]

    def spot(self):
        start = self.base + self.rows * self.at[3]
        return self.line.at[pl.ds(pl.multiple_of(start, 16), self.rows)]

    def local(self, i):
        if i < self.n_small:
            return pltpu.make_async_copy(
                self.small.at[i, pl.ds(0, SPAD)],
                self.line.at[pl.ds(i * SPAD, SPAD)],
                self.sems.at[i],
            )
        return pltpu.make_async_copy(self.large.at[self.at[3]], self.spot(), self.sems.at[i])

    def remote(self):
        z, x, c, y = self.at
        return pltpu.make_async_remote_copy(
            src_ref=self.large.at[1 - y],
            dst_ref=self.spot(),
            send_sem=self.send,
            recv_sem=self.recv,
            device_id=device(z, x, c, 1 - y),
            device_id_type=MESH,
        )

    def begin(self):
        self.remote().start()
        for i in range(self.n_small + 1):
            self.local(i).start()

    def wait_small(self):
        for i in range(self.n_small):
            self.local(i).wait()

    def wait_large(self):
        self.local(self.n_small).wait()
        self.remote().wait()


def add_rows(target, source, shape):
    rows, cols = shape
    many = max(n for n in range(16, rows + 1, 16) if rows % n == 0 and n * cols <= 65536)

    def strip(i, unused):
        at = pl.ds(pl.multiple_of(i * many, 16), many)
        target[at, :] = (target[at, :].astype(F32) + source[at, :].astype(F32)).astype(BF16)
        return unused

    lax.fori_loop(0, rows // many, strip, 0)


class Reduce:
    n_sems = 21
    n_scratch = 6

    def __init__(self, grad, out, held, core, first, second, last, edge, send, recv, own, x_first):
        self.x_first = x_first
        self.grad, self.held, self.core = grad, held, core
        self.first, self.second, self.last, self.edge, self.out = first, second, last, edge, out
        self.send, self.recv, self.own = send, recv, own
        self.rows, self.width = out.shape
        self.at = place()
        self.mine = half_of(self.width, self.at[3])
        self.other = half_of(self.width, 1 - self.at[3])

    @staticmethod
    def scratch(rows, width):
        half = width // 2
        return [
            pltpu.VMEM((ZS, 2, rows, width), BF16),
            pltpu.VMEM((ZS, 2, rows, width), BF16),
            pltpu.VMEM((ZS, 2, rows, half), BF16),
            pltpu.VMEM((ZS, rows, half), BF16),
            pltpu.VMEM((ZS, rows, half), BF16),
            pltpu.VMEM((2, rows, half), BF16),
        ]

    def copy(self, source, target, index, peer):
        return pltpu.make_async_remote_copy(
            src_ref=source,
            dst_ref=target,
            send_sem=self.send.at[index],
            recv_sem=self.recv.at[index],
            device_id=peer,
            device_id_type=MESH,
        )

    def load(self, s):
        return pltpu.make_async_copy(
            self.grad.at[s, :, self.at[2]], self.held.at[s], self.own.at[s]
        )

    def between_cores(self, s):
        z, x, c, y = self.at
        return self.copy(self.grad.at[s, :, 1 - c], self.core.at[s], s, device(z, x, 1 - c, y))

    def leg_one(self, s, i):
        z, x, c, y = self.at
        half = self.width // 2
        if s in self.x_first:
            source = self.held.at[s, 1 - x, :, pl.ds(i * half, half)]
            peer = device(z, 1 - x, c, y)
        else:
            source = self.held.at[s, i, :, self.other]
            peer = device(z, x, c, 1 - y)
        return self.copy(source, self.first.at[s, i], 4 + 2 * s + i, peer)

    def leg_two(self, s):
        z, x, c, y = self.at
        if s in self.x_first:
            source = self.held.at[s, x, :, self.other]
            peer = device(z, x, c, 1 - y)
        else:
            source = self.held.at[s, 1 - x, :, self.mine]
            peer = device(z, 1 - x, c, y)
        return self.copy(source, self.second.at[s], 12 + s, peer)

    def leg_three(self, s):
        z, x, c, y = self.at
        hop = (z + s) % 2 + 2 * ((z // 2 + s // 2) % 2)
        source = self.held.at[s, x, :, self.mine]
        return self.copy(source, self.last.at[hop], 16 + hop, device(s, x, c, y))

    def from_z(self, hop):
        z, x, c, y = self.at
        slot = self.last.at[hop]
        return self.copy(slot, slot, 16 + hop, device(z_peer(z, hop), x, c, y))

    def leg_four(self):
        z, x, c, y = self.at
        return self.copy(self.edge.at[0], self.edge.at[1], 20, device(z, x, c, 1 - y))

    def begin(self):
        for s in (0, 3, 1, 2):
            self.between_cores(s).start()
            self.load(s).start()

    def one(self, s):
        self.load(s).wait()
        self.between_cores(s).wait_recv()
        for i in range(2):
            add_rows(self.held.at[s, i], self.core.at[s, i], (self.rows, self.width))
        for i in range(2):
            self.leg_one(s, i).start()

    def two(self, s):
        x = self.at[1]
        half = self.width // 2
        for i in range(2):
            self.leg_one(s, i).wait_recv()
            if s in self.x_first:
                target = self.held.at[s, x, :, pl.ds(i * half, half)]
            else:
                target = self.held.at[s, i, :, self.mine]
            add_rows(target, self.first.at[s, i], (self.rows, half))
        self.leg_two(s).start()

    def three(self, s):
        x = self.at[1]
        self.leg_two(s).wait_recv()
        target = self.held.at[s, x, :, self.mine]
        add_rows(target, self.second.at[s], (self.rows, self.width // 2))

        @pl.when(self.at[0] != s)
        def _():
            self.leg_three(s).start()

    def four(self):
        z, x, c, y = self.at
        for hop in range(1, ZS):
            self.from_z(hop).wait_recv()
        own = self.held.at[z, x, :, self.mine]
        last, edge = self.last, self.edge

        def strip(i, unused):
            at = pl.ds(pl.multiple_of(i * 16, 16), 16)
            total = own[at, :].astype(F32)
            for hop in range(1, ZS):
                total += last[hop, at, :].astype(F32)
            edge[0, at, :] = total.astype(BF16)
            return unused

        lax.fori_loop(0, self.rows // 16, strip, 0)
        self.leg_four().start()
        self.out[:, self.mine] = edge[0].astype(F32)

    def finish(self):
        self.leg_four().wait()
        self.out[:, self.other] = self.edge[1].astype(F32)
        for s in range(ZS):
            self.between_cores(s).wait_send()
            for i in range(2):
                self.leg_one(s, i).wait_send()
            self.leg_two(s).wait_send()

            @pl.when(self.at[0] != s)
            def _():
                self.leg_three(s).wait_send()


class Total:
    long = (("c",), ("x",), ("y",), ("z",))
    short = (("c", "x", "y"), ("z",))
    n_slots = 12

    def __init__(self, part, out, leave, come, send, recv, rounds):
        self.part, self.out, self.leave, self.come = part, out, leave, come
        self.send, self.recv, self.rounds = send, recv, rounds
        self.at = place()

    @staticmethod
    def scratch(shape, kind):
        return [pltpu.VMEM((4,) + shape, kind), pltpu.VMEM((Total.n_slots,) + shape, kind)]

    def group(self, step):
        z, x, c, y = self.at
        axes = self.rounds[step]
        if axes == ("z",):
            members = [device(i, x, c, y) for i in range(ZS)]
            return 8, z, members
        number, members = 0, []
        for axis in axes:
            number = number * 2 + {"c": c, "x": x, "y": y}[axis]
        for i in range(2 ** len(axes)):
            bits = {axis: (i >> (len(axes) - 1 - k)) % 2 for k, axis in enumerate(axes)}
            members.append(device(z, bits.get("x", x), bits.get("c", c), bits.get("y", y)))
        return 2 * step, number, members

    def copy(self, step, to, source):
        first, number, members = self.group(step)
        return pltpu.make_async_remote_copy(
            src_ref=self.leave.at[step],
            dst_ref=self.come.at[first + source],
            send_sem=self.send.at[first + to],
            recv_sem=self.recv.at[first + source],
            device_id=members[to],
            device_id_type=MESH,
        )

    def give(self, step, values):
        first, number, members = self.group(step)
        low = values.astype(self.leave.dtype)
        self.leave[step] = low
        self.come[first + number] = low
        for to in range(len(members)):

            @pl.when(number != to)
            def _():
                self.copy(step, to, number).start()

    def begin(self):
        self.give(0, self.part[...])

    def advance(self, step):
        first, number, members = self.group(step)
        for other in range(len(members)):

            @pl.when(number != other)
            def _():
                self.copy(step, other, other).wait_recv()
                self.copy(step, other, number).wait_send()

        total = self.come[first].astype(F32)
        for other in range(1, len(members)):
            total += self.come[first + other].astype(F32)
        if step + 1 < len(self.rounds):
            self.give(step + 1, total)
        else:
            self.out[...] = total


class RowsBack:
    n_sems = 3

    def __init__(self, line, blank, small, large, sems, send, recv):
        self.line, self.blank, self.small, self.large = line, blank, small, large
        self.sems, self.send, self.recv = sems, send, recv
        self.at = place()
        self.n_small = small.shape[0]
        self.rows = large.shape[1]

    def half(self, y):
        start = self.n_small * SPAD + self.rows * y
        return self.line.at[pl.ds(pl.multiple_of(start, 16), self.rows)]

    def local(self, i):
        n = self.n_small
        if i < n:
            source, target = self.line.at[pl.ds(i * SPAD, SPAD)], self.small.at[i, pl.ds(0, SPAD)]
        elif i < 2 * n:
            source, target = self.blank, self.small.at[i - n, pl.ds(SPAD, SLEN - SPAD)]
        else:
            y = self.at[3]
            source, target = self.half(y), self.large.at[y]
        return pltpu.make_async_copy(source, target, self.sems.at[i])

    def remote(self):
        z, x, c, y = self.at
        return pltpu.make_async_remote_copy(
            src_ref=self.half(1 - y),
            dst_ref=self.large.at[y],
            send_sem=self.send,
            recv_sem=self.recv,
            device_id=device(z, x, c, 1 - y),
            device_id_type=MESH,
        )

    def begin_large(self):
        self.remote().start()
        self.local(2 * self.n_small).start()

    def begin_small(self):
        for i in range(2 * self.n_small):
            self.local(i).start()

    def finish(self):
        for i in range(2 * self.n_small + 1):
            self.local(i).wait()
        self.remote().wait()


def begin_kernel(
    n_small,
    n_large,
    query_weight,
    key_weight,
    value_weight,
    out_weight,
    up_weight,
    down_share,
    small_in,
    large_in,
    small_cot,
    large_cot,
    table,
    gain,
    gain_bias,
    query_bias,
    value_bias,
    x_out,
    cot_out,
    qkv_out,
    turned_out,
    w_out,
    mid_whole,
    down_whole,
    out,
    out_wide,
    probs_small,
    probs_large,
    line,
    cot_line,
    hidden,
    turned,
    qkv,
    w_qkv,
    wide,
    narrow,
    bias_large,
    bias_small,
    send,
    recv,
    own,
    row_sems,
    row_send,
    row_recv,
    keep_sems,
    qkv_share,
    mid_share,
    share_sems,
    wide_table,
    low_large,
    low_small,
    high_large,
    high_small,
):
    step = pl.program_id(0)
    pairs = pl.num_programs(0)
    lows, highs = (low_large, low_small), (high_large, high_small)
    shares = []
    for target, weights in (
        (qkv_share, (query_weight, key_weight, value_weight)),
        (mid_share, (out_weight, up_weight)),
    ):
        col = 0
        for weight in weights:
            cols = slice(col, col + weight.shape[1])
            shares.append(
                pltpu.make_async_copy(weight, target.at[:, cols], share_sems.at[len(shares)])
            )
            col += weight.shape[1]
    width = hidden.shape[1]
    count = qkv.shape[1]
    masks = head_masks()
    first = Gather(qkv_share, w_qkv, send.at[0], recv.at[0], own.at[0], True)
    mid = Gather(mid_share, mid_whole, send.at[1], recv.at[1], own.at[1], False)
    down = Gather(down_share, down_whole, send.at[2], recv.at[2], own.at[2], True)
    x_rows = Rows(small_in, large_in, line, row_sems.at[0], row_send.at[0], row_recv.at[0])
    cot_rows = Rows(small_cot, large_cot, cot_line, row_sems.at[1], row_send.at[1], row_recv.at[1])
    keeps = [
        pltpu.make_async_copy(line, x_out, keep_sems.at[0]),
        pltpu.make_async_copy(qkv, qkv_out, keep_sems.at[1]),
        pltpu.make_async_copy(w_qkv, w_out, keep_sems.at[2]),
        pltpu.make_async_copy(cot_line, cot_out, keep_sems.at[3]),
        pltpu.make_async_copy(turned, turned_out, keep_sems.at[4]),
    ]

    early = (
        ((mid, 2), (mid, 1), (down, 2), (down, 1),),
        ((mid, 4), (down, 4),),
        ((mid, 3),),
    )
    slots = (
        ((down, 3),),
        ((mid, 5),),
        ((down, 5),),
        ((mid, 6),),
        ((down, 6),),
        ((mid, 7),),
        ((down, 7),),
        ((mid, 8),),
        ((down, 8),),
        ((mid, 9), (down, 9),),
        ((mid, 10),),
        ((down, 10),),
    )

    @pl.when(step == 0)
    def _():
        for share in shares:
            share.start()
        greet()
        for share in shares:
            share.wait()
        first.begin()
        x_rows.begin()
        table_sequences(table, wide_table, lows, highs)
        part = chunk_rows(count)
        chunks = [pl.ds(at, part) for at in range(0, count, part)]

        def norm(rows):
            normal, unused = normalized(line[rows, :].astype(F32))
            hidden[rows, :] = (normal * gain[...][None, :] + gain_bias[...][None, :]).astype(BF16)

        x_rows.wait_small()
        norm(chunks[0])
        for at in range(5):
            first.turn(at)
        mid.begin_z()
        down.begin_z()
        for at in range(5, 8):
            first.turn(at)
        x_rows.wait_large()
        for rows in chunks[1:]:
            norm(rows)
        keeps[0].start()
        mid.turn(0)
        down.turn(0)
        for at in range(8, 11):
            first.turn(at)
        first.arrive()
        mid.begin_across()
        down.begin_across()
        cot_rows.begin()
        keeps[2].start()
        scale = jnp.asarray(float(width // HEADS) ** (-0.5), BF16)
        for at, rows in enumerate(chunks):
            for kind in range(3):
                cols = slice(kind * width, (kind + 1) * width)
                weight = w_qkv[:, :, :, :, cols].reshape(width, width)
                made = dot_nn(hidden[rows, :], weight)
                if kind != 1:
                    made += (query_bias, None, value_bias)[kind][...][None, :]
                made = made.astype(BF16)
                if kind == 0:
                    made = made * scale
                for j in range(HEADS // 2):
                    qkv[kind * (HEADS // 2) + j, rows, :] = made[:, j * LANES : (j + 1) * LANES]
            for job, turn in early[at]:
                job.turn(turn)
        keeps[1].start()
        turned[...] = hidden[...].T
        keeps[4].start()

    query = qkv.at[step]
    key = qkv.at[pairs + step]
    value = qkv.at[2 * pairs + step]

    @pl.when(pl.program_id(0) == 0)
    def _():
        bias_small[...] = jnp.zeros_like(bias_small)

    members = [(i * SPAD, SPAD, bias_small, probs_small, i) for i in range(n_small)]
    members += [
        (n_small * SPAD + i * LPAD, LPAD, bias_large, probs_large, i) for i in range(n_large)
    ]
    halves = [[] for _ in members]
    for head in range(2):
        at_head = pl.ds(2 * step + head, 1)
        transposed_biases(
            (lows[0][at_head, :], highs[0][at_head, :]),
            (lows[1][at_head, :], highs[1][at_head, :]),
            wide_table[at_head, T_WIDTH - 256 :],
            wide,
            narrow,
            bias_large,
            bias_small,
        )
        for at, (start, count, bias, probs, which) in enumerate(members):
            rows = pl.ds(start, count)
            scores = dot_nt(key[rows, :], query[rows, :] * masks[head]) + bias[:, :count]
            top = jnp.max(scores, axis=0, keepdims=True)
            weights = jnp.exp(scores - top)
            total = jnp.sum(weights, axis=0, keepdims=True)
            prob = (weights * (1.0 / total)).astype(BF16)
            probs[head, which] = prob
            turned = value[rows, :].T
            halves[at].append(dot_nn(turned[head * 64 : head * 64 + 64, :], prob))
        for at in range(HEADS // 2):
            if slots[2 * at + head]:

                @pl.when(step == at)
                def _():
                    for job, turn in slots[2 * at + head]:
                        job.turn(turn)

    for at, (start, count, bias, probs, which) in enumerate(members):
        both = jnp.concatenate(halves[at], axis=0).T
        out[pl.ds(start, count), :] = both.astype(BF16)
        out_wide[pl.ds(start, count), :] = both

    @pl.when(step == pairs - 3)
    def _():
        cot_rows.wait_small()
        cot_rows.wait_large()
        keeps[3].start()

    @pl.when(step == pairs - 1)
    def _():
        for job in (mid, down):
            job.arrive()
        for job in (first, mid, down):
            job.drain()
        for keep in keeps:
            keep.wait()


EARLY = 4


def end_kernel(
    n_small,
    n_large,
    query,
    key,
    value,
    dout,
    out_wide,
    probs_small,
    probs_large,
    g_mid,
    g_down,
    x_hbm,
    turned_hbm,
    w_hbm,
    dres_hbm,
    feed_grads,
    gain,
    small_grad,
    large_grad,
    mid_out,
    down_out,
    early_out,
    late_out,
    feed_total,
    input_total,
    table_total,
    *scratch,
):
    scratch = list(scratch)

    def take(count):
        taken = scratch[:count]
        del scratch[:count]
        return taken

    wide, narrow, dsum_small, dscore_large, dqkv, hidden_turned, w_qkv, line, blank = take(9)
    early_grad, late_grad, input_part, table_part = take(4)
    large_part = table_part.at[:, :L_WIDTH]
    small_part = table_part.at[:, L_WIDTH:]
    mid_bufs, down_bufs, early_bufs, late_bufs = [take(Reduce.n_scratch) for unused in range(4)]
    feed_bufs, input_bufs, table_bufs = [take(2) for unused in range(3)]
    send, recv, own, total_send, total_recv, load_sems, row_sems, row_send, row_recv = scratch

    step = pl.program_id(0)
    pairs = HEADS // 2
    width = x_hbm.shape[1]
    all_rows = dqkv.shape[1]
    masks = head_masks()
    query, key, value = query.at[0], key.at[0], value.at[0]
    both_ways, mostly_x = (0, 1), (0, 1)
    mid = Reduce(g_mid, mid_out, *mid_bufs, send.at[0], recv.at[0], own.at[0], both_ways)
    down = Reduce(g_down, down_out, *down_bufs, send.at[1], recv.at[1], own.at[1], both_ways)
    early = Reduce(early_grad, early_out, *early_bufs, send.at[2], recv.at[2], own.at[2], mostly_x)
    late = Reduce(late_grad, late_out, *late_bufs, send.at[3], recv.at[3], own.at[3], mostly_x)
    sums = [
        Total(part, total, *bufs, total_send.at[i], total_recv.at[i], rounds)
        for i, (part, total, bufs, rounds) in enumerate(
            (
                (feed_grads, feed_total, feed_bufs, Total.long),
                (input_part, input_total, input_bufs, Total.short),
                (table_part, table_total, table_bufs, Total.long),
            )
        )
    ]
    feed_sum, input_sum, table_sum = sums
    grad_rows = RowsBack(
        line, blank, small_grad, large_grad, row_sems.at[1], row_send.at[1], row_recv.at[1]
    )
    load_x = pltpu.make_async_copy(x_hbm, line, load_sems.at[1])
    load_turned = pltpu.make_async_copy(turned_hbm, hidden_turned, load_sems.at[2])
    load_w = pltpu.make_async_copy(w_hbm, w_qkv, load_sems.at[3])

    def take_turns(by_step):
        for at, turns in enumerate(by_step):
            if turns:

                @pl.when(step == at)
                def _():
                    for turn in turns:
                        turn[0](*turn[1:])

    slots = (
        ([(mid.one, 0), (mid.one, 3)], [], [], [(mid.three, 0), (mid.three, 3), (down.one, 1), (down.one, 2)], [(mid.three, 1), (mid.three, 2)], [(down.three, 0), (down.three, 3), (early.one, 1), (early.one, 2)]),
        ([], [(mid.one, 1), (mid.one, 2)], [(down.one, 0), (down.one, 3)], [], [], []),
        ([], [(feed_sum.advance, 1)], [(feed_sum.advance, 2)], [(down.two, 0), (down.two, 3)], [(down.two, 1), (down.two, 2), (early.one, 0), (early.one, 3)], [(early.two, 0), (early.two, 3), (down.three, 1), (down.three, 2)]),
        ([(feed_sum.advance, 0)], [(mid.two, 0), (mid.two, 3)], [(mid.two, 1), (mid.two, 2)], [(feed_sum.advance, 3)], [], []),
    )

    @pl.when(step == 0)
    def _():
        greet()
        mid.begin()
        down.begin()
        load_turned.start()
        load_x.start()
        load_w.start()
        blank[...] = jnp.zeros_like(blank)
        table_part[...] = jnp.zeros_like(table_part)
        feed_sum.begin()

    lane = iota((1, LANES), 1)
    scale = float(64) ** (-0.5)
    members = [(i * SPAD, SPAD, probs_small, i) for i in range(n_small)]
    members += [(n_small * SPAD + i * LPAD, LPAD, probs_large, i) for i in range(n_large)]
    keep = []
    for head in range(2):
        spot = 64 * (1 - head)
        minus = jnp.where((lane == spot) | (lane == spot + 1), -1.0, 0.0).astype(BF16)
        mask32 = masks[head].astype(F32)
        for at, (start, count, probs, which) in enumerate(members):
            rows = pl.ds(start, count)
            grad = dout[rows, :]
            grad32 = grad.astype(F32) * mask32
            delta = jnp.sum(grad32 * out_wide[rows, :], axis=1, keepdims=True)
            coarse = delta.astype(BF16).astype(F32)
            fine = delta - coarse
            side = jnp.where(lane == spot, coarse, jnp.where(lane == spot + 1, fine, grad32))
            values = value[rows, :] * masks[head] + minus
            prob = probs[head, which]
            dscore = prob.astype(F32) * dot_nt(values, side.astype(BF16))
            if count == SPAD:
                if which == 0:
                    dsum_small[:, :SPAD] = dscore
                else:
                    dsum_small[:, :SPAD] += dscore
            elif which == 0:
                dscore_large[:, :LPAD] = dscore
            else:
                dscore_large[:, :LPAD] += dscore
            low = dscore.astype(BF16)
            turned = key[rows, :].T
            dq = dot_nn(turned[head * 64 : head * 64 + 64, :], low)
            dk = dot_nn(low, query[rows, :])
            dv = dot_nn(prob, grad)
            if head == 0:
                keep.append((dq, dk, dv))
            else:
                first = iota((count, LANES), 1) < 64
                dq0, dk0, dv0 = keep[at]
                dqkv[step, rows, :] = (jnp.concatenate([dq0, dq], axis=0).T * scale).astype(BF16)
                dqkv[pairs + step, rows, :] = jnp.where(first, dk0, dk).astype(BF16)
                dqkv[2 * pairs + step, rows, :] = jnp.where(first, dv0, dv).astype(BF16)
        take_turns(slots[2 * head])
        wide[...] = jnp.zeros_like(wide)
        dscore_large[:, LPAD:] = jnp.zeros((LPAD, 768 - LPAD), F32)
        edge_lane = iota((24, 768), 1)
        edge_row = iota((24, 768), 0)
        class_column = jnp.zeros((24, 768), F32)
        class_row = None
        for block in range(LGRID + 1):
            at, turn = large_window(block)
            piece = dscore_large[pl.ds(block * 24, 24), :]
            if block == 0:
                class_row = piece[0:1, :]
                piece = jnp.where(edge_row == 0, 0.0, piece)
            class_column = class_column + piece
            piece = jnp.where(edge_lane == 0, 0.0, piece)
            if turn:
                piece = pltpu.roll(piece, turn, 1)
            wide[:, at * LANES : at * LANES + 768] += piece
        low_sum, high_sum = gather_sequences(wide[...], 24, L_WIDTH, LGRID, 1)
        spot_row = step * 2 + head
        large_part[pl.ds(spot_row, 1), :] = low_sum
        large_part[pl.ds(16 + spot_row, 1), :] = high_sum
        narrow[...] = jnp.zeros_like(narrow)
        dsum_small[:, SPAD:] = jnp.zeros((SPAD, 384 - SPAD), F32)
        small_lane = iota((SGRID, 384), 1)
        small_column = jnp.zeros((SGRID, 384), F32)
        for block in range(SGRID):
            at, turn = small_window(block)
            piece = dsum_small[pl.ds(1 + SGRID * block, SGRID), :]
            small_column = small_column + piece
            piece = jnp.where(small_lane == 0, 0.0, piece)
            piece = jnp.concatenate([piece, jnp.zeros((2, 384), F32)], axis=0)
            if turn:
                piece = pltpu.roll(piece, turn, 1)
            narrow[:, at * LANES : at * LANES + 384] += piece
        low_sum, high_sum = gather_sequences(narrow[...], 16, S_WIDTH, SGRID, 0)
        by_query = row_sum(class_column)[:, :LANES] + row_sum(small_column)[:, :LANES]
        both_rows = class_row + jnp.concatenate(
            [dsum_small[0:1, :], jnp.zeros((1, 384), F32)], axis=1
        )
        class_key = jnp.sum(
            jnp.where(iota((1, 768), 1) == 0, 0.0, both_rows), axis=1, keepdims=True
        )
        spot = iota((1, S_WIDTH), 1)
        low_sum = jnp.where(spot == S_WIDTH - 3, by_query[:, 0:1], low_sum)
        low_sum = jnp.where(spot == S_WIDTH - 2, class_key, low_sum)
        low_sum = jnp.where(spot == S_WIDTH - 1, both_rows[:, 0:1], low_sum)
        small_part[pl.ds(spot_row, 1), :] = low_sum
        small_part[pl.ds(16 + spot_row, 1), :] = high_sum
        take_turns(slots[1 + 2 * head])

    @pl.when(step == 0)
    def _():
        load_turned.wait()

    @pl.when(step % 2 == 1)
    def _():
        pieces = [dqkv[kind * pairs + step - 1 + i] for i in range(2) for kind in range(3)]
        made = dot_nn(hidden_turned[...], jnp.concatenate(pieces, axis=1)).astype(BF16)
        made = made.reshape(ZS, 2, 2, width // 16, width)
        for at in range(pairs // 2):

            @pl.when(step == 2 * at + 1)
            def _():
                if at < EARLY // 2:
                    early_grad[:, :, :, :, at * width : (at + 1) * width] = made
                else:
                    late_grad[...] = made

    @pl.when(step == EARLY - 1)
    def _():
        early.begin()

    @pl.when(step == pairs - 1)
    def _():
        late.begin()
        table_sum.begin()
        load_x.wait()
        load_w.wait()
        part = chunk_rows(all_rows)
        zeros = jnp.zeros((1, width), F32)
        input_part[...] = jnp.zeros_like(input_part)
        end_turns = (
            [(late.one, 0), (late.one, 3), (late.one, 1), (late.one, 2), (early.two, 1), (early.two, 2), (table_sum.advance, 0)],
            [(mid.four,), (late.two, 0), (late.two, 3), (early.three, 0), (early.three, 3), (table_sum.advance, 1)],
            [(late.two, 1), (late.two, 2), (early.three, 1), (early.three, 2), (down.four,), (table_sum.advance, 2)],
        )
        for at, first in enumerate(reversed(range(0, all_rows, part))):
            rows = pl.ds(first, part)
            load_dres = pltpu.make_async_copy(
                dres_hbm.at[rows], dscore_large.at[pl.ds(0, part)], load_sems.at[4]
            )
            load_dres.start()
            dhidden = jnp.zeros((part, width), F32)
            for kind in range(3):
                piece = jnp.concatenate(
                    [dqkv[kind * pairs + j, rows, :] for j in range(pairs)], axis=1
                )
                weight = w_qkv[:, :, :, :, kind * width : (kind + 1) * width]
                dhidden += dot_nt(piece, weight.reshape(width, width))
                if kind != 1:
                    input_part[kind : kind + 1, :] += row_sum(piece.astype(F32))
            normal, rate = normalized(line[rows, :].astype(F32))
            input_part[3:4, :] += row_sum(dhidden * normal)
            input_part[4:5, :] += row_sum(dhidden)
            back = norm_back(dhidden * gain[...][None, :], normal, rate)
            load_dres.wait()
            line[rows, :] = (dscore_large[pl.ds(0, part), :] + back).astype(BF16)
            if at == 0:
                line[pl.ds(all_rows, line.shape[0] - all_rows), :] = jnp.zeros(
                    (line.shape[0] - all_rows, width), BF16
                )
            if first <= n_small * SPAD < first + part:
                grad_rows.begin_large()
            for turn in end_turns[at]:
                turn[0](*turn[1:])
        grad_rows.begin_small()
        input_sum.begin()
        for turn in (
            [(input_sum.advance, 0), (late.three, 0), (late.three, 3), (late.three, 1), (late.three, 2), (table_sum.advance, 3), (early.four,), (input_sum.advance, 1), (late.four,)]
        ):
            turn[0](*turn[1:])
        grad_rows.finish()
        for job in (mid, down, early, late):
            job.finish()


def gelu_pair(upper):
    normal_cdf = 0.5 * (1.0 + lax.erf(upper * (0.5**0.5)))
    density = jnp.exp(-0.5 * upper * upper) * 0.3989422804014327
    return upper * normal_cdf, normal_cdf + upper * density


def valid_rows(first, count, n_small):
    row = iota((count, 1), 0) + first
    in_small = row < n_small * SPAD
    small_ok = row % SPAD < SGRID * SGRID + 1
    large_ok = (row - n_small * SPAD) % LPAD < LGRID * LGRID + 1
    return jnp.where(in_small, small_ok.astype(F32), large_ok.astype(F32))


def feed_kernel(
    n_small,
    tiles,
    x,
    attended,
    cot,
    mid_hbm,
    down_hbm,
    out_bias,
    attend_scale,
    second_gain,
    second_bias,
    down_bias,
    feed_scale,
    up_bias,
    small_out,
    large_out,
    dresidual,
    dattended,
    vector_grads,
    g_mid,
    g_down,
    w_mid,
    w_down,
    active,
    slope,
    acc_out,
    acc_up,
    acc_down,
    sems,
    line,
    blank,
    row_sems,
    row_send,
    row_recv,
):
    step = pl.program_id(0)
    count, width = x.shape
    all_rows = n_small * SPAD + LPAD
    w_out = w_mid.at[:, :width]
    w_up = w_mid.at[:, width:]
    tile = w_up.shape[1] // tiles

    final = pl.num_programs(0) - 1
    out_rows = RowsBack(line, blank, small_out, large_out, row_sems, row_send.at[0], row_recv.at[0])
    pieces = [(mid_hbm, w_mid, g_mid, (slice(None), slice(0, width)))]
    for t in range(tiles):
        cols = slice(width + t * tile, width + (t + 1) * tile)
        pieces.append((mid_hbm, w_mid, g_mid, (slice(None), cols)))
    for t in range(tiles):
        rows = slice(t * tile, (t + 1) * tile)
        pieces.append((down_hbm, w_down, g_down, (rows, slice(None))))

    def load(at):
        source, held, target, where = pieces[at]
        return pltpu.make_async_copy(source.at[where], held.at[where], sems.at[at])

    def store(at):
        source, held, target, where = pieces[at]
        return pltpu.make_async_copy(held.at[where], target.at[where], sems.at[at])

    @pl.when(step == 0)
    def _():
        for at in range(len(pieces)):
            load(at).start()
        greet_seq()
        acc_out[...] = jnp.zeros_like(acc_out)
        acc_up[...] = jnp.zeros_like(acc_up)
        acc_down[...] = jnp.zeros_like(acc_down)
        vector_grads[...] = jnp.zeros_like(vector_grads)
        load(0).wait()

    out_bias, attend_scale, second_gain, second_bias, down_bias, feed_scale = (
        v[...][None, :]
        for v in (out_bias, attend_scale, second_gain, second_bias, down_bias, feed_scale)
    )

    valid = valid_rows(step * count, count, n_small)
    mixed = attended[...]
    branch = dot_nn(mixed, w_out[...]) + out_bias
    residual = x[...].astype(F32) + attend_scale * branch
    normal, scale = normalized(residual)
    hidden = (normal * second_gain + second_bias).astype(BF16)

    @pl.when(step == 0)
    def _():
        for at in range(1, len(pieces)):
            load(at).wait()

    lower = jnp.zeros((count, width), F32)
    for t in range(tiles):
        cols = slice(t * tile, (t + 1) * tile)
        upper = dot_nn(hidden, w_up[:, cols]) + up_bias[cols][None, :]
        made, rate = gelu_pair(upper)
        made = made.astype(BF16)
        active[:, cols] = made
        slope[:, cols] = rate.astype(BF16)
        lower += dot_nn(made, w_down[cols, :])
    lower += down_bias
    spot = pl.ds(pl.multiple_of(step * count, 16), count)
    line[spot, :] = ((residual + feed_scale * lower) * valid).astype(BF16)

    @pl.when(step == final)
    def _():
        blank[...] = jnp.zeros_like(blank)
        rest = line.shape[0] - all_rows
        line[pl.ds(all_rows, rest), :] = jnp.zeros((rest, width), BF16)
        out_rows.begin_large()
        out_rows.begin_small()

    upstream = cot[...].astype(F32) * valid
    vector_grads[5:6, :] += row_sum(upstream * lower)
    dlower = (upstream * feed_scale).astype(BF16)
    vector_grads[4:5, :] += row_sum(dlower.astype(F32))
    turned = hidden.T
    dhidden = jnp.zeros((count, width), F32)
    for t in range(tiles):
        cols = slice(t * tile, (t + 1) * tile)
        dupper = (dot_nt(dlower, w_down[cols, :]) * slope[:, cols].astype(F32)).astype(BF16)
        vector_grads[8 + t : 9 + t, :] += row_sum(dupper.astype(F32))
        acc_down[cols, :] += dot_nn(active[:, cols].T, dlower)
        acc_up[:, cols] += dot_nn(turned, dupper)
        dhidden += dot_nt(dupper, w_up[:, cols])

    @pl.when(step == final)
    def _():
        for t in range(tiles):
            cols = slice(t * tile, (t + 1) * tile)
            w_up[:, cols] = acc_up[:, cols].astype(BF16)
            store(1 + t).start()
            w_down[cols, :] = acc_down[cols, :].astype(BF16)
            store(1 + tiles + t).start()

    vector_grads[2:3, :] += row_sum(dhidden * normal)
    vector_grads[3:4, :] += row_sum(dhidden)
    dres = upstream + norm_back(dhidden * second_gain, normal, scale)
    dresidual[...] = dres
    vector_grads[1:2, :] += row_sum(dres * branch)
    dbranch = (dres * attend_scale).astype(BF16)
    vector_grads[0:1, :] += row_sum(dbranch.astype(F32))
    acc_out[...] += dot_nn(mixed.T, dbranch)
    dattended[...] = dot_nt(dbranch, w_out[...]).astype(BF16)

    @pl.when(step == final)
    def _():
        w_out[...] = acc_out[...].astype(BF16)
        store(0).start()
        for at in range(len(pieces)):
            store(at).wait()
        out_rows.finish()


def chunk_rows(total):
    return max(size for size in range(16, 481, 16) if total % size == 0)


def params(collective=None):
    if collective is None:
        return pltpu.CompilerParams(vmem_limit_bytes=VMEM_BYTES)
    return pltpu.CompilerParams(
        vmem_limit_bytes=VMEM_BYTES, collective_id=collective, has_side_effects=True
    )


def held(shape):
    rank = len(shape)
    return pl.BlockSpec(shape, lambda i: (0,) * rank, pipeline_mode=pl.Buffered(1))


def resident(shape):
    rank = len(shape)
    return pl.BlockSpec(shape, lambda i: (0,) * rank)


def run_begin(weights, rows, table, vectors, collective):
    small, large = rows[:2]
    n_small, n_large = small.shape[0], 1
    width = small.shape[-1]
    pairs = HEADS // 2
    count = n_small * SPAD + n_large * LPAD
    line = n_small * SPAD + n_large * LLEN
    anywhere = pl.BlockSpec(memory_space=pl.ANY)
    sems = pltpu.SemaphoreType.DMA
    column = pl.BlockSpec((count, LANES), lambda i: (0, i))
    strip = width // 16
    qkv_share, mid_share = (strip, 3 * width), (strip, width + weights[4].shape[1])
    wholes = [(ZS, 2, 2) + s for s in (qkv_share, mid_share, weights[5].shape)]

    def per_pair(shape):
        tail = (0,) * (len(shape) - 1)
        return pl.BlockSpec((2,) + shape[1:], lambda i: (i,) + tail)

    probs = [(HEADS, n_small, SPAD, SPAD), (HEADS, n_large, LPAD, LPAD)]
    return pl.pallas_call(
        functools.partial(begin_kernel, n_small, n_large),
        grid=(pairs,),
        in_specs=[anywhere] * 10 + [held(v.shape) for v in (table,) + vectors],
        out_specs=[anywhere] * 7 + [column, column] + [per_pair(p) for p in probs],
        out_shape=[
            jax.ShapeDtypeStruct((line, width), BF16),
            jax.ShapeDtypeStruct((line, width), BF16),
            jax.ShapeDtypeStruct((3 * pairs, count, LANES), BF16),
            jax.ShapeDtypeStruct((width, count), BF16),
        ]
        + [jax.ShapeDtypeStruct(w, BF16) for w in wholes]
        + [
            jax.ShapeDtypeStruct((count, width), BF16),
            jax.ShapeDtypeStruct((count, width), F32),
        ]
        + [jax.ShapeDtypeStruct(p, BF16) for p in probs],
        scratch_shapes=[
            pltpu.VMEM((line, width), BF16),
            pltpu.VMEM((line, width), BF16),
            pltpu.VMEM((count, width), BF16),
            pltpu.VMEM((width, count), BF16),
            pltpu.VMEM((3 * pairs, count, LANES), BF16),
            pltpu.VMEM(wholes[0], BF16),
            pltpu.VMEM((24, L_WIDTH), F32),
            pltpu.VMEM((16, S_WIDTH), F32),
            pltpu.VMEM((LPAD, 640), F32),
            pltpu.VMEM((SPAD, 256), F32),
            sems((3, Gather.n_sems)),
            sems((3, Gather.n_sems)),
            sems((3,)),
            sems((2, n_small + 1)),
            sems((2,)),
            sems((2,)),
            sems((5,)),
            pltpu.VMEM(qkv_share, BF16),
            pltpu.VMEM(mid_share, BF16),
            sems((5,)),
            pltpu.VMEM((16, T_WIDTH), F32),
            pltpu.VMEM((16, L_WIDTH), F32),
            pltpu.VMEM((16, S_WIDTH), F32),
            pltpu.VMEM((16, L_WIDTH), F32),
            pltpu.VMEM((16, S_WIDTH), F32),
        ],
        compiler_params=params(collective),
    )(*weights, *rows, table, *vectors)


def run_end(qkv, dattended, out_wide, probs, grads, rows, feed_grads, gain, n_small, collective):
    count, width = dattended.shape
    pairs = HEADS // 2
    line = rows[0].shape[0]
    anywhere = pl.BlockSpec(memory_space=pl.ANY)
    inside = pl.BlockSpec(memory_space=pltpu.VMEM)
    sems = pltpu.SemaphoreType.DMA
    column = pl.BlockSpec((count, LANES), lambda i: (0, i))
    shares = [(g.shape[0] // 16, g.shape[1]) for g in grads]
    shares += [(width // 16, 3 * LANES * many) for many in (EARLY, pairs - EARLY)]
    smalls = [feed_grads.shape, (8, width), (32, L_WIDTH + S_WIDTH)]

    def third(which):
        return pl.BlockSpec((1, count, LANES), lambda i: (which * pairs + i, 0, 0))

    def per_pair(shape):
        tail = (0,) * (len(shape) - 1)
        return pl.BlockSpec((2,) + shape[1:], lambda i: (i,) + tail)

    scratch = [
        pltpu.VMEM((24, L_WIDTH), F32),
        pltpu.VMEM((16, S_WIDTH), F32),
        pltpu.VMEM((SPAD, 384), F32),
        pltpu.VMEM((LPAD, 768), F32),
        pltpu.VMEM((3 * pairs, count, LANES), BF16),
        pltpu.VMEM((width, count), BF16),
        pltpu.VMEM((ZS, 2, 2, width // 16, 3 * width), BF16),
        pltpu.VMEM((line, width), BF16),
        pltpu.VMEM((SLEN - SPAD, width), BF16),
        pltpu.VMEM((ZS, 2, 2) + shares[2], BF16),
        pltpu.VMEM((ZS, 2, 2) + shares[3], BF16),
        pltpu.VMEM(smalls[1], F32),
        pltpu.VMEM(smalls[2], F32),
    ]
    for shape in shares:
        scratch += Reduce.scratch(*shape)
    for shape, kind in zip(smalls, (F32, F32, BF16)):
        scratch += Total.scratch(shape, kind)
    scratch += [
        sems((4, Reduce.n_sems)),
        sems((4, Reduce.n_sems)),
        sems((4, ZS)),
        sems((3, Total.n_slots)),
        sems((3, Total.n_slots)),
        sems((5,)),
        sems((2, 2 * n_small + 1)),
        sems((2,)),
        sems((2,)),
    ]
    small = jax.ShapeDtypeStruct((n_small, SLEN, width), BF16)
    large = jax.ShapeDtypeStruct((2, LLEN // 2, width), BF16)
    return pl.pallas_call(
        functools.partial(end_kernel, n_small, 1),
        grid=(pairs,),
        in_specs=[third(0), third(1), third(2), column, column]
        + [per_pair(p.shape) for p in probs]
        + [anywhere] * 6
        + [held(feed_grads.shape), held(gain.shape)],
        out_specs=[anywhere] * 2 + [inside] * 7,
        out_shape=[small, large]
        + [jax.ShapeDtypeStruct(s, F32) for s in shares + smalls],
        scratch_shapes=scratch,
        compiler_params=params(collective),
        cost_estimate=pl.CostEstimate(
            flops=40 * 10**9, bytes_accessed=50 * 10**6, transcendentals=0
        ),
    )(
        qkv,
        qkv,
        qkv,
        dattended,
        out_wide,
        *probs,
        *[g.reshape((ZS, 2, 2) + s) for g, s in zip(grads, shares)],
        *rows,
        feed_grads,
        gain,
    )


def run_feed(x, attended, cot, w_mid, w_down, vectors, n_small, collective):
    rows, width = attended.shape
    size = chunk_rows(rows)
    hidden = w_down.shape[0]
    tiles = hidden // width
    block = pl.BlockSpec((size, width), lambda i: (i, 0))
    anywhere = pl.BlockSpec(memory_space=pl.ANY)
    return pl.pallas_call(
        functools.partial(feed_kernel, n_small, tiles),
        grid=(rows // size,),
        in_specs=[
            block,
            block,
            block,
            anywhere,
            anywhere,
        ]
        + [held(v.shape) for v in vectors],
        out_specs=[
            anywhere,
            anywhere,
            block,
            block,
            resident((16, width)),
            anywhere,
            anywhere,
        ],
        out_shape=[
            jax.ShapeDtypeStruct((n_small, SLEN, width), BF16),
            jax.ShapeDtypeStruct((2, LLEN // 2, width), BF16),
            jax.ShapeDtypeStruct((rows, width), F32),
            jax.ShapeDtypeStruct((rows, width), BF16),
            jax.ShapeDtypeStruct((16, width), F32),
            jax.ShapeDtypeStruct((width, width + hidden), BF16),
            jax.ShapeDtypeStruct((hidden, width), BF16),
        ],
        scratch_shapes=[
            pltpu.VMEM((width, width + hidden), BF16),
            pltpu.VMEM((hidden, width), BF16),
            pltpu.VMEM((size, hidden), BF16),
            pltpu.VMEM((size, hidden), BF16),
            pltpu.VMEM((width, width), F32),
            pltpu.VMEM((width, hidden), F32),
            pltpu.VMEM((hidden, width), F32),
            pltpu.SemaphoreType.DMA((1 + 2 * tiles,)),
            pltpu.VMEM((x.shape[0], width), BF16),
            pltpu.VMEM((SLEN - SPAD, width), BF16),
            pltpu.SemaphoreType.DMA((2 * n_small + 1,)),
            pltpu.SemaphoreType.DMA((1,)),
            pltpu.SemaphoreType.DMA((1,)),
        ],
        compiler_params=params(collective),
        cost_estimate=pl.CostEstimate(
            flops=6 * rows * width * (width + 2 * hidden),
            bytes_accessed=40 * 10**6,
            transcendentals=2 * rows * hidden,
        ),
    )(x, attended, cot, w_mid, w_down, *vectors)


def finish_kernel(
    feed_total,
    input_total,
    table_total,
    mid_share,
    down_share,
    early_share,
    late_share,
    first_gain,
    first_bias,
    query,
    query_bias,
    key,
    value,
    value_bias,
    out,
    out_bias,
    attend_scale,
    second_gain,
    second_bias,
    up,
    up_bias,
    down,
    down_bias,
    feed_scale,
    table,
    wide_table,
):
    width = out.shape[1]
    for at, ref in enumerate(
        (out_bias, attend_scale, second_gain, second_bias, down_bias, feed_scale)
    ):
        ref[...] = feed_total[at, :]
    for t in range(up_bias.shape[0] // width):
        up_bias[t * width : (t + 1) * width] = feed_total[8 + t, :]
    for at, ref in ((0, query_bias), (2, value_bias), (3, first_gain), (4, first_bias)):
        ref[...] = input_total[at, :]
    out[...] = mid_share[:, :width]
    up[...] = mid_share[:, width:]
    down[...] = down_share[...]
    pair = 0
    for share in (early_share, late_share):
        for at in range(share.shape[1] // (3 * LANES)):
            for kind, ref in enumerate((query, key, value)):
                place_at = (3 * at + kind) * LANES
                ref[:, pair * LANES : (pair + 1) * LANES] = share[:, place_at : place_at + LANES]
            pair += 1
    lows = (table_total.at[pl.ds(0, 16), :L_WIDTH], table_total.at[pl.ds(0, 16), L_WIDTH:])
    highs = (table_total.at[pl.ds(16, 16), :L_WIDTH], table_total.at[pl.ds(16, 16), L_WIDTH:])
    table_from_sequences(lows, highs, wide_table)
    table[...] = wide_table[pl.ds(0, table.shape[0]), pl.ds(0, table.shape[1])]


def run_finish(totals, shares, entries):
    width = totals[0].shape[1]
    strip, hidden = shares[0].shape[0], shares[0].shape[1] - width
    vector = jax.ShapeDtypeStruct((width,), F32)
    square = jax.ShapeDtypeStruct((strip, width), F32)
    inside = pl.BlockSpec(memory_space=pltpu.VMEM)
    out_shape = [vector, vector, square, vector, square, square, vector, square]
    out_shape += [vector, vector, vector, vector]
    out_shape += [jax.ShapeDtypeStruct((strip, hidden), F32), jax.ShapeDtypeStruct((hidden,), F32)]
    out_shape += [jax.ShapeDtypeStruct(shares[1].shape, F32), vector, vector]
    out_shape += [jax.ShapeDtypeStruct((HEADS, entries), F32)]
    return pl.pallas_call(
        finish_kernel,
        in_specs=[inside] * 7,
        out_specs=[inside] * len(out_shape),
        out_shape=out_shape,
        scratch_shapes=[pltpu.VMEM((16, T_WIDTH), F32)],
        compiler_params=params(),
    )(*totals, *shares)


def shifted(array, axis, by):
    count = lax.axis_size(axis)
    return lax.ppermute(array, axis, [(i, (i + by) % count) for i in range(count)])


def layer_norm(values, gain, bias):
    center = values - jnp.mean(values, axis=-1, keepdims=True)
    spread = jnp.mean(center * center, axis=-1, keepdims=True)
    return center * lax.rsqrt(spread + EPSILON) * gain + bias


def matmul(left, right):
    return jnp.dot(left, right, preferred_element_type=jnp.float32)


def position_bias(table, places, length, grid):
    heads = table.shape[0]
    span = 2 * LGRID - 1
    total_rel = table.shape[1]
    queries_count = places.shape[0]
    grid_table = table[:, : span * span].reshape(heads, span, span)
    patch = places - 1
    query_row = patch // grid
    query_col = patch % grid
    steps_all = jnp.arange(span, dtype=jnp.int32)
    cells = jnp.arange(grid, dtype=jnp.int32)
    row_hot = (
        steps_all[None, :, None] == query_row[:, None, None] - cells[None, None, :] + LGRID - 1
    ).astype(jnp.float32)
    col_hot = (
        steps_all[None, :, None] == query_col[:, None, None] - cells[None, None, :] + LGRID - 1
    ).astype(jnp.float32)
    partial_bias = jnp.einsum("hab,qbc->hqac", grid_table, col_hot, precision=lax.Precision.HIGHEST)
    patches = jnp.einsum(
        "qar,hqac->hqrc", row_hot, partial_bias, precision=lax.Precision.HIGHEST
    ).reshape(heads, queries_count, grid * grid)
    rest = length - 1 - grid * grid
    class_key = jnp.broadcast_to(table[:, total_rel - 2][:, None, None], (heads, queries_count, 1))
    patch_rows = jnp.concatenate(
        [class_key, patches, jnp.zeros((heads, queries_count, rest), jnp.float32)], axis=2
    )
    class_row = jnp.concatenate(
        [
            table[:, total_rel - 1][:, None],
            jnp.broadcast_to(table[:, total_rel - 3][:, None], (heads, grid * grid)),
            jnp.zeros((heads, rest), jnp.float32),
        ],
        axis=1,
    )
    is_class = (places == 0)[None, :, None]
    return jnp.where(is_class, class_row[:, None, :], patch_rows)


def to_heads(block, heads):
    groups, rows, width = block.shape
    return block.reshape(groups, rows, heads, width // heads)


def block_scores(query, key, query_rows, key_rows, length, bias_full):
    size = query.shape[-1] // HEADS
    raw = jnp.einsum(
        "gqhd,gkhd->ghqk",
        to_heads(query, HEADS),
        to_heads(key, HEADS),
        preferred_element_type=jnp.float32,
    )
    key_place = key_rows % length
    select = (key_place[:, None] == jnp.arange(length, dtype=jnp.int32)[None, :]).astype(
        jnp.float32
    )
    bias_block = jnp.einsum("hql,kl->hqk", bias_full, select, precision=lax.Precision.HIGHEST)
    allowed = (query_rows // length)[:, None] == (key_rows // length)[None, :]
    scores = raw * float(size) ** (-0.5) + bias_block[None]
    return (scores, allowed, select)


def key_rows_of(source, count_keys):
    return source * count_keys + jnp.arange(count_keys, dtype=jnp.int32)


def allowed_mask(allowed, key_rows, length, grid):
    return allowed & (key_rows % length < grid * grid + 1)[None, :]


def absorb_one(state, query, key, value, query_rows, key_rows, info):
    length, grid, bias_full = info
    maximum, total, accum = state
    scores, allowed, select = block_scores(query, key, query_rows, key_rows, length, bias_full)
    allowed = allowed_mask(allowed, key_rows, length, grid)
    masked = jnp.where(allowed[None, None], scores, NEGATIVE)
    newmax = jnp.maximum(maximum, jnp.max(masked, axis=-1))
    weights = jnp.where(allowed[None, None], jnp.exp(scores - newmax[..., None]), 0.0)
    factor = jnp.exp(maximum - newmax)
    total = total * factor + jnp.sum(weights, axis=-1)
    accum = accum * factor[..., None] + jnp.einsum(
        "ghqk,gkhd->ghqd",
        weights.astype(jnp.bfloat16),
        to_heads(value, HEADS),
        preferred_element_type=jnp.float32,
    )
    return (newmax, total, accum)


def absorb_cycle(states, queries, moving, members, query_rows, source, info):
    states = list(states)
    for which, offset, rows in members:
        key = moving[0][:, offset : offset + rows]
        value = moving[1][:, offset : offset + rows]
        states[which] = absorb_one(
            states[which],
            queries[which],
            key,
            value,
            query_rows[which],
            key_rows_of(source, rows),
            info[which],
        )
    return tuple(states)


def pass_forward(moving):
    return shifted((moving[0], moving[1]), "seq", 1)


def cycle_forward(queries, cycle_pair, members, query_rows, info):
    position = lax.axis_index("seq")
    count = lax.axis_size("seq")
    states = []
    for which in range(2):
        groups, rows, width = queries[which].shape
        states.append(
            (
                jnp.full((groups, HEADS, rows), NEGATIVE, jnp.float32),
                jnp.zeros((groups, HEADS, rows), jnp.float32),
                jnp.zeros((groups, HEADS, rows, width // HEADS), jnp.float32),
            )
        )
    states = absorb_cycle(tuple(states), queries, cycle_pair, members, query_rows, position, info)

    def turn(step, carry):
        held_states, moving = carry
        moving = tuple(pass_forward(moving))
        held_states = absorb_cycle(
            held_states, queries, moving, members, query_rows, (position - step) % count, info
        )
        return (held_states, moving)

    states, moving = lax.fori_loop(1, count, turn, (states, cycle_pair))
    attended = []
    logsums = []
    for which in range(2):
        maximum, total, accum = states[which]
        groups, heads_count, rows, size = accum.shape
        attended.append(
            jnp.transpose(accum / total[..., None], (0, 2, 1, 3)).reshape(
                groups, rows, heads_count * size
            )
        )
        logsums.append(maximum + jnp.log(total))
    return (tuple(attended), tuple(logsums))


def visit_one(query, dout, logsum, delta, key, value, query_rows, key_rows, info):
    length, grid, bias_full = info
    groups, count_keys, width = key.shape
    scale = float(width // HEADS) ** (-0.5)
    scores, allowed, select = block_scores(query, key, query_rows, key_rows, length, bias_full)
    allowed = allowed_mask(allowed, key_rows, length, grid)
    probs = jnp.where(allowed[None, None], jnp.exp(scores - logsum[..., None]), 0.0)
    dout_heads = to_heads(dout, HEADS)
    dprobs = jnp.einsum(
        "gqhd,gkhd->ghqk", dout_heads, to_heads(value, HEADS), preferred_element_type=jnp.float32
    )
    dscores = (probs * (dprobs - delta[..., None])).astype(jnp.bfloat16)
    dq_term = scale * jnp.einsum(
        "ghqk,gkhd->gqhd", dscores, to_heads(key, HEADS), preferred_element_type=jnp.float32
    )
    dkey_term = jnp.einsum(
        "ghqk,gqhd->gkhd", dscores, to_heads(query, HEADS), preferred_element_type=jnp.float32
    )
    dvalue_term = jnp.einsum(
        "ghqk,gqhd->gkhd",
        probs.astype(jnp.bfloat16),
        dout_heads,
        preferred_element_type=jnp.float32,
    )
    summed = jnp.sum(dscores.astype(jnp.float32), axis=0)
    bias_term = jnp.einsum("hqk,kl->hql", summed, select, precision=lax.Precision.HIGHEST)
    return (
        dq_term,
        scale * dkey_term.reshape(groups, count_keys, width),
        dvalue_term.reshape(groups, count_keys, width),
        bias_term,
    )


def visit_cycle(carry, queries, douts, logsums, deltas, moving, members, query_rows, source, info):
    dqueries, dpair, bias_grads = carry
    dqueries = list(dqueries)
    bias_grads = list(bias_grads)
    key_pieces = []
    value_pieces = []
    for which, offset, rows in members:
        key = moving[0][:, offset : offset + rows]
        value = moving[1][:, offset : offset + rows]
        dq_term, dk_term, dv_term, bias_term = visit_one(
            queries[which],
            douts[which],
            logsums[which],
            deltas[which],
            key,
            value,
            query_rows[which],
            key_rows_of(source, rows),
            info[which],
        )
        dqueries[which] = dqueries[which] + dq_term
        key_pieces.append(dk_term)
        value_pieces.append(dv_term)
        bias_grads[which] = bias_grads[which] + bias_term
    new_pair = (
        dpair[0] + jnp.concatenate(key_pieces, axis=1),
        dpair[1] + jnp.concatenate(value_pieces, axis=1),
    )
    return (tuple(dqueries), new_pair, tuple(bias_grads))


def send_grads(dpair):
    return tuple(shifted((dpair[0], dpair[1]), "seq", 1))


def cycle_backward(queries, douts, logsums, deltas, cycle_pair, members, query_rows, info, start):
    position = lax.axis_index("seq")
    count = lax.axis_size("seq")
    dpair = tuple((jnp.zeros(item.shape, jnp.float32) for item in cycle_pair))

    def turn(step, state):
        carry, moving = state
        carry = visit_cycle(
            carry,
            queries,
            douts,
            logsums,
            deltas,
            moving,
            members,
            query_rows,
            (position - step) % count,
            info,
        )
        moving = tuple(shifted((moving[0], moving[1]), "seq", 1))
        return ((carry[0], send_grads(carry[1]), carry[2]), moving)

    carry, moving = lax.fori_loop(0, count - 1, turn, ((start[0], dpair, start[1]), cycle_pair))
    carry = visit_cycle(
        carry,
        queries,
        douts,
        logsums,
        deltas,
        moving,
        members,
        query_rows,
        (position - count + 1) % count,
        info,
    )
    return (carry[0], send_grads(carry[1]), carry[2])


def general_device(
    small_in,
    large_in,
    small_cot,
    large_cot,
    first_gain,
    first_bias,
    query_weight,
    query_bias,
    key_weight,
    value_weight,
    value_bias,
    out_weight,
    out_bias,
    attend_scale,
    second_gain,
    second_bias,
    up_weight,
    up_bias,
    down_weight,
    down_bias,
    feed_scale,
    rel_table,
):
    groups, small_rows, width = small_in.shape
    large_rows = large_in.shape[1]
    all_rows = small_rows + large_rows
    position = lax.axis_index("seq")
    query_rows = (
        position * small_rows + jnp.arange(small_rows, dtype=jnp.int32),
        position * large_rows + jnp.arange(large_rows, dtype=jnp.int32),
    )
    small_places = query_rows[0] % SLEN
    large_places = query_rows[1] % LLEN

    def make_biases(table):
        return (
            position_bias(table, small_places, SLEN, SGRID),
            position_bias(table, large_places, LLEN, LGRID),
        )

    biases, bias_back = jax.vjp(make_biases, rel_table)
    info = ((SLEN, SGRID, biases[0]), (LLEN, LGRID, biases[1]))
    valid_rows = jnp.concatenate(
        [small_places < SGRID * SGRID + 1, large_places < LGRID * LGRID + 1]
    )
    valid_flat = jnp.broadcast_to(valid_rows[None, :], (groups, all_rows)).reshape(-1)
    w_query, w_key, w_value, w_out, w_up, w_down = (
        lax.all_gather(query_weight, "img", axis=0, tiled=True),
        lax.all_gather(key_weight, "img", axis=0, tiled=True),
        lax.all_gather(value_weight, "img", axis=0, tiled=True),
        lax.all_gather(out_weight, "img", axis=0, tiled=True),
        lax.all_gather(up_weight, "img", axis=0, tiled=True),
        lax.all_gather(down_weight, "img", axis=0, tiled=True),
    )

    def split(rows_array):
        shaped = rows_array.reshape(groups, all_rows, -1)
        return (shaped[:, :small_rows], shaped[:, small_rows:])

    inputs = jnp.concatenate([small_in, large_in], axis=1).astype(jnp.float32).reshape(-1, width)
    hidden = layer_norm(inputs, first_gain, first_bias).astype(jnp.bfloat16)
    query = (matmul(hidden, w_query) + query_bias).astype(jnp.bfloat16)
    key = matmul(hidden, w_key).astype(jnp.bfloat16)
    value = (matmul(hidden, w_value) + value_bias).astype(jnp.bfloat16)
    queries = split(query)
    cycle_pair = (key.reshape(groups, all_rows, width), value.reshape(groups, all_rows, width))
    members = ((0, 0, small_rows), (1, small_rows, large_rows))
    attended, logsums = cycle_forward(queries, cycle_pair, members, query_rows, info)
    mixed = (
        jnp.concatenate([attended[0], attended[1]], axis=1).reshape(-1, width).astype(jnp.bfloat16)
    )
    branch = matmul(mixed, w_out) + out_bias
    residual = inputs + attend_scale * branch
    hidden2 = layer_norm(residual, second_gain, second_bias).astype(jnp.bfloat16)
    upper = matmul(hidden2, w_up) + up_bias
    active = jax.nn.gelu(upper, approximate=False).astype(jnp.bfloat16)
    lower = matmul(active, w_down) + down_bias
    output = jnp.where(valid_flat[:, None], residual + feed_scale * lower, 0.0).astype(jnp.bfloat16)
    small_out, large_out = split(output)
    upstream = (
        jnp.concatenate([small_cot, large_cot], axis=1).astype(jnp.float32).reshape(-1, width)
    )
    upstream = upstream * valid_flat[:, None].astype(jnp.float32)
    grad_feed_scale = jnp.sum(upstream * lower, axis=0)
    dlower = (upstream * feed_scale).astype(jnp.bfloat16)
    grad_down_bias = jnp.sum(dlower.astype(jnp.float32), axis=0)
    grad_down = jnp.einsum("rf,rd->fd", active, dlower, preferred_element_type=jnp.float32)
    dactive = jnp.einsum("rd,fd->rf", dlower, w_down, preferred_element_type=jnp.float32)
    unused, gelu_back = jax.vjp(lambda inner: jax.nn.gelu(inner, approximate=False), upper)
    dupper = gelu_back(dactive)[0].astype(jnp.bfloat16)
    grad_up_bias = jnp.sum(dupper.astype(jnp.float32), axis=0)
    grad_up = jnp.einsum("rd,rf->df", hidden2, dupper, preferred_element_type=jnp.float32)
    dhidden2 = jnp.einsum("rf,df->rd", dupper, w_up, preferred_element_type=jnp.float32)
    unused, second_back = jax.vjp(layer_norm, residual, second_gain, second_bias)
    dres_part, grad_second_gain, grad_second_bias = second_back(dhidden2)
    dresidual = upstream + dres_part
    grad_attend_scale = jnp.sum(dresidual * branch, axis=0)
    dbranch = (dresidual * attend_scale).astype(jnp.bfloat16)
    grad_out_bias = jnp.sum(dbranch.astype(jnp.float32), axis=0)
    grad_out = jnp.einsum("rd,re->de", mixed, dbranch, preferred_element_type=jnp.float32)
    dmixed = jnp.einsum("re,de->rd", dbranch, w_out, preferred_element_type=jnp.float32).astype(
        jnp.bfloat16
    )
    held, held_sums = cycle_forward(queries, cycle_pair, members, query_rows, info)
    douts = split(dmixed)
    deltas = tuple(
        (
            jnp.einsum(
                "gqhd,gqhd->ghq",
                to_heads(douts[which].astype(jnp.float32), HEADS),
                to_heads(held[which], HEADS),
            )
            for which in range(2)
        )
    )
    dq_start = tuple(
        (jnp.zeros(to_heads(queries[which], HEADS).shape, jnp.float32) for which in range(2))
    )
    bias_start = tuple((jnp.zeros(item.shape, jnp.float32) for item in biases))
    dqueries, dpair, bias_grads = cycle_backward(
        queries,
        douts,
        held_sums,
        deltas,
        cycle_pair,
        members,
        query_rows,
        info,
        (dq_start, bias_start),
    )
    table_grad = bias_back(bias_grads)[0]
    dquery = jnp.concatenate(
        [
            dqueries[0].reshape(groups, small_rows, width),
            dqueries[1].reshape(groups, large_rows, width),
        ],
        axis=1,
    )
    dquery = dquery.reshape(-1, width).astype(jnp.bfloat16)
    dkey = dpair[0].reshape(-1, width).astype(jnp.bfloat16)
    dvalue = dpair[1].reshape(-1, width).astype(jnp.bfloat16)
    grad_query_bias = jnp.sum(dquery.astype(jnp.float32), axis=0)
    grad_value_bias = jnp.sum(dvalue.astype(jnp.float32), axis=0)
    grad_query = jnp.einsum("rd,re->de", hidden, dquery, preferred_element_type=jnp.float32)
    grad_key = jnp.einsum("rd,re->de", hidden, dkey, preferred_element_type=jnp.float32)
    grad_value = jnp.einsum("rd,re->de", hidden, dvalue, preferred_element_type=jnp.float32)
    dhidden = (
        jnp.einsum("re,de->rd", dquery, w_query, preferred_element_type=jnp.float32)
        + jnp.einsum("re,de->rd", dkey, w_key, preferred_element_type=jnp.float32)
        + jnp.einsum("re,de->rd", dvalue, w_value, preferred_element_type=jnp.float32)
    )
    unused, first_back = jax.vjp(layer_norm, inputs, first_gain, first_bias)
    dinput_part, grad_first_gain, grad_first_bias = first_back(dhidden)
    dinputs = (dresidual + dinput_part).astype(jnp.bfloat16)
    small_grad, large_grad = split(dinputs)
    shares = (
        lax.psum_scatter(grad_query, "img", scatter_dimension=0, tiled=True),
        lax.psum_scatter(grad_key, "img", scatter_dimension=0, tiled=True),
        lax.psum_scatter(grad_value, "img", scatter_dimension=0, tiled=True),
        lax.psum_scatter(grad_out, "img", scatter_dimension=0, tiled=True),
        lax.psum_scatter(grad_up, "img", scatter_dimension=0, tiled=True),
        lax.psum_scatter(grad_down, "img", scatter_dimension=0, tiled=True),
    )
    shares = lax.psum((shares[0], shares[1], shares[2], shares[3], shares[4], shares[5]), "seq")
    smalls = lax.psum(
        (
            grad_first_gain,
            grad_first_bias,
            grad_query_bias,
            grad_value_bias,
            grad_out_bias,
            grad_attend_scale,
            grad_second_gain,
            grad_second_bias,
            grad_up_bias,
            grad_down_bias,
            grad_feed_scale,
            table_grad,
        ),
        ("img", "seq"),
    )
    return (
        small_out,
        large_out,
        small_grad,
        large_grad,
        smalls[0],
        smalls[1],
        shares[0],
        smalls[2],
        shares[1],
        shares[2],
        smalls[3],
        shares[3],
        smalls[4],
        smalls[5],
        smalls[6],
        smalls[7],
        shares[4],
        smalls[8],
        shares[5],
        smalls[9],
        smalls[10],
        smalls[11],
    )


def image_device(
    small_in,
    large_in,
    small_cot,
    large_cot,
    first_gain,
    first_bias,
    query_weight,
    query_bias,
    key_weight,
    value_weight,
    value_bias,
    out_weight,
    out_bias,
    attend_scale,
    second_gain,
    second_bias,
    up_weight,
    up_bias,
    down_weight,
    down_bias,
    feed_scale,
    rel_table,
):
    groups, small_rows, width = small_in.shape
    n_small = groups * small_rows // SLEN

    x, cot, qkv, turned, w_qkv, w_mid, w_down, attended, out_wide, *probs = run_begin(
        (query_weight, key_weight, value_weight, out_weight, up_weight, down_weight),
        (
            small_in.reshape(n_small, SLEN, width),
            large_in,
            small_cot.reshape(n_small, SLEN, width),
            large_cot,
        ),
        rel_table,
        (first_gain, first_bias, query_bias, value_bias),
        1,
    )
    w_mid, w_down = (w.reshape(-1, w.shape[-1]) for w in (w_mid, w_down))
    small_out, large_out, dresidual, dattended, feed_grads, g_mid, g_down = run_feed(
        x,
        attended,
        cot,
        w_mid,
        w_down,
        (out_bias, attend_scale, second_gain, second_bias, down_bias, feed_scale, up_bias),
        n_small,
        3,
    )
    small_grad, large_grad, *made = run_end(
        qkv,
        dattended,
        out_wide,
        probs,
        [g_mid, g_down],
        [x, turned, w_qkv, dresidual],
        feed_grads,
        first_gain,
        n_small,
        2,
    )
    grads = run_finish(made[4:], made[:4], rel_table.shape[1])
    small_out, small_grad = (v.reshape(groups, small_rows, width) for v in (small_out, small_grad))
    return (small_out, large_out, small_grad, large_grad, *grads)


def per_device(*args):
    groups, small_rows, unused = args[0].shape
    if lax.axis_size("seq") == 2 and groups == 2 and small_rows % SLEN == 0:
        return image_device(*args)
    return general_device(*args)


def solution(mesh):
    return jax.shard_map(
        per_device,
        mesh=mesh,
        in_specs=(
            P("img", "seq", None),
            P("img", "seq", None),
            P("img", "seq", None),
            P("img", "seq", None),
            P(),
            P(),
            P("img", None),
            P(),
            P("img", None),
            P("img", None),
            P(),
            P("img", None),
            P(),
            P(),
            P(),
            P(),
            P("img", None),
            P(),
            P("img", None),
            P(),
            P(),
            P(),
        ),
        out_specs=(
            P("img", "seq", None),
            P("img", "seq", None),
            P("img", "seq", None),
            P("img", "seq", None),
            P(),
            P(),
            P("img", None),
            P(),
            P("img", None),
            P("img", None),
            P(),
            P("img", None),
            P(),
            P(),
            P(),
            P(),
            P("img", None),
            P(),
            P("img", None),
            P(),
            P(),
            P(),
        ),
        check_vma=False,
    )
```

```python
import functools

import jax
import jax.numpy as jnp
from jax import lax
from jax.experimental import pallas as pl
from jax.experimental.pallas import tpu as pltpu
from jax.sharding import PartitionSpec as P

HEADS = 12
SGRID = 14
LGRID = 24
SLEN = 256
LLEN = 640
SPAD = 208
LPAD = 608
LANES = 128

NEGATIVE = -1e30
EPSILON = 1e-06
F32 = jnp.float32
BF16 = jnp.bfloat16
VMEM_BYTES = 125 << 19


def dot_nn(left, right):
    return lax.dot_general(left, right, (((1,), (0,)), ((), ())), preferred_element_type=F32)


def dot_nt(left, right):
    return lax.dot_general(left, right, (((1,), (1,)), ((), ())), preferred_element_type=F32)


def normalized(values):
    center = values - jnp.mean(values, axis=-1, keepdims=True)
    spread = jnp.mean(center * center, axis=-1, keepdims=True)
    scale = lax.rsqrt(spread + EPSILON)
    return center * scale, scale


def norm_back(grad, normal, scale):
    return scale * (
        grad
        - jnp.mean(grad, axis=-1, keepdims=True)
        - normal * jnp.mean(grad * normal, axis=-1, keepdims=True)
    )


def row_sum(values):
    return jnp.sum(values, axis=0, keepdims=True)


def iota(shape, axis):
    return lax.broadcasted_iota(jnp.int32, shape, axis)


L_WIDTH = 1280
S_WIDTH = 512


SPAN = 2 * LGRID - 1
CELLS = SPAN * SPAN
T_WIDTH = 2304


def row_moves():
    off = LGRID - SGRID
    moves = []
    for m in range(SPAN):
        moves.append((m * SPAN, m * LGRID, LGRID, False, True))
        moves.append((m * SPAN + LGRID, (m + 1) * LGRID, LGRID - 1, True, True))
    for m in range(2 * SGRID - 1):
        start = (m + off) * SPAN + off
        moves.append((start, m * SGRID, SGRID, False, False))
        moves.append((start + SGRID, (m + 1) * SGRID, SGRID - 1, True, False))
    return moves


def moved(source, start, target, width, count):
    source_tile = min(start // LANES, source.shape[1] // LANES - 2)
    target_tile = min(target // LANES, width // LANES - 2)
    piece = source[:, source_tile * LANES : source_tile * LANES + 256]
    turn = (target - target_tile * LANES - start + source_tile * LANES) % 256
    if turn:
        piece = pltpu.roll(piece, turn, 1)
    lane = iota(piece.shape, 1) - (target - target_tile * LANES)
    return slice(target_tile * LANES, target_tile * LANES + 256), piece, (lane >= 0) & (lane < count)


def table_sequences(table, wide_table, lows, highs):
    heads, entries = table.shape
    wide_table[...] = jnp.zeros_like(wide_table)
    wide_table[pl.ds(0, heads), pl.ds(0, entries)] = table[...]
    for ref in lows + highs:
        ref[...] = jnp.zeros_like(ref)
    for start, place_at, count, high, large in row_moves():
        ref = (highs if high else lows)[0 if large else 1]
        where, piece, inside = moved(wide_table, start, place_at, ref.shape[1], count)
        ref[:, where] = jnp.where(inside, piece, ref[:, where])


def table_from_sequences(lows, highs, wide_table):
    wide_table[...] = jnp.zeros_like(wide_table)
    for start, place_at, count, high, large in row_moves():
        ref = (highs if high else lows)[0 if large else 1]
        where, piece, inside = moved(ref, place_at, start, T_WIDTH, count)
        wide_table[:, where] += jnp.where(inside, piece, 0.0)
    where, piece, inside = moved(lows[1], S_WIDTH - 3, CELLS, T_WIDTH, 3)
    wide_table[:, where] += jnp.where(inside, piece, 0.0)


def one_entry(row, place_at):
    return jnp.sum(jnp.where(iota(row.shape, 1) == place_at, row, 0.0), axis=1, keepdims=True)


def takes_low(rows, width, grid, first):
    step = iota((rows, width), 1) % grid
    row = iota((rows, width), 0)
    low = step >= grid - 1 + first - row
    if first == 1:
        low = low | (row == 0)
    return low


def spread_sequences(low, high, rows, width, grid, first):
    low = jnp.broadcast_to(low, (rows, width))
    high = jnp.broadcast_to(high, (rows, width))
    chosen = jnp.where(takes_low(rows, width, grid, first), low, high)
    return pltpu.roll(chosen, 1, 1, stride=1, stride_axis=0)


def gather_sequences(spread, rows, width, grid, first):
    row = iota((rows, width), 0) + 1
    for bit in (1, 2, 4, 8, 16):
        spread = jnp.where((row & bit) != 0, pltpu.roll(spread, width - bit, 1), spread)
    low = takes_low(rows, width, grid, first)
    return (
        row_sum(jnp.where(low, spread, 0.0)),
        row_sum(jnp.where(low, 0.0, spread)),
    )


def large_window(block):
    start = (LGRID - block) * LGRID
    return start // LANES, start % LANES


def small_window(block):
    start = (SGRID - 1 - block) * SGRID + SGRID - 1
    return start // LANES, start % LANES


def head_masks():
    lane = iota((1, LANES), 1)
    return (
        jnp.where(lane < LANES // 2, 1.0, 0.0).astype(BF16),
        jnp.where(lane < LANES // 2, 0.0, 1.0).astype(BF16),
    )


def transposed_biases(large_seq, small_seq, entries, wide, narrow, bias_large, bias_small):
    patch_q, patch_k, both = (one_entry(entries, CELLS + i - T_WIDTH + 256) for i in range(3))
    wide[...] = spread_sequences(*large_seq, 24, L_WIDTH, LGRID, 1)
    lane = iota((24, LANES), 1)
    row = iota((24, LANES), 0)
    for block in range(LGRID + 1):
        at, turn = large_window(block)
        piece = wide[:, at * LANES : at * LANES + 768]
        if turn:
            piece = pltpu.roll(piece, 768 - turn, 1)
        piece = piece[:, :640]
        if block == 0:
            rest = jnp.where(iota((24, 640), 0) == 0, patch_k, piece)
        elif block == LGRID:
            rest = jnp.where(iota((24, 640), 0) == 0, piece, NEGATIVE)
        else:
            rest = piece
        first = jnp.where(lane == 0, patch_q, rest[:, :LANES])
        if block == 0:
            first = jnp.where((lane == 0) & (row == 0), both, first)
        if block == LGRID:
            first = jnp.where(row == 0, first, NEGATIVE)
        bias_large[pl.ds(block * 24, 24), 0:LANES] = first
        bias_large[pl.ds(block * 24, 24), LANES:640] = rest[:, LANES:]
    bias_large[pl.ds(600, 8), :] = jnp.full((8, 640), NEGATIVE, F32)
    narrow[...] = spread_sequences(*small_seq, 16, S_WIDTH, SGRID, 0)
    for block in range(SGRID):
        at, turn = small_window(block)
        piece = narrow[:, at * LANES : at * LANES + 384]
        if turn:
            piece = pltpu.roll(piece, 384 - turn, 1)
        bias_small[pl.ds(1 + SGRID * block, SGRID), :] = piece[:SGRID, :256]
    whole = bias_small[...]
    lane = iota((SPAD, 256), 1)
    row = iota((SPAD, 256), 0)
    whole = jnp.where(lane == 0, patch_q, whole)
    whole = jnp.where(row == 0, patch_k, whole)
    whole = jnp.where((lane == 0) & (row == 0), both, whole)
    bias_small[...] = jnp.where(row > SGRID * SGRID, NEGATIVE, whole)


MESH = pl.DeviceIdType.MESH
ZS = 4


def place():
    img = lax.axis_index("img")
    return img // 4, (img // 2) % 2, img % 2, lax.axis_index("seq")


def device(z, x, c, y):
    return ((z * 2 + x) * 2 + c, y)


def z_peer(z, hop):
    low = (z % 2) * (1 - 2 * (hop % 2)) + hop % 2
    high = (z // 2) * (1 - 2 * (hop // 2)) + hop // 2
    return high * 2 + low


def greet():
    z, x, c, y = place()
    barrier = pltpu.get_barrier_semaphore()
    peers = [device(z_peer(z, hop), x, c, y) for hop in range(1, ZS)]
    for flip in range(1, 8):
        peers.append(
            device(
                z,
                1 - x if flip & 1 else x,
                1 - c if flip & 2 else c,
                1 - y if flip & 4 else y,
            )
        )
    for peer in peers:
        pl.semaphore_signal(barrier, inc=1, device_id=peer, device_id_type=MESH)
    pl.semaphore_wait(barrier, len(peers))


def greet_seq():
    z, x, c, y = place()
    barrier = pltpu.get_barrier_semaphore()
    pl.semaphore_signal(barrier, inc=1, device_id=device(z, x, c, 1 - y), device_id_type=MESH)
    pl.semaphore_wait(barrier, 1)


def half_of(width, y):
    return pl.ds(pl.multiple_of(y * (width // 2), 128), width // 2)


class Gather:
    n_sems = 21

    def __init__(self, share, whole, send, recv, own, spare_seq):
        self.share, self.whole, self.send, self.recv, self.own = share, whole, send, recv, own
        self.spare_seq = spare_seq
        self.width = share.shape[1]
        self.at = z, x, c, y = place()
        self.inner = z % 3 != 0

    def copy(self, source, target, index, peer, recv=None):
        return pltpu.make_async_remote_copy(
            src_ref=source,
            dst_ref=target,
            send_sem=self.send.at[index],
            recv_sem=self.recv.at[index if recv is None else recv],
            device_id=peer,
            device_id_type=MESH,
        )

    def source_z(self, turn):
        z = self.at[0]
        is_inner = jnp.minimum(z % 3, 1)
        hop = (0, 1, 2 + is_inner, 3 - is_inner)[turn]
        return z_peer(z, hop)

    def along_z(self, turn, onto, recv):
        z, x, c, y = self.at
        cols = half_of(self.width, y)
        target = self.whole.at[self.source_z(turn), x, c, :, cols]
        source = self.share.at[:, cols] if turn == 0 else target
        index = {(0, 1): 0, (0, 3): 1, (1, 3): 2, (2, 1): 19, (3, 1): 20}[turn, onto]
        return self.copy(source, target, index, device(z_peer(z, onto), x, c, y), recv - 1)

    def from_z(self, turn):
        z, x, c, y = self.at
        cols = half_of(self.width, y)
        block = self.whole.at[self.source_z(turn), x, c, :, cols]
        return self.copy(block, block, turn - 1, device(z_peer(z, 1), x, c, y))

    def across(self, turn, axis):
        z, x, c, y = self.at
        cols = half_of(self.width, y)
        target = self.whole.at[self.source_z(turn), x, c, :, cols]
        source = self.share.at[:, cols] if turn == 0 else target
        peer = device(z, 1 - x, c, y) if axis == 0 else device(z, x, c, 1 - y)
        return self.copy(source, target, 3 + 4 * axis + turn, peer)

    def onward(self, turn):
        z, x, c, y = self.at
        source_z = self.source_z(turn)
        even = 1 if turn == 0 else 0 if self.spare_seq else 1 - source_z % 2
        side = x + even * (1 - 2 * x)
        cols = half_of(self.width, y + (1 - even) * (1 - 2 * y))
        block = self.whole.at[source_z, side, c, :, cols]
        peer = device(z, x + (1 - even) * (1 - 2 * x), c, y + even * (1 - 2 * y))
        return self.copy(block, block, 11 + turn, peer)

    def to_core(self, turn):
        z, x, c, y = self.at
        block = self.whole.at[self.source_z(turn), :, c]
        return self.copy(block, block, 15 + turn, device(z, x, 1 - c, y))

    def keep_own(self):
        z, x, c, y = self.at
        return pltpu.make_async_copy(self.share, self.whole.at[z, x, c], self.own)

    def begin(self):
        self.begin_z()
        self.begin_across()

    def begin_across(self):
        self.keep_own().start()
        self.across(0, 0).start()

    def begin_z(self):
        self.along_z(0, 1, 1).start()

        @pl.when(self.inner)
        def _():
            self.along_z(0, 3, 2).start()

    def come(self, hop):
        self.from_z(hop).wait_recv()

        @pl.when(self.inner)
        def _():
            if hop == 1:
                self.along_z(1, 3, 3).start()
            else:
                self.along_z(hop, 1, hop).start()

        for axis in range(2):
            self.across(hop, axis).start()

    def pass_on(self, hop):
        for axis in range(2 if hop else 1):
            self.across(hop, axis).wait_recv()
        self.onward(hop).start()

    def give(self, hop):
        if hop == 0:
            self.keep_own().wait()
        self.onward(hop).wait_recv()
        self.to_core(hop).start()

    def turn(self, at):
        stage, hop = (
            (self.come, 1),
            (self.pass_on, 0),
            (self.come, 2),
            (self.pass_on, 1),
            (self.come, 3),
            (self.pass_on, 2),
            (self.give, 0),
            (self.pass_on, 3),
            (self.give, 1),
            (self.give, 2),
            (self.give, 3),
        )[at]
        stage(hop)

    def arrive(self):
        for hop in range(ZS):
            self.to_core(hop).wait_recv()

    def drain(self):
        for hop in range(ZS):
            self.to_core(hop).wait_send()
            self.onward(hop).wait_send()
            for axis in range(2 if hop else 1):
                self.across(hop, axis).wait_send()
        self.along_z(0, 1, 1).wait_send()

        @pl.when(self.inner)
        def _():
            self.along_z(0, 3, 2).wait_send()
            self.along_z(1, 3, 3).wait_send()
            self.along_z(2, 1, 2).wait_send()
            self.along_z(3, 1, 3).wait_send()


class Rows:
    n_sems = 2

    def __init__(self, small, large, line, sems, send, recv):
        self.small, self.large, self.line = small, large, line
        self.sems, self.send, self.recv = sems, send, recv
        self.at = place()
        self.n_small = small.shape[0]
        self.base = self.n_small * SPAD
        self.rows = large.shape[1]

    def spot(self):
        start = self.base + self.rows * self.at[3]
        return self.line.at[pl.ds(pl.multiple_of(start, 16), self.rows)]

    def local(self, i):
        if i < self.n_small:
            return pltpu.make_async_copy(
                self.small.at[i, pl.ds(0, SPAD)],
                self.line.at[pl.ds(i * SPAD, SPAD)],
                self.sems.at[i],
            )
        return pltpu.make_async_copy(self.large.at[self.at[3]], self.spot(), self.sems.at[i])

    def remote(self):
        z, x, c, y = self.at
        return pltpu.make_async_remote_copy(
            src_ref=self.large.at[1 - y],
            dst_ref=self.spot(),
            send_sem=self.send,
            recv_sem=self.recv,
            device_id=device(z, x, c, 1 - y),
            device_id_type=MESH,
        )

    def begin(self):
        self.remote().start()
        for i in range(self.n_small + 1):
            self.local(i).start()

    def wait_small(self):
        for i in range(self.n_small):
            self.local(i).wait()

    def wait_large(self):
        self.local(self.n_small).wait()
        self.remote().wait()


def add_rows(target, source, shape):
    rows, cols = shape
    many = max(n for n in range(16, rows + 1, 16) if rows % n == 0 and n * cols <= 65536)

    def strip(i, unused):
        at = pl.ds(pl.multiple_of(i * many, 16), many)
        target[at, :] = (target[at, :].astype(F32) + source[at, :].astype(F32)).astype(BF16)
        return unused

    lax.fori_loop(0, rows // many, strip, 0)


class Reduce:
    n_sems = 21
    n_scratch = 6

    def __init__(self, grad, out, held, core, first, second, last, edge, send, recv, own, x_first):
        self.x_first = x_first
        self.grad, self.held, self.core = grad, held, core
        self.first, self.second, self.last, self.edge, self.out = first, second, last, edge, out
        self.send, self.recv, self.own = send, recv, own
        self.rows, self.width = out.shape
        self.at = place()
        self.mine = half_of(self.width, self.at[3])
        self.other = half_of(self.width, 1 - self.at[3])

    @staticmethod
    def scratch(rows, width):
        half = width // 2
        return [
            pltpu.VMEM((ZS, 2, rows, width), BF16),
            pltpu.VMEM((ZS, 2, rows, width), BF16),
            pltpu.VMEM((ZS, 2, rows, half), BF16),
            pltpu.VMEM((ZS, rows, half), BF16),
            pltpu.VMEM((ZS, rows, half), BF16),
            pltpu.VMEM((2, rows, half), BF16),
        ]

    def copy(self, source, target, index, peer):
        return pltpu.make_async_remote_copy(
            src_ref=source,
            dst_ref=target,
            send_sem=self.send.at[index],
            recv_sem=self.recv.at[index],
            device_id=peer,
            device_id_type=MESH,
        )

    def load(self, s):
        return pltpu.make_async_copy(
            self.grad.at[s, :, self.at[2]], self.held.at[s], self.own.at[s]
        )

    def between_cores(self, s):
        z, x, c, y = self.at
        return self.copy(self.grad.at[s, :, 1 - c], self.core.at[s], s, device(z, x, 1 - c, y))

    def leg_one(self, s, i):
        z, x, c, y = self.at
        half = self.width // 2
        if s in self.x_first:
            source = self.held.at[s, 1 - x, :, pl.ds(i * half, half)]
            peer = device(z, 1 - x, c, y)
        else:
            source = self.held.at[s, i, :, self.other]
            peer = device(z, x, c, 1 - y)
        return self.copy(source, self.first.at[s, i], 4 + 2 * s + i, peer)

    def leg_two(self, s):
        z, x, c, y = self.at
        if s in self.x_first:
            source = self.held.at[s, x, :, self.other]
            peer = device(z, x, c, 1 - y)
        else:
            source = self.held.at[s, 1 - x, :, self.mine]
            peer = device(z, 1 - x, c, y)
        return self.copy(source, self.second.at[s], 12 + s, peer)

    def leg_three(self, s):
        z, x, c, y = self.at
        hop = (z + s) % 2 + 2 * ((z // 2 + s // 2) % 2)
        source = self.held.at[s, x, :, self.mine]
        return self.copy(source, self.last.at[hop], 16 + hop, device(s, x, c, y))

    def from_z(self, hop):
        z, x, c, y = self.at
        slot = self.last.at[hop]
        return self.copy(slot, slot, 16 + hop, device(z_peer(z, hop), x, c, y))

    def leg_four(self):
        z, x, c, y = self.at
        return self.copy(self.edge.at[0], self.edge.at[1], 20, device(z, x, c, 1 - y))

    def begin(self):
        for s in (0, 3, 1, 2):
            self.between_cores(s).start()
            self.load(s).start()

    def one(self, s):
        self.load(s).wait()
        self.between_cores(s).wait_recv()
        for i in range(2):
            add_rows(self.held.at[s, i], self.core.at[s, i], (self.rows, self.width))
        for i in range(2):
            self.leg_one(s, i).start()

    def two(self, s):
        x = self.at[1]
        half = self.width // 2
        for i in range(2):
            self.leg_one(s, i).wait_recv()
            if s in self.x_first:
                target = self.held.at[s, x, :, pl.ds(i * half, half)]
            else:
                target = self.held.at[s, i, :, self.mine]
            add_rows(target, self.first.at[s, i], (self.rows, half))
        self.leg_two(s).start()

    def three(self, s):
        x = self.at[1]
        self.leg_two(s).wait_recv()
        target = self.held.at[s, x, :, self.mine]
        add_rows(target, self.second.at[s], (self.rows, self.width // 2))

        @pl.when(self.at[0] != s)
        def _():
            self.leg_three(s).start()

    def four(self):
        z, x, c, y = self.at
        for hop in range(1, ZS):
            self.from_z(hop).wait_recv()
        own = self.held.at[z, x, :, self.mine]
        last, edge = self.last, self.edge

        def strip(i, unused):
            at = pl.ds(pl.multiple_of(i * 16, 16), 16)
            total = own[at, :].astype(F32)
            for hop in range(1, ZS):
                total += last[hop, at, :].astype(F32)
            edge[0, at, :] = total.astype(BF16)
            return unused

        lax.fori_loop(0, self.rows // 16, strip, 0)
        self.leg_four().start()
        self.out[:, self.mine] = edge[0].astype(F32)

    def finish(self):
        self.leg_four().wait()
        self.out[:, self.other] = self.edge[1].astype(F32)
        for s in range(ZS):
            self.between_cores(s).wait_send()
            for i in range(2):
                self.leg_one(s, i).wait_send()
            self.leg_two(s).wait_send()

            @pl.when(self.at[0] != s)
            def _():
                self.leg_three(s).wait_send()


class Total:
    long = (("c",), ("x",), ("y",), ("z",))
    short = (("c", "x", "y"), ("z",))
    n_slots = 12

    def __init__(self, part, out, leave, come, send, recv, rounds):
        self.part, self.out, self.leave, self.come = part, out, leave, come
        self.send, self.recv, self.rounds = send, recv, rounds
        self.at = place()

    @staticmethod
    def scratch(shape, kind, rounds):
        return [
            pltpu.VMEM((len(rounds),) + shape, kind),
            pltpu.VMEM((Total.n_slots,) + shape, kind),
        ]

    def group(self, step):
        z, x, c, y = self.at
        axes = self.rounds[step]
        if axes == ("z",):
            members = [device(i, x, c, y) for i in range(ZS)]
            return 8, z, members
        number, members = 0, []
        for axis in axes:
            number = number * 2 + {"c": c, "x": x, "y": y}[axis]
        for i in range(2 ** len(axes)):
            bits = {axis: (i >> (len(axes) - 1 - k)) % 2 for k, axis in enumerate(axes)}
            members.append(device(z, bits.get("x", x), bits.get("c", c), bits.get("y", y)))
        return 2 * step, number, members

    def copy(self, step, to, source):
        first, number, members = self.group(step)
        return pltpu.make_async_remote_copy(
            src_ref=self.leave.at[step],
            dst_ref=self.come.at[first + source],
            send_sem=self.send.at[first + to],
            recv_sem=self.recv.at[first + source],
            device_id=members[to],
            device_id_type=MESH,
        )

    def give(self, step, values):
        first, number, members = self.group(step)
        low = values.astype(self.leave.dtype)
        self.leave[step] = low
        self.come[first + number] = low
        for to in range(len(members)):

            @pl.when(number != to)
            def _():
                self.copy(step, to, number).start()

    def begin(self):
        self.give(0, self.part[...])

    def advance(self, step):
        first, number, members = self.group(step)
        for other in range(len(members)):

            @pl.when(number != other)
            def _():
                self.copy(step, other, other).wait_recv()
                self.copy(step, other, number).wait_send()

        total = self.come[first].astype(F32)
        for other in range(1, len(members)):
            total += self.come[first + other].astype(F32)
        if step + 1 < len(self.rounds):
            self.give(step + 1, total)
        else:
            self.out[...] = total


class RowsBack:
    n_sems = 3

    def __init__(self, line, blank, small, large, sems, send, recv):
        self.line, self.blank, self.small, self.large = line, blank, small, large
        self.sems, self.send, self.recv = sems, send, recv
        self.at = place()
        self.n_small = small.shape[0]
        self.rows = large.shape[1]

    def half(self, y):
        start = self.n_small * SPAD + self.rows * y
        return self.line.at[pl.ds(pl.multiple_of(start, 16), self.rows)]

    def local(self, i):
        n = self.n_small
        if i < n:
            source, target = self.line.at[pl.ds(i * SPAD, SPAD)], self.small.at[i, pl.ds(0, SPAD)]
        elif i < 2 * n:
            source, target = self.blank, self.small.at[i - n, pl.ds(SPAD, SLEN - SPAD)]
        else:
            y = self.at[3]
            source, target = self.half(y), self.large.at[y]
        return pltpu.make_async_copy(source, target, self.sems.at[i])

    def remote(self):
        z, x, c, y = self.at
        return pltpu.make_async_remote_copy(
            src_ref=self.half(1 - y),
            dst_ref=self.large.at[y],
            send_sem=self.send,
            recv_sem=self.recv,
            device_id=device(z, x, c, 1 - y),
            device_id_type=MESH,
        )

    def begin_large(self):
        self.remote().start()
        self.local(2 * self.n_small).start()

    def begin_small(self):
        for i in range(2 * self.n_small):
            self.local(i).start()

    def finish(self):
        for i in range(2 * self.n_small + 1):
            self.local(i).wait()
        self.remote().wait()


def begin_kernel(
    n_small,
    n_large,
    query_weight,
    key_weight,
    value_weight,
    out_weight,
    up_weight,
    down_share,
    small_in,
    large_in,
    small_cot,
    large_cot,
    table,
    gain,
    gain_bias,
    query_bias,
    value_bias,
    x_out,
    cot_out,
    qkv_out,
    turned_out,
    w_out,
    mid_whole,
    down_whole,
    out,
    out_wide,
    probs_small,
    probs_large,
    line,
    cot_line,
    hidden,
    turned,
    qkv,
    w_qkv,
    wide,
    narrow,
    bias_large,
    bias_small,
    send,
    recv,
    own,
    row_sems,
    row_send,
    row_recv,
    keep_sems,
    qkv_share,
    mid_share,
    share_sems,
    wide_table,
    low_large,
    low_small,
    high_large,
    high_small,
):
    step = pl.program_id(0)
    pairs = pl.num_programs(0)
    lows, highs = (low_large, low_small), (high_large, high_small)
    shares = []
    for target, weights in (
        (qkv_share, (query_weight, key_weight, value_weight)),
        (mid_share, (out_weight, up_weight)),
    ):
        col = 0
        for weight in weights:
            cols = slice(col, col + weight.shape[1])
            shares.append(
                pltpu.make_async_copy(weight, target.at[:, cols], share_sems.at[len(shares)])
            )
            col += weight.shape[1]
    width = hidden.shape[1]
    count = qkv.shape[1]
    masks = head_masks()
    first = Gather(qkv_share, w_qkv, send.at[0], recv.at[0], own.at[0], True)
    mid = Gather(mid_share, mid_whole, send.at[1], recv.at[1], own.at[1], False)
    down = Gather(down_share, down_whole, send.at[2], recv.at[2], own.at[2], True)
    x_rows = Rows(small_in, large_in, line, row_sems.at[0], row_send.at[0], row_recv.at[0])
    cot_rows = Rows(small_cot, large_cot, cot_line, row_sems.at[1], row_send.at[1], row_recv.at[1])
    keeps = [
        pltpu.make_async_copy(line, x_out, keep_sems.at[0]),
        pltpu.make_async_copy(qkv, qkv_out, keep_sems.at[1]),
        pltpu.make_async_copy(w_qkv, w_out, keep_sems.at[2]),
        pltpu.make_async_copy(cot_line, cot_out, keep_sems.at[3]),
        pltpu.make_async_copy(turned, turned_out, keep_sems.at[4]),
    ]

    early = (
        ((mid, 2), (mid, 1), (down, 2), (down, 1),),
        ((mid, 4), (down, 4),),
        ((mid, 3),),
    )
    slots = (
        ((down, 3),),
        ((mid, 5),),
        ((down, 5),),
        ((mid, 6),),
        ((down, 6),),
        ((mid, 7),),
        ((down, 7),),
        ((mid, 8),),
        ((down, 8),),
        ((mid, 9), (down, 9),),
        ((mid, 10),),
        ((down, 10),),
    )

    @pl.when(step == 0)
    def _():
        for share in shares:
            share.start()
        greet()
        for share in shares:
            share.wait()
        first.begin()
        x_rows.begin()
        table_sequences(table, wide_table, lows, highs)
        part = chunk_rows(count)
        chunks = [pl.ds(at, part) for at in range(0, count, part)]

        def norm(rows):
            normal, unused = normalized(line[rows, :].astype(F32))
            hidden[rows, :] = (normal * gain[...][None, :] + gain_bias[...][None, :]).astype(BF16)

        x_rows.wait_small()
        norm(chunks[0])
        for at in range(5):
            first.turn(at)
        mid.begin_z()
        down.begin_z()
        for at in range(5, 8):
            first.turn(at)
        x_rows.wait_large()
        for rows in chunks[1:]:
            norm(rows)
        keeps[0].start()
        mid.turn(0)
        down.turn(0)
        for at in range(8, 11):
            first.turn(at)
        first.arrive()
        mid.begin_across()
        down.begin_across()
        cot_rows.begin()
        keeps[2].start()
        scale = jnp.asarray(float(width // HEADS) ** (-0.5), BF16)
        for at, rows in enumerate(chunks):
            for kind in range(3):
                cols = slice(kind * width, (kind + 1) * width)
                weight = w_qkv[:, :, :, :, cols].reshape(width, width)
                made = dot_nn(hidden[rows, :], weight)
                if kind != 1:
                    made += (query_bias, None, value_bias)[kind][...][None, :]
                made = made.astype(BF16)
                if kind == 0:
                    made = made * scale
                for j in range(HEADS // 2):
                    qkv[kind * (HEADS // 2) + j, rows, :] = made[:, j * LANES : (j + 1) * LANES]
            for job, turn in early[at]:
                job.turn(turn)
        keeps[1].start()
        turned[...] = hidden[...].T
        keeps[4].start()

    query = qkv.at[step]
    key = qkv.at[pairs + step]
    value = qkv.at[2 * pairs + step]

    @pl.when(pl.program_id(0) == 0)
    def _():
        bias_small[...] = jnp.zeros_like(bias_small)

    members = [(i * SPAD, SPAD, bias_small, probs_small, i) for i in range(n_small)]
    members += [
        (n_small * SPAD + i * LPAD, LPAD, bias_large, probs_large, i) for i in range(n_large)
    ]
    halves = [[] for _ in members]
    for head in range(2):
        at_head = pl.ds(2 * step + head, 1)
        transposed_biases(
            (lows[0][at_head, :], highs[0][at_head, :]),
            (lows[1][at_head, :], highs[1][at_head, :]),
            wide_table[at_head, T_WIDTH - 256 :],
            wide,
            narrow,
            bias_large,
            bias_small,
        )
        for at, (start, count, bias, probs, which) in enumerate(members):
            rows = pl.ds(start, count)
            scores = dot_nt(key[rows, :], query[rows, :] * masks[head]) + bias[:, :count]
            top = jnp.max(scores, axis=0, keepdims=True)
            weights = jnp.exp(scores - top)
            total = jnp.sum(weights, axis=0, keepdims=True)
            prob = (weights * (1.0 / total)).astype(BF16)
            probs[head, which] = prob
            turned = value[rows, :].T
            halves[at].append(dot_nn(turned[head * 64 : head * 64 + 64, :], prob))
        for at in range(HEADS // 2):
            if slots[2 * at + head]:

                @pl.when(step == at)
                def _():
                    for job, turn in slots[2 * at + head]:
                        job.turn(turn)

    for at, (start, count, bias, probs, which) in enumerate(members):
        both = jnp.concatenate(halves[at], axis=0).T
        out[pl.ds(start, count), :] = both.astype(BF16)
        out_wide[pl.ds(start, count), :] = both

    @pl.when(step == pairs - 3)
    def _():
        cot_rows.wait_small()
        cot_rows.wait_large()
        keeps[3].start()

    @pl.when(step == pairs - 1)
    def _():
        for job in (mid, down):
            job.arrive()
        for job in (first, mid, down):
            job.drain()
        for keep in keeps:
            keep.wait()


EARLY = 4


def end_kernel(
    n_small,
    n_large,
    query,
    key,
    value,
    dout,
    out_wide,
    probs_small,
    probs_large,
    g_mid,
    g_down,
    x_hbm,
    turned_hbm,
    w_hbm,
    dres_hbm,
    feed_grads,
    gain,
    small_grad,
    large_grad,
    mid_out,
    down_out,
    early_out,
    late_out,
    feed_total,
    input_total,
    table_total,
    last_total,
    *scratch,
):
    scratch = list(scratch)

    def take(count):
        taken = scratch[:count]
        del scratch[:count]
        return taken

    wide, narrow, dsum_small, dscore_large, dqkv, hidden_turned, w_qkv, line, blank = take(9)
    early_grad, late_grad, input_part, table_part, last_part = take(5)
    mid_bufs, down_bufs, early_bufs, late_bufs = [take(Reduce.n_scratch) for unused in range(4)]
    feed_bufs, input_bufs, table_bufs, last_bufs = [take(2) for unused in range(4)]
    send, recv, own, total_send, total_recv, load_sems, row_sems, row_send, row_recv = scratch

    step = pl.program_id(0)
    pairs = HEADS // 2
    width = x_hbm.shape[1]
    all_rows = dqkv.shape[1]
    masks = head_masks()
    query, key, value = query.at[0], key.at[0], value.at[0]
    both_ways, mostly_x = (0, 1), (0, 1)
    mid = Reduce(g_mid, mid_out, *mid_bufs, send.at[0], recv.at[0], own.at[0], both_ways)
    down = Reduce(g_down, down_out, *down_bufs, send.at[1], recv.at[1], own.at[1], both_ways)
    early = Reduce(early_grad, early_out, *early_bufs, send.at[2], recv.at[2], own.at[2], mostly_x)
    late = Reduce(late_grad, late_out, *late_bufs, send.at[3], recv.at[3], own.at[3], mostly_x)
    sums = [
        Total(part, total, *bufs, total_send.at[i], total_recv.at[i], rounds)
        for i, (part, total, bufs, rounds) in enumerate(
            (
                (feed_grads, feed_total, feed_bufs, Total.long),
                (input_part, input_total, input_bufs, Total.short),
                (table_part, table_total, table_bufs, Total.long),
                (last_part, last_total, last_bufs, Total.short),
            )
        )
    ]
    feed_sum, input_sum, table_sum, last_sum = sums
    grad_rows = RowsBack(
        line, blank, small_grad, large_grad, row_sems.at[1], row_send.at[1], row_recv.at[1]
    )
    load_x = pltpu.make_async_copy(x_hbm, line, load_sems.at[1])
    load_turned = pltpu.make_async_copy(turned_hbm, hidden_turned, load_sems.at[2])
    load_w = pltpu.make_async_copy(w_hbm, w_qkv, load_sems.at[3])

    def take_turns(by_step):
        for at, turns in enumerate(by_step):
            if turns:

                @pl.when(step == at)
                def _():
                    for turn in turns:
                        turn[0](*turn[1:])

    slots = (
        ([(mid.one, 0), (mid.one, 3)], [], [], [(mid.three, 0), (mid.three, 3), (down.one, 1), (down.one, 2)], [(mid.three, 1), (mid.three, 2)], [(down.three, 0), (down.three, 3), (early.one, 1), (early.one, 2)]),
        ([], [(mid.one, 1), (mid.one, 2)], [(down.one, 0), (down.one, 3)], [], [], [(table_sum.advance, 0)]),
        ([], [(feed_sum.advance, 1)], [(feed_sum.advance, 2)], [(down.two, 0), (down.two, 3)], [(down.two, 1), (down.two, 2), (early.one, 0), (early.one, 3)], [(early.two, 0), (early.two, 3), (down.three, 1), (down.three, 2)]),
        ([(feed_sum.advance, 0)], [(mid.two, 0), (mid.two, 3)], [(mid.two, 1), (mid.two, 2)], [(feed_sum.advance, 3)], [(table_sum.begin,)], [(table_sum.advance, 1)]),
    )

    @pl.when(step == 0)
    def _():
        greet()
        mid.begin()
        down.begin()
        load_turned.start()
        load_x.start()
        load_w.start()
        blank[...] = jnp.zeros_like(blank)
        table_part[...] = jnp.zeros_like(table_part)
        last_part[...] = jnp.zeros_like(last_part)
        feed_sum.begin()

    lane = iota((1, LANES), 1)
    scale = float(64) ** (-0.5)
    members = [(i * SPAD, SPAD, probs_small, i) for i in range(n_small)]
    members += [(n_small * SPAD + i * LPAD, LPAD, probs_large, i) for i in range(n_large)]
    keep = []
    for head in range(2):
        spot = 64 * (1 - head)
        minus = jnp.where((lane == spot) | (lane == spot + 1), -1.0, 0.0).astype(BF16)
        mask32 = masks[head].astype(F32)
        for at, (start, count, probs, which) in enumerate(members):
            rows = pl.ds(start, count)
            grad = dout[rows, :]
            grad32 = grad.astype(F32) * mask32
            delta = jnp.sum(grad32 * out_wide[rows, :], axis=1, keepdims=True)
            coarse = delta.astype(BF16).astype(F32)
            fine = delta - coarse
            side = jnp.where(lane == spot, coarse, jnp.where(lane == spot + 1, fine, grad32))
            values = value[rows, :] * masks[head] + minus
            prob = probs[head, which]
            dscore = prob.astype(F32) * dot_nt(values, side.astype(BF16))
            if count == SPAD:
                if which == 0:
                    dsum_small[:, :SPAD] = dscore
                else:
                    dsum_small[:, :SPAD] += dscore
            elif which == 0:
                dscore_large[:, :LPAD] = dscore
            else:
                dscore_large[:, :LPAD] += dscore
            low = dscore.astype(BF16)
            turned = key[rows, :].T
            dq = dot_nn(turned[head * 64 : head * 64 + 64, :], low)
            dk = dot_nn(low, query[rows, :])
            dv = dot_nn(prob, grad)
            if head == 0:
                keep.append((dq, dk, dv))
            else:
                first = iota((count, LANES), 1) < 64
                dq0, dk0, dv0 = keep[at]
                dqkv[step, rows, :] = (jnp.concatenate([dq0, dq], axis=0).T * scale).astype(BF16)
                dqkv[pairs + step, rows, :] = jnp.where(first, dk0, dk).astype(BF16)
                dqkv[2 * pairs + step, rows, :] = jnp.where(first, dv0, dv).astype(BF16)
        take_turns(slots[2 * head])
        wide[...] = jnp.zeros_like(wide)
        dscore_large[:, LPAD:] = jnp.zeros((LPAD, 768 - LPAD), F32)
        edge_lane = iota((24, 768), 1)
        edge_row = iota((24, 768), 0)
        class_column = jnp.zeros((24, 768), F32)
        class_row = None
        for block in range(LGRID + 1):
            at, turn = large_window(block)
            piece = dscore_large[pl.ds(block * 24, 24), :]
            if block == 0:
                class_row = piece[0:1, :]
                piece = jnp.where(edge_row == 0, 0.0, piece)
            class_column = class_column + piece
            piece = jnp.where(edge_lane == 0, 0.0, piece)
            if turn:
                piece = pltpu.roll(piece, turn, 1)
            wide[:, at * LANES : at * LANES + 768] += piece
        low_sum, high_sum = gather_sequences(wide[...], 24, L_WIDTH, LGRID, 1)
        large_sums = (low_sum, high_sum)
        narrow[...] = jnp.zeros_like(narrow)
        dsum_small[:, SPAD:] = jnp.zeros((SPAD, 384 - SPAD), F32)
        small_lane = iota((SGRID, 384), 1)
        small_column = jnp.zeros((SGRID, 384), F32)
        for block in range(SGRID):
            at, turn = small_window(block)
            piece = dsum_small[pl.ds(1 + SGRID * block, SGRID), :]
            small_column = small_column + piece
            piece = jnp.where(small_lane == 0, 0.0, piece)
            piece = jnp.concatenate([piece, jnp.zeros((2, 384), F32)], axis=0)
            if turn:
                piece = pltpu.roll(piece, turn, 1)
            narrow[:, at * LANES : at * LANES + 384] += piece
        low_sum, high_sum = gather_sequences(narrow[...], 16, S_WIDTH, SGRID, 0)
        by_query = row_sum(class_column)[:, :LANES] + row_sum(small_column)[:, :LANES]
        both_rows = class_row + jnp.concatenate(
            [dsum_small[0:1, :], jnp.zeros((1, 384), F32)], axis=1
        )
        class_key = jnp.sum(
            jnp.where(iota((1, 768), 1) == 0, 0.0, both_rows), axis=1, keepdims=True
        )
        spot = iota((1, S_WIDTH), 1)
        low_sum = jnp.where(spot == S_WIDTH - 3, by_query[:, 0:1], low_sum)
        low_sum = jnp.where(spot == S_WIDTH - 2, class_key, low_sum)
        low_sum = jnp.where(spot == S_WIDTH - 1, both_rows[:, 0:1], low_sum)

        @pl.when(step < pairs - 1)
        def _():
            for kind, sums_pair in enumerate(zip(large_sums, (low_sum, high_sum))):
                row = pl.ds(16 * kind + step * 2 + head, 1)
                table_part[row, :L_WIDTH] = sums_pair[0]
                table_part[row, L_WIDTH:] = sums_pair[1]

        @pl.when(step == pairs - 1)
        def _():
            for kind, sums_pair in enumerate(zip(large_sums, (low_sum, high_sum))):
                row = pl.ds(4 * kind + head, 1)
                last_part[row, :L_WIDTH] = sums_pair[0]
                last_part[row, L_WIDTH:] = sums_pair[1]

        take_turns(slots[1 + 2 * head])

    @pl.when(step == 0)
    def _():
        load_turned.wait()

    @pl.when(step % 2 == 1)
    def _():
        pieces = [dqkv[kind * pairs + step - 1 + i] for i in range(2) for kind in range(3)]
        made = dot_nn(hidden_turned[...], jnp.concatenate(pieces, axis=1)).astype(BF16)
        made = made.reshape(ZS, 2, 2, width // 16, width)
        for at in range(pairs // 2):

            @pl.when(step == 2 * at + 1)
            def _():
                if at < EARLY // 2:
                    early_grad[:, :, :, :, at * width : (at + 1) * width] = made
                else:
                    late_grad[...] = made

    @pl.when(step == EARLY - 1)
    def _():
        early.begin()

    @pl.when(step == pairs - 1)
    def _():
        late.begin()
        last_sum.begin()
        load_x.wait()
        load_w.wait()
        part = chunk_rows(all_rows)
        zeros = jnp.zeros((1, width), F32)
        input_part[...] = jnp.zeros_like(input_part)
        end_turns = (
            [(late.one, 0), (late.one, 3), (late.one, 1), (late.one, 2), (early.two, 1), (early.two, 2), (table_sum.advance, 2)],
            [(mid.four,), (late.two, 0), (late.two, 3), (early.three, 0), (early.three, 3), (last_sum.advance, 0)],
            [(late.two, 1), (late.two, 2), (early.three, 1), (early.three, 2), (down.four,)],
        )
        for at, first in enumerate(reversed(range(0, all_rows, part))):
            rows = pl.ds(first, part)
            load_dres = pltpu.make_async_copy(
                dres_hbm.at[rows], dscore_large.at[pl.ds(0, part)], load_sems.at[4]
            )
            load_dres.start()
            dhidden = jnp.zeros((part, width), F32)
            for kind in range(3):
                piece = jnp.concatenate(
                    [dqkv[kind * pairs + j, rows, :] for j in range(pairs)], axis=1
                )
                weight = w_qkv[:, :, :, :, kind * width : (kind + 1) * width]
                dhidden += dot_nt(piece, weight.reshape(width, width))
                if kind != 1:
                    input_part[kind : kind + 1, :] += row_sum(piece.astype(F32))
            normal, rate = normalized(line[rows, :].astype(F32))
            input_part[3:4, :] += row_sum(dhidden * normal)
            input_part[4:5, :] += row_sum(dhidden)
            back = norm_back(dhidden * gain[...][None, :], normal, rate)
            load_dres.wait()
            line[rows, :] = (dscore_large[pl.ds(0, part), :] + back).astype(BF16)
            if at == 0:
                line[pl.ds(all_rows, line.shape[0] - all_rows), :] = jnp.zeros(
                    (line.shape[0] - all_rows, width), BF16
                )
            if first <= n_small * SPAD < first + part:
                grad_rows.begin_large()
            for turn in end_turns[at]:
                turn[0](*turn[1:])
        grad_rows.begin_small()
        input_sum.begin()
        for turn in (
            [(input_sum.advance, 0), (late.three, 0), (late.three, 3), (late.three, 1), (late.three, 2), (table_sum.advance, 3), (last_sum.advance, 1), (early.four,), (input_sum.advance, 1), (late.four,)]
        ):
            turn[0](*turn[1:])
        grad_rows.finish()
        for job in (mid, down, early, late):
            job.finish()


def gelu_pair(upper):
    normal_cdf = 0.5 * (1.0 + lax.erf(upper * (0.5**0.5)))
    density = jnp.exp(-0.5 * upper * upper) * 0.3989422804014327
    return upper * normal_cdf, normal_cdf + upper * density


def valid_rows(first, count, n_small):
    row = iota((count, 1), 0) + first
    in_small = row < n_small * SPAD
    small_ok = row % SPAD < SGRID * SGRID + 1
    large_ok = (row - n_small * SPAD) % LPAD < LGRID * LGRID + 1
    return jnp.where(in_small, small_ok.astype(F32), large_ok.astype(F32))


def feed_kernel(
    n_small,
    tiles,
    x,
    attended,
    cot,
    mid_hbm,
    down_hbm,
    out_bias,
    attend_scale,
    second_gain,
    second_bias,
    down_bias,
    feed_scale,
    up_bias,
    small_out,
    large_out,
    dresidual,
    dattended,
    vector_grads,
    g_mid,
    g_down,
    w_mid,
    w_down,
    active,
    slope,
    acc_out,
    acc_up,
    acc_down,
    sems,
    line,
    blank,
    row_sems,
    row_send,
    row_recv,
):
    step = pl.program_id(0)
    count, width = x.shape
    all_rows = n_small * SPAD + LPAD
    w_out = w_mid.at[:, :width]
    w_up = w_mid.at[:, width:]
    tile = w_up.shape[1] // tiles

    final = pl.num_programs(0) - 1
    out_rows = RowsBack(line, blank, small_out, large_out, row_sems, row_send.at[0], row_recv.at[0])
    pieces = [(mid_hbm, w_mid, g_mid, (slice(None), slice(0, width)))]
    for t in range(tiles):
        cols = slice(width + t * tile, width + (t + 1) * tile)
        pieces.append((mid_hbm, w_mid, g_mid, (slice(None), cols)))
    for t in range(tiles):
        rows = slice(t * tile, (t + 1) * tile)
        pieces.append((down_hbm, w_down, g_down, (rows, slice(None))))

    def load(at):
        source, held, target, where = pieces[at]
        return pltpu.make_async_copy(source.at[where], held.at[where], sems.at[at])

    def store(at):
        source, held, target, where = pieces[at]
        return pltpu.make_async_copy(held.at[where], target.at[where], sems.at[at])

    @pl.when(step == 0)
    def _():
        for at in range(len(pieces)):
            load(at).start()
        greet_seq()
        acc_out[...] = jnp.zeros_like(acc_out)
        acc_up[...] = jnp.zeros_like(acc_up)
        acc_down[...] = jnp.zeros_like(acc_down)
        vector_grads[...] = jnp.zeros_like(vector_grads)
        load(0).wait()

    out_bias, attend_scale, second_gain, second_bias, down_bias, feed_scale = (
        v[...][None, :]
        for v in (out_bias, attend_scale, second_gain, second_bias, down_bias, feed_scale)
    )

    valid = valid_rows(step * count, count, n_small)
    mixed = attended[...]
    branch = dot_nn(mixed, w_out[...]) + out_bias
    residual = x[...].astype(F32) + attend_scale * branch
    normal, scale = normalized(residual)
    hidden = (normal * second_gain + second_bias).astype(BF16)

    @pl.when(step == 0)
    def _():
        for at in range(1, len(pieces)):
            load(at).wait()

    lower = jnp.zeros((count, width), F32)
    for t in range(tiles):
        cols = slice(t * tile, (t + 1) * tile)
        upper = dot_nn(hidden, w_up[:, cols]) + up_bias[cols][None, :]
        made, rate = gelu_pair(upper)
        made = made.astype(BF16)
        active[:, cols] = made
        slope[:, cols] = rate.astype(BF16)
        lower += dot_nn(made, w_down[cols, :])
    lower += down_bias
    spot = pl.ds(pl.multiple_of(step * count, 16), count)
    line[spot, :] = ((residual + feed_scale * lower) * valid).astype(BF16)

    @pl.when(step == final)
    def _():
        blank[...] = jnp.zeros_like(blank)
        rest = line.shape[0] - all_rows
        line[pl.ds(all_rows, rest), :] = jnp.zeros((rest, width), BF16)
        out_rows.begin_large()
        out_rows.begin_small()

    upstream = cot[...].astype(F32) * valid
    vector_grads[5:6, :] += row_sum(upstream * lower)
    dlower = (upstream * feed_scale).astype(BF16)
    vector_grads[4:5, :] += row_sum(dlower.astype(F32))
    turned = hidden.T
    dhidden = jnp.zeros((count, width), F32)
    for t in range(tiles):
        cols = slice(t * tile, (t + 1) * tile)
        dupper = (dot_nt(dlower, w_down[cols, :]) * slope[:, cols].astype(F32)).astype(BF16)
        vector_grads[8 + t : 9 + t, :] += row_sum(dupper.astype(F32))
        acc_down[cols, :] += dot_nn(active[:, cols].T, dlower)
        acc_up[:, cols] += dot_nn(turned, dupper)
        dhidden += dot_nt(dupper, w_up[:, cols])

    @pl.when(step == final)
    def _():
        for t in range(tiles):
            cols = slice(t * tile, (t + 1) * tile)
            w_up[:, cols] = acc_up[:, cols].astype(BF16)
            store(1 + t).start()
            w_down[cols, :] = acc_down[cols, :].astype(BF16)
            store(1 + tiles + t).start()

    vector_grads[2:3, :] += row_sum(dhidden * normal)
    vector_grads[3:4, :] += row_sum(dhidden)
    dres = upstream + norm_back(dhidden * second_gain, normal, scale)
    dresidual[...] = dres
    vector_grads[1:2, :] += row_sum(dres * branch)
    dbranch = (dres * attend_scale).astype(BF16)
    vector_grads[0:1, :] += row_sum(dbranch.astype(F32))
    acc_out[...] += dot_nn(mixed.T, dbranch)
    dattended[...] = dot_nt(dbranch, w_out[...]).astype(BF16)

    @pl.when(step == final)
    def _():
        w_out[...] = acc_out[...].astype(BF16)
        store(0).start()
        for at in range(len(pieces)):
            store(at).wait()
        out_rows.finish()


def chunk_rows(total):
    return max(size for size in range(16, 481, 16) if total % size == 0)


def params(collective=None):
    if collective is None:
        return pltpu.CompilerParams(vmem_limit_bytes=VMEM_BYTES)
    return pltpu.CompilerParams(
        vmem_limit_bytes=VMEM_BYTES, collective_id=collective, has_side_effects=True
    )


def held(shape):
    rank = len(shape)
    return pl.BlockSpec(shape, lambda i: (0,) * rank, pipeline_mode=pl.Buffered(1))


def resident(shape):
    rank = len(shape)
    return pl.BlockSpec(shape, lambda i: (0,) * rank)


def run_begin(weights, rows, table, vectors, collective):
    small, large = rows[:2]
    n_small, n_large = small.shape[0], 1
    width = small.shape[-1]
    pairs = HEADS // 2
    count = n_small * SPAD + n_large * LPAD
    line = n_small * SPAD + n_large * LLEN
    anywhere = pl.BlockSpec(memory_space=pl.ANY)
    sems = pltpu.SemaphoreType.DMA
    column = pl.BlockSpec((count, LANES), lambda i: (0, i))
    strip = width // 16
    qkv_share, mid_share = (strip, 3 * width), (strip, width + weights[4].shape[1])
    wholes = [(ZS, 2, 2) + s for s in (qkv_share, mid_share, weights[5].shape)]

    def per_pair(shape):
        tail = (0,) * (len(shape) - 1)
        return pl.BlockSpec((2,) + shape[1:], lambda i: (i,) + tail)

    probs = [(HEADS, n_small, SPAD, SPAD), (HEADS, n_large, LPAD, LPAD)]
    return pl.pallas_call(
        functools.partial(begin_kernel, n_small, n_large),
        grid=(pairs,),
        in_specs=[anywhere] * 10 + [held(v.shape) for v in (table,) + vectors],
        out_specs=[anywhere] * 7 + [column, column] + [per_pair(p) for p in probs],
        out_shape=[
            jax.ShapeDtypeStruct((line, width), BF16),
            jax.ShapeDtypeStruct((line, width), BF16),
            jax.ShapeDtypeStruct((3 * pairs, count, LANES), BF16),
            jax.ShapeDtypeStruct((width, count), BF16),
        ]
        + [jax.ShapeDtypeStruct(w, BF16) for w in wholes]
        + [
            jax.ShapeDtypeStruct((count, width), BF16),
            jax.ShapeDtypeStruct((count, width), F32),
        ]
        + [jax.ShapeDtypeStruct(p, BF16) for p in probs],
        scratch_shapes=[
            pltpu.VMEM((line, width), BF16),
            pltpu.VMEM((line, width), BF16),
            pltpu.VMEM((count, width), BF16),
            pltpu.VMEM((width, count), BF16),
            pltpu.VMEM((3 * pairs, count, LANES), BF16),
            pltpu.VMEM(wholes[0], BF16),
            pltpu.VMEM((24, L_WIDTH), F32),
            pltpu.VMEM((16, S_WIDTH), F32),
            pltpu.VMEM((LPAD, 640), F32),
            pltpu.VMEM((SPAD, 256), F32),
            sems((3, Gather.n_sems)),
            sems((3, Gather.n_sems)),
            sems((3,)),
            sems((2, n_small + 1)),
            sems((2,)),
            sems((2,)),
            sems((5,)),
            pltpu.VMEM(qkv_share, BF16),
            pltpu.VMEM(mid_share, BF16),
            sems((5,)),
            pltpu.VMEM((16, T_WIDTH), F32),
            pltpu.VMEM((16, L_WIDTH), F32),
            pltpu.VMEM((16, S_WIDTH), F32),
            pltpu.VMEM((16, L_WIDTH), F32),
            pltpu.VMEM((16, S_WIDTH), F32),
        ],
        compiler_params=params(collective),
    )(*weights, *rows, table, *vectors)


def run_end(qkv, dattended, out_wide, probs, grads, rows, feed_grads, gain, n_small, collective):
    count, width = dattended.shape
    pairs = HEADS // 2
    line = rows[0].shape[0]
    anywhere = pl.BlockSpec(memory_space=pl.ANY)
    inside = pl.BlockSpec(memory_space=pltpu.VMEM)
    sems = pltpu.SemaphoreType.DMA
    column = pl.BlockSpec((count, LANES), lambda i: (0, i))
    shares = [(g.shape[0] // 16, g.shape[1]) for g in grads]
    shares += [(width // 16, 3 * LANES * many) for many in (EARLY, pairs - EARLY)]
    smalls = [feed_grads.shape, (8, width), (32, L_WIDTH + S_WIDTH)]
    smalls.append((8, L_WIDTH + S_WIDTH))

    def third(which):
        return pl.BlockSpec((1, count, LANES), lambda i: (which * pairs + i, 0, 0))

    def per_pair(shape):
        tail = (0,) * (len(shape) - 1)
        return pl.BlockSpec((2,) + shape[1:], lambda i: (i,) + tail)

    scratch = [
        pltpu.VMEM((24, L_WIDTH), F32),
        pltpu.VMEM((16, S_WIDTH), F32),
        pltpu.VMEM((SPAD, 384), F32),
        pltpu.VMEM((LPAD, 768), F32),
        pltpu.VMEM((3 * pairs, count, LANES), BF16),
        pltpu.VMEM((width, count), BF16),
        pltpu.VMEM((ZS, 2, 2, width // 16, 3 * width), BF16),
        pltpu.VMEM((line, width), BF16),
        pltpu.VMEM((SLEN - SPAD, width), BF16),
        pltpu.VMEM((ZS, 2, 2) + shares[2], BF16),
        pltpu.VMEM((ZS, 2, 2) + shares[3], BF16),
        pltpu.VMEM(smalls[1], F32),
        pltpu.VMEM(smalls[2], F32),
        pltpu.VMEM(smalls[3], F32),
    ]
    for shape in shares:
        scratch += Reduce.scratch(*shape)
    rounds = (Total.long, Total.short, Total.long, Total.short)
    for shape, kind, some in zip(smalls, (F32, F32, BF16, BF16), rounds):
        scratch += Total.scratch(shape, kind, some)
    scratch += [
        sems((4, Reduce.n_sems)),
        sems((4, Reduce.n_sems)),
        sems((4, ZS)),
        sems((4, Total.n_slots)),
        sems((4, Total.n_slots)),
        sems((5,)),
        sems((2, 2 * n_small + 1)),
        sems((2,)),
        sems((2,)),
    ]
    small = jax.ShapeDtypeStruct((n_small, SLEN, width), BF16)
    large = jax.ShapeDtypeStruct((2, LLEN // 2, width), BF16)
    return pl.pallas_call(
        functools.partial(end_kernel, n_small, 1),
        grid=(pairs,),
        in_specs=[third(0), third(1), third(2), column, column]
        + [per_pair(p.shape) for p in probs]
        + [anywhere] * 6
        + [held(feed_grads.shape), held(gain.shape)],
        out_specs=[anywhere] * 2 + [inside] * 8,
        out_shape=[small, large]
        + [jax.ShapeDtypeStruct(s, F32) for s in shares + smalls],
        scratch_shapes=scratch,
        compiler_params=params(collective),
        cost_estimate=pl.CostEstimate(
            flops=40 * 10**9, bytes_accessed=50 * 10**6, transcendentals=0
        ),
    )(
        qkv,
        qkv,
        qkv,
        dattended,
        out_wide,
        *probs,
        *[g.reshape((ZS, 2, 2) + s) for g, s in zip(grads, shares)],
        *rows,
        feed_grads,
        gain,
    )


def run_feed(x, attended, cot, w_mid, w_down, vectors, n_small, collective):
    rows, width = attended.shape
    size = chunk_rows(rows)
    hidden = w_down.shape[0]
    tiles = hidden // width
    block = pl.BlockSpec((size, width), lambda i: (i, 0))
    anywhere = pl.BlockSpec(memory_space=pl.ANY)
    return pl.pallas_call(
        functools.partial(feed_kernel, n_small, tiles),
        grid=(rows // size,),
        in_specs=[
            block,
            block,
            block,
            anywhere,
            anywhere,
        ]
        + [held(v.shape) for v in vectors],
        out_specs=[
            anywhere,
            anywhere,
            block,
            block,
            resident((16, width)),
            anywhere,
            anywhere,
        ],
        out_shape=[
            jax.ShapeDtypeStruct((n_small, SLEN, width), BF16),
            jax.ShapeDtypeStruct((2, LLEN // 2, width), BF16),
            jax.ShapeDtypeStruct((rows, width), F32),
            jax.ShapeDtypeStruct((rows, width), BF16),
            jax.ShapeDtypeStruct((16, width), F32),
            jax.ShapeDtypeStruct((width, width + hidden), BF16),
            jax.ShapeDtypeStruct((hidden, width), BF16),
        ],
        scratch_shapes=[
            pltpu.VMEM((width, width + hidden), BF16),
            pltpu.VMEM((hidden, width), BF16),
            pltpu.VMEM((size, hidden), BF16),
            pltpu.VMEM((size, hidden), BF16),
            pltpu.VMEM((width, width), F32),
            pltpu.VMEM((width, hidden), F32),
            pltpu.VMEM((hidden, width), F32),
            pltpu.SemaphoreType.DMA((1 + 2 * tiles,)),
            pltpu.VMEM((x.shape[0], width), BF16),
            pltpu.VMEM((SLEN - SPAD, width), BF16),
            pltpu.SemaphoreType.DMA((2 * n_small + 1,)),
            pltpu.SemaphoreType.DMA((1,)),
            pltpu.SemaphoreType.DMA((1,)),
        ],
        compiler_params=params(collective),
        cost_estimate=pl.CostEstimate(
            flops=6 * rows * width * (width + 2 * hidden),
            bytes_accessed=40 * 10**6,
            transcendentals=2 * rows * hidden,
        ),
    )(x, attended, cot, w_mid, w_down, *vectors)


def finish_kernel(
    feed_total,
    input_total,
    table_total,
    last_total,
    mid_share,
    down_share,
    early_share,
    late_share,
    first_gain,
    first_bias,
    query,
    query_bias,
    key,
    value,
    value_bias,
    out,
    out_bias,
    attend_scale,
    second_gain,
    second_bias,
    up,
    up_bias,
    down,
    down_bias,
    feed_scale,
    table,
    wide_table,
    sequences,
):
    width = out.shape[1]
    for at, ref in enumerate(
        (out_bias, attend_scale, second_gain, second_bias, down_bias, feed_scale)
    ):
        ref[...] = feed_total[at, :]
    for t in range(up_bias.shape[0] // width):
        up_bias[t * width : (t + 1) * width] = feed_total[8 + t, :]
    for at, ref in ((0, query_bias), (2, value_bias), (3, first_gain), (4, first_bias)):
        ref[...] = input_total[at, :]
    out[...] = mid_share[:, :width]
    up[...] = mid_share[:, width:]
    down[...] = down_share[...]
    pair = 0
    for share in (early_share, late_share):
        for at in range(share.shape[1] // (3 * LANES)):
            for kind, ref in enumerate((query, key, value)):
                place_at = (3 * at + kind) * LANES
                ref[:, pair * LANES : (pair + 1) * LANES] = share[:, place_at : place_at + LANES]
            pair += 1
    sequences[...] = table_total[...]
    for kind in range(2):
        sequences[pl.ds(16 * kind + HEADS - 2, 2), :] = last_total[pl.ds(4 * kind, 2), :]
    lows = (sequences.at[pl.ds(0, 16), :L_WIDTH], sequences.at[pl.ds(0, 16), L_WIDTH:])
    highs = (sequences.at[pl.ds(16, 16), :L_WIDTH], sequences.at[pl.ds(16, 16), L_WIDTH:])
    table_from_sequences(lows, highs, wide_table)
    table[...] = wide_table[pl.ds(0, table.shape[0]), pl.ds(0, table.shape[1])]


def run_finish(totals, shares, entries):
    width = totals[0].shape[1]
    strip, hidden = shares[0].shape[0], shares[0].shape[1] - width
    vector = jax.ShapeDtypeStruct((width,), F32)
    square = jax.ShapeDtypeStruct((strip, width), F32)
    inside = pl.BlockSpec(memory_space=pltpu.VMEM)
    out_shape = [vector, vector, square, vector, square, square, vector, square]
    out_shape += [vector, vector, vector, vector]
    out_shape += [jax.ShapeDtypeStruct((strip, hidden), F32), jax.ShapeDtypeStruct((hidden,), F32)]
    out_shape += [jax.ShapeDtypeStruct(shares[1].shape, F32), vector, vector]
    out_shape += [jax.ShapeDtypeStruct((HEADS, entries), F32)]
    return pl.pallas_call(
        finish_kernel,
        in_specs=[inside] * 8,
        out_specs=[inside] * len(out_shape),
        out_shape=out_shape,
        scratch_shapes=[pltpu.VMEM((16, T_WIDTH), F32), pltpu.VMEM(totals[2].shape, F32)],
        compiler_params=params(),
    )(*totals, *shares)


def shifted(array, axis, by):
    count = lax.axis_size(axis)
    return lax.ppermute(array, axis, [(i, (i + by) % count) for i in range(count)])


def layer_norm(values, gain, bias):
    center = values - jnp.mean(values, axis=-1, keepdims=True)
    spread = jnp.mean(center * center, axis=-1, keepdims=True)
    return center * lax.rsqrt(spread + EPSILON) * gain + bias


def matmul(left, right):
    return jnp.dot(left, right, preferred_element_type=jnp.float32)


def position_bias(table, places, length, grid):
    heads = table.shape[0]
    span = 2 * LGRID - 1
    total_rel = table.shape[1]
    queries_count = places.shape[0]
    grid_table = table[:, : span * span].reshape(heads, span, span)
    patch = places - 1
    query_row = patch // grid
    query_col = patch % grid
    steps_all = jnp.arange(span, dtype=jnp.int32)
    cells = jnp.arange(grid, dtype=jnp.int32)
    row_hot = (
        steps_all[None, :, None] == query_row[:, None, None] - cells[None, None, :] + LGRID - 1
    ).astype(jnp.float32)
    col_hot = (
        steps_all[None, :, None] == query_col[:, None, None] - cells[None, None, :] + LGRID - 1
    ).astype(jnp.float32)
    partial_bias = jnp.einsum("hab,qbc->hqac", grid_table, col_hot, precision=lax.Precision.HIGHEST)
    patches = jnp.einsum(
        "qar,hqac->hqrc", row_hot, partial_bias, precision=lax.Precision.HIGHEST
    ).reshape(heads, queries_count, grid * grid)
    rest = length - 1 - grid * grid
    class_key = jnp.broadcast_to(table[:, total_rel - 2][:, None, None], (heads, queries_count, 1))
    patch_rows = jnp.concatenate(
        [class_key, patches, jnp.zeros((heads, queries_count, rest), jnp.float32)], axis=2
    )
    class_row = jnp.concatenate(
        [
            table[:, total_rel - 1][:, None],
            jnp.broadcast_to(table[:, total_rel - 3][:, None], (heads, grid * grid)),
            jnp.zeros((heads, rest), jnp.float32),
        ],
        axis=1,
    )
    is_class = (places == 0)[None, :, None]
    return jnp.where(is_class, class_row[:, None, :], patch_rows)


def to_heads(block, heads):
    groups, rows, width = block.shape
    return block.reshape(groups, rows, heads, width // heads)


def block_scores(query, key, query_rows, key_rows, length, bias_full):
    size = query.shape[-1] // HEADS
    raw = jnp.einsum(
        "gqhd,gkhd->ghqk",
        to_heads(query, HEADS),
        to_heads(key, HEADS),
        preferred_element_type=jnp.float32,
    )
    key_place = key_rows % length
    select = (key_place[:, None] == jnp.arange(length, dtype=jnp.int32)[None, :]).astype(
        jnp.float32
    )
    bias_block = jnp.einsum("hql,kl->hqk", bias_full, select, precision=lax.Precision.HIGHEST)
    allowed = (query_rows // length)[:, None] == (key_rows // length)[None, :]
    scores = raw * float(size) ** (-0.5) + bias_block[None]
    return (scores, allowed, select)


def key_rows_of(source, count_keys):
    return source * count_keys + jnp.arange(count_keys, dtype=jnp.int32)


def allowed_mask(allowed, key_rows, length, grid):
    return allowed & (key_rows % length < grid * grid + 1)[None, :]


def absorb_one(state, query, key, value, query_rows, key_rows, info):
    length, grid, bias_full = info
    maximum, total, accum = state
    scores, allowed, select = block_scores(query, key, query_rows, key_rows, length, bias_full)
    allowed = allowed_mask(allowed, key_rows, length, grid)
    masked = jnp.where(allowed[None, None], scores, NEGATIVE)
    newmax = jnp.maximum(maximum, jnp.max(masked, axis=-1))
    weights = jnp.where(allowed[None, None], jnp.exp(scores - newmax[..., None]), 0.0)
    factor = jnp.exp(maximum - newmax)
    total = total * factor + jnp.sum(weights, axis=-1)
    accum = accum * factor[..., None] + jnp.einsum(
        "ghqk,gkhd->ghqd",
        weights.astype(jnp.bfloat16),
        to_heads(value, HEADS),
        preferred_element_type=jnp.float32,
    )
    return (newmax, total, accum)


def absorb_cycle(states, queries, moving, members, query_rows, source, info):
    states = list(states)
    for which, offset, rows in members:
        key = moving[0][:, offset : offset + rows]
        value = moving[1][:, offset : offset + rows]
        states[which] = absorb_one(
            states[which],
            queries[which],
            key,
            value,
            query_rows[which],
            key_rows_of(source, rows),
            info[which],
        )
    return tuple(states)


def pass_forward(moving):
    return shifted((moving[0], moving[1]), "seq", 1)


def cycle_forward(queries, cycle_pair, members, query_rows, info):
    position = lax.axis_index("seq")
    count = lax.axis_size("seq")
    states = []
    for which in range(2):
        groups, rows, width = queries[which].shape
        states.append(
            (
                jnp.full((groups, HEADS, rows), NEGATIVE, jnp.float32),
                jnp.zeros((groups, HEADS, rows), jnp.float32),
                jnp.zeros((groups, HEADS, rows, width // HEADS), jnp.float32),
            )
        )
    states = absorb_cycle(tuple(states), queries, cycle_pair, members, query_rows, position, info)

    def turn(step, carry):
        held_states, moving = carry
        moving = tuple(pass_forward(moving))
        held_states = absorb_cycle(
            held_states, queries, moving, members, query_rows, (position - step) % count, info
        )
        return (held_states, moving)

    states, moving = lax.fori_loop(1, count, turn, (states, cycle_pair))
    attended = []
    logsums = []
    for which in range(2):
        maximum, total, accum = states[which]
        groups, heads_count, rows, size = accum.shape
        attended.append(
            jnp.transpose(accum / total[..., None], (0, 2, 1, 3)).reshape(
                groups, rows, heads_count * size
            )
        )
        logsums.append(maximum + jnp.log(total))
    return (tuple(attended), tuple(logsums))


def visit_one(query, dout, logsum, delta, key, value, query_rows, key_rows, info):
    length, grid, bias_full = info
    groups, count_keys, width = key.shape
    scale = float(width // HEADS) ** (-0.5)
    scores, allowed, select = block_scores(query, key, query_rows, key_rows, length, bias_full)
    allowed = allowed_mask(allowed, key_rows, length, grid)
    probs = jnp.where(allowed[None, None], jnp.exp(scores - logsum[..., None]), 0.0)
    dout_heads = to_heads(dout, HEADS)
    dprobs = jnp.einsum(
        "gqhd,gkhd->ghqk", dout_heads, to_heads(value, HEADS), preferred_element_type=jnp.float32
    )
    dscores = (probs * (dprobs - delta[..., None])).astype(jnp.bfloat16)
    dq_term = scale * jnp.einsum(
        "ghqk,gkhd->gqhd", dscores, to_heads(key, HEADS), preferred_element_type=jnp.float32
    )
    dkey_term = jnp.einsum(
        "ghqk,gqhd->gkhd", dscores, to_heads(query, HEADS), preferred_element_type=jnp.float32
    )
    dvalue_term = jnp.einsum(
        "ghqk,gqhd->gkhd",
        probs.astype(jnp.bfloat16),
        dout_heads,
        preferred_element_type=jnp.float32,
    )
    summed = jnp.sum(dscores.astype(jnp.float32), axis=0)
    bias_term = jnp.einsum("hqk,kl->hql", summed, select, precision=lax.Precision.HIGHEST)
    return (
        dq_term,
        scale * dkey_term.reshape(groups, count_keys, width),
        dvalue_term.reshape(groups, count_keys, width),
        bias_term,
    )


def visit_cycle(carry, queries, douts, logsums, deltas, moving, members, query_rows, source, info):
    dqueries, dpair, bias_grads = carry
    dqueries = list(dqueries)
    bias_grads = list(bias_grads)
    key_pieces = []
    value_pieces = []
    for which, offset, rows in members:
        key = moving[0][:, offset : offset + rows]
        value = moving[1][:, offset : offset + rows]
        dq_term, dk_term, dv_term, bias_term = visit_one(
            queries[which],
            douts[which],
            logsums[which],
            deltas[which],
            key,
            value,
            query_rows[which],
            key_rows_of(source, rows),
            info[which],
        )
        dqueries[which] = dqueries[which] + dq_term
        key_pieces.append(dk_term)
        value_pieces.append(dv_term)
        bias_grads[which] = bias_grads[which] + bias_term
    new_pair = (
        dpair[0] + jnp.concatenate(key_pieces, axis=1),
        dpair[1] + jnp.concatenate(value_pieces, axis=1),
    )
    return (tuple(dqueries), new_pair, tuple(bias_grads))


def send_grads(dpair):
    return tuple(shifted((dpair[0], dpair[1]), "seq", 1))


def cycle_backward(queries, douts, logsums, deltas, cycle_pair, members, query_rows, info, start):
    position = lax.axis_index("seq")
    count = lax.axis_size("seq")
    dpair = tuple((jnp.zeros(item.shape, jnp.float32) for item in cycle_pair))

    def turn(step, state):
        carry, moving = state
        carry = visit_cycle(
            carry,
            queries,
            douts,
            logsums,
            deltas,
            moving,
            members,
            query_rows,
            (position - step) % count,
            info,
        )
        moving = tuple(shifted((moving[0], moving[1]), "seq", 1))
        return ((carry[0], send_grads(carry[1]), carry[2]), moving)

    carry, moving = lax.fori_loop(0, count - 1, turn, ((start[0], dpair, start[1]), cycle_pair))
    carry = visit_cycle(
        carry,
        queries,
        douts,
        logsums,
        deltas,
        moving,
        members,
        query_rows,
        (position - count + 1) % count,
        info,
    )
    return (carry[0], send_grads(carry[1]), carry[2])


def general_device(
    small_in,
    large_in,
    small_cot,
    large_cot,
    first_gain,
    first_bias,
    query_weight,
    query_bias,
    key_weight,
    value_weight,
    value_bias,
    out_weight,
    out_bias,
    attend_scale,
    second_gain,
    second_bias,
    up_weight,
    up_bias,
    down_weight,
    down_bias,
    feed_scale,
    rel_table,
):
    groups, small_rows, width = small_in.shape
    large_rows = large_in.shape[1]
    all_rows = small_rows + large_rows
    position = lax.axis_index("seq")
    query_rows = (
        position * small_rows + jnp.arange(small_rows, dtype=jnp.int32),
        position * large_rows + jnp.arange(large_rows, dtype=jnp.int32),
    )
    small_places = query_rows[0] % SLEN
    large_places = query_rows[1] % LLEN

    def make_biases(table):
        return (
            position_bias(table, small_places, SLEN, SGRID),
            position_bias(table, large_places, LLEN, LGRID),
        )

    biases, bias_back = jax.vjp(make_biases, rel_table)
    info = ((SLEN, SGRID, biases[0]), (LLEN, LGRID, biases[1]))
    valid_rows = jnp.concatenate(
        [small_places < SGRID * SGRID + 1, large_places < LGRID * LGRID + 1]
    )
    valid_flat = jnp.broadcast_to(valid_rows[None, :], (groups, all_rows)).reshape(-1)
    w_query, w_key, w_value, w_out, w_up, w_down = (
        lax.all_gather(query_weight, "img", axis=0, tiled=True),
        lax.all_gather(key_weight, "img", axis=0, tiled=True),
        lax.all_gather(value_weight, "img", axis=0, tiled=True),
        lax.all_gather(out_weight, "img", axis=0, tiled=True),
        lax.all_gather(up_weight, "img", axis=0, tiled=True),
        lax.all_gather(down_weight, "img", axis=0, tiled=True),
    )

    def split(rows_array):
        shaped = rows_array.reshape(groups, all_rows, -1)
        return (shaped[:, :small_rows], shaped[:, small_rows:])

    inputs = jnp.concatenate([small_in, large_in], axis=1).astype(jnp.float32).reshape(-1, width)
    hidden = layer_norm(inputs, first_gain, first_bias).astype(jnp.bfloat16)
    query = (matmul(hidden, w_query) + query_bias).astype(jnp.bfloat16)
    key = matmul(hidden, w_key).astype(jnp.bfloat16)
    value = (matmul(hidden, w_value) + value_bias).astype(jnp.bfloat16)
    queries = split(query)
    cycle_pair = (key.reshape(groups, all_rows, width), value.reshape(groups, all_rows, width))
    members = ((0, 0, small_rows), (1, small_rows, large_rows))
    attended, logsums = cycle_forward(queries, cycle_pair, members, query_rows, info)
    mixed = (
        jnp.concatenate([attended[0], attended[1]], axis=1).reshape(-1, width).astype(jnp.bfloat16)
    )
    branch = matmul(mixed, w_out) + out_bias
    residual = inputs + attend_scale * branch
    hidden2 = layer_norm(residual, second_gain, second_bias).astype(jnp.bfloat16)
    upper = matmul(hidden2, w_up) + up_bias
    active = jax.nn.gelu(upper, approximate=False).astype(jnp.bfloat16)
    lower = matmul(active, w_down) + down_bias
    output = jnp.where(valid_flat[:, None], residual + feed_scale * lower, 0.0).astype(jnp.bfloat16)
    small_out, large_out = split(output)
    upstream = (
        jnp.concatenate([small_cot, large_cot], axis=1).astype(jnp.float32).reshape(-1, width)
    )
    upstream = upstream * valid_flat[:, None].astype(jnp.float32)
    grad_feed_scale = jnp.sum(upstream * lower, axis=0)
    dlower = (upstream * feed_scale).astype(jnp.bfloat16)
    grad_down_bias = jnp.sum(dlower.astype(jnp.float32), axis=0)
    grad_down = jnp.einsum("rf,rd->fd", active, dlower, preferred_element_type=jnp.float32)
    dactive = jnp.einsum("rd,fd->rf", dlower, w_down, preferred_element_type=jnp.float32)
    unused, gelu_back = jax.vjp(lambda inner: jax.nn.gelu(inner, approximate=False), upper)
    dupper = gelu_back(dactive)[0].astype(jnp.bfloat16)
    grad_up_bias = jnp.sum(dupper.astype(jnp.float32), axis=0)
    grad_up = jnp.einsum("rd,rf->df", hidden2, dupper, preferred_element_type=jnp.float32)
    dhidden2 = jnp.einsum("rf,df->rd", dupper, w_up, preferred_element_type=jnp.float32)
    unused, second_back = jax.vjp(layer_norm, residual, second_gain, second_bias)
    dres_part, grad_second_gain, grad_second_bias = second_back(dhidden2)
    dresidual = upstream + dres_part
    grad_attend_scale = jnp.sum(dresidual * branch, axis=0)
    dbranch = (dresidual * attend_scale).astype(jnp.bfloat16)
    grad_out_bias = jnp.sum(dbranch.astype(jnp.float32), axis=0)
    grad_out = jnp.einsum("rd,re->de", mixed, dbranch, preferred_element_type=jnp.float32)
    dmixed = jnp.einsum("re,de->rd", dbranch, w_out, preferred_element_type=jnp.float32).astype(
        jnp.bfloat16
    )
    held, held_sums = cycle_forward(queries, cycle_pair, members, query_rows, info)
    douts = split(dmixed)
    deltas = tuple(
        (
            jnp.einsum(
                "gqhd,gqhd->ghq",
                to_heads(douts[which].astype(jnp.float32), HEADS),
                to_heads(held[which], HEADS),
            )
            for which in range(2)
        )
    )
    dq_start = tuple(
        (jnp.zeros(to_heads(queries[which], HEADS).shape, jnp.float32) for which in range(2))
    )
    bias_start = tuple((jnp.zeros(item.shape, jnp.float32) for item in biases))
    dqueries, dpair, bias_grads = cycle_backward(
        queries,
        douts,
        held_sums,
        deltas,
        cycle_pair,
        members,
        query_rows,
        info,
        (dq_start, bias_start),
    )
    table_grad = bias_back(bias_grads)[0]
    dquery = jnp.concatenate(
        [
            dqueries[0].reshape(groups, small_rows, width),
            dqueries[1].reshape(groups, large_rows, width),
        ],
        axis=1,
    )
    dquery = dquery.reshape(-1, width).astype(jnp.bfloat16)
    dkey = dpair[0].reshape(-1, width).astype(jnp.bfloat16)
    dvalue = dpair[1].reshape(-1, width).astype(jnp.bfloat16)
    grad_query_bias = jnp.sum(dquery.astype(jnp.float32), axis=0)
    grad_value_bias = jnp.sum(dvalue.astype(jnp.float32), axis=0)
    grad_query = jnp.einsum("rd,re->de", hidden, dquery, preferred_element_type=jnp.float32)
    grad_key = jnp.einsum("rd,re->de", hidden, dkey, preferred_element_type=jnp.float32)
    grad_value = jnp.einsum("rd,re->de", hidden, dvalue, preferred_element_type=jnp.float32)
    dhidden = (
        jnp.einsum("re,de->rd", dquery, w_query, preferred_element_type=jnp.float32)
        + jnp.einsum("re,de->rd", dkey, w_key, preferred_element_type=jnp.float32)
        + jnp.einsum("re,de->rd", dvalue, w_value, preferred_element_type=jnp.float32)
    )
    unused, first_back = jax.vjp(layer_norm, inputs, first_gain, first_bias)
    dinput_part, grad_first_gain, grad_first_bias = first_back(dhidden)
    dinputs = (dresidual + dinput_part).astype(jnp.bfloat16)
    small_grad, large_grad = split(dinputs)
    shares = (
        lax.psum_scatter(grad_query, "img", scatter_dimension=0, tiled=True),
        lax.psum_scatter(grad_key, "img", scatter_dimension=0, tiled=True),
        lax.psum_scatter(grad_value, "img", scatter_dimension=0, tiled=True),
        lax.psum_scatter(grad_out, "img", scatter_dimension=0, tiled=True),
        lax.psum_scatter(grad_up, "img", scatter_dimension=0, tiled=True),
        lax.psum_scatter(grad_down, "img", scatter_dimension=0, tiled=True),
    )
    shares = lax.psum((shares[0], shares[1], shares[2], shares[3], shares[4], shares[5]), "seq")
    smalls = lax.psum(
        (
            grad_first_gain,
            grad_first_bias,
            grad_query_bias,
            grad_value_bias,
            grad_out_bias,
            grad_attend_scale,
            grad_second_gain,
            grad_second_bias,
            grad_up_bias,
            grad_down_bias,
            grad_feed_scale,
            table_grad,
        ),
        ("img", "seq"),
    )
    return (
        small_out,
        large_out,
        small_grad,
        large_grad,
        smalls[0],
        smalls[1],
        shares[0],
        smalls[2],
        shares[1],
        shares[2],
        smalls[3],
        shares[3],
        smalls[4],
        smalls[5],
        smalls[6],
        smalls[7],
        shares[4],
        smalls[8],
        shares[5],
        smalls[9],
        smalls[10],
        smalls[11],
    )


def image_device(
    small_in,
    large_in,
    small_cot,
    large_cot,
    first_gain,
    first_bias,
    query_weight,
    query_bias,
    key_weight,
    value_weight,
    value_bias,
    out_weight,
    out_bias,
    attend_scale,
    second_gain,
    second_bias,
    up_weight,
    up_bias,
    down_weight,
    down_bias,
    feed_scale,
    rel_table,
):
    groups, small_rows, width = small_in.shape
    n_small = groups * small_rows // SLEN

    x, cot, qkv, turned, w_qkv, w_mid, w_down, attended, out_wide, *probs = run_begin(
        (query_weight, key_weight, value_weight, out_weight, up_weight, down_weight),
        (
            small_in.reshape(n_small, SLEN, width),
            large_in,
            small_cot.reshape(n_small, SLEN, width),
            large_cot,
        ),
        rel_table,
        (first_gain, first_bias, query_bias, value_bias),
        1,
    )
    w_mid, w_down = (w.reshape(-1, w.shape[-1]) for w in (w_mid, w_down))
    small_out, large_out, dresidual, dattended, feed_grads, g_mid, g_down = run_feed(
        x,
        attended,
        cot,
        w_mid,
        w_down,
        (out_bias, attend_scale, second_gain, second_bias, down_bias, feed_scale, up_bias),
        n_small,
        3,
    )
    small_grad, large_grad, *made = run_end(
        qkv,
        dattended,
        out_wide,
        probs,
        [g_mid, g_down],
        [x, turned, w_qkv, dresidual],
        feed_grads,
        first_gain,
        n_small,
        2,
    )
    grads = run_finish(made[4:], made[:4], rel_table.shape[1])
    small_out, small_grad = (v.reshape(groups, small_rows, width) for v in (small_out, small_grad))
    return (small_out, large_out, small_grad, large_grad, *grads)


def per_device(*args):
    groups, small_rows, unused = args[0].shape
    if lax.axis_size("seq") == 2 and groups == 2 and small_rows % SLEN == 0:
        return image_device(*args)
    return general_device(*args)


def solution(mesh):
    return jax.shard_map(
        per_device,
        mesh=mesh,
        in_specs=(
            P("img", "seq", None),
            P("img", "seq", None),
            P("img", "seq", None),
            P("img", "seq", None),
            P(),
            P(),
            P("img", None),
            P(),
            P("img", None),
            P("img", None),
            P(),
            P("img", None),
            P(),
            P(),
            P(),
            P(),
            P("img", None),
            P(),
            P("img", None),
            P(),
            P(),
            P(),
        ),
        out_specs=(
            P("img", "seq", None),
            P("img", "seq", None),
            P("img", "seq", None),
            P("img", "seq", None),
            P(),
            P(),
            P("img", None),
            P(),
            P("img", None),
            P("img", None),
            P(),
            P("img", None),
            P(),
            P(),
            P(),
            P(),
            P("img", None),
            P(),
            P("img", None),
            P(),
            P(),
            P(),
        ),
        check_vma=False,
    )
```
